32 devices in a mesh: rep: 2 (over x), fsdp: 16 (over z, y, core).
Axes of the slice: x: 2, y: 2, z: 4, core: 2. Of those that a mesh axis runs over, the one named last changes fastest.
Arguments:
- mel_frames: bfloat16 [32, 80, 384], P(('rep', 'fsdp')), may hold values from -6 to 6
- text_ids: int32 [32, 128], P(('rep', 'fsdp')), may hold values from 0 to 51967
- text_lengths: int32 [32], replicated, may hold values from 16 to 128, as said below
- language: int32 [32], P(('rep', 'fsdp')), may hold values from 0 to 98
- vocab_mask: int32 [51968], replicated, may hold values 0 or 1
- step_count: int32 [1], replicated, may hold values from 2 to 20
- matrices: float32 [768, 24176], P('fsdp')
- matrix_moment: float32 [768, 24176], P('fsdp'), may hold values from -0.00021362305 to 0.00021362305
- matrix_square: float32 [768, 24176], P('fsdp'), may hold values from 8.546209e-12 to 1.3673934e-10
- embedding: float32 [51968, 768], P('fsdp'), may hold values from -0.4375 to 0.4375
- embed_moment: float32 [51968, 768], P('fsdp'), may hold values from -0.00021362305 to 0.00021362305
- embed_square: float32 [51968, 768], P('fsdp'), may hold values from 8.546209e-12 to 1.3673934e-10
- vectors: float32 [768, 35], P('fsdp')
- vector_moment: float32 [768, 35], P('fsdp'), may hold values from -0.00021362305 to 0.00021362305
- vector_square: float32 [768, 35], P('fsdp'), may hold values from 8.546209e-12 to 1.3673934e-10
Outputs:
- mean_loss: float32 [], replicated
- nonfinite: int32 [], replicated
- gradient_norm: float32 [], replicated
- group_norms: float32 [16, 2], replicated
- updated_matrices: float32 [768, 24176], P('fsdp')
- moment_matrices: float32 [768, 24176], P('fsdp')
- square_matrices: float32 [768, 24176], P('fsdp')
- updated_embedding: float32 [51968, 768], P('fsdp')
- moment_embedding: float32 [51968, 768], P('fsdp')
- square_embedding: float32 [51968, 768], P('fsdp')
- updated_vectors: float32 [768, 35], P('fsdp')
- moment_vectors: float32 [768, 35], P('fsdp')
- square_vectors: float32 [768, 35], P('fsdp')
The draws below stay inside these ranges and needn't reach their ends.
Inputs may be any that keep to these rules, and one draw needn't show every extreme that they name: `text_lengths`: some clip has exactly 128 counted positions.
All inputs are finite; a program needn't handle non-finite values.
Results may differ from the reference program's by a relative error of at most 0.0015.
The reference program's roundings to bfloat16 on the way count: a program that leaves them out, or rounds other values in their place, can miss the bound.
Values may be sent and summed in bfloat16 or wider, within the bound.
A program may use at most 448 MiB of HBM per device.

```python
import math
import jax
import jax.numpy as jnp
import numpy as np
from jax import lax

D = 768
H = 12
HD = 64
FF = 3072
VOCAB = 51968
MELS = 80
NLANG = 99
FR = 192
TLEN = 128
LMIN = 16
LANGTOK = 50259
NVEC = 35
CLIPS = 32
TOTC = 24176
PARAMS = 58505472


GAIN_COLUMNS = (2, 7, 14, 16, 21, 26, 33)


def column_spreads():
    return [(3 * D, D ** (-0.5)), (D, 6.0 * D ** (-0.5)), (FF, D ** (-0.5)), (FF, FF ** (-0.5)), (3 * D, D ** (-0.5)), (D, 3.0 * D ** (-0.5)), (D, D ** (-0.5)), (2 * D, D ** (-0.5)), (D, 6.0 * D ** (-0.5)), (FF, D ** (-0.5)), (FF, FF ** (-0.5)), (3 * D, (3 * D) ** (-0.5)), (3 * MELS, (3 * MELS) ** (-0.5)), (TLEN, 0.1)]


def draw_matrices(key, part):
    spreads = jnp.concatenate([jnp.full((extent,), spread, jnp.float32) for extent, spread in column_spreads()])
    return jax.random.normal(key, (D, TOTC), jnp.float32) * spreads[None, :]


def draw_vectors(key, part):
    uniform_noise = jax.random.uniform(key, (D, NVEC), jnp.float32, -1.0, 1.0)
    column = jnp.arange(NVEC)
    is_gain = jnp.any(column[None, :] == jnp.array(GAIN_COLUMNS)[:, None], axis=0)
    return jnp.where(is_gain[None, :], 1.0 + 0.3 * uniform_noise, 0.5 * uniform_noise)


def draw_text_lengths(key, part):
    lengths = jax.random.randint(key, (CLIPS,), LMIN, TLEN + 1)
    chosen = jax.random.randint(jax.random.fold_in(key, 7), (), 0, CLIPS)
    return jnp.where(jnp.arange(CLIPS) == chosen, TLEN, lengths).astype(jnp.int32)


def place_ends(drawn, stream_key, low, high):
    spot = [jax.random.randint(jax.random.fold_in(stream_key, axis), (), 0, length) for axis, length in enumerate(drawn.shape)]
    longest = drawn.shape.index(max(drawn.shape))
    neighbour = spot[:longest] + [(spot[longest] + 1) % drawn.shape[longest]] + spot[longest + 1:]
    return drawn.at[tuple(spot)].set(low).at[tuple(neighbour)].set(high)


def block_levels(own_key, shape, shards, smallest, high):
    factor_of, own = 1.0, jax.random.fold_in(own_key, 6)
    for dim, blocks in shards:
        heights = jnp.exp(jax.random.uniform(jax.random.fold_in(own, dim), (blocks,), jnp.float32, smallest / len(shards), high / len(shards)))
        factor_of = factor_of * jnp.repeat(heights, shape[dim] // blocks).reshape([-1 if axis == dim else 1 for axis in range(len(shape))])
    return factor_of


def cumulative_ranks(number_of, lean):
    loads = [(1 << 20) // math.isqrt(standing ** lean) + 1 for standing in range(1, number_of + 1)]
    scale = 1 + sum(loads) // (1 << 30)
    return np.cumsum(np.array([max(1, weight // scale) for weight in loads]))


def ranked(key, dims, amount, slope):
    grid = cumulative_ranks(amount, slope)
    pick = jax.random.randint(jax.random.fold_in(key, 1), dims, 0, int(grid[amount - 1]))
    standing = jnp.searchsorted(jnp.asarray(grid, jnp.int32), pick, side="right")
    return jax.random.permutation(jax.random.fold_in(key, 2), amount)[standing].astype(jnp.int32)


def scatter_about(key, dims, scale, most, pieces=(), held_as=jnp.bfloat16):
    level = block_levels(key, dims, pieces, -0.22, 0.18) if pieces else 1.0
    values = jax.random.normal(key, dims, jnp.float32) * scale * level
    return jnp.minimum(jnp.maximum(values, -most), most).astype(held_as)


def setup_inputs(seed: int = 0) -> dict:
    key_list = jax.random.split(jax.random.key(seed), 16)
    mel_frames = scatter_about(key_list[0], (CLIPS, MELS, 2 * FR), 1.0, 6.0, ((0, 32),))
    text_ids = place_ends(ranked(key_list[1], (CLIPS, TLEN), VOCAB, 2), jax.random.fold_in(key_list[1], 3), 0, VOCAB - 1).astype(jnp.int32)
    text_lengths = draw_text_lengths(jax.random.fold_in(key_list[15], 71), 0)
    language = place_ends(jax.random.randint(key_list[3], (CLIPS,), 0, NLANG), jax.random.fold_in(key_list[3], 1), 0, NLANG - 1).astype(jnp.int32)
    vocab_mask = place_ends((jax.random.randint(key_list[4], (VOCAB,), 0, 8) < 7).astype(jnp.int32), jax.random.fold_in(key_list[4], 1), 0, 1)
    step_count = jax.random.randint(key_list[5], (1,), 2, 21).astype(jnp.int32)
    matrices = draw_matrices(jax.random.fold_in(key_list[15], 71), 0)
    matrix_moment = scatter_about(key_list[7], (D, TOTC), (0.11 / PARAMS ** 0.5), 0.00021362305, ((0, 16),), jnp.float32)
    matrix_square = jnp.clip(jnp.exp(math.log(1.3673934207147909e-10) - 2.7725887 * jax.random.uniform(key_list[8], (D, TOTC), jnp.float32) ** block_levels(key_list[8], (D, TOTC), ((0, 16),), -0.2, 0.2)), 8.546208879467443e-12, 1.3673934207147909e-10)
    embedding = scatter_about(key_list[9], (VOCAB, D), (D // 4) ** -0.5, 0.4375, ((0, 16),), jnp.float32)
    embed_moment = scatter_about(key_list[10], (VOCAB, D), (0.11 / PARAMS ** 0.5), 0.00021362305, ((0, 16),), jnp.float32)
    embed_square = jnp.clip(jnp.exp(math.log(1.3673934207147909e-10) - 2.7725887 * jax.random.uniform(key_list[11], (VOCAB, D), jnp.float32) ** block_levels(key_list[11], (VOCAB, D), ((0, 16),), -0.2, 0.2)), 8.546208879467443e-12, 1.3673934207147909e-10)
    vectors = draw_vectors(jax.random.fold_in(key_list[15], 71), 0)
    vector_moment = scatter_about(key_list[13], (D, NVEC), (0.11 / PARAMS ** 0.5), 0.00021362305, ((0, 16),), jnp.float32)
    vector_square = jnp.clip(jnp.exp(math.log(1.3673934207147909e-10) - 2.7725887 * jax.random.uniform(key_list[14], (D, NVEC), jnp.float32) ** block_levels(key_list[14], (D, NVEC), ((0, 16),), -0.2, 0.2)), 8.546208879467443e-12, 1.3673934207147909e-10)
    return dict(mel_frames=mel_frames, text_ids=text_ids, text_lengths=text_lengths, language=language, vocab_mask=vocab_mask, step_count=step_count, matrices=matrices, matrix_moment=matrix_moment, matrix_square=matrix_square, embedding=embedding, embed_moment=embed_moment, embed_square=embed_square, vectors=vectors, vector_moment=vector_moment, vector_square=vector_square)


HIGH = lax.Precision.HIGHEST
LN_EPS = 1e-05
SMOOTH = 0.1
CLIP_AT = 1.0
BETA_ONE = 0.9
BETA_TWO = 0.999
ADAM_EPS = 1e-06
DECAY = 0.01
RATE = 0.5
NEG_BIG = -1e+30
ENC_SLOTS = {'norm_gain': 2, 'norm_bias': 3, 'query_bias': 4, 'value_bias': 5, 'out_bias': 6, 'mlp_gain': 7, 'mlp_bias': 8, 'up_bias': 9, 'down_bias': 13, 'final_gain': 14, 'final_bias': 15}
DEC_SLOTS = {'norm_gain': 16, 'norm_bias': 17, 'query_bias': 18, 'value_bias': 19, 'out_bias': 20, 'cross_gain': 21, 'cross_bias': 22, 'xquery_bias': 23, 'xvalue_bias': 24, 'xout_bias': 25, 'mlp_gain': 26, 'mlp_bias': 27, 'up_bias': 28, 'down_bias': 32, 'final_gain': 33, 'final_bias': 34}

@jax.custom_vjp
def low(v):
    return lax.optimization_barrier(v.astype(jnp.bfloat16)).astype(jnp.float32)

@jax.custom_vjp
def low_back(v):
    return v

def low_keep(v):
    return (low(v), None)

def low_pass(kept, grad):
    return (grad,)

def back_keep(v):
    return (v, None)

def back_low(kept, grad):
    return (low(grad),)
low.defvjp(low_keep, low_pass)
low_back.defvjp(back_keep, back_low)

def layout(width, hidden, mels, text_len):
    names = ('e_qkv', 'e_out', 'e_up', 'e_down', 'd_qkv', 'd_out', 'x_query', 'x_keyval', 'x_out', 'd_up', 'd_down', 'conv_two', 'conv_one', 'dec_pos')
    widths = (3 * width, width, hidden, hidden, 3 * width, width, width, 2 * width, width, hidden, hidden, 3 * width, 3 * mels, text_len)
    bounds = {}
    offset = 0
    for piece_name, extent in zip(names, widths):
        bounds[piece_name] = (offset, offset + extent)
        offset = offset + extent
    return (names, bounds)

def columns_of(weights, bounds, piece_name):
    span_start, span_stop = bounds[piece_name]
    return weights[:, span_start:span_stop]

def sinusoid(length, width):
    halfway = width // 2
    increment = jnp.log(10000.0) / (halfway - 1)
    rates = jnp.exp(-increment * jnp.arange(halfway, dtype=jnp.float32))
    angles = jnp.arange(length, dtype=jnp.float32)[:, None] * rates[None, :]
    return jnp.concatenate([jnp.sin(angles), jnp.cos(angles)], axis=1)

def layer_norm(inputs, gain, offset):
    average = lax.optimization_barrier(jnp.mean(inputs, axis=-1, keepdims=True))
    centred = inputs - average
    spread = lax.optimization_barrier(jnp.mean(centred * centred, axis=-1, keepdims=True))
    return centred * lax.rsqrt(spread + LN_EPS) * gain + offset

def softmax_rows(scores):
    row_top = lax.optimization_barrier(jnp.max(scores, axis=-1, keepdims=True))
    log_total = row_top + jnp.log(lax.optimization_barrier(jnp.sum(jnp.exp(scores - row_top), axis=-1, keepdims=True)))
    return jnp.exp(scores - log_total)

def matmul(inputs, weight):
    return low_back(jnp.dot(low(inputs), weight, precision=HIGH))

def matmul_t(inputs, weight):
    return low_back(jnp.dot(low(inputs), weight.T, precision=HIGH))

def attention(queries, keys, values, causal):
    length = queries.shape[0]
    query_heads = low(queries).reshape(length, H, HD)
    key_heads = low(keys).reshape(keys.shape[0], H, HD)
    value_heads = low(values).reshape(values.shape[0], H, HD)
    scores = low_back(jnp.einsum('qhd,khd->hqk', query_heads, key_heads, precision=HIGH)) * HD ** (-0.5)
    if causal:
        rows = lax.broadcasted_iota(jnp.int32, scores.shape, 1)
        cols = lax.broadcasted_iota(jnp.int32, scores.shape, 2)
        scores = jnp.where(rows >= cols, scores, NEG_BIG)
    weights = softmax_rows(scores)
    attended = low_back(jnp.einsum('hqk,khd->qhd', low(weights), value_heads, precision=HIGH))
    return attended.reshape(length, H * HD)

def self_attend(stream, weights, small_params, slots, bounds, qkv_name, out_name, causal):
    normed = layer_norm(stream, small_params[:, slots['norm_gain']], small_params[:, slots['norm_bias']])
    projected = matmul(normed, columns_of(weights, bounds, qkv_name))
    queries = projected[:, :D] + small_params[:, slots['query_bias']]
    keys = projected[:, D:2 * D]
    values = projected[:, 2 * D:] + small_params[:, slots['value_bias']]
    attended = attention(queries, keys, values, causal)
    return stream + matmul(attended, columns_of(weights, bounds, out_name)) + small_params[:, slots['out_bias']]

def feed_forward(stream, weights, small_params, slots, bounds, up_name, down_name):
    normed = layer_norm(stream, small_params[:, slots['mlp_gain']], small_params[:, slots['mlp_bias']])
    up_bias = small_params[:, slots['up_bias']:slots['up_bias'] + 4].T.reshape(-1)
    active = jax.nn.gelu(matmul(normed, columns_of(weights, bounds, up_name)) + up_bias, approximate=False)
    return stream + matmul_t(active, columns_of(weights, bounds, down_name)) + small_params[:, slots['down_bias']]

def encode(mel_clip, weights, small_params, bounds):
    frames_in = mel_clip.shape[1]
    padded = jnp.pad(mel_clip, ((0, 0), (1, 1)))
    columns = jnp.concatenate([padded[:, tap_index:tap_index + frames_in].T for tap_index in range(3)], axis=1)
    first_act = jax.nn.gelu(matmul_t(columns, columns_of(weights, bounds, 'conv_one')) + small_params[:, 0], approximate=False)
    shifted = jnp.pad(low(first_act), ((1, 1), (0, 0)))
    conv_start = bounds['conv_two'][0]
    conv_sum = jnp.dot(shifted[0:frames_in:2], weights[:, conv_start:conv_start + D], precision=HIGH)
    for tap_index in range(1, 3):
        tap_weight = weights[:, conv_start + tap_index * D:conv_start + (tap_index + 1) * D]
        conv_sum = conv_sum + jnp.dot(shifted[tap_index:tap_index + frames_in:2], tap_weight, precision=HIGH)
    stream = jax.nn.gelu(low_back(conv_sum) + small_params[:, 1], approximate=False) + sinusoid(frames_in // 2, D)
    stream = self_attend(stream, weights, small_params, ENC_SLOTS, bounds, 'e_qkv', 'e_out', False)
    stream = feed_forward(stream, weights, small_params, ENC_SLOTS, bounds, 'e_up', 'e_down')
    return layer_norm(stream, small_params[:, ENC_SLOTS['final_gain']], small_params[:, ENC_SLOTS['final_bias']])

def decode(ids_clip, memory, weights, table, small_params, bounds):
    stream = low_back(jnp.take(table, ids_clip, axis=0)) + columns_of(weights, bounds, 'dec_pos').T
    stream = self_attend(stream, weights, small_params, DEC_SLOTS, bounds, 'd_qkv', 'd_out', True)
    normed = layer_norm(stream, small_params[:, DEC_SLOTS['cross_gain']], small_params[:, DEC_SLOTS['cross_bias']])
    queries = matmul(normed, columns_of(weights, bounds, 'x_query')) + small_params[:, DEC_SLOTS['xquery_bias']]
    keyval = matmul(memory, columns_of(weights, bounds, 'x_keyval'))
    values = keyval[:, D:] + small_params[:, DEC_SLOTS['xvalue_bias']]
    attended = attention(queries, keyval[:, :D], values, False)
    stream = stream + matmul(attended, columns_of(weights, bounds, 'x_out')) + small_params[:, DEC_SLOTS['xout_bias']]
    stream = feed_forward(stream, weights, small_params, DEC_SLOTS, bounds, 'd_up', 'd_down')
    return layer_norm(stream, small_params[:, DEC_SLOTS['final_gain']], small_params[:, DEC_SLOTS['final_bias']])

def clip_loss(weights, table, small_params, vocab_keep, vocab_count, mel_clip, ids_clip, target_clip, length):
    names, bounds = layout(D, FF, MELS, TLEN)
    memory = encode(mel_clip, weights, small_params, bounds)
    hidden = decode(ids_clip, memory, weights, table, small_params, bounds)
    logits = matmul_t(hidden, table)
    masked = jnp.where(vocab_keep[None, :], logits, NEG_BIG)
    row_top = lax.optimization_barrier(jnp.max(masked, axis=1, keepdims=True))
    log_total = row_top[:, 0] + jnp.log(lax.optimization_barrier(jnp.sum(jnp.where(vocab_keep[None, :], jnp.exp(masked - row_top), 0.0), axis=1)))
    target_logit = jnp.take_along_axis(logits, target_clip[:, None], axis=1)[:, 0]
    logit_mean = lax.optimization_barrier(jnp.sum(jnp.where(vocab_keep[None, :], logits, 0.0), axis=1)) / vocab_count
    entropy = log_total - (1.0 - SMOOTH) * target_logit - SMOOTH * logit_mean
    counted = jnp.arange(TLEN) < length
    return jnp.sum(jnp.where(counted, entropy, 0.0))

def moments(weight, moment, square, gradient, factor, first_fix, second_fix):
    scaled = gradient * factor
    new_moment = BETA_ONE * moment + (1.0 - BETA_ONE) * scaled
    new_square = BETA_TWO * square + (1.0 - BETA_TWO) * scaled * scaled
    update = new_moment / first_fix / (jnp.sqrt(new_square / second_fix) + ADAM_EPS) + DECAY * weight
    return (new_moment, new_square, update)

def group_squares(mat_part, embed_part, vec_part, bounds, names):
    parts = [jnp.sum(columns_of(mat_part, bounds, piece_name) ** 2) for piece_name in names]
    parts = parts + [jnp.sum(embed_part * embed_part), jnp.sum(vec_part * vec_part)]
    return jnp.stack(parts)

def reference(mel_frames, text_ids, text_lengths, language, vocab_mask, step_count, matrices, matrix_moment, matrix_square, embedding, embed_moment, embed_square, vectors, vector_moment, vector_square):
    names, bounds = layout(D, FF, MELS, TLEN)
    inputs_ids = jnp.concatenate([(LANGTOK + language)[:, None], text_ids[:, :-1]], axis=1).astype(jnp.int32)
    vocab_keep = vocab_mask == 1
    vocab_count = jnp.sum(vocab_mask).astype(jnp.float32)
    mel_float = mel_frames.astype(jnp.float32)

    def total_loss(weight_all, embed_all, vector_all):
        weights = low(weight_all)
        table = low(embed_all)
        small_params = low(vector_all)
        counted = jax.checkpoint(clip_loss)

        def one_clip(carry, clip):
            return (carry + counted(weights, table, small_params, vocab_keep, vocab_count, clip[0], clip[1], clip[2], clip[3]), None)
        total, _ = lax.scan(one_clip, jnp.float32(0.0), (mel_float, inputs_ids, text_ids, text_lengths))
        return total
    loss_sum, pull = jax.vjp(total_loss, matrices, embedding, vectors)
    mat_grad, embed_grad, vec_grad = pull(jnp.ones((), jnp.float32))
    nonfinite = jnp.sum(jnp.logical_not(jnp.isfinite(mat_grad))).astype(jnp.int32) + jnp.sum(jnp.logical_not(jnp.isfinite(embed_grad))).astype(jnp.int32) + jnp.sum(jnp.logical_not(jnp.isfinite(vec_grad))).astype(jnp.int32)
    gradient_norm = jnp.sqrt(jnp.sum(mat_grad * mat_grad) + jnp.sum(vec_grad * vec_grad) + jnp.sum(embed_grad * embed_grad))
    factor = CLIP_AT / jnp.maximum(gradient_norm, CLIP_AT)
    steps = step_count[0].astype(jnp.float32)
    first_fix = 1.0 - jnp.power(jnp.float32(BETA_ONE), steps)
    second_fix = 1.0 - jnp.power(jnp.float32(BETA_TWO), steps)
    mat_moment, mat_square, mat_update = moments(matrices, matrix_moment, matrix_square, mat_grad, factor, first_fix, second_fix)
    emb_moment, emb_square, emb_update = moments(embedding, embed_moment, embed_square, embed_grad, factor, first_fix, second_fix)
    vec_moment, vec_square, vec_update = moments(vectors, vector_moment, vector_square, vec_grad, factor, first_fix, second_fix)
    weight_norms = jnp.sqrt(group_squares(matrices, embedding, vectors, bounds, names))
    update_norms = jnp.sqrt(group_squares(mat_update, emb_update, vec_update, bounds, names))
    ratio = weight_norms / update_norms
    ratio_columns = jnp.concatenate([jnp.full((bounds[piece_name][1] - bounds[piece_name][0],), 1.0, jnp.float32) * ratio[position] for position, piece_name in enumerate(names)])
    new_matrices = matrices - RATE * ratio_columns[None, :] * mat_update
    new_embedding = embedding - RATE * ratio[len(names)] * emb_update
    new_vectors = vectors - RATE * ratio[len(names) + 1] * vec_update
    mean_loss = loss_sum / jnp.sum(text_lengths).astype(jnp.float32)
    group_norms = jnp.stack([weight_norms, update_norms], axis=1)
    return (mean_loss, nonfinite, gradient_norm, group_norms, new_matrices, mat_moment, mat_square, new_embedding, emb_moment, emb_square, new_vectors, vec_moment, vec_square)
```

```python
import jax
import jax.numpy as jnp
from jax import lax
from jax.sharding import PartitionSpec as P

D = 768
H = 12
HD = 64
FF = 3072
MELS = 80
TLEN = 128
LANGTOK = 50259
NVEC = 35


LN_EPS = 1e-05
SMOOTH = 0.1
CLIP_AT = 1.0
BETA_ONE = 0.9
BETA_TWO = 0.999
ADAM_EPS = 1e-06
DECAY = 0.01
RATE = 0.5
NEG_BIG = -1e30
ENC_SLOTS = {
    "norm_gain": 2,
    "norm_bias": 3,
    "query_bias": 4,
    "value_bias": 5,
    "out_bias": 6,
    "mlp_gain": 7,
    "mlp_bias": 8,
    "up_bias": 9,
    "down_bias": 13,
    "final_gain": 14,
    "final_bias": 15,
}
DEC_SLOTS = {
    "norm_gain": 16,
    "norm_bias": 17,
    "query_bias": 18,
    "value_bias": 19,
    "out_bias": 20,
    "cross_gain": 21,
    "cross_bias": 22,
    "xquery_bias": 23,
    "xvalue_bias": 24,
    "xout_bias": 25,
    "mlp_gain": 26,
    "mlp_bias": 27,
    "up_bias": 28,
    "down_bias": 32,
    "final_gain": 33,
    "final_bias": 34,
}


CORES = 2
LINE = 4


def mesh_shape():
    members = lax.axis_size("fsdp")
    return (lax.axis_size("rep"), LINE, members // (LINE * CORES), CORES)


def places():
    reps, line, side, cores = mesh_shape()
    index = lax.axis_index("fsdp")
    return (
        lax.axis_index("rep"),
        index // (side * cores),
        (index // cores) % side,
        index % cores,
    )


def send(values, move):
    reps, line, side, cores = mesh_shape()
    members = line * side * cores
    pairs = []
    for rep in range(reps):
        for far in range(line):
            for near in range(side):
                for core in range(cores):
                    target = move(rep, far, near, core)
                    if target is None:
                        continue
                    rep_to, far_to, near_to, core_to = target
                    pairs.append(
                        (
                            rep * members + (far * side + near) * cores + core,
                            rep_to * members + (far_to * side + near_to) * cores + core_to,
                        )
                    )
    return lax.ppermute(values, ("rep", "fsdp"), pairs)


def send_core(values):
    return send(values, lambda rep, far, near, core: (rep, far, near, 1 - core))


def send_rep(values, shift):
    reps = lax.axis_size("rep")
    return send(values, lambda rep, far, near, core: ((rep + shift) % reps, far, near, core))


def pick(values, index, axis):
    return lax.dynamic_index_in_dim(values, index, axis, keepdims=False)


def block(values, index, width):
    return lax.dynamic_slice_in_dim(values, index * width, width, axis=1)


def pool(narrows, wides):
    reps = lax.axis_size("rep")
    rep, _, _, core = places()
    tall = sum(part.shape[1] for part in narrows)
    spans = [part.shape[1] // reps for part in wides]
    got = []
    for shift in range(reps):
        parts = list(narrows) + [
            block(part, (rep + shift) % reps, span) for part, span in zip(wides, spans)
        ]
        joint = parts[0] if len(parts) == 1 else jnp.concatenate(parts, axis=1)
        got.append(send_rep(joint, shift) if shift else joint)
    joint = jnp.concatenate(got, axis=0)
    offsets = [tall + sum(spans[:position]) for position in range(len(spans))]

    def halves(side):
        parts = [joint[:, :tall]] if tall else []
        for offset, span in zip(offsets, spans):
            parts.append(block(joint[:, offset : offset + span], side, span // CORES))
        return parts[0] if len(parts) == 1 else jnp.concatenate(parts, axis=1)

    both = jnp.concatenate([halves(core), send_core(halves(1 - core))], axis=0)
    results = []
    offset = 0
    for part in narrows:
        results.append(both[:, offset : offset + part.shape[1]])
        offset = offset + part.shape[1]
    for span in spans:
        results.append(both[:, offset : offset + span // CORES])
        offset = offset + span // CORES
    return results


def pool_sum(values):
    reps = lax.axis_size("rep")
    rep, _, _, core = places()
    span = values.shape[1] // reps
    total = block(values, rep, span)
    for shift in range(1, reps):
        total = total + send_rep(block(values, (rep + shift) % reps, span), shift)
    return block(total, core, span // CORES) + send_core(
        block(total, 1 - core, span // CORES)
    )


def line_sum(values, axis, position, towards):
    length = values.shape[axis]
    if length == 1:
        return pick(values, 0, axis)
    if length == 2:
        return pick(values, position, axis) + towards(pick(values, 1 - position, axis), None)
    rising = None
    falling = None
    for step in range(1, length):
        up = pick(values, jnp.clip(length - step + position, 0, length - 1), axis)
        down = pick(values, jnp.clip(step + position - length, 0, length - 1), axis)
        if rising is not None:
            up = up + rising
            down = down + falling
        rising = towards(up, ("up", step))
        falling = towards(down, ("down", step))
    return pick(values, position, axis) + rising + falling


def stepper(length, along_far):
    def towards(values, way):
        def move(rep, far, near, core):
            here = far if along_far else near
            if way is None:
                there = 1 - here
            elif way[0] == "up":
                if way[1] < here + 1 or here + 1 >= length:
                    return None
                there = here + 1
            else:
                if way[1] < length - here or here == 0:
                    return None
                there = here - 1
            return (rep, there, near, core) if along_far else (rep, far, there, core)

        return send(values, move)

    return towards


def scatter_rows(pieces):
    reps, line, side, cores = mesh_shape()
    rep, far, near, core = places()
    rows = pieces[0].shape[0]
    own_rows = rows // (line * side * cores)
    joint = jnp.concatenate(
        [part.reshape(line, side, rows // (line * side), part.shape[1]) for part in pieces], axis=3
    )
    near_sum = line_sum(joint, 1, near, stepper(side, False))
    chip_rows = line_sum(near_sum, 0, far, stepper(line, True))
    return chip_rows.reshape(cores, own_rows, chip_rows.shape[1])


def in_order(stack, position):
    count = len(stack)
    joint = jnp.stack(stack)
    return jnp.stack([pick(joint, (position - place) % count, 0) for place in range(count)])


def whole_rows(pieces):
    reps = lax.axis_size("rep")
    rep, _, _, core = places()
    by_core = scatter_rows(pieces)
    cores_joint = in_order([pick(by_core, core, 0), send_core(pick(by_core, 1 - core, 0))], core)
    reps_joint = in_order(
        [cores_joint] + [send_rep(cores_joint, shift) for shift in range(1, reps)], rep
    )
    results = []
    offset = 0
    for part in pieces:
        span = part.shape[1]
        own = reps_joint[:, :, :, offset : offset + span]
        results.append(
            jnp.transpose(own, (2, 0, 1, 3)).reshape(own.shape[2], reps * CORES * span)
        )
        offset = offset + span
    return results


def summed_rows(values):
    reps = lax.axis_size("rep")
    _, _, _, core = places()
    total = values
    for shift in range(1, reps):
        total = total + send_rep(values, shift)
    total = total + send_core(total)
    return pick(scatter_rows([total]), core, 0)


def across_reps(values):
    reps = lax.axis_size("rep")
    _, _, _, core = places()
    half = values.shape[0] // CORES
    own_half = lax.dynamic_slice_in_dim(values, core * half, half, axis=0)
    results = [values]
    for shift in range(1, reps):
        got = send_rep(own_half, shift)
        both = in_order([got, send_core(got)], core)
        results.append(both.reshape(values.shape))
    return results


def layout(width, hidden, mels, text_len):
    names = (
        "e_qkv",
        "e_out",
        "e_up",
        "e_down",
        "d_qkv",
        "d_out",
        "x_query",
        "x_keyval",
        "x_out",
        "d_up",
        "d_down",
        "conv_two",
        "conv_one",
        "dec_pos",
    )
    widths = (
        3 * width,
        width,
        hidden,
        hidden,
        3 * width,
        width,
        width,
        2 * width,
        width,
        hidden,
        hidden,
        3 * width,
        3 * mels,
        text_len,
    )
    bounds = {}
    offset = 0
    for piece_name, extent in zip(names, widths):
        bounds[piece_name] = (offset, offset + extent)
        offset = offset + extent
    return (names, bounds)


def columns_of(weights, bounds, piece_name):
    span_start, span_stop = bounds[piece_name]
    return weights[:, span_start:span_stop]


def sinusoid(length, width):
    halfway = width // 2
    increment = jnp.log(10000.0) / (halfway - 1)
    rates = jnp.exp(-increment * jnp.arange(halfway, dtype=jnp.float32))
    angles = jnp.arange(length, dtype=jnp.float32)[:, None] * rates[None, :]
    return jnp.concatenate([jnp.sin(angles), jnp.cos(angles)], axis=1)


def layer_norm(inputs, gain, offset):
    average = jnp.mean(inputs, axis=-1, keepdims=True)
    centred = inputs - average
    spread = jnp.mean(centred * centred, axis=-1, keepdims=True)
    return centred * lax.rsqrt(spread + LN_EPS) * gain + offset


def norm_back(inputs, gain, offset, upstream):
    _, pull = jax.vjp(layer_norm, inputs, gain, offset)
    return pull(upstream)


def gelu_exact(values):
    return jax.nn.gelu(values, approximate=False)


def gelu_back(values, upstream):
    _, pull = jax.vjp(gelu_exact, values)
    return pull(upstream)[0]


def to_half(values):
    return values.astype(jnp.bfloat16)


def matmul(left, right):
    return jnp.dot(left, right, preferred_element_type=jnp.float32)


def matmul_t(left, right):
    return lax.dot_general(
        left, right, (((1,), (1,)), ((), ())), preferred_element_type=jnp.float32
    )


def tmatmul(left, right):
    return lax.dot_general(
        left, right, (((0,), (0,)), ((), ())), preferred_element_type=jnp.float32
    )


def heads(values):
    return values.reshape(values.shape[0], H, HD)


def merged(values):
    return values.reshape(values.shape[0], H * HD)


def scores_of(query_heads, key_heads, causal):
    scores = jnp.einsum(
        "qhd,khd->hqk", query_heads, key_heads, preferred_element_type=jnp.float32
    ) * HD ** (-0.5)
    if causal:
        rows = lax.broadcasted_iota(jnp.int32, scores.shape, 1)
        cols = lax.broadcasted_iota(jnp.int32, scores.shape, 2)
        scores = jnp.where(rows >= cols, scores, NEG_BIG)
    return scores


def attend(queries, keys_half, values_half, causal):
    scores = scores_of(heads(queries), heads(keys_half), causal)
    row_top = jnp.max(scores, axis=-1, keepdims=True)
    log_total = row_top + jnp.log(jnp.sum(jnp.exp(scores - row_top), axis=-1, keepdims=True))
    weights_soft = jnp.exp(scores - log_total)
    attended = jnp.einsum(
        "hqk,khd->qhd",
        to_half(weights_soft),
        heads(values_half),
        preferred_element_type=jnp.float32,
    )
    return (to_half(merged(attended)), log_total)


def attend_back(queries, keys_half, values_half, causal, log_total, back_attended):
    query_heads = heads(queries)
    key_heads = heads(keys_half)
    grad_heads = heads(back_attended)
    weights_soft = jnp.exp(scores_of(query_heads, key_heads, causal) - log_total)
    back_weights = jnp.einsum(
        "qhd,khd->hqk", grad_heads, heads(values_half), preferred_element_type=jnp.float32
    )
    back_values = jnp.einsum(
        "hqk,qhd->khd", to_half(weights_soft), grad_heads, preferred_element_type=jnp.float32
    )
    inner = jnp.sum(weights_soft * back_weights, axis=-1, keepdims=True)
    back_scores = to_half(weights_soft * (back_weights - inner) * HD ** (-0.5))
    back_queries = jnp.einsum(
        "hqk,khd->qhd", back_scores, key_heads, preferred_element_type=jnp.float32
    )
    back_keys = jnp.einsum(
        "hqk,qhd->khd", back_scores, query_heads, preferred_element_type=jnp.float32
    )
    return (merged(back_queries), merged(back_keys), merged(back_values))


def self_block(stream, weights, small_params, slots, bounds, qkv_name, out_name, causal):
    normed = layer_norm(
        stream, small_params[:, slots["norm_gain"]], small_params[:, slots["norm_bias"]]
    )
    projected = matmul(to_half(normed), columns_of(weights, bounds, qkv_name))
    queries = to_half(projected[:, :D] + small_params[:, slots["query_bias"]])
    keys_half = to_half(projected[:, D : 2 * D])
    values_half = to_half(projected[:, 2 * D :] + small_params[:, slots["value_bias"]])
    attended, log_total = attend(queries, keys_half, values_half, causal)
    output = (
        stream
        + matmul(attended, columns_of(weights, bounds, out_name))
        + small_params[:, slots["out_bias"]]
    )
    return (output, (stream, normed, queries, keys_half, values_half, attended, log_total))


def self_block_back(
    saved,
    pooled,
    upstream,
    weights,
    small_params,
    slots,
    bounds,
    qkv_name,
    out_name,
    causal,
    matrix_grads,
    vector_grads,
):
    stream, normed, queries, keys_half, values_half, attended, log_total = saved
    grad_out = to_half(upstream)
    back_attended = to_half(matmul_t(grad_out, columns_of(weights, bounds, out_name)))
    back_queries, back_keys, back_values = attend_back(
        queries, keys_half, values_half, causal, log_total, back_attended
    )
    grad_proj = to_half(jnp.concatenate([back_queries, back_keys, back_values], axis=1))
    attended_all, normed_all = pooled
    grad_out_all, grad_proj_all = pool([], [grad_out, grad_proj])
    matrix_grads[out_name] = tmatmul(attended_all, grad_out_all)
    matrix_grads[qkv_name] = tmatmul(normed_all, grad_proj_all)
    back_normed = matmul_t(grad_proj, columns_of(weights, bounds, qkv_name))
    back_stream, back_gain, back_bias = norm_back(
        stream,
        small_params[:, slots["norm_gain"]],
        small_params[:, slots["norm_bias"]],
        back_normed,
    )
    vector_grads[slots["norm_gain"]] = back_gain
    vector_grads[slots["norm_bias"]] = back_bias
    vector_grads[slots["query_bias"]] = jnp.sum(back_queries, axis=0)
    vector_grads[slots["value_bias"]] = jnp.sum(back_values, axis=0)
    vector_grads[slots["out_bias"]] = jnp.sum(upstream, axis=0)
    return upstream + back_stream


def cross_block(stream, memory_half, weights, small_params, bounds):
    normed = layer_norm(
        stream, small_params[:, DEC_SLOTS["cross_gain"]], small_params[:, DEC_SLOTS["cross_bias"]]
    )
    queries = to_half(
        matmul(to_half(normed), columns_of(weights, bounds, "x_query"))
        + small_params[:, DEC_SLOTS["xquery_bias"]]
    )
    keyval = matmul(memory_half, columns_of(weights, bounds, "x_keyval"))
    keys_half = to_half(keyval[:, :D])
    values_half = to_half(keyval[:, D:] + small_params[:, DEC_SLOTS["xvalue_bias"]])
    attended, log_total = attend(queries, keys_half, values_half, False)
    output = (
        stream
        + matmul(attended, columns_of(weights, bounds, "x_out"))
        + small_params[:, DEC_SLOTS["xout_bias"]]
    )
    return (output, (stream, normed, queries, keys_half, values_half, attended, log_total))


def cross_block_back(
    saved, pooled, upstream, weights, small_params, bounds, matrix_grads, vector_grads
):
    stream, normed, queries, keys_half, values_half, attended, log_total = saved
    grad_out = to_half(upstream)
    back_attended = to_half(matmul_t(grad_out, columns_of(weights, bounds, "x_out")))
    back_queries, back_keys, back_values = attend_back(
        queries, keys_half, values_half, False, log_total, back_attended
    )
    grad_query = to_half(back_queries)
    back_normed = matmul_t(grad_query, columns_of(weights, bounds, "x_query"))
    grad_keyval = to_half(jnp.concatenate([back_keys, back_values], axis=1))
    attended_all, normed_all, memory_all = pooled
    grad_out_all, grad_query_all = pool([], [grad_out, grad_query])
    (grad_keyval_all,) = pool([], [grad_keyval])
    matrix_grads["x_out"] = tmatmul(attended_all, grad_out_all)
    matrix_grads["x_query"] = tmatmul(normed_all, grad_query_all)
    matrix_grads["x_keyval"] = tmatmul(memory_all, grad_keyval_all)
    back_memory = matmul_t(grad_keyval, columns_of(weights, bounds, "x_keyval"))
    back_stream, back_gain, back_bias = norm_back(
        stream,
        small_params[:, DEC_SLOTS["cross_gain"]],
        small_params[:, DEC_SLOTS["cross_bias"]],
        back_normed,
    )
    vector_grads[DEC_SLOTS["cross_gain"]] = back_gain
    vector_grads[DEC_SLOTS["cross_bias"]] = back_bias
    vector_grads[DEC_SLOTS["xquery_bias"]] = jnp.sum(back_queries, axis=0)
    vector_grads[DEC_SLOTS["xvalue_bias"]] = jnp.sum(back_values, axis=0)
    vector_grads[DEC_SLOTS["xout_bias"]] = jnp.sum(upstream, axis=0)
    return (upstream + back_stream, back_memory)


def mlp_block(stream, weights, small_params, slots, bounds, up_name, down_name):
    normed = layer_norm(
        stream, small_params[:, slots["mlp_gain"]], small_params[:, slots["mlp_bias"]]
    )
    up_bias = small_params[:, slots["up_bias"] : slots["up_bias"] + 4].T.reshape(-1)
    raised = matmul(to_half(normed), columns_of(weights, bounds, up_name)) + up_bias
    active = to_half(gelu_exact(raised))
    output = (
        stream
        + matmul_t(active, columns_of(weights, bounds, down_name))
        + small_params[:, slots["down_bias"]]
    )
    return (output, (stream, normed, raised, active))


def mlp_block_back(
    saved,
    pooled,
    upstream,
    weights,
    small_params,
    slots,
    bounds,
    up_name,
    down_name,
    matrix_grads,
    vector_grads,
):
    stream, normed, raised, active = saved
    grad_out = to_half(upstream)
    back_raised = gelu_back(raised, matmul(grad_out, columns_of(weights, bounds, down_name)))
    bias_rows = jnp.sum(back_raised, axis=0).reshape(4, D)
    for quarter in range(4):
        vector_grads[slots["up_bias"] + quarter] = bias_rows[quarter]
    grad_raised = to_half(back_raised)
    normed_all, active_all = pooled
    grad_out_all, grad_raised_all = pool([grad_out], [grad_raised])
    matrix_grads[down_name] = tmatmul(grad_out_all, active_all)
    matrix_grads[up_name] = tmatmul(normed_all, grad_raised_all)
    back_normed = matmul_t(grad_raised, columns_of(weights, bounds, up_name))
    back_stream, back_gain, back_bias = norm_back(
        stream, small_params[:, slots["mlp_gain"]], small_params[:, slots["mlp_bias"]], back_normed
    )
    vector_grads[slots["mlp_gain"]] = back_gain
    vector_grads[slots["mlp_bias"]] = back_bias
    vector_grads[slots["down_bias"]] = jnp.sum(upstream, axis=0)
    return upstream + back_stream


def stem_forward(mel_half, weights, small_params, bounds):
    frames_in = mel_half.shape[1]
    padded = jnp.pad(mel_half, ((0, 0), (1, 1)))
    columns = jnp.concatenate(
        [padded[:, tap_index : tap_index + frames_in].T for tap_index in range(3)], axis=1
    )
    first_pre = matmul_t(columns, columns_of(weights, bounds, "conv_one")) + small_params[:, 0]
    shifted = jnp.pad(to_half(gelu_exact(first_pre)), ((1, 1), (0, 0)))
    strided = [shifted[tap_index : tap_index + frames_in : 2] for tap_index in range(3)]
    conv_start = bounds["conv_two"][0]
    conv_sum = matmul(strided[0], weights[:, conv_start : conv_start + D])
    for tap_index in range(1, 3):
        conv_sum = conv_sum + matmul(
            strided[tap_index],
            weights[:, conv_start + tap_index * D : conv_start + (tap_index + 1) * D],
        )
    second_pre = conv_sum + small_params[:, 1]
    stream = gelu_exact(second_pre) + sinusoid(frames_in // 2, D)
    return ((columns, first_pre, shifted, second_pre), stream)


def stem_back(saved, upstream, weights, bounds, matrix_grads, vector_grads):
    columns, first_pre, shifted, second_pre = saved
    frames_in = columns.shape[0]
    reach = shifted.shape[0]
    back_second = gelu_back(second_pre, upstream)
    vector_grads[1] = jnp.sum(back_second, axis=0)
    grad_second = to_half(back_second)
    conv_start = bounds["conv_two"][0]
    back_shifted = jnp.zeros((frames_in + 2, D), jnp.float32)
    (shifted_all,) = pool([shifted], [])
    (grad_second_all,) = pool([], [grad_second])
    shifted_all = shifted_all.reshape(-1, reach, D)
    for tap_index in range(3):
        tap_weight = weights[:, conv_start + tap_index * D : conv_start + (tap_index + 1) * D]
        strided_all = shifted_all[:, tap_index : tap_index + frames_in : 2].reshape(-1, D)
        matrix_grads[f"conv_two_{tap_index}"] = tmatmul(strided_all, grad_second_all)
        back_shifted = back_shifted.at[tap_index : tap_index + frames_in : 2].add(
            matmul_t(grad_second, tap_weight)
        )
    back_first = gelu_back(first_pre, back_shifted[1:-1])
    vector_grads[0] = jnp.sum(back_first, axis=0)
    back_first_all, columns_all = pool([to_half(back_first)], [columns])
    matrix_grads["conv_one"] = tmatmul(back_first_all, columns_all)


def moments(weight, moment, square, gradient, factor, first_fix, second_fix):
    scaled = gradient * factor
    new_moment = BETA_ONE * moment + (1.0 - BETA_ONE) * scaled
    new_square = BETA_TWO * square + (1.0 - BETA_TWO) * scaled * scaled
    update = (
        new_moment / first_fix / (jnp.sqrt(new_square / second_fix) + ADAM_EPS) + DECAY * weight
    )
    return (new_moment, new_square, update)


def group_squares(mat_part, embed_part, vec_part, bounds, names):
    parts = [jnp.sum(columns_of(mat_part, bounds, piece_name) ** 2) for piece_name in names]
    parts = parts + [jnp.sum(embed_part * embed_part), jnp.sum(vec_part * vec_part)]
    return jnp.stack(parts)


def count_bad(values):
    return jnp.sum(jnp.where(jnp.isfinite(values), 0.0, 1.0))


def on_device(
    mel_frames,
    text_ids,
    text_lengths,
    language,
    vocab_mask,
    step_count,
    matrices,
    matrix_moment,
    matrix_square,
    embedding,
    embed_moment,
    embed_square,
    vectors,
    vector_moment,
    vector_square,
):
    names, bounds = layout(D, FF, MELS, TLEN)
    reps = lax.axis_size("rep")
    members = lax.axis_size("fsdp")
    replica = lax.axis_index("rep")
    member = lax.axis_index("fsdp")
    weights, small_half = (
        lax.all_gather(to_half(matrices), "fsdp", axis=0, tiled=True),
        lax.all_gather(to_half(vectors), "fsdp", axis=0, tiled=True),
    )
    small_params = small_half.astype(jnp.float32)
    inputs_ids = jnp.concatenate([LANGTOK + language, text_ids[0, :-1]])[None, :]
    ids_all = lax.all_gather(
        jnp.concatenate([inputs_ids, text_ids], axis=1), ("rep", "fsdp"), axis=0, tiled=True
    ).reshape(reps, members, 2, TLEN)
    order = [(replica - shift) % reps for shift in range(reps)]
    ids_by_shift = [pick(ids_all, place, 0) for place in order]
    group_inputs = [ids[:, 0].reshape(-1) for ids in ids_by_shift]
    group_targets = [ids[:, 1].reshape(-1) for ids in ids_by_shift]
    counts_by_shift = [
        (
            lax.broadcasted_iota(jnp.int32, (members, TLEN), 1)
            < lax.dynamic_slice_in_dim(text_lengths, place * members, members)[:, None]
        ).reshape(-1)
        for place in order
    ]
    vocab_rows = embedding.shape[0]
    vocab_start = member * vocab_rows
    embed_half = to_half(embedding)
    vocab_iota = lax.broadcasted_iota(jnp.int32, (members * TLEN, vocab_rows), 1)
    input_hot = [to_half(ids[:, None] - vocab_start == vocab_iota) for ids in group_inputs]
    embedded = lax.psum_scatter(
        matmul(input_hot[0], embed_half).astype(jnp.bfloat16), "fsdp", scatter_dimension=0, tiled=True
    ).astype(jnp.float32)
    stem_saved, enc_zero = stem_forward(mel_frames[0], weights, small_params, bounds)
    enc_one, enc_self = self_block(
        enc_zero, weights, small_params, ENC_SLOTS, bounds, "e_qkv", "e_out", False
    )
    enc_two, enc_mlp = mlp_block(
        enc_one, weights, small_params, ENC_SLOTS, bounds, "e_up", "e_down"
    )
    memory_half = to_half(
        layer_norm(
            enc_two,
            small_params[:, ENC_SLOTS["final_gain"]],
            small_params[:, ENC_SLOTS["final_bias"]],
        )
    )
    enc_pooled = pool(
        [to_half(enc_self[1]), enc_self[5], to_half(enc_mlp[1]), memory_half], [enc_mlp[3]]
    )
    dec_zero = embedded + columns_of(weights, bounds, "dec_pos").T.astype(jnp.float32)
    dec_one, dec_self = self_block(
        dec_zero, weights, small_params, DEC_SLOTS, bounds, "d_qkv", "d_out", True
    )
    dec_two, dec_cross = cross_block(dec_one, memory_half, weights, small_params, bounds)
    dec_three, dec_mlp = mlp_block(
        dec_two, weights, small_params, DEC_SLOTS, bounds, "d_up", "d_down"
    )
    final_out = layer_norm(
        dec_three,
        small_params[:, DEC_SLOTS["final_gain"]],
        small_params[:, DEC_SLOTS["final_bias"]],
    )
    dec_pooled = pool(
        [
            to_half(dec_self[1]),
            dec_self[5],
            to_half(dec_cross[1]),
            dec_cross[5],
            to_half(dec_mlp[1]),
        ],
        [dec_mlp[3]],
    )
    gathered_hidden = lax.all_gather(to_half(final_out), "fsdp", axis=0, tiled=True)
    logits = matmul_t(gathered_hidden, embed_half)
    vocab_keep = (lax.dynamic_slice_in_dim(vocab_mask, vocab_start, vocab_rows) == 1)[None, :]
    masked = jnp.where(vocab_keep, logits, NEG_BIG)
    local_top = jnp.max(masked, axis=1)
    local_sum = jnp.sum(jnp.where(vocab_keep, jnp.exp(masked - local_top[:, None]), 0.0), axis=1)
    target_hits = group_targets[0][:, None] - vocab_start == vocab_iota
    local_target = jnp.sum(jnp.where(target_hits, logits, 0.0), axis=1)
    local_total = jnp.sum(jnp.where(vocab_keep, logits, 0.0), axis=1)
    stats = lax.all_gather(
        jnp.stack([local_top, local_sum, local_target, local_total]), "fsdp", axis=0
    )
    row_top = jnp.max(stats[:, 0], axis=0)
    row_sums = jnp.sum(stats[:, 1] * jnp.exp(stats[:, 0] - row_top[None]), axis=0)
    target_logit = jnp.sum(stats[:, 2], axis=0)
    logit_total = jnp.sum(stats[:, 3], axis=0)
    log_norm = row_top + jnp.log(row_sums)
    vocab_count = jnp.sum(vocab_mask).astype(jnp.float32)
    entropy = log_norm - (1.0 - SMOOTH) * target_logit - SMOOTH * logit_total / vocab_count
    norm_and_loss = jnp.stack([log_norm, jnp.where(counts_by_shift[0], entropy, 0.0)])
    norms_by_shift = [norm_and_loss] + [send_rep(norm_and_loss, shift) for shift in range(1, reps)]
    loss_sum = sum(jnp.sum(part[1]) for part in norms_by_shift)
    hidden_by_shift = across_reps(gathered_hidden)

    def logit_grads(shift):
        own_logits = matmul_t(hidden_by_shift[shift], embed_half)
        hits = group_targets[shift][:, None] - vocab_start == vocab_iota
        softmax_part = jnp.where(
            vocab_keep,
            jnp.exp(
                jnp.where(vocab_keep, own_logits, NEG_BIG) - norms_by_shift[shift][0][:, None]
            ),
            0.0,
        )
        return to_half(
            jnp.where(
                counts_by_shift[shift][:, None],
                softmax_part
                - (1.0 - SMOOTH) * hits.astype(jnp.float32)
                - SMOOTH * vocab_keep.astype(jnp.float32) / vocab_count,
                0.0,
            )
        )

    back_logits = [logit_grads(shift) for shift in range(reps)]
    embed_grad = tmatmul(back_logits[0], gathered_hidden)
    for shift in range(1, reps):
        embed_grad = embed_grad + tmatmul(back_logits[shift], hidden_by_shift[shift])
    back_hidden = lax.psum_scatter(
        matmul(back_logits[0], embed_half), "fsdp", scatter_dimension=0, tiled=True
    )
    matrix_grads = {}
    vector_grads = {}
    back_three, final_gain, final_bias = norm_back(
        dec_three,
        small_params[:, DEC_SLOTS["final_gain"]],
        small_params[:, DEC_SLOTS["final_bias"]],
        back_hidden,
    )
    vector_grads[DEC_SLOTS["final_gain"]] = final_gain
    vector_grads[DEC_SLOTS["final_bias"]] = final_bias
    back_two = mlp_block_back(
        dec_mlp,
        (dec_pooled[4], dec_pooled[5]),
        back_three,
        weights,
        small_params,
        DEC_SLOTS,
        bounds,
        "d_up",
        "d_down",
        matrix_grads,
        vector_grads,
    )
    back_one, back_memory = cross_block_back(
        dec_cross,
        (dec_pooled[3], dec_pooled[2], enc_pooled[3]),
        back_two,
        weights,
        small_params,
        bounds,
        matrix_grads,
        vector_grads,
    )
    back_zero = self_block_back(
        dec_self,
        (dec_pooled[1], dec_pooled[0]),
        back_one,
        weights,
        small_params,
        DEC_SLOTS,
        bounds,
        "d_qkv",
        "d_out",
        True,
        matrix_grads,
        vector_grads,
    )
    matrix_grads["dec_pos"] = pool_sum(back_zero.T)
    back_inputs = across_reps(lax.all_gather(to_half(back_zero), "fsdp", axis=0, tiled=True))
    for shift in range(reps):
        embed_grad = embed_grad + tmatmul(input_hot[shift], back_inputs[shift])
    back_enc_two, enc_gain, enc_bias = norm_back(
        enc_two,
        small_params[:, ENC_SLOTS["final_gain"]],
        small_params[:, ENC_SLOTS["final_bias"]],
        back_memory,
    )
    vector_grads[ENC_SLOTS["final_gain"]] = enc_gain
    vector_grads[ENC_SLOTS["final_bias"]] = enc_bias
    back_enc_one = mlp_block_back(
        enc_mlp,
        (enc_pooled[2], enc_pooled[4]),
        back_enc_two,
        weights,
        small_params,
        ENC_SLOTS,
        bounds,
        "e_up",
        "e_down",
        matrix_grads,
        vector_grads,
    )
    back_enc_zero = self_block_back(
        enc_self,
        (enc_pooled[1], enc_pooled[0]),
        back_enc_one,
        weights,
        small_params,
        ENC_SLOTS,
        bounds,
        "e_qkv",
        "e_out",
        False,
        matrix_grads,
        vector_grads,
    )
    stem_back(stem_saved, back_enc_zero, weights, bounds, matrix_grads, vector_grads)
    batches = (
        ("d_down", "d_up"),
        ("x_out", "x_query", "x_keyval"),
        ("d_out", "d_qkv", "dec_pos"),
        ("e_down", "e_up"),
        ("e_out", "e_qkv"),
        ("conv_two_0", "conv_two_1", "conv_two_2", "conv_one"),
    )
    row_grads = {}
    for batch in batches:
        for piece_name, rows in zip(batch, whole_rows([matrix_grads[part] for part in batch])):
            row_grads[piece_name] = rows
    row_grads["conv_two"] = jnp.concatenate(
        [row_grads[f"conv_two_{tap_index}"] for tap_index in range(3)], axis=1
    )
    mat_grad = jnp.concatenate([row_grads[piece_name] for piece_name in names], axis=1)
    vec_grad = summed_rows(jnp.stack([vector_grads[column] for column in range(NVEC)], axis=1))
    local_squares = (
        jnp.sum(mat_grad * mat_grad)
        + jnp.sum(vec_grad * vec_grad)
        + jnp.sum(embed_grad * embed_grad)
    )
    local_bad = count_bad(mat_grad) + count_bad(embed_grad) + count_bad(vec_grad)
    total_squares, total_bad = lax.psum((local_squares, local_bad), "fsdp")
    gradient_norm = jnp.sqrt(total_squares)
    factor = CLIP_AT / jnp.maximum(gradient_norm, CLIP_AT)
    steps = step_count[0].astype(jnp.float32)
    first_fix = 1.0 - jnp.power(jnp.float32(BETA_ONE), steps)
    second_fix = 1.0 - jnp.power(jnp.float32(BETA_TWO), steps)
    mat_moment, mat_square, mat_update = moments(
        matrices, matrix_moment, matrix_square, mat_grad, factor, first_fix, second_fix
    )
    emb_moment, emb_square, emb_update = moments(
        embedding, embed_moment, embed_square, embed_grad, factor, first_fix, second_fix
    )
    vec_moment, vec_square, vec_update = moments(
        vectors, vector_moment, vector_square, vec_grad, factor, first_fix, second_fix
    )
    update_parts = group_squares(mat_update, emb_update, vec_update, bounds, names)
    weight_sums, update_sums = lax.psum(
        (group_squares(matrices, embedding, vectors, bounds, names), update_parts), "fsdp"
    )
    weight_norms = jnp.sqrt(weight_sums)
    update_norms = jnp.sqrt(update_sums)
    ratio = weight_norms / update_norms
    ratio_columns = jnp.concatenate(
        [
            jnp.full((bounds[piece_name][1] - bounds[piece_name][0],), 1.0, jnp.float32)
            * ratio[position]
            for position, piece_name in enumerate(names)
        ]
    )
    new_matrices = matrices - RATE * ratio_columns[None, :] * mat_update
    new_embedding = embedding - RATE * ratio[len(names)] * emb_update
    new_vectors = vectors - RATE * ratio[len(names) + 1] * vec_update
    mean_loss = loss_sum / jnp.sum(text_lengths).astype(jnp.float32)
    group_norms = jnp.stack([weight_norms, update_norms], axis=1)
    return (
        mean_loss,
        total_bad.astype(jnp.int32),
        gradient_norm,
        group_norms,
        new_matrices,
        mat_moment,
        mat_square,
        new_embedding,
        emb_moment,
        emb_square,
        new_vectors,
        vec_moment,
        vec_square,
    )


def solution(mesh):
    placed = (
        P(("rep", "fsdp"), None, None),
        P(("rep", "fsdp"), None),
        P(),
        P(("rep", "fsdp")),
        P(),
        P(),
        P("fsdp", None),
        P("fsdp", None),
        P("fsdp", None),
        P("fsdp", None),
        P("fsdp", None),
        P("fsdp", None),
        P("fsdp", None),
        P("fsdp", None),
        P("fsdp", None),
    )
    return jax.shard_map(
        on_device,
        mesh=mesh,
        in_specs=placed,
        out_specs=(
            P(),
            P(),
            P(),
            P(),
            P("fsdp", None),
            P("fsdp", None),
            P("fsdp", None),
            P("fsdp", None),
            P("fsdp", None),
            P("fsdp", None),
            P("fsdp", None),
            P("fsdp", None),
            P("fsdp", None),
        ),
        check_vma=False,
    )
```

```python
import jax
import jax.numpy as jnp
from jax import lax
from jax.experimental import pallas as pl
from jax.experimental.pallas import tpu as pltpu
from jax.sharding import PartitionSpec as P

D = 768
H = 12
HD = 64
FF = 3072
MELS = 80
TLEN = 128
LANGTOK = 50259
NVEC = 35


LN_EPS = 1e-05
SMOOTH = 0.1
CLIP_AT = 1.0
BETA_ONE = 0.9
BETA_TWO = 0.999
ADAM_EPS = 1e-06
DECAY = 0.01
RATE = 0.5
NEG_BIG = -1e30
class EncSlots:
    norm_gain = 2
    norm_bias = 3
    query_bias = 4
    value_bias = 5
    out_bias = 6
    mlp_gain = 7
    mlp_bias = 8
    up_bias = 9
    down_bias = 13
    final_gain = 14
    final_bias = 15


class DecSlots:
    norm_gain = 16
    norm_bias = 17
    query_bias = 18
    value_bias = 19
    out_bias = 20
    cross_gain = 21
    cross_bias = 22
    xquery_bias = 23
    xvalue_bias = 24
    xout_bias = 25
    mlp_gain = 26
    mlp_bias = 27
    up_bias = 28
    down_bias = 32
    final_gain = 33
    final_bias = 34


CORES = 2
LINE = 4


def mesh_shape():
    members = lax.axis_size("fsdp")
    return (lax.axis_size("rep"), LINE, members // (LINE * CORES), CORES)


def places():
    reps, line, side, cores = mesh_shape()
    index = lax.axis_index("fsdp")
    return (
        lax.axis_index("rep"),
        index // (side * cores),
        (index // cores) % side,
        index % cores,
    )


def send(values, move):
    reps, line, side, cores = mesh_shape()
    members = line * side * cores
    pairs = []
    for rep in range(reps):
        for far in range(line):
            for near in range(side):
                for core in range(cores):
                    target = move(rep, far, near, core)
                    if target is None:
                        continue
                    rep_to, far_to, near_to, core_to = target
                    pairs.append(
                        (
                            rep * members + (far * side + near) * cores + core,
                            rep_to * members + (far_to * side + near_to) * cores + core_to,
                        )
                    )
    return lax.ppermute(values, ("rep", "fsdp"), pairs)


def send_core(values):
    return send(values, lambda rep, far, near, core: (rep, far, near, 1 - core))


def send_rep(values, shift):
    reps = lax.axis_size("rep")
    return send(values, lambda rep, far, near, core: ((rep + shift) % reps, far, near, core))


def pick(values, index, axis):
    return lax.dynamic_index_in_dim(values, index, axis, keepdims=False)


def block(values, index, width):
    return lax.dynamic_slice_in_dim(values, index * width, width, axis=1)


def pool(narrows, wides):
    reps = lax.axis_size("rep")
    rep, _, _, core = places()
    tall = sum(part.shape[1] for part in narrows)
    spans = [part.shape[1] // reps for part in wides]
    got = []
    for shift in range(reps):
        parts = list(narrows) + [
            block(part, (rep + shift) % reps, span) for part, span in zip(wides, spans)
        ]
        joint = parts[0] if len(parts) == 1 else jnp.concatenate(parts, axis=1)
        got.append(send_rep(joint, shift) if shift else joint)
    joint = jnp.concatenate(got, axis=0)
    offsets = [tall + sum(spans[:position]) for position in range(len(spans))]

    def halves(side):
        parts = [joint[:, :tall]] if tall else []
        for offset, span in zip(offsets, spans):
            parts.append(block(joint[:, offset : offset + span], side, span // CORES))
        return parts[0] if len(parts) == 1 else jnp.concatenate(parts, axis=1)

    both = jnp.concatenate([halves(core), send_core(halves(1 - core))], axis=0)
    results = []
    offset = 0
    for part in narrows:
        results.append(both[:, offset : offset + part.shape[1]])
        offset = offset + part.shape[1]
    for span in spans:
        results.append(both[:, offset : offset + span // CORES])
        offset = offset + span // CORES
    return results


def pool_sum(values):
    reps = lax.axis_size("rep")
    rep, _, _, core = places()
    span = values.shape[1] // reps
    total = block(values, rep, span)
    for shift in range(1, reps):
        total = total + send_rep(block(values, (rep + shift) % reps, span), shift)
    return block(total, core, span // CORES) + send_core(
        block(total, 1 - core, span // CORES)
    )


def in_order(stack, position):
    count = len(stack)
    joint = jnp.stack(stack)
    return jnp.stack([pick(joint, (position - place) % count, 0) for place in range(count)])


def whole_rows(pieces):
    reps, line, side, cores = mesh_shape()
    rep, _, _, core = places()
    rows = pieces[0].shape[0]
    own_rows = rows // (line * side * cores)
    members = line * side * cores
    groups = [list(range(place, members, cores)) for place in range(cores)]
    summed = lax.psum_scatter(
        jnp.concatenate(pieces, axis=1),
        "fsdp",
        scatter_dimension=0,
        axis_index_groups=groups,
        tiled=True,
    )
    by_core = summed.reshape(cores, own_rows, summed.shape[1])
    cores_joint = in_order([pick(by_core, core, 0), send_core(pick(by_core, 1 - core, 0))], core)
    reps_joint = in_order(
        [cores_joint] + [send_rep(cores_joint, shift) for shift in range(1, reps)], rep
    )
    results = []
    offset = 0
    for part in pieces:
        span = part.shape[1]
        own = reps_joint[:, :, :, offset : offset + span]
        results.append(
            jnp.transpose(own, (2, 0, 1, 3)).reshape(own.shape[2], reps * CORES * span)
        )
        offset = offset + span
    return results


def gather_body(values, gathered, leaving, landing):
    members = lax.axis_size("fsdp")
    here = lax.axis_index("fsdp")
    barrier = pltpu.get_barrier_semaphore()
    for shift in range(1, members):
        pl.semaphore_signal(barrier, inc=1, device_id={"fsdp": lax.rem(here + shift, members)})
    pl.semaphore_wait(barrier, members - 1)
    copies = []
    for shift in range(1, members):
        copies.append(
            pltpu.make_async_remote_copy(
                src_ref=values,
                dst_ref=gathered.at[here],
                send_sem=leaving.at[shift - 1],
                recv_sem=landing.at[shift - 1],
                device_id={"fsdp": lax.rem(here + shift, members)},
            )
        )
        copies[-1].start()
    gathered[here] = values[...]
    for copy in copies:
        copy.wait()


def gather_small(values, tag):
    members = lax.axis_size("fsdp")
    return pl.pallas_call(
        gather_body,
        out_shape=jax.ShapeDtypeStruct((members,) + values.shape, values.dtype),
        in_specs=[pl.BlockSpec(memory_space=pltpu.VMEM)],
        out_specs=pl.BlockSpec(memory_space=pltpu.VMEM),
        scratch_shapes=[
            pltpu.SemaphoreType.DMA((members - 1,)),
            pltpu.SemaphoreType.DMA((members - 1,)),
        ],
        compiler_params=pltpu.CompilerParams(collective_id=tag, has_side_effects=True),
    )(values)


def total_of(values, tag):
    count = values.shape[0]
    padded = jnp.zeros((8, 128), jnp.float32).at[0, :count].set(values)
    return jnp.sum(gather_small(padded, tag), axis=0)[0, :count]


def layout(width, hidden, mels, text_len):
    names = (
        "eq",
        "eo",
        "eu",
        "ed",
        "dq",
        "do",
        "xq",
        "xk",
        "xo",
        "du",
        "dd",
        "c2",
        "c1",
        "dp",
    )
    widths = (
        3 * width,
        width,
        hidden,
        hidden,
        3 * width,
        width,
        width,
        2 * width,
        width,
        hidden,
        hidden,
        3 * width,
        3 * mels,
        text_len,
    )
    bounds = {}
    offset = 0
    for piece_name, extent in zip(names, widths):
        bounds[piece_name] = (offset, offset + extent)
        offset = offset + extent
    return (names, bounds)


def columns_of(weights, bounds, piece_name):
    span_start, span_stop = bounds[piece_name]
    return weights[:, span_start:span_stop]


def sinusoid(length, width):
    halfway = width // 2
    increment = jnp.log(10000.0) / (halfway - 1)
    rates = jnp.exp(-increment * jnp.arange(halfway, dtype=jnp.float32))
    angles = jnp.arange(length, dtype=jnp.float32)[:, None] * rates[None, :]
    return jnp.concatenate([jnp.sin(angles), jnp.cos(angles)], axis=1)


def layer_norm(inputs, gain, offset):
    average = jnp.mean(inputs, axis=-1, keepdims=True)
    centred = inputs - average
    spread = jnp.mean(centred * centred, axis=-1, keepdims=True)
    return centred * lax.rsqrt(spread + LN_EPS) * gain + offset


def norm_back(inputs, gain, offset, upstream):
    _, pull = jax.vjp(layer_norm, inputs, gain, offset)
    return pull(upstream)


def gelu_exact(values):
    return jax.nn.gelu(values, approximate=False)


def gelu_back(values, upstream):
    _, pull = jax.vjp(gelu_exact, values)
    return pull(upstream)[0]


def to_half(values):
    return values.astype(jnp.bfloat16)


def matmul(left, right):
    return jnp.dot(left, right, preferred_element_type=jnp.float32)


def matmul_t(left, right):
    return lax.dot_general(
        left, right, (((1,), (1,)), ((), ())), preferred_element_type=jnp.float32
    )


def tmatmul(left, right):
    return lax.dot_general(
        left, right, (((0,), (0,)), ((), ())), preferred_element_type=jnp.float32
    )


def heads(values):
    return values.reshape(values.shape[0], H, HD)


def merged(values):
    return values.reshape(values.shape[0], H * HD)


def scores_of(query_heads, key_heads, causal):
    scores = jnp.einsum(
        "qhd,khd->hqk", query_heads, key_heads, preferred_element_type=jnp.float32
    ) * HD ** (-0.5)
    if causal:
        rows = lax.broadcasted_iota(jnp.int32, scores.shape, 1)
        cols = lax.broadcasted_iota(jnp.int32, scores.shape, 2)
        scores = jnp.where(rows >= cols, scores, NEG_BIG)
    return scores


def attend(queries, keys_half, values_half, causal):
    scores = scores_of(heads(queries), heads(keys_half), causal)
    row_top = jnp.max(scores, axis=-1, keepdims=True)
    log_total = row_top + jnp.log(jnp.sum(jnp.exp(scores - row_top), axis=-1, keepdims=True))
    weights_soft = jnp.exp(scores - log_total)
    attended = jnp.einsum(
        "hqk,khd->qhd",
        to_half(weights_soft),
        heads(values_half),
        preferred_element_type=jnp.float32,
    )
    return (to_half(merged(attended)), log_total)


def attend_back(queries, keys_half, values_half, causal, log_total, back_attended):
    query_heads = heads(queries)
    key_heads = heads(keys_half)
    grad_heads = heads(back_attended)
    weights_soft = jnp.exp(scores_of(query_heads, key_heads, causal) - log_total)
    back_weights = jnp.einsum(
        "qhd,khd->hqk", grad_heads, heads(values_half), preferred_element_type=jnp.float32
    )
    back_values = jnp.einsum(
        "hqk,qhd->khd", to_half(weights_soft), grad_heads, preferred_element_type=jnp.float32
    )
    inner = jnp.sum(weights_soft * back_weights, axis=-1, keepdims=True)
    back_scores = to_half(weights_soft * (back_weights - inner) * HD ** (-0.5))
    back_queries = jnp.einsum(
        "hqk,khd->qhd", back_scores, key_heads, preferred_element_type=jnp.float32
    )
    back_keys = jnp.einsum(
        "hqk,qhd->khd", back_scores, query_heads, preferred_element_type=jnp.float32
    )
    return (merged(back_queries), merged(back_keys), merged(back_values))


def self_block(stream, weights, small_params, slots, qkv_name, out_name, causal):
    normed = layer_norm(
        stream, small_params[:, slots.norm_gain], small_params[:, slots.norm_bias]
    )
    normed_half = to_half(normed)
    projected = matmul(normed_half, weights[qkv_name])
    queries = to_half(projected[:, :D] + small_params[:, slots.query_bias])
    keys_half = to_half(projected[:, D : 2 * D])
    values_half = to_half(projected[:, 2 * D :] + small_params[:, slots.value_bias])
    attended, log_total = attend(queries, keys_half, values_half, causal)
    output = (
        stream + matmul(attended, weights[out_name]) + small_params[:, slots.out_bias]
    )
    return (output, (stream, queries, keys_half, values_half, log_total), (normed_half, attended))


def self_block_back(
    saved, upstream, weights, small_params, slots, qkv_name, out_name, causal, vector_grads
):
    stream, queries, keys_half, values_half, log_total = saved
    grad_out = to_half(upstream)
    back_attended = to_half(matmul_t(grad_out, weights[out_name]))
    back_queries, back_keys, back_values = attend_back(
        queries, keys_half, values_half, causal, log_total, back_attended
    )
    grad_proj = to_half(jnp.concatenate([back_queries, back_keys, back_values], axis=1))
    back_normed = matmul_t(grad_proj, weights[qkv_name])
    back_stream, back_gain, back_bias = norm_back(
        stream,
        small_params[:, slots.norm_gain],
        small_params[:, slots.norm_bias],
        back_normed,
    )
    vector_grads[slots.norm_gain] = back_gain
    vector_grads[slots.norm_bias] = back_bias
    vector_grads[slots.query_bias] = jnp.sum(back_queries, axis=0)
    vector_grads[slots.value_bias] = jnp.sum(back_values, axis=0)
    vector_grads[slots.out_bias] = jnp.sum(upstream, axis=0)
    return (upstream + back_stream, grad_out, grad_proj)


def cross_block(stream, memory_half, weights, small_params):
    normed = layer_norm(
        stream, small_params[:, DecSlots.cross_gain], small_params[:, DecSlots.cross_bias]
    )
    normed_half = to_half(normed)
    queries = to_half(
        matmul(normed_half, weights["xq"]) + small_params[:, DecSlots.xquery_bias]
    )
    keyval = matmul(memory_half, weights["xk"])
    keys_half = to_half(keyval[:, :D])
    values_half = to_half(keyval[:, D:] + small_params[:, DecSlots.xvalue_bias])
    attended, log_total = attend(queries, keys_half, values_half, False)
    output = (
        stream + matmul(attended, weights["xo"]) + small_params[:, DecSlots.xout_bias]
    )
    return (output, (stream, queries, keys_half, values_half, log_total), (normed_half, attended))


def cross_block_back(saved, upstream, weights, small_params, vector_grads):
    stream, queries, keys_half, values_half, log_total = saved
    grad_out = to_half(upstream)
    back_attended = to_half(matmul_t(grad_out, weights["xo"]))
    back_queries, back_keys, back_values = attend_back(
        queries, keys_half, values_half, False, log_total, back_attended
    )
    grad_query = to_half(back_queries)
    back_normed = matmul_t(grad_query, weights["xq"])
    grad_keyval = to_half(jnp.concatenate([back_keys, back_values], axis=1))
    back_memory = matmul_t(grad_keyval, weights["xk"])
    back_stream, back_gain, back_bias = norm_back(
        stream,
        small_params[:, DecSlots.cross_gain],
        small_params[:, DecSlots.cross_bias],
        back_normed,
    )
    vector_grads[DecSlots.cross_gain] = back_gain
    vector_grads[DecSlots.cross_bias] = back_bias
    vector_grads[DecSlots.xquery_bias] = jnp.sum(back_queries, axis=0)
    vector_grads[DecSlots.xvalue_bias] = jnp.sum(back_values, axis=0)
    vector_grads[DecSlots.xout_bias] = jnp.sum(upstream, axis=0)
    return (upstream + back_stream, back_memory, grad_out, grad_query, grad_keyval)


def mlp_block(stream, weights, small_params, slots, up_name, down_name):
    normed = layer_norm(
        stream, small_params[:, slots.mlp_gain], small_params[:, slots.mlp_bias]
    )
    normed_half = to_half(normed)
    up_bias = small_params[:, slots.up_bias : slots.up_bias + 4].T.reshape(-1)
    raised = matmul(normed_half, weights[up_name]) + up_bias
    active = to_half(gelu_exact(raised))
    output = (
        stream + matmul_t(active, weights[down_name]) + small_params[:, slots.down_bias]
    )
    return (output, (stream, raised), (normed_half, active))


def mlp_block_back(saved, upstream, weights, small_params, slots, up_name, down_name, vector_grads):
    stream, raised = saved
    grad_out = to_half(upstream)
    back_raised = gelu_back(raised, matmul(grad_out, weights[down_name]))
    bias_rows = jnp.sum(back_raised, axis=0).reshape(4, D)
    for quarter in range(4):
        vector_grads[slots.up_bias + quarter] = bias_rows[quarter]
    grad_raised = to_half(back_raised)
    back_normed = matmul_t(grad_raised, weights[up_name])
    back_stream, back_gain, back_bias = norm_back(
        stream, small_params[:, slots.mlp_gain], small_params[:, slots.mlp_bias], back_normed
    )
    vector_grads[slots.mlp_gain] = back_gain
    vector_grads[slots.mlp_bias] = back_bias
    vector_grads[slots.down_bias] = jnp.sum(upstream, axis=0)
    return (upstream + back_stream, grad_out, grad_raised)


def down_one(values):
    return jnp.pad(values, ((1, 0), (0, 0)))[:-1]


def up_one(values):
    return jnp.pad(values, ((0, 1), (0, 0)))[1:]


def stem_forward(mel_half, weights, small_params):
    bins, frames_in = mel_half.shape
    paired = mel_half.T.reshape(frames_in // 2, 2 * bins)
    mel_even, mel_odd = paired[:, :bins], paired[:, bins:]
    cols_even = jnp.concatenate([down_one(mel_odd), mel_even, mel_odd], axis=1)
    cols_odd = jnp.concatenate([mel_even, mel_odd, up_one(mel_even)], axis=1)
    pre_even = matmul_t(cols_even, weights["c1"]) + small_params[:, 0]
    pre_odd = matmul_t(cols_odd, weights["c1"]) + small_params[:, 0]
    act_even = to_half(gelu_exact(pre_even))
    act_odd = to_half(gelu_exact(pre_odd))
    taps = weights["c2"]
    conv_sum = (
        matmul(down_one(act_odd), taps[:, :D])
        + matmul(act_even, taps[:, D : 2 * D])
        + matmul(act_odd, taps[:, 2 * D :])
    )
    second_pre = conv_sum + small_params[:, 1]
    stream = gelu_exact(second_pre) + sinusoid(frames_in // 2, D)
    return (stream, (pre_even, pre_odd, second_pre), (cols_even, cols_odd, act_even, act_odd))


def stem_back(saved, upstream, weights, vector_grads):
    pre_even, pre_odd, second_pre = saved
    back_second = gelu_back(second_pre, upstream)
    vector_grads[1] = jnp.sum(back_second, axis=0)
    grad_second = to_half(back_second)
    taps = weights["c2"]
    back_even = gelu_back(pre_even, matmul_t(grad_second, taps[:, D : 2 * D]))
    back_odd = gelu_back(
        pre_odd,
        matmul_t(grad_second, taps[:, 2 * D :])
        + matmul_t(up_one(grad_second), taps[:, :D]),
    )
    vector_grads[0] = jnp.sum(back_even, axis=0) + jnp.sum(back_odd, axis=0)
    return (grad_second, to_half(back_even), to_half(back_odd))


def token_rows(parts):
    return jnp.concatenate(parts, axis=0)


def moments(weight, moment, square, gradient, factor, first_fix, second_fix):
    scaled = gradient * factor
    new_moment = BETA_ONE * moment + (1.0 - BETA_ONE) * scaled
    new_square = BETA_TWO * square + (1.0 - BETA_TWO) * scaled * scaled
    update = (
        new_moment / first_fix / (jnp.sqrt(new_square / second_fix) + ADAM_EPS) + DECAY * weight
    )
    return (new_moment, new_square, update)


def group_squares(mat_part, embed_part, vec_part, bounds, names):
    parts = [jnp.sum(columns_of(mat_part, bounds, piece_name) ** 2) for piece_name in names]
    parts = parts + [jnp.sum(embed_part * embed_part), jnp.sum(vec_part * vec_part)]
    return jnp.stack(parts)


def count_bad(values):
    return jnp.sum(jnp.where(jnp.isfinite(values), 0.0, 1.0))


def on_device(
    mel_frames,
    text_ids,
    text_lengths,
    language,
    vocab_mask,
    step_count,
    matrices,
    matrix_moment,
    matrix_square,
    embedding,
    embed_moment,
    embed_square,
    vectors,
    vector_moment,
    vector_square,
):
    names, bounds = layout(D, FF, MELS, TLEN)
    reps = lax.axis_size("rep")
    members = lax.axis_size("fsdp")
    replica = lax.axis_index("rep")
    member = lax.axis_index("fsdp")
    first_names = ("c1", "c2", "eq", "eo", "eu", "ed")
    last_names = ("dq", "do", "xq", "xk", "xo", "du", "dd", "dp")
    first_half = jnp.concatenate(
        [to_half(columns_of(matrices, bounds, piece)) for piece in first_names]
        + [to_half(vectors)],
        axis=1,
    )
    last_half = jnp.concatenate(
        [to_half(columns_of(matrices, bounds, piece)) for piece in last_names], axis=1
    )
    weights = {}
    for batch, batch_half in ((first_names, first_half), (last_names, last_half)):
        gathered = lax.all_gather(batch_half, "fsdp", axis=0, tiled=True)
        offset = 0
        for piece in batch:
            extent = bounds[piece][1] - bounds[piece][0]
            weights[piece] = gathered[:, offset : offset + extent]
            offset = offset + extent
        if batch is first_names:
            small_params = gathered[:, offset:].astype(jnp.float32)
    inputs_ids = jnp.concatenate([LANGTOK + language, text_ids[0, :-1]])[None, :]
    ids_all = lax.all_gather(
        jnp.concatenate([inputs_ids, text_ids], axis=1), ("rep", "fsdp"), axis=0, tiled=True
    ).reshape(reps, members, 2, TLEN)
    order = [(replica - shift) % reps for shift in range(reps)]
    ids_by_shift = [pick(ids_all, place, 0) for place in order]
    group_inputs = [ids[:, 0].reshape(-1) for ids in ids_by_shift]
    group_targets = [ids[:, 1].reshape(-1) for ids in ids_by_shift]
    counts_by_shift = [
        (
            lax.broadcasted_iota(jnp.int32, (members, TLEN), 1)
            < lax.dynamic_slice_in_dim(text_lengths, place * members, members)[:, None]
        ).reshape(-1)
        for place in order
    ]
    vocab_rows = embedding.shape[0]
    vocab_start = member * vocab_rows
    embed_half = to_half(embedding)
    vocab_iota = lax.broadcasted_iota(jnp.int32, (members * TLEN, vocab_rows), 1)
    input_hot = [to_half(ids[:, None] - vocab_start == vocab_iota) for ids in group_inputs]
    embedded = lax.psum_scatter(
        matmul(input_hot[0], embed_half).astype(jnp.bfloat16), "fsdp", scatter_dimension=0, tiled=True
    ).astype(jnp.float32)
    enc_zero, stem_saved, stem_acts = stem_forward(mel_frames[0], weights, small_params)
    enc_one, enc_self, enc_self_acts = self_block(
        enc_zero, weights, small_params, EncSlots, "eq", "eo", False
    )
    enc_two, enc_mlp, enc_mlp_acts = mlp_block(
        enc_one, weights, small_params, EncSlots, "eu", "ed"
    )
    memory_half = to_half(
        layer_norm(
            enc_two,
            small_params[:, EncSlots.final_gain],
            small_params[:, EncSlots.final_bias],
        )
    )
    cols_even, cols_odd, act_even, act_odd = stem_acts
    (
        act_even_all,
        act_odd_all,
        enc_normed_all,
        enc_attended_all,
        enc_mid_all,
        memory_all,
        enc_active_all,
        cols_even_all,
        cols_odd_all,
    ) = pool(
        [act_even, act_odd, *enc_self_acts, enc_mlp_acts[0], memory_half],
        [enc_mlp_acts[1], cols_even, cols_odd],
    )
    dec_zero = embedded + weights["dp"].T.astype(jnp.float32)
    dec_one, dec_self, dec_self_acts = self_block(
        dec_zero, weights, small_params, DecSlots, "dq", "do", True
    )
    dec_two, dec_cross, dec_cross_acts = cross_block(dec_one, memory_half, weights, small_params)
    dec_three, dec_mlp, dec_mlp_acts = mlp_block(
        dec_two, weights, small_params, DecSlots, "du", "dd"
    )
    (
        dec_normed_all,
        dec_attended_all,
        cross_normed_all,
        cross_attended_all,
        dec_mid_all,
        dec_active_all,
    ) = pool([*dec_self_acts, *dec_cross_acts, dec_mlp_acts[0]], [dec_mlp_acts[1]])
    final_out = layer_norm(
        dec_three,
        small_params[:, DecSlots.final_gain],
        small_params[:, DecSlots.final_bias],
    )
    gathered_hidden = lax.all_gather(to_half(final_out), "fsdp", axis=0, tiled=True)
    logits = matmul_t(gathered_hidden, embed_half)
    vocab_keep = (lax.dynamic_slice_in_dim(vocab_mask, vocab_start, vocab_rows) == 1)[None, :]
    masked = jnp.where(vocab_keep, logits, NEG_BIG)
    local_top = jnp.max(masked, axis=1)
    local_sum = jnp.sum(jnp.where(vocab_keep, jnp.exp(masked - local_top[:, None]), 0.0), axis=1)
    target_hits = group_targets[0][:, None] - vocab_start == vocab_iota
    local_target = jnp.sum(jnp.where(target_hits, logits, 0.0), axis=1)
    local_total = jnp.sum(jnp.where(vocab_keep, logits, 0.0), axis=1)
    stats = gather_small(
        jnp.stack([local_top, local_sum, local_target, local_total]).reshape(-1, 128), 0
    ).reshape(members, 4, members * TLEN)
    row_top = jnp.max(stats[:, 0], axis=0)
    row_sums = jnp.sum(stats[:, 1] * jnp.exp(stats[:, 0] - row_top[None]), axis=0)
    target_logit = jnp.sum(stats[:, 2], axis=0)
    logit_total = jnp.sum(stats[:, 3], axis=0)
    log_norm = row_top + jnp.log(row_sums)
    vocab_count = jnp.sum(vocab_mask).astype(jnp.float32)
    entropy = log_norm - (1.0 - SMOOTH) * target_logit - SMOOTH * logit_total / vocab_count
    norm_and_loss = jnp.stack([log_norm, jnp.where(counts_by_shift[0], entropy, 0.0)])
    norms_by_shift = [norm_and_loss] + [send_rep(norm_and_loss, shift) for shift in range(1, reps)]
    loss_sum = sum(jnp.sum(part[1]) for part in norms_by_shift)

    def logit_grads(shift, own_logits):
        hits = group_targets[shift][:, None] - vocab_start == vocab_iota
        softmax_part = jnp.where(
            vocab_keep,
            jnp.exp(
                jnp.where(vocab_keep, own_logits, NEG_BIG) - norms_by_shift[shift][0][:, None]
            ),
            0.0,
        )
        return to_half(
            jnp.where(
                counts_by_shift[shift][:, None],
                softmax_part
                - (1.0 - SMOOTH) * hits.astype(jnp.float32)
                - SMOOTH * vocab_keep.astype(jnp.float32) / vocab_count,
                0.0,
            )
        )

    back_logits = logit_grads(0, logits)
    back_hidden = lax.psum_scatter(
        matmul(back_logits, embed_half), "fsdp", scatter_dimension=0, tiled=True
    )
    vector_grads = {}
    back_three, final_gain, final_bias = norm_back(
        dec_three,
        small_params[:, DecSlots.final_gain],
        small_params[:, DecSlots.final_bias],
        back_hidden,
    )
    vector_grads[DecSlots.final_gain] = final_gain
    vector_grads[DecSlots.final_bias] = final_bias
    back_two, dec_down_grad, dec_up_grad = mlp_block_back(
        dec_mlp, back_three, weights, small_params, DecSlots, "du", "dd", vector_grads
    )
    dec_down_all, dec_up_all = pool([dec_down_grad], [dec_up_grad])
    back_one, back_memory, xout_grad, xquery_grad, xkeyval_grad = cross_block_back(
        dec_cross, back_two, weights, small_params, vector_grads
    )
    back_zero, dec_out_grad, dec_qkv_grad = self_block_back(
        dec_self, back_one, weights, small_params, DecSlots, "dq", "do", True, vector_grads
    )
    xout_all, xquery_all, dec_out_all, dec_qkv_all = pool(
        [], [xout_grad, xquery_grad, dec_out_grad, dec_qkv_grad]
    )
    grads = {}
    dec_names = ("dd", "du", "xo", "xq", "do", "dq")
    for piece, rows in zip(
        dec_names,
        whole_rows(
            [
                tmatmul(dec_down_all, dec_active_all),
                tmatmul(dec_mid_all, dec_up_all),
                tmatmul(cross_attended_all, xout_all),
                tmatmul(cross_normed_all, xquery_all),
                tmatmul(dec_attended_all, dec_out_all),
                tmatmul(dec_normed_all, dec_qkv_all),
            ]
        ),
    ):
        grads[piece] = rows
    gathered_back = lax.all_gather(to_half(back_zero), "fsdp", axis=0, tiled=True)
    back_enc_two, enc_gain, enc_bias = norm_back(
        enc_two,
        small_params[:, EncSlots.final_gain],
        small_params[:, EncSlots.final_bias],
        back_memory,
    )
    vector_grads[EncSlots.final_gain] = enc_gain
    vector_grads[EncSlots.final_bias] = enc_bias
    back_enc_one, enc_down_grad, enc_up_grad = mlp_block_back(
        enc_mlp, back_enc_two, weights, small_params, EncSlots, "eu", "ed", vector_grads
    )
    enc_down_all, enc_up_all, xkeyval_all = pool([enc_down_grad], [enc_up_grad, xkeyval_grad])
    back_enc_zero, enc_out_grad, enc_qkv_grad = self_block_back(
        enc_self, back_enc_one, weights, small_params, EncSlots, "eq", "eo", False, vector_grads
    )
    grad_second, grad_even, grad_odd = stem_back(stem_saved, back_enc_zero, weights, vector_grads)
    grad_even_all, grad_odd_all, enc_out_all, enc_qkv_all, second_all = pool(
        [grad_even, grad_odd], [enc_out_grad, enc_qkv_grad, grad_second]
    )
    frames = act_odd.shape[0]
    shifted_all = jnp.pad(act_odd_all.reshape(-1, frames, D), ((0, 0), (1, 0), (0, 0)))[
        :, :-1
    ].reshape(-1, D)
    vector_total = jnp.stack([vector_grads[column] for column in range(NVEC)], axis=1)
    extra = TLEN + NVEC
    extra_pad = -extra % (8 * CORES * reps)
    loose = pool_sum(
        jnp.concatenate(
            [back_zero.T, vector_total, jnp.zeros((D, extra_pad), jnp.float32)], axis=1
        )
    )
    enc_names = ("ed", "eu", "xk", "eo", "eq", "c2a", "c2b", "c2c", "c1", "dp")
    for piece, rows in zip(
        enc_names,
        whole_rows(
            [
                tmatmul(enc_down_all, enc_active_all),
                tmatmul(enc_mid_all, enc_up_all),
                tmatmul(memory_all, xkeyval_all),
                tmatmul(enc_attended_all, enc_out_all),
                tmatmul(enc_normed_all, enc_qkv_all),
                tmatmul(shifted_all, second_all),
                tmatmul(act_even_all, second_all),
                tmatmul(act_odd_all, second_all),
                tmatmul(
                    token_rows([grad_even_all, grad_odd_all]),
                    token_rows([cols_even_all, cols_odd_all]),
                ),
                loose,
            ]
        ),
    ):
        grads[piece] = rows
    grads["c2"] = jnp.concatenate([grads["c2a"], grads["c2b"], grads["c2c"]], axis=1)
    vec_grad = grads["dp"][:, TLEN : TLEN + NVEC]
    grads["dp"] = grads["dp"][:, :TLEN]
    mat_grad = jnp.concatenate([grads[piece] for piece in names], axis=1)
    head_terms = [tmatmul(back_logits, gathered_hidden)]
    lookup_terms = [tmatmul(input_hot[0], gathered_back)]
    for shift in range(1, reps):
        other_hidden = send_rep(gathered_hidden, shift)
        other_logits = logit_grads(shift, matmul_t(other_hidden, embed_half))
        head_terms.append(tmatmul(other_logits, other_hidden))
        lookup_terms.append(tmatmul(input_hot[shift], send_rep(gathered_back, shift)))
    embed_grad = sum(head_terms[1:], head_terms[0]) + sum(lookup_terms[1:], lookup_terms[0])
    sums = total_of(
        jnp.stack(
            [
                jnp.sum(mat_grad * mat_grad)
                + jnp.sum(vec_grad * vec_grad)
                + jnp.sum(embed_grad * embed_grad),
                count_bad(mat_grad) + count_bad(embed_grad) + count_bad(vec_grad),
            ]
        ),
        1,
    )
    total_squares, total_bad = sums[0], sums[1]
    gradient_norm = jnp.sqrt(total_squares)
    factor = CLIP_AT / jnp.maximum(gradient_norm, CLIP_AT)
    steps = step_count[0].astype(jnp.float32)
    first_fix = 1.0 - jnp.power(jnp.float32(BETA_ONE), steps)
    second_fix = 1.0 - jnp.power(jnp.float32(BETA_TWO), steps)
    mat_moment, mat_square, mat_update = moments(
        matrices, matrix_moment, matrix_square, mat_grad, factor, first_fix, second_fix
    )
    emb_moment, emb_square, emb_update = moments(
        embedding, embed_moment, embed_square, embed_grad, factor, first_fix, second_fix
    )
    vec_moment, vec_square, vec_update = moments(
        vectors, vector_moment, vector_square, vec_grad, factor, first_fix, second_fix
    )
    update_parts = group_squares(mat_update, emb_update, vec_update, bounds, names)
    weight_parts = group_squares(matrices, embedding, vectors, bounds, names)
    groups = len(names) + 2
    both_sums = total_of(jnp.concatenate([weight_parts, update_parts]), 2)
    weight_norms = jnp.sqrt(both_sums[:groups])
    update_norms = jnp.sqrt(both_sums[groups:])
    ratio = weight_norms / update_norms
    ratio_columns = jnp.concatenate(
        [
            jnp.full((bounds[piece_name][1] - bounds[piece_name][0],), 1.0, jnp.float32)
            * ratio[position]
            for position, piece_name in enumerate(names)
        ]
    )
    new_matrices = matrices - RATE * ratio_columns[None, :] * mat_update
    new_embedding = embedding - RATE * ratio[len(names)] * emb_update
    new_vectors = vectors - RATE * ratio[len(names) + 1] * vec_update
    mean_loss = loss_sum / jnp.sum(text_lengths).astype(jnp.float32)
    group_norms = jnp.stack([weight_norms, update_norms], axis=1)
    return (
        mean_loss,
        total_bad.astype(jnp.int32),
        gradient_norm,
        group_norms,
        new_matrices,
        mat_moment,
        mat_square,
        new_embedding,
        emb_moment,
        emb_square,
        new_vectors,
        vec_moment,
        vec_square,
    )


def solution(mesh):
    placed = (
        P(("rep", "fsdp"), None, None),
        P(("rep", "fsdp"), None),
        P(),
        P(("rep", "fsdp")),
        P(),
        P(),
        P("fsdp", None),
        P("fsdp", None),
        P("fsdp", None),
        P("fsdp", None),
        P("fsdp", None),
        P("fsdp", None),
        P("fsdp", None),
        P("fsdp", None),
        P("fsdp", None),
    )
    return jax.shard_map(
        on_device,
        mesh=mesh,
        in_specs=placed,
        out_specs=(
            P(),
            P(),
            P(),
            P(),
            P("fsdp", None),
            P("fsdp", None),
            P("fsdp", None),
            P("fsdp", None),
            P("fsdp", None),
            P("fsdp", None),
            P("fsdp", None),
            P("fsdp", None),
            P("fsdp", None),
        ),
        check_vma=False,
    )
```

```python
import functools

import jax
import jax.numpy as jnp
from jax import lax
from jax.experimental import pallas as pl
from jax.experimental.pallas import tpu as pltpu
from jax.sharding import PartitionSpec as P

D = 768
H = 12
HD = 64
FF = 3072
MELS = 80
TLEN = 128
LANGTOK = 50259
NVEC = 35


LN_EPS = 1e-05
SMOOTH = 0.1
CLIP_AT = 1.0
BETA_ONE = 0.9
BETA_TWO = 0.999
ADAM_EPS = 1e-06
DECAY = 0.01
RATE = 0.5
NEG_BIG = -1e30
class EncSlots:
    norm_gain = 2
    norm_bias = 3
    query_bias = 4
    value_bias = 5
    out_bias = 6
    mlp_gain = 7
    mlp_bias = 8
    up_bias = 9
    down_bias = 13
    final_gain = 14
    final_bias = 15


class DecSlots:
    norm_gain = 16
    norm_bias = 17
    query_bias = 18
    value_bias = 19
    out_bias = 20
    cross_gain = 21
    cross_bias = 22
    xquery_bias = 23
    xvalue_bias = 24
    xout_bias = 25
    mlp_gain = 26
    mlp_bias = 27
    up_bias = 28
    down_bias = 32
    final_gain = 33
    final_bias = 34


CORES = 2
LINE = 4


def mesh_shape():
    members = lax.axis_size("fsdp")
    return (lax.axis_size("rep"), LINE, members // (LINE * CORES), CORES)


def places():
    reps, line, side, cores = mesh_shape()
    index = lax.axis_index("fsdp")
    return (
        lax.axis_index("rep"),
        index // (side * cores),
        (index // cores) % side,
        index % cores,
    )


def send(values, move):
    reps, line, side, cores = mesh_shape()
    members = line * side * cores
    pairs = []
    for rep in range(reps):
        for far in range(line):
            for near in range(side):
                for core in range(cores):
                    target = move(rep, far, near, core)
                    if target is None:
                        continue
                    rep_to, far_to, near_to, core_to = target
                    pairs.append(
                        (
                            rep * members + (far * side + near) * cores + core,
                            rep_to * members + (far_to * side + near_to) * cores + core_to,
                        )
                    )
    return lax.ppermute(values, ("rep", "fsdp"), pairs)


def send_core(values):
    return send(values, lambda rep, far, near, core: (rep, far, near, 1 - core))


def send_rep(values, shift):
    reps = lax.axis_size("rep")
    return send(values, lambda rep, far, near, core: ((rep + shift) % reps, far, near, core))


def pick(values, index, axis):
    return lax.dynamic_index_in_dim(values, index, axis, keepdims=False)


def block(values, index, width):
    return lax.dynamic_slice_in_dim(values, index * width, width, axis=1)


def pool(narrows, wides):
    reps = lax.axis_size("rep")
    rep, _, _, core = places()
    tall = sum(part.shape[1] for part in narrows)
    spans = [part.shape[1] // reps for part in wides]
    got = []
    for shift in range(reps):
        parts = list(narrows) + [
            block(part, (rep + shift) % reps, span) for part, span in zip(wides, spans)
        ]
        joint = parts[0] if len(parts) == 1 else jnp.concatenate(parts, axis=1)
        got.append(send_rep(joint, shift) if shift else joint)
    joint = jnp.concatenate(got, axis=0)
    offsets = [tall + sum(spans[:position]) for position in range(len(spans))]

    def halves(side):
        parts = [joint[:, :tall]] if tall else []
        for offset, span in zip(offsets, spans):
            parts.append(block(joint[:, offset : offset + span], side, span // CORES))
        return parts[0] if len(parts) == 1 else jnp.concatenate(parts, axis=1)

    both = jnp.concatenate([halves(core), send_core(halves(1 - core))], axis=0)
    results = []
    offset = 0
    for part in narrows:
        results.append(both[:, offset : offset + part.shape[1]])
        offset = offset + part.shape[1]
    for span in spans:
        results.append(both[:, offset : offset + span // CORES])
        offset = offset + span // CORES
    return results


def pool_sum(values):
    reps = lax.axis_size("rep")
    rep, _, _, core = places()
    span = values.shape[1] // reps
    total = block(values, rep, span)
    for shift in range(1, reps):
        total = total + send_rep(block(values, (rep + shift) % reps, span), shift)
    return block(total, core, span // CORES) + send_core(
        block(total, 1 - core, span // CORES)
    )


def in_order(stack, position):
    count = len(stack)
    joint = jnp.stack(stack)
    return jnp.stack([pick(joint, (position - place) % count, 0) for place in range(count)])


def scatter_body(cored, count, values, output, *scratch):
    reps, line, side, cores = mesh_shape()
    rep, far, near, core = places()
    members = line * side * cores
    if cored:
        core_in, core_sum = scratch[:2]
        scratch = scratch[2:]
    near_in, near_sum, far_in, leaving, landing = scratch
    wide = output.shape[-1] // count

    def at(far_to, near_to, core_to):
        return {"fsdp": (far_to * side + near_to) * cores + core_to}

    barrier = pltpu.get_barrier_semaphore()
    partners = [at(lax.rem(far + step, line), near, core) for step in range(1, line)]
    partners += [at(far, lax.rem(near + step, side), core) for step in range(1, side)]
    if cored:
        partners.append(at(far, near, 1 - core))
    for partner in partners:
        pl.semaphore_signal(barrier, inc=1, device_id=partner)
    pl.semaphore_wait(barrier, len(partners))

    started = []

    def start(source, target, device):
        slot = len(started)
        copy = pltpu.make_async_remote_copy(
            src_ref=source,
            dst_ref=target,
            send_sem=leaving.at[slot],
            recv_sem=landing.at[slot],
            device_id=device,
        )
        copy.start()
        started.append(copy)
        return copy

    spans = [pl.ds(part * wide, wide) for part in range(count)]
    core_moves = []
    if cored:
        for part in range(count):
            core_moves.append(
                start(
                    values.at[:, :, 1 - core, :, spans[part]],
                    core_in.at[part],
                    at(far, near, 1 - core),
                )
            )
    near_moves = []
    for part in range(count):
        if cored:
            core_moves[part].wait_recv()
            core_sum[part] = values[:, :, core, :, spans[part]] + core_in[part]
        moves = []
        for step in range(1, side):
            there = lax.rem(near + step, side)
            source = core_sum.at[part, :, there] if cored else values.at[:, there, :, spans[part]]
            moves.append(start(source, near_in.at[part, step - 1], at(far, there, core)))
        near_moves.append(moves)
    far_moves = []
    for part in range(count):
        total = core_sum[part, :, near] if cored else values[:, near, :, spans[part]]
        for step, move in enumerate(near_moves[part]):
            move.wait_recv()
            total = total + near_in[part, step]
        near_sum[part] = total
        moves = []
        for step in range(1, line):
            there = lax.rem(far + step, line)
            moves.append(
                start(near_sum.at[part, there], far_in.at[part, step - 1], at(there, near, core))
            )
        far_moves.append(moves)
    for part in range(count):
        total = near_sum[part, far]
        for step, move in enumerate(far_moves[part]):
            move.wait_recv()
            total = total + far_in[part, step]
        output[:, spans[part]] = total
    for move in started:
        move.wait_send()


def scatter_sum(values, count, cored, tag):
    reps, line, side, cores = mesh_shape()
    rows = values.shape[0] // (line * side * (cores if cored else 1))
    width = values.shape[1]
    wide = width // count
    kind = values.dtype
    shape = (line, side) + ((cores,) if cored else ()) + (rows, width)
    copies = count * ((1 if cored else 0) + (side - 1) + (line - 1))
    cube = (count, line, side, rows, wide)
    scratch = [pltpu.VMEM(cube, kind), pltpu.VMEM(cube, kind)] if cored else []
    scratch += [
        pltpu.VMEM((count, side - 1, line, rows, wide), kind),
        pltpu.VMEM((count, line, rows, wide), kind),
        pltpu.VMEM((count, line - 1, rows, wide), kind),
        pltpu.SemaphoreType.DMA((copies,)),
        pltpu.SemaphoreType.DMA((copies,)),
    ]
    return pl.pallas_call(
        functools.partial(scatter_body, cored, count),
        out_shape=jax.ShapeDtypeStruct((rows, width), kind),
        in_specs=[pl.BlockSpec(memory_space=pltpu.VMEM)],
        out_specs=pl.BlockSpec(memory_space=pltpu.VMEM),
        scratch_shapes=scratch,
        compiler_params=pltpu.CompilerParams(
            collective_id=tag, has_side_effects=True, vmem_limit_bytes=60 << 20
        ),
    )(values.reshape(shape))


def whole_rows(pieces, tag=None):
    reps, line, side, cores = mesh_shape()
    rep, _, _, core = places()
    rows = pieces[0].shape[0]
    own_rows = rows // (line * side * cores)
    members = line * side * cores
    joint = jnp.concatenate(pieces, axis=1)
    if tag is None:
        groups = [list(range(place, members, cores)) for place in range(cores)]
        summed = lax.psum_scatter(
            joint, "fsdp", scatter_dimension=0, axis_index_groups=groups, tiled=True
        )
    else:
        summed = scatter_sum(joint, 3, False, tag)
    by_core = summed.reshape(cores, own_rows, summed.shape[1])
    cores_joint = in_order([pick(by_core, core, 0), send_core(pick(by_core, 1 - core, 0))], core)
    reps_joint = in_order(
        [cores_joint] + [send_rep(cores_joint, shift) for shift in range(1, reps)], rep
    )
    results = []
    offset = 0
    for part in pieces:
        span = part.shape[1]
        own = reps_joint[:, :, :, offset : offset + span]
        results.append(
            jnp.transpose(own, (2, 0, 1, 3)).reshape(own.shape[2], reps * CORES * span)
        )
        offset = offset + span
    return results


def gather_body(values, gathered, leaving, landing):
    members = lax.axis_size("fsdp")
    here = lax.axis_index("fsdp")
    barrier = pltpu.get_barrier_semaphore()
    for shift in range(1, members):
        pl.semaphore_signal(barrier, inc=1, device_id={"fsdp": lax.rem(here + shift, members)})
    pl.semaphore_wait(barrier, members - 1)
    copies = []
    for shift in range(1, members):
        copies.append(
            pltpu.make_async_remote_copy(
                src_ref=values,
                dst_ref=gathered.at[here],
                send_sem=leaving.at[shift - 1],
                recv_sem=landing.at[shift - 1],
                device_id={"fsdp": lax.rem(here + shift, members)},
            )
        )
        copies[-1].start()
    gathered[here] = values[...]
    for copy in copies:
        copy.wait()


def gather_small(values, tag):
    members = lax.axis_size("fsdp")
    return pl.pallas_call(
        gather_body,
        out_shape=jax.ShapeDtypeStruct((members,) + values.shape, values.dtype),
        in_specs=[pl.BlockSpec(memory_space=pltpu.VMEM)],
        out_specs=pl.BlockSpec(memory_space=pltpu.VMEM),
        scratch_shapes=[
            pltpu.SemaphoreType.DMA((members - 1,)),
            pltpu.SemaphoreType.DMA((members - 1,)),
        ],
        compiler_params=pltpu.CompilerParams(collective_id=tag, has_side_effects=True),
    )(values)


def total_of(values, tag):
    count = values.shape[0]
    padded = jnp.zeros((8, 128), jnp.float32).at[0, :count].set(values)
    return jnp.sum(gather_small(padded, tag), axis=0)[0, :count]


def layout(width, hidden, mels, text_len):
    names = (
        "eq",
        "eo",
        "eu",
        "ed",
        "dq",
        "do",
        "xq",
        "xk",
        "xo",
        "du",
        "dd",
        "c2",
        "c1",
        "dp",
    )
    widths = (
        3 * width,
        width,
        hidden,
        hidden,
        3 * width,
        width,
        width,
        2 * width,
        width,
        hidden,
        hidden,
        3 * width,
        3 * mels,
        text_len,
    )
    bounds = {}
    offset = 0
    for piece_name, extent in zip(names, widths):
        bounds[piece_name] = (offset, offset + extent)
        offset = offset + extent
    return (names, bounds)


def columns_of(weights, bounds, piece_name):
    span_start, span_stop = bounds[piece_name]
    return weights[:, span_start:span_stop]


def sinusoid(length, width):
    halfway = width // 2
    increment = jnp.log(10000.0) / (halfway - 1)
    rates = jnp.exp(-increment * jnp.arange(halfway, dtype=jnp.float32))
    angles = jnp.arange(length, dtype=jnp.float32)[:, None] * rates[None, :]
    return jnp.concatenate([jnp.sin(angles), jnp.cos(angles)], axis=1)


def layer_norm(inputs, gain, offset):
    average = jnp.mean(inputs, axis=-1, keepdims=True)
    centred = inputs - average
    spread = jnp.mean(centred * centred, axis=-1, keepdims=True)
    return centred * lax.rsqrt(spread + LN_EPS) * gain + offset


def norm_back(inputs, gain, offset, upstream):
    _, pull = jax.vjp(layer_norm, inputs, gain, offset)
    return pull(upstream)


def gelu_exact(values):
    return jax.nn.gelu(values, approximate=False)


def gelu_back(values, upstream):
    _, pull = jax.vjp(gelu_exact, values)
    return pull(upstream)[0]


def to_half(values):
    return values.astype(jnp.bfloat16)


def matmul(left, right):
    return jnp.dot(left, right, preferred_element_type=jnp.float32)


def matmul_t(left, right):
    return lax.dot_general(
        left, right, (((1,), (1,)), ((), ())), preferred_element_type=jnp.float32
    )


def tmatmul(left, right):
    return lax.dot_general(
        left, right, (((0,), (0,)), ((), ())), preferred_element_type=jnp.float32
    )


def heads(values):
    return values.reshape(values.shape[0], H, HD)


def merged(values):
    return values.reshape(values.shape[0], H * HD)


def scores_of(query_heads, key_heads, causal):
    scores = jnp.einsum(
        "qhd,khd->hqk", query_heads, key_heads, preferred_element_type=jnp.float32
    ) * HD ** (-0.5)
    if causal:
        rows = lax.broadcasted_iota(jnp.int32, scores.shape, 1)
        cols = lax.broadcasted_iota(jnp.int32, scores.shape, 2)
        scores = jnp.where(rows >= cols, scores, NEG_BIG)
    return scores


def attend(queries, keys_half, values_half, causal):
    scores = scores_of(heads(queries), heads(keys_half), causal)
    row_top = jnp.max(scores, axis=-1, keepdims=True)
    log_total = row_top + jnp.log(jnp.sum(jnp.exp(scores - row_top), axis=-1, keepdims=True))
    weights_soft = jnp.exp(scores - log_total)
    attended = jnp.einsum(
        "hqk,khd->qhd",
        to_half(weights_soft),
        heads(values_half),
        preferred_element_type=jnp.float32,
    )
    return (to_half(merged(attended)), log_total)


def attend_back(queries, keys_half, values_half, causal, log_total, back_attended):
    query_heads = heads(queries)
    key_heads = heads(keys_half)
    grad_heads = heads(back_attended)
    weights_soft = jnp.exp(scores_of(query_heads, key_heads, causal) - log_total)
    back_weights = jnp.einsum(
        "qhd,khd->hqk", grad_heads, heads(values_half), preferred_element_type=jnp.float32
    )
    back_values = jnp.einsum(
        "hqk,qhd->khd", to_half(weights_soft), grad_heads, preferred_element_type=jnp.float32
    )
    inner = jnp.sum(weights_soft * back_weights, axis=-1, keepdims=True)
    back_scores = to_half(weights_soft * (back_weights - inner) * HD ** (-0.5))
    back_queries = jnp.einsum(
        "hqk,khd->qhd", back_scores, key_heads, preferred_element_type=jnp.float32
    )
    back_keys = jnp.einsum(
        "hqk,qhd->khd", back_scores, query_heads, preferred_element_type=jnp.float32
    )
    return (merged(back_queries), merged(back_keys), merged(back_values))


def self_block(stream, weights, small_params, slots, qkv_name, out_name, causal):
    normed = layer_norm(
        stream, small_params[:, slots.norm_gain], small_params[:, slots.norm_bias]
    )
    normed_half = to_half(normed)
    projected = matmul(normed_half, weights[qkv_name])
    queries = to_half(projected[:, :D] + small_params[:, slots.query_bias])
    keys_half = to_half(projected[:, D : 2 * D])
    values_half = to_half(projected[:, 2 * D :] + small_params[:, slots.value_bias])
    attended, log_total = attend(queries, keys_half, values_half, causal)
    output = (
        stream + matmul(attended, weights[out_name]) + small_params[:, slots.out_bias]
    )
    return (output, (stream, queries, keys_half, values_half, log_total), (normed_half, attended))


def self_block_back(
    saved, upstream, weights, small_params, slots, qkv_name, out_name, causal, vector_grads
):
    stream, queries, keys_half, values_half, log_total = saved
    grad_out = to_half(upstream)
    back_attended = to_half(matmul_t(grad_out, weights[out_name]))
    back_queries, back_keys, back_values = attend_back(
        queries, keys_half, values_half, causal, log_total, back_attended
    )
    grad_proj = to_half(jnp.concatenate([back_queries, back_keys, back_values], axis=1))
    back_normed = matmul_t(grad_proj, weights[qkv_name])
    back_stream, back_gain, back_bias = norm_back(
        stream,
        small_params[:, slots.norm_gain],
        small_params[:, slots.norm_bias],
        back_normed,
    )
    vector_grads[slots.norm_gain] = back_gain
    vector_grads[slots.norm_bias] = back_bias
    vector_grads[slots.query_bias] = jnp.sum(back_queries, axis=0)
    vector_grads[slots.value_bias] = jnp.sum(back_values, axis=0)
    vector_grads[slots.out_bias] = jnp.sum(upstream, axis=0)
    return (upstream + back_stream, grad_out, grad_proj)


def cross_block(stream, memory_half, weights, small_params):
    normed = layer_norm(
        stream, small_params[:, DecSlots.cross_gain], small_params[:, DecSlots.cross_bias]
    )
    normed_half = to_half(normed)
    queries = to_half(
        matmul(normed_half, weights["xq"]) + small_params[:, DecSlots.xquery_bias]
    )
    keyval = matmul(memory_half, weights["xk"])
    keys_half = to_half(keyval[:, :D])
    values_half = to_half(keyval[:, D:] + small_params[:, DecSlots.xvalue_bias])
    attended, log_total = attend(queries, keys_half, values_half, False)
    output = (
        stream + matmul(attended, weights["xo"]) + small_params[:, DecSlots.xout_bias]
    )
    return (output, (stream, queries, keys_half, values_half, log_total), (normed_half, attended))


def cross_block_back(saved, upstream, weights, small_params, vector_grads):
    stream, queries, keys_half, values_half, log_total = saved
    grad_out = to_half(upstream)
    back_attended = to_half(matmul_t(grad_out, weights["xo"]))
    back_queries, back_keys, back_values = attend_back(
        queries, keys_half, values_half, False, log_total, back_attended
    )
    grad_query = to_half(back_queries)
    back_normed = matmul_t(grad_query, weights["xq"])
    grad_keyval = to_half(jnp.concatenate([back_keys, back_values], axis=1))
    back_memory = matmul_t(grad_keyval, weights["xk"])
    back_stream, back_gain, back_bias = norm_back(
        stream,
        small_params[:, DecSlots.cross_gain],
        small_params[:, DecSlots.cross_bias],
        back_normed,
    )
    vector_grads[DecSlots.cross_gain] = back_gain
    vector_grads[DecSlots.cross_bias] = back_bias
    vector_grads[DecSlots.xquery_bias] = jnp.sum(back_queries, axis=0)
    vector_grads[DecSlots.xvalue_bias] = jnp.sum(back_values, axis=0)
    vector_grads[DecSlots.xout_bias] = jnp.sum(upstream, axis=0)
    return (upstream + back_stream, back_memory, grad_out, grad_query, grad_keyval)


def mlp_block(stream, weights, small_params, slots, up_name, down_name):
    normed = layer_norm(
        stream, small_params[:, slots.mlp_gain], small_params[:, slots.mlp_bias]
    )
    normed_half = to_half(normed)
    up_bias = small_params[:, slots.up_bias : slots.up_bias + 4].T.reshape(-1)
    raised = matmul(normed_half, weights[up_name]) + up_bias
    active = to_half(gelu_exact(raised))
    output = (
        stream + matmul_t(active, weights[down_name]) + small_params[:, slots.down_bias]
    )
    return (output, (stream, raised), (normed_half, active))


def mlp_block_back(saved, upstream, weights, small_params, slots, up_name, down_name, vector_grads):
    stream, raised = saved
    grad_out = to_half(upstream)
    back_raised = gelu_back(raised, matmul(grad_out, weights[down_name]))
    bias_rows = jnp.sum(back_raised, axis=0).reshape(4, D)
    for quarter in range(4):
        vector_grads[slots.up_bias + quarter] = bias_rows[quarter]
    grad_raised = to_half(back_raised)
    back_normed = matmul_t(grad_raised, weights[up_name])
    back_stream, back_gain, back_bias = norm_back(
        stream, small_params[:, slots.mlp_gain], small_params[:, slots.mlp_bias], back_normed
    )
    vector_grads[slots.mlp_gain] = back_gain
    vector_grads[slots.mlp_bias] = back_bias
    vector_grads[slots.down_bias] = jnp.sum(upstream, axis=0)
    return (upstream + back_stream, grad_out, grad_raised)


def down_one(values):
    return jnp.pad(values, ((1, 0), (0, 0)))[:-1]


def up_one(values):
    return jnp.pad(values, ((0, 1), (0, 0)))[1:]


def stem_forward(mel_half, weights, small_params):
    bins, frames_in = mel_half.shape
    paired = mel_half.T.reshape(frames_in // 2, 2 * bins)
    mel_even, mel_odd = paired[:, :bins], paired[:, bins:]
    cols_even = jnp.concatenate([down_one(mel_odd), mel_even, mel_odd], axis=1)
    cols_odd = jnp.concatenate([mel_even, mel_odd, up_one(mel_even)], axis=1)
    pre_even = matmul_t(cols_even, weights["c1"]) + small_params[:, 0]
    pre_odd = matmul_t(cols_odd, weights["c1"]) + small_params[:, 0]
    act_even = to_half(gelu_exact(pre_even))
    act_odd = to_half(gelu_exact(pre_odd))
    taps = weights["c2"]
    conv_sum = (
        matmul(down_one(act_odd), taps[:, :D])
        + matmul(act_even, taps[:, D : 2 * D])
        + matmul(act_odd, taps[:, 2 * D :])
    )
    second_pre = conv_sum + small_params[:, 1]
    stream = gelu_exact(second_pre) + sinusoid(frames_in // 2, D)
    return (stream, (pre_even, pre_odd, second_pre), (cols_even, cols_odd, act_even, act_odd))


def stem_back(saved, upstream, weights, vector_grads):
    pre_even, pre_odd, second_pre = saved
    back_second = gelu_back(second_pre, upstream)
    vector_grads[1] = jnp.sum(back_second, axis=0)
    grad_second = to_half(back_second)
    taps = weights["c2"]
    back_even = gelu_back(pre_even, matmul_t(grad_second, taps[:, D : 2 * D]))
    back_odd = gelu_back(
        pre_odd,
        matmul_t(grad_second, taps[:, 2 * D :])
        + matmul_t(up_one(grad_second), taps[:, :D]),
    )
    vector_grads[0] = jnp.sum(back_even, axis=0) + jnp.sum(back_odd, axis=0)
    return (grad_second, to_half(back_even), to_half(back_odd))


def token_rows(parts):
    return jnp.concatenate(parts, axis=0)


def moments(weight, moment, square, gradient, factor, first_fix, second_fix):
    scaled = gradient * factor
    new_moment = BETA_ONE * moment + (1.0 - BETA_ONE) * scaled
    new_square = BETA_TWO * square + (1.0 - BETA_TWO) * scaled * scaled
    update = new_moment * first_fix / (jnp.sqrt(new_square * second_fix) + ADAM_EPS) + DECAY * weight
    return (new_moment, new_square, update)


def group_squares(mat_part, embed_part, vec_part, bounds, names):
    parts = [jnp.sum(columns_of(mat_part, bounds, piece_name) ** 2) for piece_name in names]
    parts = parts + [jnp.sum(embed_part * embed_part), jnp.sum(vec_part * vec_part)]
    return jnp.stack(parts)


def count_bad(values):
    return jnp.sum(jnp.where(jnp.isfinite(values), 0.0, 1.0))


def on_device(
    mel_frames,
    text_ids,
    text_lengths,
    language,
    vocab_mask,
    step_count,
    matrices,
    matrix_moment,
    matrix_square,
    embedding,
    embed_moment,
    embed_square,
    vectors,
    vector_moment,
    vector_square,
):
    names, bounds = layout(D, FF, MELS, TLEN)
    reps = lax.axis_size("rep")
    members = lax.axis_size("fsdp")
    replica = lax.axis_index("rep")
    member = lax.axis_index("fsdp")
    first_names = ("c1", "c2", "eq", "eo", "eu", "ed")
    last_names = ("dq", "do", "xq", "xk", "xo", "du", "dd", "dp")
    first_half = jnp.concatenate(
        [to_half(columns_of(matrices, bounds, piece)) for piece in first_names]
        + [to_half(vectors)],
        axis=1,
    )
    last_half = jnp.concatenate(
        [to_half(columns_of(matrices, bounds, piece)) for piece in last_names], axis=1
    )
    weights = {}
    for batch, batch_half in ((first_names, first_half), (last_names, last_half)):
        gathered = lax.all_gather(batch_half, "fsdp", axis=0, tiled=True)
        offset = 0
        for piece in batch:
            extent = bounds[piece][1] - bounds[piece][0]
            weights[piece] = gathered[:, offset : offset + extent]
            offset = offset + extent
        if batch is first_names:
            small_params = gathered[:, offset:].astype(jnp.float32)
    inputs_ids = jnp.concatenate([LANGTOK + language, text_ids[0, :-1]])[None, :]
    ids_all = lax.all_gather(
        jnp.concatenate([inputs_ids, text_ids], axis=1), ("rep", "fsdp"), axis=0, tiled=True
    ).reshape(reps, members, 2, TLEN)
    order = [(replica - shift) % reps for shift in range(reps)]
    ids_by_shift = [pick(ids_all, place, 0) for place in order]
    group_inputs = [ids[:, 0].reshape(-1) for ids in ids_by_shift]
    group_targets = [ids[:, 1].reshape(-1) for ids in ids_by_shift]
    counts_by_shift = [
        (
            lax.broadcasted_iota(jnp.int32, (members, TLEN), 1)
            < lax.dynamic_slice_in_dim(text_lengths, place * members, members)[:, None]
        ).reshape(-1)
        for place in order
    ]
    vocab_rows = embedding.shape[0]
    vocab_start = member * vocab_rows
    embed_half = to_half(embedding)
    vocab_iota = lax.broadcasted_iota(jnp.int32, (members * TLEN, vocab_rows), 1)
    input_hot = [to_half(ids[:, None] - vocab_start == vocab_iota) for ids in group_inputs]
    embedded = scatter_sum(
        matmul(input_hot[0], embed_half).astype(jnp.bfloat16), 3, True, 3
    ).astype(jnp.float32)
    enc_zero, stem_saved, stem_acts = stem_forward(mel_frames[0], weights, small_params)
    enc_one, enc_self, enc_self_acts = self_block(
        enc_zero, weights, small_params, EncSlots, "eq", "eo", False
    )
    enc_two, enc_mlp, enc_mlp_acts = mlp_block(
        enc_one, weights, small_params, EncSlots, "eu", "ed"
    )
    memory_half = to_half(
        layer_norm(
            enc_two,
            small_params[:, EncSlots.final_gain],
            small_params[:, EncSlots.final_bias],
        )
    )
    cols_even, cols_odd, act_even, act_odd = stem_acts
    (
        act_even_all,
        act_odd_all,
        enc_normed_all,
        enc_attended_all,
        enc_mid_all,
        memory_all,
        enc_active_all,
        cols_even_all,
        cols_odd_all,
    ) = pool(
        [act_even, act_odd, *enc_self_acts, enc_mlp_acts[0], memory_half],
        [enc_mlp_acts[1], cols_even, cols_odd],
    )
    dec_zero = embedded + weights["dp"].T.astype(jnp.float32)
    dec_one, dec_self, dec_self_acts = self_block(
        dec_zero, weights, small_params, DecSlots, "dq", "do", True
    )
    dec_two, dec_cross, dec_cross_acts = cross_block(dec_one, memory_half, weights, small_params)
    dec_three, dec_mlp, dec_mlp_acts = mlp_block(
        dec_two, weights, small_params, DecSlots, "du", "dd"
    )
    (
        dec_normed_all,
        dec_attended_all,
        cross_normed_all,
        cross_attended_all,
        dec_mid_all,
        dec_active_all,
    ) = pool([*dec_self_acts, *dec_cross_acts, dec_mlp_acts[0]], [dec_mlp_acts[1]])
    final_out = layer_norm(
        dec_three,
        small_params[:, DecSlots.final_gain],
        small_params[:, DecSlots.final_bias],
    )
    gathered_hidden = lax.all_gather(to_half(final_out), "fsdp", axis=0, tiled=True)
    hidden_by_shift = [gathered_hidden] + [
        send_rep(gathered_hidden, shift) for shift in range(1, reps)
    ]
    logits = matmul_t(gathered_hidden, embed_half)
    vocab_keep = (lax.dynamic_slice_in_dim(vocab_mask, vocab_start, vocab_rows) == 1)[None, :]
    masked = jnp.where(vocab_keep, logits, NEG_BIG)
    local_top = jnp.max(masked, axis=1)
    local_sum = jnp.sum(jnp.where(vocab_keep, jnp.exp(masked - local_top[:, None]), 0.0), axis=1)
    target_hits = group_targets[0][:, None] - vocab_start == vocab_iota
    local_target = jnp.sum(jnp.where(target_hits, logits, 0.0), axis=1)
    local_total = jnp.sum(jnp.where(vocab_keep, logits, 0.0), axis=1)
    stats = gather_small(
        jnp.stack([local_top, local_sum, local_target, local_total]).reshape(-1, 128), 0
    ).reshape(members, 4, members * TLEN)
    row_top = jnp.max(stats[:, 0], axis=0)
    row_sums = jnp.sum(stats[:, 1] * jnp.exp(stats[:, 0] - row_top[None]), axis=0)
    target_logit = jnp.sum(stats[:, 2], axis=0)
    logit_total = jnp.sum(stats[:, 3], axis=0)
    log_norm = row_top + jnp.log(row_sums)
    vocab_count = jnp.sum(vocab_mask).astype(jnp.float32)
    entropy = log_norm - (1.0 - SMOOTH) * target_logit - SMOOTH * logit_total / vocab_count
    norm_and_loss = jnp.stack([log_norm, jnp.where(counts_by_shift[0], entropy, 0.0)])
    norms_by_shift = [norm_and_loss] + [send_rep(norm_and_loss, shift) for shift in range(1, reps)]
    loss_sum = sum(jnp.sum(part[1]) for part in norms_by_shift)

    def logit_grads(shift, own_logits):
        hits = group_targets[shift][:, None] - vocab_start == vocab_iota
        softmax_part = jnp.where(
            vocab_keep,
            jnp.exp(
                jnp.where(vocab_keep, own_logits, NEG_BIG) - norms_by_shift[shift][0][:, None]
            ),
            0.0,
        )
        return to_half(
            jnp.where(
                counts_by_shift[shift][:, None],
                softmax_part
                - (1.0 - SMOOTH) * hits.astype(jnp.float32)
                - SMOOTH * vocab_keep.astype(jnp.float32) / vocab_count,
                0.0,
            )
        )

    back_logits = logit_grads(0, logits)
    back_hidden = lax.psum_scatter(
        matmul(back_logits, embed_half), "fsdp", scatter_dimension=0, tiled=True
    )
    head_grad = tmatmul(back_logits, gathered_hidden)
    for shift in range(1, reps):
        other_logits = logit_grads(shift, matmul_t(hidden_by_shift[shift], embed_half))
        head_grad = head_grad + tmatmul(other_logits, hidden_by_shift[shift])
    back_hidden, head_grad = lax.optimization_barrier((back_hidden, head_grad))
    vector_grads = {}
    back_three, final_gain, final_bias = norm_back(
        dec_three,
        small_params[:, DecSlots.final_gain],
        small_params[:, DecSlots.final_bias],
        back_hidden,
    )
    vector_grads[DecSlots.final_gain] = final_gain
    vector_grads[DecSlots.final_bias] = final_bias
    back_two, dec_down_grad, dec_up_grad = mlp_block_back(
        dec_mlp, back_three, weights, small_params, DecSlots, "du", "dd", vector_grads
    )
    dec_down_all, dec_up_all = pool([dec_down_grad], [dec_up_grad])
    back_one, back_memory, xout_grad, xquery_grad, xkeyval_grad = cross_block_back(
        dec_cross, back_two, weights, small_params, vector_grads
    )
    back_zero, dec_out_grad, dec_qkv_grad = self_block_back(
        dec_self, back_one, weights, small_params, DecSlots, "dq", "do", True, vector_grads
    )
    xout_all, xquery_all, dec_out_all, dec_qkv_all = pool(
        [], [xout_grad, xquery_grad, dec_out_grad, dec_qkv_grad]
    )
    grads = {}
    dec_names = ("dd", "du", "xo", "xq", "do", "dq")
    for piece, rows in zip(
        dec_names,
        whole_rows(
            [
                tmatmul(dec_down_all, dec_active_all),
                tmatmul(dec_mid_all, dec_up_all),
                tmatmul(cross_attended_all, xout_all),
                tmatmul(cross_normed_all, xquery_all),
                tmatmul(dec_attended_all, dec_out_all),
                tmatmul(dec_normed_all, dec_qkv_all),
            ]
        ),
    ):
        grads[piece] = rows
    gathered_back = lax.all_gather(to_half(back_zero), "fsdp", axis=0, tiled=True)
    back_enc_two, enc_gain, enc_bias = norm_back(
        enc_two,
        small_params[:, EncSlots.final_gain],
        small_params[:, EncSlots.final_bias],
        back_memory,
    )
    vector_grads[EncSlots.final_gain] = enc_gain
    vector_grads[EncSlots.final_bias] = enc_bias
    back_enc_one, enc_down_grad, enc_up_grad = mlp_block_back(
        enc_mlp, back_enc_two, weights, small_params, EncSlots, "eu", "ed", vector_grads
    )
    enc_down_all, enc_up_all, xkeyval_all = pool([enc_down_grad], [enc_up_grad, xkeyval_grad])
    back_enc_zero, enc_out_grad, enc_qkv_grad = self_block_back(
        enc_self, back_enc_one, weights, small_params, EncSlots, "eq", "eo", False, vector_grads
    )
    grad_second, grad_even, grad_odd = stem_back(stem_saved, back_enc_zero, weights, vector_grads)
    grad_even_all, grad_odd_all, enc_out_all, enc_qkv_all, second_all = pool(
        [grad_even, grad_odd], [enc_out_grad, enc_qkv_grad, grad_second]
    )
    frames = act_odd.shape[0]
    shifted_all = jnp.pad(act_odd_all.reshape(-1, frames, D), ((0, 0), (1, 0), (0, 0)))[
        :, :-1
    ].reshape(-1, D)
    extra = TLEN + NVEC
    tall = [
        tmatmul(enc_down_all, enc_active_all),
        tmatmul(enc_mid_all, enc_up_all),
        tmatmul(memory_all, xkeyval_all),
        tmatmul(enc_attended_all, enc_out_all),
        tmatmul(enc_normed_all, enc_qkv_all),
        tmatmul(shifted_all, second_all),
        tmatmul(act_even_all, second_all),
        tmatmul(act_odd_all, second_all),
    ]
    conv_part = tmatmul(
        token_rows([grad_even_all, grad_odd_all]), token_rows([cols_even_all, cols_odd_all])
    )
    share = CORES * reps
    extra_pad = -extra % (8 * share)
    filled = sum(part.shape[1] for part in tall) + conv_part.shape[1] + (extra + extra_pad) // share
    end_pad = -filled % (3 * 128)
    loose_rows = lax.optimization_barrier(
        jnp.concatenate(
            [back_zero]
            + [vector_grads[column][None, :] for column in range(NVEC)]
            + [jnp.zeros((extra_pad, D), jnp.float32)],
            axis=0,
        )
    )
    loose = pool_sum(loose_rows.T)
    conv_part, loose, filler = lax.optimization_barrier(
        (conv_part, loose, jnp.zeros((D, end_pad), jnp.float32))
    )
    last_part = jnp.concatenate([conv_part, loose, filler], axis=1)
    enc_names = ("ed", "eu", "xk", "eo", "eq", "c2a", "c2b", "c2c")
    *enc_rows, last_rows = whole_rows(tall + [last_part], 4)
    for piece, rows in zip(enc_names, enc_rows):
        grads[piece] = rows
    by_share = last_rows.reshape(-1, share, last_part.shape[1])
    conv_span = conv_part.shape[1]
    grads["c1"] = by_share[:, :, :conv_span].reshape(-1, share * conv_span)
    loose_own = by_share[:, :, conv_span : conv_span + loose.shape[1]].reshape(
        -1, share * loose.shape[1]
    )
    grads["dp"] = loose_own[:, :TLEN]
    vec_grad = loose_own[:, TLEN : TLEN + NVEC]
    grads["c2"] = jnp.concatenate([grads["c2a"], grads["c2b"], grads["c2c"]], axis=1)
    mat_grad = jnp.concatenate([grads[piece] for piece in names], axis=1)
    lookup = tmatmul(input_hot[0], gathered_back)
    for shift in range(1, reps):
        lookup = lookup + tmatmul(input_hot[shift], send_rep(gathered_back, shift))
    embed_grad = head_grad + lookup
    sums = total_of(
        jnp.stack(
            [
                jnp.sum(mat_grad * mat_grad)
                + jnp.sum(vec_grad * vec_grad)
                + jnp.sum(embed_grad * embed_grad),
                count_bad(mat_grad) + count_bad(embed_grad) + count_bad(vec_grad),
            ]
        ),
        1,
    )
    total_squares, total_bad = sums[0], sums[1]
    gradient_norm = jnp.sqrt(total_squares)
    factor = CLIP_AT / jnp.maximum(gradient_norm, CLIP_AT)
    steps = step_count[0].astype(jnp.float32)
    first_fix = 1.0 / (1.0 - jnp.power(jnp.float32(BETA_ONE), steps))
    second_fix = 1.0 / (1.0 - jnp.power(jnp.float32(BETA_TWO), steps))
    mat_moment, mat_square, mat_update = moments(
        matrices, matrix_moment, matrix_square, mat_grad, factor, first_fix, second_fix
    )
    emb_moment, emb_square, emb_update = moments(
        embedding, embed_moment, embed_square, embed_grad, factor, first_fix, second_fix
    )
    vec_moment, vec_square, vec_update = moments(
        vectors, vector_moment, vector_square, vec_grad, factor, first_fix, second_fix
    )
    update_parts = group_squares(mat_update, emb_update, vec_update, bounds, names)
    weight_parts = group_squares(matrices, embedding, vectors, bounds, names)
    groups = len(names) + 2
    both_sums = total_of(jnp.concatenate([weight_parts, update_parts]), 2)
    weight_norms = jnp.sqrt(both_sums[:groups])
    update_norms = jnp.sqrt(both_sums[groups:])
    ratio = weight_norms / update_norms
    ratio_columns = jnp.concatenate(
        [
            jnp.full((bounds[piece_name][1] - bounds[piece_name][0],), 1.0, jnp.float32)
            * ratio[position]
            for position, piece_name in enumerate(names)
        ]
    )
    new_matrices = matrices - RATE * ratio_columns[None, :] * mat_update
    new_embedding = embedding - RATE * ratio[len(names)] * emb_update
    new_vectors = vectors - RATE * ratio[len(names) + 1] * vec_update
    mean_loss = loss_sum / jnp.sum(text_lengths).astype(jnp.float32)
    group_norms = jnp.stack([weight_norms, update_norms], axis=1)
    return (
        mean_loss,
        total_bad.astype(jnp.int32),
        gradient_norm,
        group_norms,
        new_matrices,
        mat_moment,
        mat_square,
        new_embedding,
        emb_moment,
        emb_square,
        new_vectors,
        vec_moment,
        vec_square,
    )


def solution(mesh):
    placed = (
        P(("rep", "fsdp"), None, None),
        P(("rep", "fsdp"), None),
        P(),
        P(("rep", "fsdp")),
        P(),
        P(),
        P("fsdp", None),
        P("fsdp", None),
        P("fsdp", None),
        P("fsdp", None),
        P("fsdp", None),
        P("fsdp", None),
        P("fsdp", None),
        P("fsdp", None),
        P("fsdp", None),
    )
    return jax.shard_map(
        on_device,
        mesh=mesh,
        in_specs=placed,
        out_specs=(
            P(),
            P(),
            P(),
            P(),
            P("fsdp", None),
            P("fsdp", None),
            P("fsdp", None),
            P("fsdp", None),
            P("fsdp", None),
            P("fsdp", None),
            P("fsdp", None),
            P("fsdp", None),
            P("fsdp", None),
        ),
        check_vma=False,
    )
```

```python
import functools

import jax
import jax.numpy as jnp
from jax import lax
from jax.experimental import pallas as pl
from jax.experimental.pallas import tpu as pltpu
from jax.sharding import PartitionSpec as P

D = 768
H = 12
HD = 64
FF = 3072
MELS = 80
TLEN = 128
LANGTOK = 50259
NVEC = 35


LN_EPS = 1e-05
SMOOTH = 0.1
CLIP_AT = 1.0
BETA_ONE = 0.9
BETA_TWO = 0.999
ADAM_EPS = 1e-06
DECAY = 0.01
RATE = 0.5
NEG_BIG = -1e30
class EncSlots:
    norm_gain = 2
    norm_bias = 3
    query_bias = 4
    value_bias = 5
    out_bias = 6
    mlp_gain = 7
    mlp_bias = 8
    up_bias = 9
    down_bias = 13
    final_gain = 14
    final_bias = 15


class DecSlots:
    norm_gain = 16
    norm_bias = 17
    query_bias = 18
    value_bias = 19
    out_bias = 20
    cross_gain = 21
    cross_bias = 22
    xquery_bias = 23
    xvalue_bias = 24
    xout_bias = 25
    mlp_gain = 26
    mlp_bias = 27
    up_bias = 28
    down_bias = 32
    final_gain = 33
    final_bias = 34


CORES = 2
LINE = 4


def mesh_shape():
    members = lax.axis_size("fsdp")
    return (lax.axis_size("rep"), LINE, members // (LINE * CORES), CORES)


def places():
    reps, line, side, cores = mesh_shape()
    index = lax.axis_index("fsdp")
    return (
        lax.axis_index("rep"),
        index // (side * cores),
        (index // cores) % side,
        index % cores,
    )


def send(values, move):
    reps, line, side, cores = mesh_shape()
    members = line * side * cores
    pairs = []
    for rep in range(reps):
        for far in range(line):
            for near in range(side):
                for core in range(cores):
                    target = move(rep, far, near, core)
                    if target is None:
                        continue
                    rep_to, far_to, near_to, core_to = target
                    pairs.append(
                        (
                            rep * members + (far * side + near) * cores + core,
                            rep_to * members + (far_to * side + near_to) * cores + core_to,
                        )
                    )
    return lax.ppermute(values, ("rep", "fsdp"), pairs)


def send_core(values):
    return send(values, lambda rep, far, near, core: (rep, far, near, 1 - core))


def send_rep(values, shift):
    reps = lax.axis_size("rep")
    return send(values, lambda rep, far, near, core: ((rep + shift) % reps, far, near, core))


def pick(values, index, axis):
    return lax.dynamic_index_in_dim(values, index, axis, keepdims=False)


def block(values, index, width):
    return lax.dynamic_slice_in_dim(values, index * width, width, axis=1)


def quad_moves():
    reps = lax.axis_size("rep")
    return [(turn, flip) for turn in range(reps) for flip in range(CORES) if turn or flip]


def quad_place():
    rep, _, _, core = places()
    return rep * CORES + core


def quad_peer(turn, flip):
    rep, _, _, core = places()
    reps = lax.axis_size("rep")
    return ((rep + turn) % reps) * CORES + (1 - core if flip else core)


def quad_send(values, turn, flip):
    reps = lax.axis_size("rep")
    return send(
        values,
        lambda rep, far, near, core: (
            (rep + turn) % reps,
            far,
            near,
            1 - core if flip else core,
        ),
    )


def exchange(make):
    return [make(quad_place())] + [
        quad_send(make(quad_peer(turn, flip)), turn, flip) for turn, flip in quad_moves()
    ]


def unit_width():
    return 4 * D // (CORES * lax.axis_size("rep"))


def wide_for(values):
    unit = unit_width()
    return lambda place: block(values, place, unit)


def narrow_for(choices):
    unit = unit_width()

    def make(place):
        which = place * unit // D
        chosen = choices[-1]
        for position in range(len(choices) - 2, -1, -1):
            chosen = jnp.where(which == position, choices[position], chosen)
        return chosen

    return make


def products(narrows, wides):
    return tmatmul(jnp.concatenate(narrows, axis=0), jnp.concatenate(wides, axis=0))


def quad_rows(by_core):
    reps = lax.axis_size("rep")
    rep, _, _, core = places()
    shape = (reps * CORES,) + by_core.shape[1:]
    joint = jnp.zeros(shape, by_core.dtype)
    joint = lax.dynamic_update_index_in_dim(joint, pick(by_core, core, 0), quad_place(), 0)
    for turn, flip in quad_moves():
        got = quad_send(pick(by_core, 1 - core if flip else core, 0), turn, flip)
        source = ((rep - turn) % reps) * CORES + (1 - core if flip else core)
        joint = lax.dynamic_update_index_in_dim(joint, got, source, 0)
    return joint


def scatter_body(cored, count, values, output, *scratch):
    reps, line, side, cores = mesh_shape()
    rep, far, near, core = places()
    members = line * side * cores
    if cored:
        core_in, core_sum = scratch[:2]
        scratch = scratch[2:]
    near_in, near_sum, far_in, leaving, landing = scratch
    wide = output.shape[-1] // count

    def at(far_to, near_to, core_to):
        return {"fsdp": (far_to * side + near_to) * cores + core_to}

    barrier = pltpu.get_barrier_semaphore()
    partners = [at(lax.rem(far + step, line), near, core) for step in range(1, line)]
    partners += [at(far, lax.rem(near + step, side), core) for step in range(1, side)]
    if cored:
        partners.append(at(far, near, 1 - core))
    for partner in partners:
        pl.semaphore_signal(barrier, inc=1, device_id=partner)
    pl.semaphore_wait(barrier, len(partners))

    started = []

    def start(source, target, device):
        slot = len(started)
        copy = pltpu.make_async_remote_copy(
            src_ref=source,
            dst_ref=target,
            send_sem=leaving.at[slot],
            recv_sem=landing.at[slot],
            device_id=device,
        )
        copy.start()
        started.append(copy)
        return copy

    spans = [pl.ds(part * wide, wide) for part in range(count)]
    core_moves = []
    if cored:
        for part in range(count):
            core_moves.append(
                start(
                    values.at[:, :, 1 - core, :, spans[part]],
                    core_in.at[part],
                    at(far, near, 1 - core),
                )
            )
    near_moves = []
    for part in range(count):
        if cored:
            core_moves[part].wait_recv()
            core_sum[part] = values[:, :, core, :, spans[part]] + core_in[part]
        moves = []
        for step in range(1, side):
            there = lax.rem(near + step, side)
            source = core_sum.at[part, :, there] if cored else values.at[:, there, :, spans[part]]
            moves.append(start(source, near_in.at[part, step - 1], at(far, there, core)))
        near_moves.append(moves)
    far_moves = []
    for part in range(count):
        total = core_sum[part, :, near] if cored else values[:, near, :, spans[part]]
        for step, move in enumerate(near_moves[part]):
            move.wait_recv()
            total = total + near_in[part, step]
        near_sum[part] = total
        moves = []
        for step in range(1, line):
            there = lax.rem(far + step, line)
            moves.append(
                start(near_sum.at[part, there], far_in.at[part, step - 1], at(there, near, core))
            )
        far_moves.append(moves)
    for part in range(count):
        total = near_sum[part, far]
        for step, move in enumerate(far_moves[part]):
            move.wait_recv()
            total = total + far_in[part, step]
        output[:, spans[part]] = total
    for move in started:
        move.wait_send()


def scatter_sum(values, count, cored, tag):
    reps, line, side, cores = mesh_shape()
    rows = values.shape[0] // (line * side * (cores if cored else 1))
    width = values.shape[1]
    wide = width // count
    kind = values.dtype
    shape = (line, side) + ((cores,) if cored else ()) + (rows, width)
    copies = count * ((1 if cored else 0) + (side - 1) + (line - 1))
    cube = (count, line, side, rows, wide)
    scratch = [pltpu.VMEM(cube, kind), pltpu.VMEM(cube, kind)] if cored else []
    scratch += [
        pltpu.VMEM((count, side - 1, line, rows, wide), kind),
        pltpu.VMEM((count, line, rows, wide), kind),
        pltpu.VMEM((count, line - 1, rows, wide), kind),
        pltpu.SemaphoreType.DMA((copies,)),
        pltpu.SemaphoreType.DMA((copies,)),
    ]
    return pl.pallas_call(
        functools.partial(scatter_body, cored, count),
        out_shape=jax.ShapeDtypeStruct((rows, width), kind),
        in_specs=[pl.BlockSpec(memory_space=pltpu.VMEM)],
        out_specs=pl.BlockSpec(memory_space=pltpu.VMEM),
        scratch_shapes=scratch,
        compiler_params=pltpu.CompilerParams(
            collective_id=tag, has_side_effects=True, vmem_limit_bytes=60 << 20
        ),
    )(values.reshape(shape))


def rows_body(count, *refs):
    reps, line, side, cores = mesh_shape()
    rep, far, near, core = places()
    values = refs[:count]
    outputs = refs[count : 2 * count]
    near_in = refs[2 * count : 3 * count]
    near_sum = refs[3 * count : 4 * count]
    far_in = refs[4 * count : 5 * count]
    far_sum = refs[5 * count : 6 * count]
    leaving, landing = refs[6 * count :]
    place = rep * cores + core

    def at(rep_to, far_to, near_to, core_to):
        return {"rep": rep_to, "fsdp": (far_to * side + near_to) * cores + core_to}

    moves = [(turn, flip) for turn in range(reps) for flip in range(cores) if turn or flip]
    quad = [
        at(lax.rem(rep + turn, reps), far, near, 1 - core if flip else core)
        for turn, flip in moves
    ]
    line_peers = [at(rep, lax.rem(far + step, line), near, core) for step in range(1, line)]
    side_peers = [at(rep, far, lax.rem(near + step, side), core) for step in range(1, side)]
    barrier = pltpu.get_barrier_semaphore()
    for partner in line_peers + side_peers + quad:
        pl.semaphore_signal(barrier, inc=1, device_id=partner)
    pl.semaphore_wait(barrier, len(line_peers + side_peers + quad))

    started = []

    def start(source, target, device):
        slot = len(started)
        copy = pltpu.make_async_remote_copy(
            src_ref=source,
            dst_ref=target,
            send_sem=leaving.at[slot],
            recv_sem=landing.at[slot],
            device_id=device,
        )
        copy.start()
        started.append(copy)
        return copy

    near_moves = []
    for part in range(count):
        near_moves.append(
            [
                start(
                    values[part].at[:, lax.rem(near + step, side)],
                    near_in[part].at[step - 1],
                    side_peers[step - 1],
                )
                for step in range(1, side)
            ]
        )
    far_moves = []
    for part in range(count):
        total = values[part][:, near]
        for step, move in enumerate(near_moves[part]):
            move.wait_recv()
            total = total + near_in[part][step]
        near_sum[part][...] = total
        far_moves.append(
            [
                start(
                    near_sum[part].at[lax.rem(far + step, line)],
                    far_in[part].at[step - 1],
                    line_peers[step - 1],
                )
                for step in range(1, line)
            ]
        )
    last_moves = []
    for part in range(count):
        total = near_sum[part][far]
        for step, move in enumerate(far_moves[part]):
            move.wait_recv()
            total = total + far_in[part][step]
        far_sum[part][...] = total.reshape(far_sum[part].shape)
        outputs[part][place] = far_sum[part][core]
        for (turn, flip), device in zip(moves, quad):
            last_moves.append(
                start(
                    far_sum[part].at[1 - core if flip else core],
                    outputs[part].at[place],
                    device,
                )
            )
    for move in last_moves:
        move.wait_recv()
    for move in started:
        move.wait_send()


def rows_of(parts, tag):
    reps, line, side, cores = mesh_shape()
    count = len(parts)
    rows = parts[0].shape[0] // (line * side)
    own = rows // cores
    widths = [part.shape[1] for part in parts]
    copies = count * (side - 1 + line - 1 + reps * cores - 1)
    near_in = [pltpu.VMEM((side - 1, line, rows, width), jnp.float32) for width in widths]
    near_sum = [pltpu.VMEM((line, rows, width), jnp.float32) for width in widths]
    far_in = [pltpu.VMEM((line - 1, rows, width), jnp.float32) for width in widths]
    far_sum = [pltpu.VMEM((cores, own, width), jnp.float32) for width in widths]
    return pl.pallas_call(
        functools.partial(rows_body, count),
        out_shape=[
            jax.ShapeDtypeStruct((reps * cores, own, width), jnp.float32) for width in widths
        ],
        in_specs=[pl.BlockSpec(memory_space=pltpu.VMEM)] * count,
        out_specs=[pl.BlockSpec(memory_space=pltpu.VMEM)] * count,
        scratch_shapes=near_in
        + near_sum
        + far_in
        + far_sum
        + [pltpu.SemaphoreType.DMA((copies,)), pltpu.SemaphoreType.DMA((copies,))],
        compiler_params=pltpu.CompilerParams(
            collective_id=tag, has_side_effects=True, vmem_limit_bytes=60 << 20
        ),
    )(*[part.reshape(line, side, rows, part.shape[1]) for part in parts])


def pack_body(*refs):
    *sources, packed = refs
    offset = 0
    for source in sources:
        if len(source.shape) == 1:
            packed[offset : offset + 1, :] = source[...].reshape(1, source.shape[0])
            offset = offset + 1
        else:
            packed[offset : offset + source.shape[0], :] = source[...]
            offset = offset + source.shape[0]
    packed[offset:, :] = jnp.zeros((packed.shape[0] - offset, packed.shape[1]), jnp.float32)


def packed_rows(sources, rows):
    return pl.pallas_call(
        pack_body,
        out_shape=jax.ShapeDtypeStruct((rows, D), jnp.float32),
        compiler_params=pltpu.CompilerParams(vmem_limit_bytes=32 << 20),
    )(*sources)


def moment_body(scalars, weight, moment, square, gradient, moment_out, square_out, update_out, sums):
    scaled = gradient[...].reshape(weight.shape) * scalars[0]
    held = weight[...]
    new_moment = BETA_ONE * moment[...] + (1.0 - BETA_ONE) * scaled
    new_square = BETA_TWO * square[...] + (1.0 - BETA_TWO) * scaled * scaled
    update = new_moment * scalars[1] / (jnp.sqrt(new_square * scalars[2]) + ADAM_EPS) + DECAY * held
    moment_out[...] = new_moment
    square_out[...] = new_square
    update_out[...] = update
    sums[0, 0:1, :] = jnp.sum(held * held, axis=0, keepdims=True)
    sums[0, 1:2, :] = jnp.sum(update * update, axis=0, keepdims=True)


def moment_pass(scalars, weight, moment, square, gradient, tall, wide):
    rows, columns = weight.shape
    by_columns = rows == tall
    steps = pl.cdiv(columns, wide) if by_columns else rows // tall
    place = (lambda step: (0, step)) if by_columns else (lambda step: (step, 0))
    spec = pl.BlockSpec((tall, wide), place)
    gradient_spec = pl.BlockSpec((1, tall, wide), lambda step: (step, 0, 0)) if by_columns else spec
    shape = jax.ShapeDtypeStruct(weight.shape, jnp.float32)
    return pl.pallas_call(
        moment_body,
        grid=(steps,),
        out_shape=[shape, shape, shape, jax.ShapeDtypeStruct((steps, 2, wide), jnp.float32)],
        in_specs=[pl.BlockSpec(memory_space=pltpu.SMEM), spec, spec, spec, gradient_spec],
        out_specs=[spec, spec, spec, pl.BlockSpec((1, 2, wide), lambda step: (step, 0, 0))],
        compiler_params=pltpu.CompilerParams(vmem_limit_bytes=48 << 20),
    )(scalars, weight, moment, square, gradient)


def gather_body(values, gathered, leaving, landing):
    members = lax.axis_size("fsdp")
    here = lax.axis_index("fsdp")
    barrier = pltpu.get_barrier_semaphore()
    for shift in range(1, members):
        pl.semaphore_signal(barrier, inc=1, device_id={"fsdp": lax.rem(here + shift, members)})
    pl.semaphore_wait(barrier, members - 1)
    copies = []
    for shift in range(1, members):
        copies.append(
            pltpu.make_async_remote_copy(
                src_ref=values,
                dst_ref=gathered.at[here],
                send_sem=leaving.at[shift - 1],
                recv_sem=landing.at[shift - 1],
                device_id={"fsdp": lax.rem(here + shift, members)},
            )
        )
        copies[-1].start()
    gathered[here] = values[...]
    for copy in copies:
        copy.wait()


def gather_small(values, tag):
    members = lax.axis_size("fsdp")
    return pl.pallas_call(
        gather_body,
        out_shape=jax.ShapeDtypeStruct((members,) + values.shape, values.dtype),
        in_specs=[pl.BlockSpec(memory_space=pltpu.VMEM)],
        out_specs=pl.BlockSpec(memory_space=pltpu.VMEM),
        scratch_shapes=[
            pltpu.SemaphoreType.DMA((members - 1,)),
            pltpu.SemaphoreType.DMA((members - 1,)),
        ],
        compiler_params=pltpu.CompilerParams(collective_id=tag, has_side_effects=True),
    )(values)


def total_of(values, tag):
    rows, columns = values.shape
    padded = jnp.pad(values, ((0, 8 - rows), (0, 128 - columns)))
    return jnp.sum(gather_small(padded, tag), axis=0)[:rows, :columns]


def layout(width, hidden, mels, text_len):
    names = (
        "eq",
        "eo",
        "eu",
        "ed",
        "dq",
        "do",
        "xq",
        "xk",
        "xo",
        "du",
        "dd",
        "c2",
        "c1",
        "dp",
    )
    widths = (
        3 * width,
        width,
        hidden,
        hidden,
        3 * width,
        width,
        width,
        2 * width,
        width,
        hidden,
        hidden,
        3 * width,
        3 * mels,
        text_len,
    )
    bounds = {}
    offset = 0
    for piece_name, extent in zip(names, widths):
        bounds[piece_name] = (offset, offset + extent)
        offset = offset + extent
    return (names, bounds)


def columns_of(weights, bounds, piece_name):
    span_start, span_stop = bounds[piece_name]
    return weights[:, span_start:span_stop]


def sinusoid(length, width):
    halfway = width // 2
    increment = jnp.log(10000.0) / (halfway - 1)
    rates = jnp.exp(-increment * jnp.arange(halfway, dtype=jnp.float32))
    angles = jnp.arange(length, dtype=jnp.float32)[:, None] * rates[None, :]
    return jnp.concatenate([jnp.sin(angles), jnp.cos(angles)], axis=1)


def layer_norm(inputs, gain, offset):
    average = jnp.mean(inputs, axis=-1, keepdims=True)
    centred = inputs - average
    spread = jnp.mean(centred * centred, axis=-1, keepdims=True)
    return centred * lax.rsqrt(spread + LN_EPS) * gain + offset


def norm_back(inputs, gain, offset, upstream):
    _, pull = jax.vjp(layer_norm, inputs, gain, offset)
    return pull(upstream)


def gelu_exact(values):
    return jax.nn.gelu(values, approximate=False)


def gelu_back(values, upstream):
    _, pull = jax.vjp(gelu_exact, values)
    return pull(upstream)[0]


def to_half(values):
    return values.astype(jnp.bfloat16)


def matmul(left, right):
    return jnp.dot(left, right, preferred_element_type=jnp.float32)


def matmul_t(left, right):
    return lax.dot_general(
        left, right, (((1,), (1,)), ((), ())), preferred_element_type=jnp.float32
    )


def tmatmul(left, right):
    return lax.dot_general(
        left, right, (((0,), (0,)), ((), ())), preferred_element_type=jnp.float32
    )


def heads(values):
    return values.reshape(values.shape[0], H, HD)


def merged(values):
    return values.reshape(values.shape[0], H * HD)


def scores_of(query_heads, key_heads, causal):
    scores = jnp.einsum(
        "qhd,khd->hqk", query_heads, key_heads, preferred_element_type=jnp.float32
    ) * HD ** (-0.5)
    if causal:
        rows = lax.broadcasted_iota(jnp.int32, scores.shape, 1)
        cols = lax.broadcasted_iota(jnp.int32, scores.shape, 2)
        scores = jnp.where(rows >= cols, scores, NEG_BIG)
    return scores


def attend(queries, keys_half, values_half, causal):
    scores = scores_of(heads(queries), heads(keys_half), causal)
    row_top = jnp.max(scores, axis=-1, keepdims=True)
    log_total = row_top + jnp.log(jnp.sum(jnp.exp(scores - row_top), axis=-1, keepdims=True))
    weights_soft = jnp.exp(scores - log_total)
    attended = jnp.einsum(
        "hqk,khd->qhd",
        to_half(weights_soft),
        heads(values_half),
        preferred_element_type=jnp.float32,
    )
    return (to_half(merged(attended)), log_total)


def attend_back(queries, keys_half, values_half, causal, log_total, back_attended):
    query_heads = heads(queries)
    key_heads = heads(keys_half)
    grad_heads = heads(back_attended)
    weights_soft = jnp.exp(scores_of(query_heads, key_heads, causal) - log_total)
    back_weights = jnp.einsum(
        "qhd,khd->hqk", grad_heads, heads(values_half), preferred_element_type=jnp.float32
    )
    back_values = jnp.einsum(
        "hqk,qhd->khd", to_half(weights_soft), grad_heads, preferred_element_type=jnp.float32
    )
    inner = jnp.sum(weights_soft * back_weights, axis=-1, keepdims=True)
    back_scores = to_half(weights_soft * (back_weights - inner) * HD ** (-0.5))
    back_queries = jnp.einsum(
        "hqk,khd->qhd", back_scores, key_heads, preferred_element_type=jnp.float32
    )
    back_keys = jnp.einsum(
        "hqk,qhd->khd", back_scores, query_heads, preferred_element_type=jnp.float32
    )
    return (merged(back_queries), merged(back_keys), merged(back_values))


def self_block(stream, weights, small_params, slots, qkv_name, out_name, causal):
    normed = layer_norm(
        stream, small_params[:, slots.norm_gain], small_params[:, slots.norm_bias]
    )
    normed_half = to_half(normed)
    projected = matmul(normed_half, weights[qkv_name])
    queries = to_half(projected[:, :D] + small_params[:, slots.query_bias])
    keys_half = to_half(projected[:, D : 2 * D])
    values_half = to_half(projected[:, 2 * D :] + small_params[:, slots.value_bias])
    attended, log_total = attend(queries, keys_half, values_half, causal)
    output = (
        stream + matmul(attended, weights[out_name]) + small_params[:, slots.out_bias]
    )
    return (output, (stream, queries, keys_half, values_half, log_total), (normed_half, attended))


def self_block_back(
    saved, upstream, weights, small_params, slots, qkv_name, out_name, causal, vector_grads
):
    stream, queries, keys_half, values_half, log_total = saved
    grad_out = to_half(upstream)
    back_attended = to_half(matmul_t(grad_out, weights[out_name]))
    back_queries, back_keys, back_values = attend_back(
        queries, keys_half, values_half, causal, log_total, back_attended
    )
    grad_proj = to_half(jnp.concatenate([back_queries, back_keys, back_values], axis=1))
    back_normed = matmul_t(grad_proj, weights[qkv_name])
    back_stream, back_gain, back_bias = norm_back(
        stream,
        small_params[:, slots.norm_gain],
        small_params[:, slots.norm_bias],
        back_normed,
    )
    vector_grads[slots.norm_gain] = back_gain
    vector_grads[slots.norm_bias] = back_bias
    vector_grads[slots.query_bias] = jnp.sum(back_queries, axis=0)
    vector_grads[slots.value_bias] = jnp.sum(back_values, axis=0)
    vector_grads[slots.out_bias] = jnp.sum(upstream, axis=0)
    return (upstream + back_stream, grad_out, grad_proj)


def cross_block(stream, memory_half, weights, small_params):
    normed = layer_norm(
        stream, small_params[:, DecSlots.cross_gain], small_params[:, DecSlots.cross_bias]
    )
    normed_half = to_half(normed)
    queries = to_half(
        matmul(normed_half, weights["xq"]) + small_params[:, DecSlots.xquery_bias]
    )
    keyval = matmul(memory_half, weights["xk"])
    keys_half = to_half(keyval[:, :D])
    values_half = to_half(keyval[:, D:] + small_params[:, DecSlots.xvalue_bias])
    attended, log_total = attend(queries, keys_half, values_half, False)
    output = (
        stream + matmul(attended, weights["xo"]) + small_params[:, DecSlots.xout_bias]
    )
    return (output, (stream, queries, keys_half, values_half, log_total), (normed_half, attended))


def cross_block_back(saved, upstream, weights, small_params, vector_grads):
    stream, queries, keys_half, values_half, log_total = saved
    grad_out = to_half(upstream)
    back_attended = to_half(matmul_t(grad_out, weights["xo"]))
    back_queries, back_keys, back_values = attend_back(
        queries, keys_half, values_half, False, log_total, back_attended
    )
    grad_query = to_half(back_queries)
    back_normed = matmul_t(grad_query, weights["xq"])
    grad_keyval = to_half(jnp.concatenate([back_keys, back_values], axis=1))
    back_memory = matmul_t(grad_keyval, weights["xk"])
    back_stream, back_gain, back_bias = norm_back(
        stream,
        small_params[:, DecSlots.cross_gain],
        small_params[:, DecSlots.cross_bias],
        back_normed,
    )
    vector_grads[DecSlots.cross_gain] = back_gain
    vector_grads[DecSlots.cross_bias] = back_bias
    vector_grads[DecSlots.xquery_bias] = jnp.sum(back_queries, axis=0)
    vector_grads[DecSlots.xvalue_bias] = jnp.sum(back_values, axis=0)
    vector_grads[DecSlots.xout_bias] = jnp.sum(upstream, axis=0)
    return (upstream + back_stream, back_memory, grad_out, grad_query, grad_keyval)


def mlp_block(stream, weights, small_params, slots, up_name, down_name):
    normed = layer_norm(
        stream, small_params[:, slots.mlp_gain], small_params[:, slots.mlp_bias]
    )
    normed_half = to_half(normed)
    up_bias = small_params[:, slots.up_bias : slots.up_bias + 4].T.reshape(-1)
    raised = matmul(normed_half, weights[up_name]) + up_bias
    active = to_half(gelu_exact(raised))
    output = (
        stream + matmul_t(active, weights[down_name]) + small_params[:, slots.down_bias]
    )
    return (output, (stream, raised), (normed_half, active))


def mlp_block_back(saved, upstream, weights, small_params, slots, up_name, down_name, vector_grads):
    stream, raised = saved
    grad_out = to_half(upstream)
    back_raised = gelu_back(raised, matmul(grad_out, weights[down_name]))
    bias_rows = jnp.sum(back_raised, axis=0).reshape(4, D)
    for quarter in range(4):
        vector_grads[slots.up_bias + quarter] = bias_rows[quarter]
    grad_raised = to_half(back_raised)
    back_normed = matmul_t(grad_raised, weights[up_name])
    back_stream, back_gain, back_bias = norm_back(
        stream, small_params[:, slots.mlp_gain], small_params[:, slots.mlp_bias], back_normed
    )
    vector_grads[slots.mlp_gain] = back_gain
    vector_grads[slots.mlp_bias] = back_bias
    vector_grads[slots.down_bias] = jnp.sum(upstream, axis=0)
    return (upstream + back_stream, grad_out, grad_raised)


def down_one(values):
    return jnp.pad(values, ((1, 0), (0, 0)))[:-1]


def up_one(values):
    return jnp.pad(values, ((0, 1), (0, 0)))[1:]


def stem_forward(mel_half, weights, small_params):
    bins, frames_in = mel_half.shape
    paired = mel_half.T.reshape(frames_in // 2, 2 * bins)
    mel_even, mel_odd = paired[:, :bins], paired[:, bins:]
    cols_even = jnp.concatenate([down_one(mel_odd), mel_even, mel_odd], axis=1)
    cols_odd = jnp.concatenate([mel_even, mel_odd, up_one(mel_even)], axis=1)
    pre_even = matmul_t(cols_even, weights["c1"]) + small_params[:, 0]
    pre_odd = matmul_t(cols_odd, weights["c1"]) + small_params[:, 0]
    act_even = to_half(gelu_exact(pre_even))
    act_odd = to_half(gelu_exact(pre_odd))
    taps = weights["c2"]
    conv_sum = (
        matmul(down_one(act_odd), taps[:, :D])
        + matmul(act_even, taps[:, D : 2 * D])
        + matmul(act_odd, taps[:, 2 * D :])
    )
    second_pre = conv_sum + small_params[:, 1]
    stream = gelu_exact(second_pre) + sinusoid(frames_in // 2, D)
    return (stream, (pre_even, pre_odd, second_pre), (cols_even, cols_odd, act_even, act_odd))


def stem_back(saved, upstream, weights, vector_grads):
    pre_even, pre_odd, second_pre = saved
    back_second = gelu_back(second_pre, upstream)
    vector_grads[1] = jnp.sum(back_second, axis=0)
    grad_second = to_half(back_second)
    taps = weights["c2"]
    back_even = gelu_back(pre_even, matmul_t(grad_second, taps[:, D : 2 * D]))
    back_odd = gelu_back(
        pre_odd,
        matmul_t(grad_second, taps[:, 2 * D :])
        + matmul_t(up_one(grad_second), taps[:, :D]),
    )
    vector_grads[0] = jnp.sum(back_even, axis=0) + jnp.sum(back_odd, axis=0)
    return (grad_second, to_half(back_even), to_half(back_odd))


def fill(values, rows):
    return jnp.pad(values, ((0, rows - values.shape[0]), (0, 0)))


def moments(weight, moment, square, gradient, factor, first_fix, second_fix):
    scaled = gradient * factor
    new_moment = BETA_ONE * moment + (1.0 - BETA_ONE) * scaled
    new_square = BETA_TWO * square + (1.0 - BETA_TWO) * scaled * scaled
    update = new_moment * first_fix / (jnp.sqrt(new_square * second_fix) + ADAM_EPS) + DECAY * weight
    return (new_moment, new_square, update)


def count_bad(values):
    return jnp.sum(jnp.where(jnp.isfinite(values), 0.0, 1.0))


def on_device(
    mel_frames,
    text_ids,
    text_lengths,
    language,
    vocab_mask,
    step_count,
    matrices,
    matrix_moment,
    matrix_square,
    embedding,
    embed_moment,
    embed_square,
    vectors,
    vector_moment,
    vector_square,
):
    names, bounds = layout(D, FF, MELS, TLEN)
    reps = lax.axis_size("rep")
    members = lax.axis_size("fsdp")
    replica = lax.axis_index("rep")
    member = lax.axis_index("fsdp")
    first_names = ("c1", "c2", "eq", "eo", "eu", "ed")
    last_names = ("dq", "do", "xq", "xk", "xo", "du", "dd", "dp")
    first_half = jnp.concatenate(
        [to_half(columns_of(matrices, bounds, piece)) for piece in first_names]
        + [to_half(vectors)],
        axis=1,
    )
    last_half = jnp.concatenate(
        [to_half(columns_of(matrices, bounds, piece)) for piece in last_names], axis=1
    )
    weights = {}
    for batch, batch_half in ((first_names, first_half), (last_names, last_half)):
        gathered = lax.all_gather(batch_half, "fsdp", axis=0, tiled=True)
        offset = 0
        for piece in batch:
            extent = bounds[piece][1] - bounds[piece][0]
            weights[piece] = gathered[:, offset : offset + extent]
            offset = offset + extent
        if batch is first_names:
            small_params = gathered[:, offset:].astype(jnp.float32)
    inputs_ids = jnp.concatenate([LANGTOK + language, text_ids[0, :-1]])[None, :]
    ids_all = lax.all_gather(
        jnp.concatenate([inputs_ids, text_ids], axis=1), ("rep", "fsdp"), axis=0, tiled=True
    ).reshape(reps, members, 2, TLEN)
    order = [(replica - shift) % reps for shift in range(reps)]
    ids_by_shift = [pick(ids_all, place, 0) for place in order]
    group_inputs = [ids[:, 0].reshape(-1) for ids in ids_by_shift]
    group_targets = [ids[:, 1].reshape(-1) for ids in ids_by_shift]
    counts_by_shift = [
        (
            lax.broadcasted_iota(jnp.int32, (members, TLEN), 1)
            < lax.dynamic_slice_in_dim(text_lengths, place * members, members)[:, None]
        ).reshape(-1)
        for place in order
    ]
    vocab_rows = embedding.shape[0]
    vocab_start = member * vocab_rows
    embed_half = to_half(embedding)
    vocab_iota = lax.broadcasted_iota(jnp.int32, (members * TLEN, vocab_rows), 1)
    input_hot = [to_half(ids[:, None] - vocab_start == vocab_iota) for ids in group_inputs]
    embedded = scatter_sum(
        matmul(input_hot[0], embed_half).astype(jnp.bfloat16), 3, True, 3
    ).astype(jnp.float32)
    enc_zero, stem_saved, stem_acts = stem_forward(mel_frames[0], weights, small_params)
    enc_one, enc_self, enc_self_acts = self_block(
        enc_zero, weights, small_params, EncSlots, "eq", "eo", False
    )
    enc_two, enc_mlp, enc_mlp_acts = mlp_block(
        enc_one, weights, small_params, EncSlots, "eu", "ed"
    )
    memory_half = to_half(
        layer_norm(
            enc_two,
            small_params[:, EncSlots.final_gain],
            small_params[:, EncSlots.final_bias],
        )
    )
    cols_even, cols_odd, act_even, act_odd = stem_acts
    enc_attn_narrow = exchange(narrow_for([enc_self_acts[1], enc_self_acts[0]]))
    enc_up_narrow = exchange(narrow_for([enc_mlp_acts[0]]))
    enc_down_wide = exchange(wide_for(enc_mlp_acts[1]))
    conv_narrow = exchange(narrow_for([down_one(act_odd), act_even, act_odd]))
    dec_zero = embedded + weights["dp"].T.astype(jnp.float32)
    dec_one, dec_self, dec_self_acts = self_block(
        dec_zero, weights, small_params, DecSlots, "dq", "do", True
    )
    dec_two, dec_cross, dec_cross_acts = cross_block(dec_one, memory_half, weights, small_params)
    dec_three, dec_mlp, dec_mlp_acts = mlp_block(
        dec_two, weights, small_params, DecSlots, "du", "dd"
    )
    frames = memory_half.shape[0]
    dec_attn_narrow = exchange(narrow_for([dec_self_acts[1], dec_self_acts[0]]))
    cross_narrow = exchange(
        narrow_for(
            [fill(dec_cross_acts[0], frames), fill(dec_cross_acts[1], frames), memory_half]
        )
    )
    dec_up_narrow = exchange(narrow_for([dec_mlp_acts[0]]))
    dec_down_wide = exchange(wide_for(dec_mlp_acts[1]))
    final_out = layer_norm(
        dec_three,
        small_params[:, DecSlots.final_gain],
        small_params[:, DecSlots.final_bias],
    )
    final_half = to_half(final_out)
    other_half = [send_rep(final_half, shift) for shift in range(1, reps)]
    gathered_hidden = lax.all_gather(final_half, "fsdp", axis=0, tiled=True)
    hidden_by_shift = [gathered_hidden] + [
        lax.all_gather(part, "fsdp", axis=0, tiled=True) for part in other_half
    ]
    logits = matmul_t(gathered_hidden, embed_half)
    vocab_keep = (lax.dynamic_slice_in_dim(vocab_mask, vocab_start, vocab_rows) == 1)[None, :]
    masked = jnp.where(vocab_keep, logits, NEG_BIG)
    local_top = jnp.max(masked, axis=1)
    local_sum = jnp.sum(jnp.where(vocab_keep, jnp.exp(masked - local_top[:, None]), 0.0), axis=1)
    target_hits = group_targets[0][:, None] - vocab_start == vocab_iota
    local_target = jnp.sum(jnp.where(target_hits, logits, 0.0), axis=1)
    local_total = jnp.sum(jnp.where(vocab_keep, logits, 0.0), axis=1)
    stats = gather_small(
        jnp.stack([local_top, local_sum, local_target, local_total]).reshape(-1, 128), 0
    ).reshape(members, 4, members * TLEN)
    row_top = jnp.max(stats[:, 0], axis=0)
    row_sums = jnp.sum(stats[:, 1] * jnp.exp(stats[:, 0] - row_top[None]), axis=0)
    target_logit = jnp.sum(stats[:, 2], axis=0)
    logit_total = jnp.sum(stats[:, 3], axis=0)
    log_norm = row_top + jnp.log(row_sums)
    vocab_count = jnp.sum(vocab_mask).astype(jnp.float32)
    entropy = log_norm - (1.0 - SMOOTH) * target_logit - SMOOTH * logit_total / vocab_count
    norm_and_loss = jnp.stack([log_norm, jnp.where(counts_by_shift[0], entropy, 0.0)])
    norms_by_shift = [norm_and_loss] + [send_rep(norm_and_loss, shift) for shift in range(1, reps)]
    loss_sum = sum(jnp.sum(part[1]) for part in norms_by_shift)

    def logit_grads(shift, own_logits):
        hits = group_targets[shift][:, None] - vocab_start == vocab_iota
        softmax_part = jnp.where(
            vocab_keep,
            jnp.exp(
                jnp.where(vocab_keep, own_logits, NEG_BIG) - norms_by_shift[shift][0][:, None]
            ),
            0.0,
        )
        return to_half(
            jnp.where(
                counts_by_shift[shift][:, None],
                softmax_part
                - (1.0 - SMOOTH) * hits.astype(jnp.float32)
                - SMOOTH * vocab_keep.astype(jnp.float32) / vocab_count,
                0.0,
            )
        )

    back_logits = logit_grads(0, logits)
    back_hidden = lax.psum_scatter(
        matmul(back_logits, embed_half), "fsdp", scatter_dimension=0, tiled=True
    )
    head_grad = tmatmul(back_logits, gathered_hidden)
    back_hidden, head_grad = lax.optimization_barrier((back_hidden, head_grad))
    for shift in range(1, reps):
        other_logits = logit_grads(shift, matmul_t(hidden_by_shift[shift], embed_half))
        head_grad = head_grad + tmatmul(other_logits, hidden_by_shift[shift])
    vector_grads = {}
    back_three, final_gain, final_bias = norm_back(
        dec_three,
        small_params[:, DecSlots.final_gain],
        small_params[:, DecSlots.final_bias],
        back_hidden,
    )
    vector_grads[DecSlots.final_gain] = final_gain
    vector_grads[DecSlots.final_bias] = final_bias
    back_two, dec_down_grad, dec_up_grad = mlp_block_back(
        dec_mlp, back_three, weights, small_params, DecSlots, "du", "dd", vector_grads
    )
    dec_down_narrow = exchange(narrow_for([dec_down_grad]))
    dec_up_wide = exchange(wide_for(dec_up_grad))
    back_one, back_memory, xout_grad, xquery_grad, xkeyval_grad = cross_block_back(
        dec_cross, back_two, weights, small_params, vector_grads
    )
    back_zero, dec_out_grad, dec_qkv_grad = self_block_back(
        dec_self, back_one, weights, small_params, DecSlots, "dq", "do", True, vector_grads
    )
    dec_attn_wide = exchange(wide_for(jnp.concatenate([dec_out_grad, dec_qkv_grad], axis=1)))
    cross_wide = exchange(
        wide_for(
            jnp.concatenate(
                [fill(jnp.concatenate([xquery_grad, xout_grad], axis=1), frames), xkeyval_grad],
                axis=1,
            )
        )
    )
    unit = unit_width()
    share = 4 * D // unit
    cores = CORES
    groups = [list(range(place, members, cores)) for place in range(cores)]
    dec_rows = lax.psum_scatter(
        jnp.concatenate(
            [
                products(dec_down_narrow, dec_down_wide),
                products(dec_up_narrow, dec_up_wide),
                products(dec_attn_narrow, dec_attn_wide),
            ],
            axis=1,
        ),
        "fsdp",
        scatter_dimension=0,
        axis_index_groups=groups,
        tiled=True,
    )
    dec_quads = quad_rows(dec_rows.reshape(cores, -1, 3 * unit))
    down_units, up_units, attn_units = [
        dec_quads[:, :, part * unit : (part + 1) * unit] for part in range(3)
    ]
    back_half = to_half(back_zero)
    back_stack = jnp.zeros((reps,) + back_half.shape, jnp.bfloat16)
    for shift, place in enumerate(order):
        part = send_rep(back_half, shift) if shift else back_half
        back_stack = lax.dynamic_update_index_in_dim(back_stack, part, place, 0)
    gathered_back = lax.all_gather(back_stack, "fsdp", axis=0)
    back_enc_two, enc_gain, enc_bias = norm_back(
        enc_two,
        small_params[:, EncSlots.final_gain],
        small_params[:, EncSlots.final_bias],
        back_memory,
    )
    vector_grads[EncSlots.final_gain] = enc_gain
    vector_grads[EncSlots.final_bias] = enc_bias
    back_enc_one, enc_down_grad, enc_up_grad = mlp_block_back(
        enc_mlp, back_enc_two, weights, small_params, EncSlots, "eu", "ed", vector_grads
    )
    enc_down_narrow = exchange(narrow_for([enc_down_grad]))
    enc_up_wide = exchange(wide_for(enc_up_grad))
    back_enc_zero, enc_out_grad, enc_qkv_grad = self_block_back(
        enc_self, back_enc_one, weights, small_params, EncSlots, "eq", "eo", False, vector_grads
    )
    grad_second, grad_even, grad_odd = stem_back(stem_saved, back_enc_zero, weights, vector_grads)
    enc_attn_wide = exchange(wide_for(jnp.concatenate([enc_out_grad, enc_qkv_grad], axis=1)))
    conv_wide = exchange(
        lambda place: lax.dynamic_slice_in_dim(grad_second, place * unit % D, unit, axis=1)
    )
    first_grad = tmatmul(cols_even, grad_even) + tmatmul(cols_odd, grad_odd)
    loose_rows = packed_rows(
        [first_grad, back_zero] + [vector_grads[column] for column in range(NVEC)], share * 128
    )
    loose_parts = exchange(lambda place: lax.dynamic_slice_in_dim(loose_rows, place * 128, 128, 0))
    loose = sum(loose_parts[1:], loose_parts[0]).T
    cross_units, enc_down_units, enc_up_units, enc_attn_units, conv_units, loose_units = rows_of(
        [
            products(cross_narrow, cross_wide),
            products(enc_down_narrow, enc_down_wide),
            products(enc_up_narrow, enc_up_wide),
            products(enc_attn_narrow, enc_attn_wide),
            products(conv_narrow, conv_wide),
            loose,
        ],
        4,
    )
    loose_own = jnp.transpose(loose_units, (1, 0, 2)).reshape(-1, share * 128)
    odd_end = 3 * MELS + TLEN
    vec_grad = loose_own[:, odd_end : odd_end + NVEC]
    last_unit = jnp.pad(loose_own[:, :odd_end], ((0, 0), (0, unit - odd_end)))
    per = D // unit
    mat_grad = jnp.concatenate(
        [
            enc_attn_units[per:],
            enc_attn_units[:per],
            enc_up_units,
            enc_down_units,
            attn_units[per:],
            attn_units[:per],
            cross_units[:per],
            cross_units[2 * per :],
            cross_units[per : 2 * per],
            up_units,
            down_units,
            conv_units[: 3 * per],
            last_unit[None],
        ],
        axis=0,
    )
    hot_all = to_half(
        ids_all[:, :, 0].transpose(1, 0, 2).reshape(-1, 1)
        - vocab_start
        == lax.broadcasted_iota(jnp.int32, (reps * members * TLEN, vocab_rows), 1)
    )
    embed_grad = head_grad + tmatmul(hot_all, gathered_back.reshape(-1, D))
    first_lane = lax.broadcasted_iota(jnp.int32, (1, 2), 1) == 0
    sums = total_of(
        jnp.where(
            first_lane,
            jnp.sum(mat_grad * mat_grad)
            + jnp.sum(vec_grad * vec_grad)
            + jnp.sum(embed_grad * embed_grad),
            count_bad(mat_grad) + count_bad(embed_grad) + count_bad(vec_grad),
        ),
        1,
    )
    total_squares, total_bad = sums[0, 0], sums[0, 1]
    gradient_norm = jnp.sqrt(total_squares)
    factor = CLIP_AT / jnp.maximum(gradient_norm, CLIP_AT)
    steps = step_count[0].astype(jnp.float32)
    first_fix = 1.0 / (1.0 - jnp.power(jnp.float32(BETA_ONE), steps))
    second_fix = 1.0 / (1.0 - jnp.power(jnp.float32(BETA_TWO), steps))
    scalars = jnp.stack([factor, first_fix, second_fix])
    mat_moment, mat_square, mat_update, mat_sums = moment_pass(
        scalars, matrices, matrix_moment, matrix_square, mat_grad, matrices.shape[0], unit
    )
    emb_moment, emb_square, emb_update, emb_sums = moment_pass(
        scalars, embedding, embed_moment, embed_square, embed_grad, vocab_rows // 7, D
    )
    vec_moment, vec_square, vec_update = moments(
        vectors, vector_moment, vector_square, vec_grad, factor, first_fix, second_fix
    )
    groups_all = len(names) + 2
    columns = matrices.shape[1]
    column = lax.broadcasted_iota(jnp.int32, (groups_all, columns), 1)
    group = lax.broadcasted_iota(jnp.int32, (groups_all, columns), 0)
    group_of = sum((column >= bounds[piece][1]).astype(jnp.int32) for piece in names)
    in_group = group_of == group
    by_column = jnp.transpose(mat_sums, (1, 0, 2)).reshape(2, -1)[:, :columns]
    lone = jnp.stack([jnp.sum(vectors * vectors), jnp.sum(vec_update * vec_update)])
    place = lax.broadcasted_iota(jnp.int32, (2, groups_all), 1)
    both = jnp.sum(jnp.where(in_group[None], by_column[:, None, :], 0.0), axis=2)
    both = jnp.where(place == groups_all - 2, jnp.sum(emb_sums, axis=(0, 2))[:, None], both)
    both = jnp.where(place == groups_all - 1, lone[:, None], both)
    norms = jnp.sqrt(total_of(both, 2))
    weight_norms, update_norms = norms[0], norms[1]
    ratio = weight_norms / update_norms
    ratio_columns = jnp.sum(jnp.where(in_group, ratio[:, None], 0.0), axis=0)
    new_matrices = matrices - RATE * ratio_columns[None, :] * mat_update
    new_embedding = embedding - RATE * ratio[len(names)] * emb_update
    new_vectors = vectors - RATE * ratio[len(names) + 1] * vec_update
    mean_loss = loss_sum / jnp.sum(text_lengths).astype(jnp.float32)
    group_norms = jnp.stack([weight_norms, update_norms], axis=1)
    return (
        mean_loss,
        total_bad.astype(jnp.int32),
        gradient_norm,
        group_norms,
        new_matrices,
        mat_moment,
        mat_square,
        new_embedding,
        emb_moment,
        emb_square,
        new_vectors,
        vec_moment,
        vec_square,
    )


def solution(mesh):
    placed = (
        P(("rep", "fsdp"), None, None),
        P(("rep", "fsdp"), None),
        P(),
        P(("rep", "fsdp")),
        P(),
        P(),
        P("fsdp", None),
        P("fsdp", None),
        P("fsdp", None),
        P("fsdp", None),
        P("fsdp", None),
        P("fsdp", None),
        P("fsdp", None),
        P("fsdp", None),
        P("fsdp", None),
    )
    return jax.shard_map(
        on_device,
        mesh=mesh,
        in_specs=placed,
        out_specs=(
            P(),
            P(),
            P(),
            P(),
            P("fsdp", None),
            P("fsdp", None),
            P("fsdp", None),
            P("fsdp", None),
            P("fsdp", None),
            P("fsdp", None),
            P("fsdp", None),
            P("fsdp", None),
            P("fsdp", None),
        ),
        check_vma=False,
    )
```

```python
import functools

import jax
import jax.numpy as jnp
from jax import lax
from jax.experimental import pallas as pl
from jax.experimental.pallas import tpu as pltpu
from jax.sharding import PartitionSpec as P

D = 768
H = 12
HD = 64
FF = 3072
MELS = 80
TLEN = 128
LANGTOK = 50259
NVEC = 35


LN_EPS = 1e-05
SMOOTH = 0.1
CLIP_AT = 1.0
BETA_ONE = 0.9
BETA_TWO = 0.999
ADAM_EPS = 1e-06
DECAY = 0.01
RATE = 0.5
NEG_BIG = -1e30
class EncSlots:
    norm_gain = 2
    norm_bias = 3
    query_bias = 4
    value_bias = 5
    out_bias = 6
    mlp_gain = 7
    mlp_bias = 8
    up_bias = 9
    down_bias = 13
    final_gain = 14
    final_bias = 15


class DecSlots:
    norm_gain = 16
    norm_bias = 17
    query_bias = 18
    value_bias = 19
    out_bias = 20
    cross_gain = 21
    cross_bias = 22
    xquery_bias = 23
    xvalue_bias = 24
    xout_bias = 25
    mlp_gain = 26
    mlp_bias = 27
    up_bias = 28
    down_bias = 32
    final_gain = 33
    final_bias = 34


CORES = 2
LINE = 4


def mesh_shape():
    members = lax.axis_size("fsdp")
    return (lax.axis_size("rep"), LINE, members // (LINE * CORES), CORES)


def places():
    reps, line, side, cores = mesh_shape()
    index = lax.axis_index("fsdp")
    return (
        lax.axis_index("rep"),
        index // (side * cores),
        (index // cores) % side,
        index % cores,
    )


def send(values, move):
    reps, line, side, cores = mesh_shape()
    members = line * side * cores
    pairs = []
    for rep in range(reps):
        for far in range(line):
            for near in range(side):
                for core in range(cores):
                    target = move(rep, far, near, core)
                    if target is None:
                        continue
                    rep_to, far_to, near_to, core_to = target
                    pairs.append(
                        (
                            rep * members + (far * side + near) * cores + core,
                            rep_to * members + (far_to * side + near_to) * cores + core_to,
                        )
                    )
    return lax.ppermute(values, ("rep", "fsdp"), pairs)


def send_core(values):
    return send(values, lambda rep, far, near, core: (rep, far, near, 1 - core))


def send_rep(values, shift):
    reps = lax.axis_size("rep")
    return send(values, lambda rep, far, near, core: ((rep + shift) % reps, far, near, core))


def pick(values, index, axis):
    return lax.dynamic_index_in_dim(values, index, axis, keepdims=False)


def block(values, index, width):
    return lax.dynamic_slice_in_dim(values, index * width, width, axis=1)


def share_count():
    return CORES * lax.axis_size("rep")


def quad_place():
    return lax.axis_index("rep") * CORES + lax.axis_index("fsdp") % CORES


def quad_swap(values):
    reps, members = lax.axis_size("rep"), lax.axis_size("fsdp")
    groups = [
        [rep * members + chip * CORES + core for rep in range(reps) for core in range(CORES)]
        for chip in range(members // CORES)
    ]
    return lax.all_to_all(values, ("rep", "fsdp"), 0, 0, axis_index_groups=groups, tiled=True)


def exchange(*makers):
    share = share_count()
    if unit_width() != D and len(makers) > 1:
        return [exchange(make)[0] for make in makers]
    parts = [[make(place) for make in makers] for place in range(share)]
    sizes = [part.shape[0] for part in parts[0]]
    got = quad_swap(jnp.concatenate([part for row in parts for part in row], axis=0))
    got = got.reshape(share, sum(sizes), got.shape[1])
    columns = []
    offset = 0
    for size in sizes:
        columns.append(got[:, offset : offset + size].reshape(share * size, got.shape[2]))
        offset = offset + size
    return columns


def settle(value, *others):
    flat, tree = jax.tree.flatten((value, others))
    return jax.tree.unflatten(tree, lax.optimization_barrier(flat))


def unit_width():
    return 4 * D // share_count()


def wide_for(values):
    unit = unit_width()
    return lambda place: lax.optimization_barrier(values[:, place * unit : (place + 1) * unit])


def narrow_for(choices):
    unit = unit_width()
    return lambda place: choices[min(place * unit // D, len(choices) - 1)]


def quad_rows(by_core):
    reps = lax.axis_size("rep")
    message = jnp.concatenate([by_core] * reps, axis=0)
    swapped = quad_swap(message.reshape(-1, by_core.shape[2]))
    return swapped.reshape(message.shape)


def scatter_body(cored, count, values, output, *scratch):
    reps, line, side, cores = mesh_shape()
    rep, far, near, core = places()
    members = line * side * cores
    if cored:
        core_in, core_sum = scratch[:2]
        scratch = scratch[2:]
    near_in, near_sum, far_in, leaving, landing = scratch
    wide = output.shape[-1] // count

    def at(far_to, near_to, core_to):
        return {"fsdp": (far_to * side + near_to) * cores + core_to}

    barrier = pltpu.get_barrier_semaphore()
    partners = [at(lax.rem(far + step, line), near, core) for step in range(1, line)]
    partners += [at(far, lax.rem(near + step, side), core) for step in range(1, side)]
    if cored:
        partners.append(at(far, near, 1 - core))
    for partner in partners:
        pl.semaphore_signal(barrier, inc=1, device_id=partner)
    pl.semaphore_wait(barrier, len(partners))

    started = []

    def start(source, target, device):
        slot = len(started)
        copy = pltpu.make_async_remote_copy(
            src_ref=source,
            dst_ref=target,
            send_sem=leaving.at[slot],
            recv_sem=landing.at[slot],
            device_id=device,
        )
        copy.start()
        started.append(copy)
        return copy

    spans = [pl.ds(part * wide, wide) for part in range(count)]
    core_moves = []
    if cored:
        for part in range(count):
            core_moves.append(
                start(
                    values.at[:, :, 1 - core, :, spans[part]],
                    core_in.at[part],
                    at(far, near, 1 - core),
                )
            )
    near_moves = []
    for part in range(count):
        if cored:
            core_moves[part].wait_recv()
            core_sum[part] = values[:, :, core, :, spans[part]] + core_in[part]
        moves = []
        for step in range(1, side):
            there = lax.rem(near + step, side)
            source = core_sum.at[part, :, there] if cored else values.at[:, there, :, spans[part]]
            moves.append(start(source, near_in.at[part, step - 1], at(far, there, core)))
        near_moves.append(moves)
    far_moves = []
    for part in range(count):
        total = core_sum[part, :, near] if cored else values[:, near, :, spans[part]]
        for step, move in enumerate(near_moves[part]):
            move.wait_recv()
            total = total + near_in[part, step]
        near_sum[part] = total
        moves = []
        for step in range(1, line):
            there = lax.rem(far + step, line)
            moves.append(
                start(near_sum.at[part, there], far_in.at[part, step - 1], at(there, near, core))
            )
        far_moves.append(moves)
    for part in range(count):
        total = near_sum[part, far]
        for step, move in enumerate(far_moves[part]):
            move.wait_recv()
            total = total + far_in[part, step]
        output[:, spans[part]] = total
    for move in started:
        move.wait_send()


def scatter_sum(values, count, cored, tag):
    reps, line, side, cores = mesh_shape()
    rows = values.shape[0] // (line * side * (cores if cored else 1))
    width = values.shape[1]
    wide = width // count
    kind = values.dtype
    shape = (line, side) + ((cores,) if cored else ()) + (rows, width)
    copies = count * ((1 if cored else 0) + (side - 1) + (line - 1))
    cube = (count, line, side, rows, wide)
    scratch = [pltpu.VMEM(cube, kind), pltpu.VMEM(cube, kind)] if cored else []
    scratch += [
        pltpu.VMEM((count, side - 1, line, rows, wide), kind),
        pltpu.VMEM((count, line, rows, wide), kind),
        pltpu.VMEM((count, line - 1, rows, wide), kind),
        pltpu.SemaphoreType.DMA((copies,)),
        pltpu.SemaphoreType.DMA((copies,)),
    ]
    return pl.pallas_call(
        functools.partial(scatter_body, cored, count),
        out_shape=jax.ShapeDtypeStruct((rows, width), kind),
        in_specs=[pl.BlockSpec(memory_space=pltpu.VMEM)],
        out_specs=pl.BlockSpec(memory_space=pltpu.VMEM),
        scratch_shapes=scratch,
        compiler_params=pltpu.CompilerParams(
            collective_id=tag, has_side_effects=True, vmem_limit_bytes=60 << 20
        ),
    )(values.reshape(shape))


def rows_body(pieces, count, *refs):
    reps, line, side, cores = mesh_shape()
    rep, far, near, core = places()
    total = len(pieces)
    values, outputs = refs[:count], refs[count : 2 * count]
    rest = refs[2 * count :]
    near_in, near_sum = rest[:total], rest[total : 2 * total]
    far_in, far_sum = rest[2 * total : 3 * total], rest[3 * total : 4 * total]
    leaving, landing = rest[4 * total :]
    place = rep * cores + core

    def at(rep_to, far_to, near_to, core_to):
        return {"rep": rep_to, "fsdp": (far_to * side + near_to) * cores + core_to}

    moves = [(turn, flip) for turn in range(reps) for flip in range(cores) if turn or flip]
    quad = [
        at(lax.rem(rep + turn, reps), far, near, 1 - core if flip else core)
        for turn, flip in moves
    ]
    line_peers = [at(rep, lax.rem(far + step, line), near, core) for step in range(1, line)]
    side_peers = [at(rep, far, lax.rem(near + step, side), core) for step in range(1, side)]
    barrier = pltpu.get_barrier_semaphore()
    for partner in line_peers + side_peers + quad:
        pl.semaphore_signal(barrier, inc=1, device_id=partner)
    pl.semaphore_wait(barrier, len(line_peers + side_peers + quad))

    started = []

    def start(source, target, device):
        slot = len(started)
        copy = pltpu.make_async_remote_copy(
            src_ref=source,
            dst_ref=target,
            send_sem=leaving.at[slot],
            recv_sem=landing.at[slot],
            device_id=device,
        )
        copy.start()
        started.append(copy)
        return copy

    near_moves = []
    for piece, (part, span) in enumerate(pieces):
        near_moves.append(
            [
                start(
                    values[part].at[:, lax.rem(near + step, side), :, span],
                    near_in[piece].at[step - 1],
                    side_peers[step - 1],
                )
                for step in range(1, side)
            ]
        )
    far_moves = []
    last_moves = []

    def finish(piece):
        part, span = pieces[piece]
        summed = near_sum[piece][far]
        for step, move in enumerate(far_moves[piece]):
            move.wait_recv()
            summed = summed + far_in[piece][step]
        far_sum[piece][...] = summed.reshape(far_sum[piece].shape)
        outputs[part][place, :, span] = far_sum[piece][core]
        for (turn, flip), device in zip(moves, quad):
            last_moves.append(
                start(
                    far_sum[piece].at[1 - core if flip else core],
                    outputs[part].at[place, :, span],
                    device,
                )
            )

    lag = 2
    for piece, (part, span) in enumerate(pieces):
        summed = values[part][:, near, :, span]
        for step, move in enumerate(near_moves[piece]):
            move.wait_recv()
            summed = summed + near_in[piece][step]
        near_sum[piece][...] = summed
        far_moves.append(
            [
                start(
                    near_sum[piece].at[lax.rem(far + step, line)],
                    far_in[piece].at[step - 1],
                    line_peers[step - 1],
                )
                for step in range(1, line)
            ]
        )
        if piece >= lag:
            finish(piece - lag)
    for piece in range(max(total - lag, 0), total):
        finish(piece)
    for move in last_moves:
        move.wait_recv()
    for move in started:
        move.wait_send()


def rows_of(parts, tag):
    reps, line, side, cores = mesh_shape()
    count = len(parts)
    rows = parts[0].shape[0] // (line * side)
    own = rows // cores
    widths = [part.shape[1] for part in parts]
    pieces = []
    for part, width in enumerate(widths):
        offset = 0
        while offset < width:
            size = min(384, width - offset)
            pieces.append((part, pl.ds(offset, size)))
            offset = offset + size
    sizes = [span.size for _, span in pieces]
    copies = len(pieces) * (side - 1 + line - 1 + reps * cores - 1)
    near_in = [pltpu.VMEM((side - 1, line, rows, size), jnp.float32) for size in sizes]
    near_sum = [pltpu.VMEM((line, rows, size), jnp.float32) for size in sizes]
    far_in = [pltpu.VMEM((line - 1, rows, size), jnp.float32) for size in sizes]
    far_sum = [pltpu.VMEM((cores, own, size), jnp.float32) for size in sizes]
    return pl.pallas_call(
        functools.partial(rows_body, pieces, count),
        out_shape=[
            jax.ShapeDtypeStruct((reps * cores, own, width), jnp.float32) for width in widths
        ],
        in_specs=[pl.BlockSpec(memory_space=pltpu.VMEM)] * count,
        out_specs=[pl.BlockSpec(memory_space=pltpu.VMEM)] * count,
        scratch_shapes=near_in
        + near_sum
        + far_in
        + far_sum
        + [pltpu.SemaphoreType.DMA((copies,)), pltpu.SemaphoreType.DMA((copies,))],
        compiler_params=pltpu.CompilerParams(
            collective_id=tag, has_side_effects=True, vmem_limit_bytes=60 << 20
        ),
    )(*[part.reshape(line, side, rows, part.shape[1]) for part in parts])


def pack_body(*refs):
    *sources, packed = refs
    offset = 0
    for source in sources:
        if len(source.shape) == 1:
            packed[offset : offset + 1, :] = source[...].reshape(1, source.shape[0])
            offset = offset + 1
        else:
            packed[offset : offset + source.shape[0], :] = source[...]
            offset = offset + source.shape[0]
    packed[offset:, :] = jnp.zeros((packed.shape[0] - offset, packed.shape[1]), jnp.float32)


def packed_rows(sources, rows):
    return pl.pallas_call(
        pack_body,
        out_shape=jax.ShapeDtypeStruct((rows, D), jnp.float32),
        compiler_params=pltpu.CompilerParams(vmem_limit_bytes=32 << 20),
    )(*sources)


def moment_body(
    scalars, weight, moment, square, gradient, moment_out, square_out, update_out, sums
):
    wide = sums.shape[2]
    for part in range(weight.shape[1] // wide):
        span = pl.ds(part * wide, wide)
        raw = gradient[part] if len(gradient.shape) == 3 else gradient[...]
        scaled = raw * scalars[0]
        held = weight[:, span]
        new_moment = BETA_ONE * moment[:, span] + (1.0 - BETA_ONE) * scaled
        new_square = BETA_TWO * square[:, span] + (1.0 - BETA_TWO) * scaled * scaled
        update = (
            new_moment * scalars[1] / (jnp.sqrt(new_square * scalars[2]) + ADAM_EPS) + DECAY * held
        )
        moment_out[:, span] = new_moment
        square_out[:, span] = new_square
        update_out[:, span] = update
        sums[part, 0:1, :] = jnp.sum(held * held, axis=0, keepdims=True)
        sums[part, 1:2, :] = jnp.sum(update * update, axis=0, keepdims=True)


def moment_pass(scalars, weight, moment, square, gradient, tall, wide):
    rows, columns = weight.shape
    by_columns = rows == tall
    units = 4 if by_columns else 1
    steps = gradient.shape[0] // units if by_columns else rows // tall
    place = (lambda step: (0, step)) if by_columns else (lambda step: (step, 0))
    spec = pl.BlockSpec((tall, units * wide), place)
    gradient_spec = (
        pl.BlockSpec((units, tall, wide), lambda step: (step, 0, 0)) if by_columns else spec
    )
    shape = jax.ShapeDtypeStruct(weight.shape, jnp.float32)
    return pl.pallas_call(
        moment_body,
        grid=(steps,),
        out_shape=[shape, shape, shape, jax.ShapeDtypeStruct((steps * units, 2, wide), jnp.float32)],
        in_specs=[pl.BlockSpec(memory_space=pltpu.SMEM), spec, spec, spec, gradient_spec],
        out_specs=[spec, spec, spec, pl.BlockSpec((units, 2, wide), lambda step: (step, 0, 0))],
        cost_estimate=pl.CostEstimate(
            flops=20 * weight.size, bytes_accessed=28 * weight.size, transcendentals=0
        ),
        compiler_params=pltpu.CompilerParams(vmem_limit_bytes=48 << 20),
    )(scalars, weight, moment, square, gradient)


def gather_body(everyone, values, gathered, leaving, landing):
    members = lax.axis_size("fsdp")
    reps = lax.axis_size("rep") if everyone else 1
    rep, member = lax.axis_index("rep"), lax.axis_index("fsdp")
    peers = []
    for turn in range(reps):
        for shift in range(members):
            if turn or shift:
                device = {"fsdp": lax.rem(member + shift, members)}
                if everyone:
                    device["rep"] = lax.rem(rep + turn, reps)
                peers.append(device)
    here = rep * members + member if everyone else member
    barrier = pltpu.get_barrier_semaphore()
    for peer in peers:
        pl.semaphore_signal(barrier, inc=1, device_id=peer)
    pl.semaphore_wait(barrier, len(peers))
    copies = []
    for slot, peer in enumerate(peers):
        copies.append(
            pltpu.make_async_remote_copy(
                src_ref=values,
                dst_ref=gathered.at[here],
                send_sem=leaving.at[slot],
                recv_sem=landing.at[slot],
                device_id=peer,
            )
        )
        copies[-1].start()
    gathered[here] = values[...]
    for copy in copies:
        copy.wait()


def gather_small(values, tag, everyone=False):
    count = lax.axis_size("fsdp") * (lax.axis_size("rep") if everyone else 1)
    return pl.pallas_call(
        functools.partial(gather_body, everyone),
        out_shape=jax.ShapeDtypeStruct((count,) + values.shape, values.dtype),
        in_specs=[pl.BlockSpec(memory_space=pltpu.VMEM)],
        out_specs=pl.BlockSpec(memory_space=pltpu.VMEM),
        scratch_shapes=[
            pltpu.SemaphoreType.DMA((count - 1,)),
            pltpu.SemaphoreType.DMA((count - 1,)),
        ],
        compiler_params=pltpu.CompilerParams(collective_id=tag, has_side_effects=True),
    )(values)


def total_of(values, tag, everyone=False):
    rows, columns = values.shape
    padded = jnp.pad(values, ((0, 8 - rows), (0, 128 - columns)))
    return jnp.sum(gather_small(padded, tag, everyone), axis=0)[:rows, :columns]


def rows_gather_body(values, gathered, leaving, landing):
    reps, line, side, cores = mesh_shape()
    rep, far, near, core = places()

    def at(far_to, near_to, core_to):
        return {"fsdp": (far_to * side + near_to) * cores + core_to}

    line_peers = [at(lax.rem(far + step, line), near, core) for step in range(1, line)]
    side_peers = [at(far, lax.rem(near + step, side), core) for step in range(1, side)]
    twin = at(far, near, 1 - core)
    barrier = pltpu.get_barrier_semaphore()
    for partner in line_peers + side_peers + [twin]:
        pl.semaphore_signal(barrier, inc=1, device_id=partner)
    pl.semaphore_wait(barrier, len(line_peers + side_peers) + 1)
    started = []

    def start(source, target, device):
        slot = len(started)
        copy = pltpu.make_async_remote_copy(
            src_ref=source,
            dst_ref=target,
            send_sem=leaving.at[slot],
            recv_sem=landing.at[slot],
            device_id=device,
        )
        copy.start()
        started.append(copy)
        return copy

    line_moves, side_moves, core_moves = [], [], []
    for step in range(1, line):
        line_moves.append(start(values, gathered.at[far, near, core], line_peers[step - 1]))

    def pass_on(step):
        origin = lax.rem(far - step + line, line)
        held = values if step == 0 else gathered.at[origin, near, core]
        for turn in range(1, side):
            side_moves.append(
                (step, turn, start(held, gathered.at[origin, near, core], side_peers[turn - 1]))
            )
        core_moves.append(start(held, gathered.at[origin, near, core], twin))

    pass_on(0)
    gathered[far, near, core] = values[...]
    for step in range(1, line):
        line_moves[step - 1].wait_recv()
        pass_on(step)
    for step, turn, move in list(side_moves):
        move.wait_recv()
        origin = lax.rem(far - step + line, line)
        beside = lax.rem(near - turn + side, side)
        held = gathered.at[origin, beside, core]
        core_moves.append(start(held, gathered.at[origin, beside, core], twin))
    for move in core_moves:
        move.wait_recv()
    for move in started:
        move.wait_send()


def gather_rows(values, tag):
    reps, line, side, cores = mesh_shape()
    copies = line - 1 + line * (side - 1) + line * side
    shape = (line, side, cores) + values.shape
    return pl.pallas_call(
        rows_gather_body,
        out_shape=jax.ShapeDtypeStruct(shape, values.dtype),
        in_specs=[pl.BlockSpec(memory_space=pltpu.VMEM)],
        out_specs=pl.BlockSpec(memory_space=pltpu.VMEM),
        scratch_shapes=[pltpu.SemaphoreType.DMA((copies,)), pltpu.SemaphoreType.DMA((copies,))],
        compiler_params=pltpu.CompilerParams(
            collective_id=tag, has_side_effects=True, vmem_limit_bytes=32 << 20
        ),
    )(values).reshape(-1, values.shape[1])


VOCAB_STEPS = 7
TOKEN_SPAN = 512


def fixed(shape):
    return pl.BlockSpec(shape, lambda step: (0,) * len(shape), pipeline_mode=pl.Buffered(1))


def by_step(tall, wide):
    return pl.BlockSpec((tall, wide), lambda step: (step, 0))


def token_spans(count):
    return [slice(start, start + TOKEN_SPAN) for start in range(0, count, TOKEN_SPAN)]


def stats_body(hidden, table, shut, keep, target, stats):
    step = pl.program_id(0)

    @pl.when(step == 0)
    def _():
        stats[0:1, :] = jnp.full((1, stats.shape[1]), NEG_BIG, jnp.float32)
        stats[1:, :] = jnp.zeros((stats.shape[0] - 1, stats.shape[1]), jnp.float32)

    tall = table.shape[0]
    part = table[...]
    row = lax.broadcasted_iota(jnp.int32, (tall, TOKEN_SPAN), 0) + step * tall
    for span in token_spans(stats.shape[1]):
        logits = matmul_t(part, hidden[span, :])
        masked = logits + shut[...]
        former = stats[0:1, span]
        top = jnp.maximum(former, jnp.max(masked, axis=0, keepdims=True))
        stats[1:2, span] = stats[1:2, span] * jnp.exp(former - top) + jnp.sum(
            jnp.exp(masked - top), axis=0, keepdims=True
        )
        stats[0:1, span] = top
        stats[2:3, span] += jnp.sum(
            jnp.where(row == target[:, span], logits, 0.0), axis=0, keepdims=True
        )
        stats[3:4, span] += jnp.sum(
            jnp.where(keep[...] > 0.0, logits, 0.0), axis=0, keepdims=True
        )


def vocab_stats(hidden, table, shut, keep, target):
    rows, vocab_rows = hidden.shape[0], table.shape[0]
    tall = vocab_rows // VOCAB_STEPS
    return pl.pallas_call(
        stats_body,
        grid=(VOCAB_STEPS,),
        out_shape=jax.ShapeDtypeStruct((4, rows), jnp.float32),
        in_specs=[
            fixed(hidden.shape),
            by_step(tall, D),
            by_step(tall, 1),
            by_step(tall, 1),
            fixed((1, rows)),
        ],
        out_specs=pl.BlockSpec((4, rows), lambda step: (0, 0)),
        compiler_params=pltpu.CompilerParams(vmem_limit_bytes=60 << 20),
    )(hidden, table, shut, keep, target)


def slopes_into(slopes, hidden, table, shut, pull, target, log_norm):
    tall = table.shape[0]
    part = table[...]
    row = lax.broadcasted_iota(jnp.int32, (tall, TOKEN_SPAN), 0) + pl.program_id(0) * tall
    for span in token_spans(slopes.shape[1]):
        logits = matmul_t(part, hidden[span, :])
        soft = jnp.exp((logits - log_norm[:, span]) + shut[...])
        hits = jnp.where(row == target[:, span], 1.0 - SMOOTH, 0.0)
        slopes[:, span] = to_half(soft - hits - pull[...])


def own_body(
    hidden, table, shut, pull, target, log_norm, counted, table_grad, hidden_grad, slopes, total
):
    step = pl.program_id(0)
    slopes_into(slopes, hidden, table, shut, pull, target, log_norm)
    table_grad[...] = matmul(slopes[...], hidden[...])
    part = tmatmul(table[...], slopes[...])

    @pl.when(step == 0)
    def _():
        total[...] = part

    @pl.when(step > 0)
    def _():
        total[...] += part

    @pl.when(step == VOCAB_STEPS - 1)
    def _():
        hidden_grad[...] = jnp.where(counted[...] > 0.0, total[...], 0.0).T


def own_slopes(hidden, table, shut, pull, target, log_norm, counted):
    rows, vocab_rows = hidden.shape[0], table.shape[0]
    tall = vocab_rows // VOCAB_STEPS
    flat = fixed((1, rows))
    column = by_step(tall, 1)
    return pl.pallas_call(
        own_body,
        grid=(VOCAB_STEPS,),
        out_shape=[
            jax.ShapeDtypeStruct((vocab_rows, D), jnp.float32),
            jax.ShapeDtypeStruct((rows, D), jnp.float32),
        ],
        in_specs=[fixed(hidden.shape), by_step(tall, D), column, column, flat, flat, flat],
        out_specs=[by_step(tall, D), fixed((rows, D))],
        scratch_shapes=[pltpu.VMEM((tall, rows), jnp.bfloat16), pltpu.VMEM((D, rows), jnp.float32)],
        compiler_params=pltpu.CompilerParams(vmem_limit_bytes=60 << 20),
    )(hidden, table, shut, pull, target, log_norm, counted)


def other_body(hidden, table, shut, pull, target, log_norm, former, table_grad, slopes):
    slopes_into(slopes, hidden, table, shut, pull, target, log_norm)
    table_grad[...] = former[...] + matmul(slopes[...], hidden[...])


def other_slopes(former, hidden, table, shut, pull, target, log_norm):
    rows, vocab_rows = hidden.shape[0], table.shape[0]
    tall = vocab_rows // VOCAB_STEPS
    flat = fixed((1, rows))
    column = by_step(tall, 1)
    return pl.pallas_call(
        other_body,
        grid=(VOCAB_STEPS,),
        out_shape=jax.ShapeDtypeStruct((vocab_rows, D), jnp.float32),
        in_specs=[
            fixed(hidden.shape),
            by_step(tall, D),
            column,
            column,
            flat,
            flat,
            by_step(tall, D),
        ],
        out_specs=by_step(tall, D),
        scratch_shapes=[pltpu.VMEM((tall, rows), jnp.bfloat16)],
        cost_estimate=pl.CostEstimate(
            flops=4 * rows * vocab_rows * D,
            bytes_accessed=10 * vocab_rows * D,
            transcendentals=rows * vocab_rows,
        ),
        compiler_params=pltpu.CompilerParams(vmem_limit_bytes=60 << 20),
    )(hidden, table, shut, pull, target, log_norm, former)


def layout(width, hidden, mels, text_len):
    names = (
        "eq",
        "eo",
        "eu",
        "ed",
        "dq",
        "do",
        "xq",
        "xk",
        "xo",
        "du",
        "dd",
        "c2",
        "c1",
        "dp",
    )
    widths = (
        3 * width,
        width,
        hidden,
        hidden,
        3 * width,
        width,
        width,
        2 * width,
        width,
        hidden,
        hidden,
        3 * width,
        3 * mels,
        text_len,
    )
    bounds = {}
    offset = 0
    for piece_name, extent in zip(names, widths):
        bounds[piece_name] = (offset, offset + extent)
        offset = offset + extent
    return (names, bounds)


def columns_of(weights, bounds, piece_name):
    span_start, span_stop = bounds[piece_name]
    return weights[:, span_start:span_stop]


def sinusoid(length, width):
    halfway = width // 2
    increment = jnp.log(10000.0) / (halfway - 1)
    rates = jnp.exp(-increment * jnp.arange(halfway, dtype=jnp.float32))
    angles = jnp.arange(length, dtype=jnp.float32)[:, None] * rates[None, :]
    return jnp.concatenate([jnp.sin(angles), jnp.cos(angles)], axis=1)


def layer_norm(inputs, gain, offset):
    average = jnp.mean(inputs, axis=-1, keepdims=True)
    centred = inputs - average
    spread = jnp.mean(centred * centred, axis=-1, keepdims=True)
    return centred * lax.rsqrt(spread + LN_EPS) * gain + offset


def norm_back(inputs, gain, offset, upstream):
    _, pull = jax.vjp(layer_norm, inputs, gain, offset)
    return pull(upstream)


def gelu_exact(values):
    return jax.nn.gelu(values, approximate=False)


def gelu_back(values, upstream):
    _, pull = jax.vjp(gelu_exact, values)
    return pull(upstream)[0]


def to_half(values):
    return values.astype(jnp.bfloat16)


def matmul(left, right):
    return jnp.dot(left, right, preferred_element_type=jnp.float32)


def matmul_t(left, right):
    return lax.dot_general(
        left, right, (((1,), (1,)), ((), ())), preferred_element_type=jnp.float32
    )


def tmatmul(left, right):
    return lax.dot_general(
        left, right, (((0,), (0,)), ((), ())), preferred_element_type=jnp.float32
    )


def heads(values):
    return values.reshape(values.shape[0], H, HD)


def merged(values):
    return values.reshape(values.shape[0], H * HD)


def scores_of(query_heads, key_heads, causal):
    scores = jnp.einsum(
        "qhd,khd->hqk", query_heads, key_heads, preferred_element_type=jnp.float32
    ) * HD ** (-0.5)
    if causal:
        rows = lax.broadcasted_iota(jnp.int32, scores.shape, 1)
        cols = lax.broadcasted_iota(jnp.int32, scores.shape, 2)
        scores = jnp.where(rows >= cols, scores, NEG_BIG)
    return scores


def attend(queries, keys_half, values_half, causal):
    scores = scores_of(heads(queries), heads(keys_half), causal)
    row_top = jnp.max(scores, axis=-1, keepdims=True)
    log_total = row_top + jnp.log(jnp.sum(jnp.exp(scores - row_top), axis=-1, keepdims=True))
    weights_soft = jnp.exp(scores - log_total)
    attended = jnp.einsum(
        "hqk,khd->qhd",
        to_half(weights_soft),
        heads(values_half),
        preferred_element_type=jnp.float32,
    )
    return (to_half(merged(attended)), log_total)


def attend_back(queries, keys_half, values_half, causal, log_total, back_attended):
    query_heads = heads(queries)
    key_heads = heads(keys_half)
    grad_heads = heads(back_attended)
    weights_soft = jnp.exp(scores_of(query_heads, key_heads, causal) - log_total)
    back_weights = jnp.einsum(
        "qhd,khd->hqk", grad_heads, heads(values_half), preferred_element_type=jnp.float32
    )
    back_values = jnp.einsum(
        "hqk,qhd->khd", to_half(weights_soft), grad_heads, preferred_element_type=jnp.float32
    )
    inner = jnp.sum(weights_soft * back_weights, axis=-1, keepdims=True)
    back_scores = to_half(weights_soft * (back_weights - inner) * HD ** (-0.5))
    back_queries = jnp.einsum(
        "hqk,khd->qhd", back_scores, key_heads, preferred_element_type=jnp.float32
    )
    back_keys = jnp.einsum(
        "hqk,qhd->khd", back_scores, query_heads, preferred_element_type=jnp.float32
    )
    return (merged(back_queries), merged(back_keys), merged(back_values))


def self_block(stream, weights, small_params, slots, qkv_name, out_name, causal):
    normed = layer_norm(
        stream, small_params[:, slots.norm_gain], small_params[:, slots.norm_bias]
    )
    normed_half = to_half(normed)
    projected = matmul(normed_half, weights[qkv_name])
    queries = to_half(projected[:, :D] + small_params[:, slots.query_bias])
    keys_half = to_half(projected[:, D : 2 * D])
    values_half = to_half(projected[:, 2 * D :] + small_params[:, slots.value_bias])
    attended, log_total = attend(queries, keys_half, values_half, causal)
    output = (
        stream + matmul(attended, weights[out_name]) + small_params[:, slots.out_bias]
    )
    return (output, (stream, queries, keys_half, values_half, log_total), (normed_half, attended))


def self_block_back(
    saved, upstream, weights, small_params, slots, qkv_name, out_name, causal, vector_grads
):
    stream, queries, keys_half, values_half, log_total = saved
    grad_out = to_half(upstream)
    back_attended = to_half(matmul_t(grad_out, weights[out_name]))
    back_queries, back_keys, back_values = attend_back(
        queries, keys_half, values_half, causal, log_total, back_attended
    )
    grad_proj = to_half(jnp.concatenate([back_queries, back_keys, back_values], axis=1))
    back_normed = matmul_t(grad_proj, weights[qkv_name])
    back_stream, back_gain, back_bias = norm_back(
        stream,
        small_params[:, slots.norm_gain],
        small_params[:, slots.norm_bias],
        back_normed,
    )
    vector_grads[slots.norm_gain] = back_gain
    vector_grads[slots.norm_bias] = back_bias
    vector_grads[slots.query_bias] = jnp.sum(back_queries, axis=0)
    vector_grads[slots.value_bias] = jnp.sum(back_values, axis=0)
    vector_grads[slots.out_bias] = jnp.sum(upstream, axis=0)
    return (upstream + back_stream, grad_out, grad_proj)


def cross_block(stream, memory_half, weights, small_params):
    normed = layer_norm(
        stream, small_params[:, DecSlots.cross_gain], small_params[:, DecSlots.cross_bias]
    )
    normed_half = to_half(normed)
    queries = to_half(
        matmul(normed_half, weights["xq"]) + small_params[:, DecSlots.xquery_bias]
    )
    keyval = matmul(memory_half, weights["xk"])
    keys_half = to_half(keyval[:, :D])
    values_half = to_half(keyval[:, D:] + small_params[:, DecSlots.xvalue_bias])
    attended, log_total = attend(queries, keys_half, values_half, False)
    output = (
        stream + matmul(attended, weights["xo"]) + small_params[:, DecSlots.xout_bias]
    )
    return (output, (stream, queries, keys_half, values_half, log_total), (normed_half, attended))


def cross_block_back(saved, upstream, weights, small_params, vector_grads):
    stream, queries, keys_half, values_half, log_total = saved
    grad_out = to_half(upstream)
    back_attended = to_half(matmul_t(grad_out, weights["xo"]))
    back_queries, back_keys, back_values = attend_back(
        queries, keys_half, values_half, False, log_total, back_attended
    )
    grad_query = to_half(back_queries)
    back_normed = matmul_t(grad_query, weights["xq"])
    grad_keyval = to_half(jnp.concatenate([back_keys, back_values], axis=1))
    back_memory = matmul_t(grad_keyval, weights["xk"])
    back_stream, back_gain, back_bias = norm_back(
        stream,
        small_params[:, DecSlots.cross_gain],
        small_params[:, DecSlots.cross_bias],
        back_normed,
    )
    vector_grads[DecSlots.cross_gain] = back_gain
    vector_grads[DecSlots.cross_bias] = back_bias
    vector_grads[DecSlots.xquery_bias] = jnp.sum(back_queries, axis=0)
    vector_grads[DecSlots.xvalue_bias] = jnp.sum(back_values, axis=0)
    vector_grads[DecSlots.xout_bias] = jnp.sum(upstream, axis=0)
    return (upstream + back_stream, back_memory, grad_out, grad_query, grad_keyval)


def mlp_block(stream, weights, small_params, slots, up_name, down_name):
    normed = layer_norm(
        stream, small_params[:, slots.mlp_gain], small_params[:, slots.mlp_bias]
    )
    normed_half = to_half(normed)
    up_bias = small_params[:, slots.up_bias : slots.up_bias + 4].T.reshape(-1)
    raised = matmul(normed_half, weights[up_name]) + up_bias
    active = to_half(gelu_exact(raised))
    output = (
        stream + matmul_t(active, weights[down_name]) + small_params[:, slots.down_bias]
    )
    return (output, (stream, raised), (normed_half, active))


def mlp_block_back(saved, upstream, weights, small_params, slots, up_name, down_name, vector_grads):
    stream, raised = saved
    grad_out = to_half(upstream)
    back_raised = gelu_back(raised, matmul(grad_out, weights[down_name]))
    bias_rows = jnp.sum(back_raised, axis=0).reshape(4, D)
    for quarter in range(4):
        vector_grads[slots.up_bias + quarter] = bias_rows[quarter]
    grad_raised = to_half(back_raised)
    back_normed = matmul_t(grad_raised, weights[up_name])
    back_stream, back_gain, back_bias = norm_back(
        stream, small_params[:, slots.mlp_gain], small_params[:, slots.mlp_bias], back_normed
    )
    vector_grads[slots.mlp_gain] = back_gain
    vector_grads[slots.mlp_bias] = back_bias
    vector_grads[slots.down_bias] = jnp.sum(upstream, axis=0)
    return (upstream + back_stream, grad_out, grad_raised)


def down_one(values):
    return jnp.pad(values, ((1, 0), (0, 0)))[:-1]


def up_one(values):
    return jnp.pad(values, ((0, 1), (0, 0)))[1:]


def stem_forward(mel_half, weights, small_params):
    bins, frames_in = mel_half.shape
    paired = mel_half.T.reshape(frames_in // 2, 2 * bins)
    mel_even, mel_odd = paired[:, :bins], paired[:, bins:]
    cols_even = jnp.concatenate([down_one(mel_odd), mel_even, mel_odd], axis=1)
    cols_odd = jnp.concatenate([mel_even, mel_odd, up_one(mel_even)], axis=1)
    pre_even = matmul_t(cols_even, weights["c1"]) + small_params[:, 0]
    pre_odd = matmul_t(cols_odd, weights["c1"]) + small_params[:, 0]
    act_even = to_half(gelu_exact(pre_even))
    act_odd = to_half(gelu_exact(pre_odd))
    taps = weights["c2"]
    conv_sum = (
        matmul(down_one(act_odd), taps[:, :D])
        + matmul(act_even, taps[:, D : 2 * D])
        + matmul(act_odd, taps[:, 2 * D :])
    )
    second_pre = conv_sum + small_params[:, 1]
    stream = gelu_exact(second_pre) + sinusoid(frames_in // 2, D)
    return (stream, (pre_even, pre_odd, second_pre), (cols_even, cols_odd, act_even, act_odd))


def stem_back(saved, upstream, weights, vector_grads):
    pre_even, pre_odd, second_pre = saved
    back_second = gelu_back(second_pre, upstream)
    vector_grads[1] = jnp.sum(back_second, axis=0)
    grad_second = to_half(back_second)
    taps = weights["c2"]
    back_even = gelu_back(pre_even, matmul_t(grad_second, taps[:, D : 2 * D]))
    back_odd = gelu_back(
        pre_odd,
        matmul_t(grad_second, taps[:, 2 * D :])
        + matmul_t(up_one(grad_second), taps[:, :D]),
    )
    vector_grads[0] = jnp.sum(back_even, axis=0) + jnp.sum(back_odd, axis=0)
    return (grad_second, to_half(back_even), to_half(back_odd))


def fill(values, rows):
    return jnp.pad(values, ((0, rows - values.shape[0]), (0, 0)))


def moments(weight, moment, square, gradient, factor, first_fix, second_fix):
    scaled = gradient * factor
    new_moment = BETA_ONE * moment + (1.0 - BETA_ONE) * scaled
    new_square = BETA_TWO * square + (1.0 - BETA_TWO) * scaled * scaled
    update = new_moment * first_fix / (jnp.sqrt(new_square * second_fix) + ADAM_EPS) + DECAY * weight
    return (new_moment, new_square, update)


def count_bad(values):
    return jnp.sum(jnp.where(jnp.isfinite(values), 0.0, 1.0))


def on_device(
    mel_frames,
    text_ids,
    text_lengths,
    language,
    vocab_mask,
    step_count,
    matrices,
    matrix_moment,
    matrix_square,
    embedding,
    embed_moment,
    embed_square,
    vectors,
    vector_moment,
    vector_square,
):
    names, bounds = layout(D, FF, MELS, TLEN)
    reps = lax.axis_size("rep")
    members = lax.axis_size("fsdp")
    replica = lax.axis_index("rep")
    member = lax.axis_index("fsdp")
    first_names = ("c1", "c2", "eq", "eo", "eu", "ed", "dp")
    last_names = ("dq", "do", "xq", "xk", "xo", "du", "dd")
    first_half = jnp.concatenate(
        [to_half(columns_of(matrices, bounds, piece)) for piece in first_names]
        + [to_half(vectors)],
        axis=1,
    )
    last_half = jnp.concatenate(
        [to_half(columns_of(matrices, bounds, piece)) for piece in last_names], axis=1
    )
    weights = {}
    for batch, batch_half in ((first_names, first_half), (last_names, last_half)):
        gathered = lax.all_gather(batch_half, "fsdp", axis=0, tiled=True)
        offset = 0
        for piece in batch:
            extent = bounds[piece][1] - bounds[piece][0]
            weights[piece] = gathered[:, offset : offset + extent]
            offset = offset + extent
        if batch is first_names:
            small_params = gathered[:, offset:].astype(jnp.float32)
    inputs_ids = jnp.concatenate([LANGTOK + language, text_ids[0, :-1]])[None, :]
    ids_all = lax.all_gather(
        jnp.concatenate([inputs_ids, text_ids], axis=1), ("rep", "fsdp"), axis=0, tiled=True
    ).reshape(reps, members, 2, TLEN)
    order = [(replica - shift) % reps for shift in range(reps)]
    ids_by_shift = [pick(ids_all, place, 0) for place in order]
    group_inputs = [ids[:, 0].reshape(-1) for ids in ids_by_shift]
    group_targets = [ids[:, 1].reshape(-1) for ids in ids_by_shift]
    counts_by_shift = [
        (
            lax.broadcasted_iota(jnp.int32, (members, TLEN), 1)
            < lax.dynamic_slice_in_dim(text_lengths, place * members, members)[:, None]
        ).reshape(-1)
        for place in order
    ]
    vocab_rows = embedding.shape[0]
    vocab_start = member * vocab_rows
    embed_half = to_half(embedding)
    vocab_iota = lax.broadcasted_iota(jnp.int32, (members * TLEN, vocab_rows), 1)
    input_hot = [to_half(ids[:, None] - vocab_start == vocab_iota) for ids in group_inputs]
    embedded = scatter_sum(
        matmul(input_hot[0], embed_half).astype(jnp.bfloat16), 3, True, 3
    ).astype(jnp.float32)
    enc_zero, stem_saved, stem_acts = stem_forward(mel_frames[0], weights, small_params)
    enc_one, enc_self, enc_self_acts = self_block(
        enc_zero, weights, small_params, EncSlots, "eq", "eo", False
    )
    enc_two, enc_mlp, enc_mlp_acts = mlp_block(
        enc_one, weights, small_params, EncSlots, "eu", "ed"
    )
    memory_half = to_half(
        layer_norm(
            enc_two,
            small_params[:, EncSlots.final_gain],
            small_params[:, EncSlots.final_bias],
        )
    )
    cols_even, cols_odd, act_even, act_odd = stem_acts
    enc_early = exchange(
        narrow_for([enc_self_acts[1], enc_self_acts[0]]),
        narrow_for([enc_mlp_acts[0]]),
        narrow_for([down_one(act_odd), act_even, act_odd]),
        wide_for(enc_mlp_acts[1]),
    )
    dec_zero = embedded + weights["dp"].T.astype(jnp.float32)
    dec_one, dec_self, dec_self_acts = self_block(
        dec_zero, weights, small_params, DecSlots, "dq", "do", True
    )
    dec_two, dec_cross, dec_cross_acts = cross_block(dec_one, memory_half, weights, small_params)
    dec_three, dec_mlp, dec_mlp_acts = mlp_block(
        dec_two, weights, small_params, DecSlots, "du", "dd"
    )
    frames = memory_half.shape[0]
    dec_early = exchange(
        narrow_for([dec_self_acts[1], dec_self_acts[0]]),
        narrow_for([dec_mlp_acts[0]]),
        wide_for(dec_mlp_acts[1]),
        narrow_for(
            [fill(dec_cross_acts[0], frames), fill(dec_cross_acts[1], frames), memory_half]
        ),
    )
    final_out = layer_norm(
        dec_three,
        small_params[:, DecSlots.final_gain],
        small_params[:, DecSlots.final_bias],
    )
    final_half = to_half(final_out)
    other_half = [send_rep(final_half, shift) for shift in range(1, reps)]
    gathered_hidden = gather_rows(final_half, 5)
    hidden_by_shift = [gathered_hidden] + [
        lax.all_gather(part, "fsdp", axis=0, tiled=True) for part in other_half
    ]
    vocab_keep = lax.dynamic_slice_in_dim(vocab_mask, vocab_start, vocab_rows) == 1
    keep_column = vocab_keep.astype(jnp.float32)[:, None]
    shut_column = jnp.where(vocab_keep, 0.0, -jnp.inf)[:, None]
    vocab_count = jnp.sum(vocab_mask).astype(jnp.float32)
    pull_column = SMOOTH * keep_column / vocab_count
    local_targets = [(ids - vocab_start)[None, :] for ids in group_targets]
    stats = gather_small(
        vocab_stats(
            gathered_hidden, embed_half, shut_column, keep_column, local_targets[0]
        ).reshape(-1, 128),
        0,
    ).reshape(members, 4, members * TLEN)
    row_top = jnp.max(stats[:, 0], axis=0)
    row_sums = jnp.sum(stats[:, 1] * jnp.exp(stats[:, 0] - row_top[None]), axis=0)
    target_logit = jnp.sum(stats[:, 2], axis=0)
    logit_total = jnp.sum(stats[:, 3], axis=0)
    log_norm = row_top + jnp.log(row_sums)
    entropy = log_norm - (1.0 - SMOOTH) * target_logit - SMOOTH * logit_total / vocab_count
    norm_and_loss = jnp.stack([log_norm, jnp.where(counts_by_shift[0], entropy, 0.0)])
    norms_by_shift = [norm_and_loss] + [send_rep(norm_and_loss, shift) for shift in range(1, reps)]
    loss_sum = sum(jnp.sum(part[1]) for part in norms_by_shift)

    head_grad, hidden_part = own_slopes(
        jnp.where(counts_by_shift[0][:, None], gathered_hidden, jnp.bfloat16(0.0)),
        embed_half,
        shut_column,
        pull_column,
        local_targets[0],
        log_norm[None, :],
        counts_by_shift[0].astype(jnp.float32)[None, :],
    )
    back_hidden = scatter_sum(hidden_part, 6, True, 6)
    back_hidden, (enc_early, dec_early) = settle(back_hidden, enc_early, dec_early)
    enc_attn_narrow, enc_up_narrow, conv_narrow, enc_down_wide = enc_early
    dec_attn_narrow, dec_up_narrow, dec_down_wide, cross_narrow = dec_early
    vector_grads = {}
    back_three, final_gain, final_bias = norm_back(
        dec_three,
        small_params[:, DecSlots.final_gain],
        small_params[:, DecSlots.final_bias],
        back_hidden,
    )
    vector_grads[DecSlots.final_gain] = final_gain
    vector_grads[DecSlots.final_bias] = final_bias
    back_two, dec_down_grad, dec_up_grad = mlp_block_back(
        dec_mlp, back_three, weights, small_params, DecSlots, "du", "dd", vector_grads
    )
    back_two, (hidden_by_shift,) = settle(back_two, hidden_by_shift)
    back_one, back_memory, xout_grad, xquery_grad, xkeyval_grad = cross_block_back(
        dec_cross, back_two, weights, small_params, vector_grads
    )
    back_zero, dec_out_grad, dec_qkv_grad = self_block_back(
        dec_self, back_one, weights, small_params, DecSlots, "dq", "do", True, vector_grads
    )
    dec_down_narrow, dec_up_wide, dec_attn_wide, cross_wide = exchange(
        narrow_for([dec_down_grad]),
        wide_for(dec_up_grad),
        wide_for(jnp.concatenate([dec_out_grad, dec_qkv_grad], axis=1)),
        wide_for(
            jnp.concatenate(
                [fill(jnp.concatenate([xquery_grad, xout_grad], axis=1), frames), xkeyval_grad],
                axis=1,
            )
        ),
    )
    unit = unit_width()
    share = 4 * D // unit
    cores = CORES
    groups = [list(range(place, members, cores)) for place in range(cores)]
    back_half = to_half(back_zero)
    back_stack = jnp.zeros((reps,) + back_half.shape, jnp.bfloat16)
    for shift, place in enumerate(order):
        part = send_rep(back_half, shift) if shift else back_half
        back_stack = lax.dynamic_update_index_in_dim(back_stack, part, place, 0)
    gathered_back = lax.all_gather(back_stack, "fsdp", axis=0)
    back_enc_two, enc_gain, enc_bias = norm_back(
        enc_two,
        small_params[:, EncSlots.final_gain],
        small_params[:, EncSlots.final_bias],
        back_memory,
    )
    vector_grads[EncSlots.final_gain] = enc_gain
    vector_grads[EncSlots.final_bias] = enc_bias
    back_enc_one, enc_down_grad, enc_up_grad = mlp_block_back(
        enc_mlp, back_enc_two, weights, small_params, EncSlots, "eu", "ed", vector_grads
    )
    for shift in range(1, reps):
        head_grad = other_slopes(
            head_grad,
            jnp.where(counts_by_shift[shift][:, None], hidden_by_shift[shift], jnp.bfloat16(0.0)),
            embed_half,
            shut_column,
            pull_column,
            local_targets[shift],
            norms_by_shift[shift][0:1],
        )
    back_enc_one, (dec_attn_wide, cross_wide, head_grad) = settle(
        back_enc_one, dec_attn_wide, cross_wide, head_grad
    )
    dec_down_wide, (gathered_back,) = settle(dec_down_wide, gathered_back)
    dec_rows = lax.psum_scatter(
        jnp.concatenate(
            [
                tmatmul(dec_down_narrow, dec_down_wide),
                tmatmul(dec_up_narrow, dec_up_wide),
                tmatmul(dec_attn_narrow, dec_attn_wide),
                tmatmul(cross_narrow, cross_wide),
            ],
            axis=1,
        ),
        "fsdp",
        scatter_dimension=0,
        axis_index_groups=groups,
        tiled=True,
    )
    enc_late = exchange(narrow_for([enc_down_grad]), wide_for(enc_up_grad))
    back_enc_zero, enc_out_grad, enc_qkv_grad = self_block_back(
        enc_self, back_enc_one, weights, small_params, EncSlots, "eq", "eo", False, vector_grads
    )
    back_enc_zero, (enc_late,) = settle(back_enc_zero, enc_late)
    grad_second, grad_even, grad_odd = stem_back(stem_saved, back_enc_zero, weights, vector_grads)
    enc_attn_wide, conv_wide = exchange(
        wide_for(jnp.concatenate([enc_out_grad, enc_qkv_grad], axis=1)),
        lambda place: lax.optimization_barrier(
            grad_second[:, place * unit % D : place * unit % D + unit]
        ),
    )
    enc_down_narrow, enc_up_wide = enc_late
    first_grad = tmatmul(cols_even, grad_even) + tmatmul(cols_odd, grad_odd)
    loose_rows = packed_rows(
        [first_grad, back_zero] + [vector_grads[column] for column in range(NVEC)], share * 128
    )
    hot_all = to_half(
        ids_all[:, :, 0].transpose(1, 0, 2).reshape(-1, 1)
        - vocab_start
        == lax.broadcasted_iota(jnp.int32, (reps * members * TLEN, vocab_rows), 1)
    )
    embed_grad = head_grad + tmatmul(hot_all, gathered_back.reshape(-1, D))
    loose_rows, (embed_grad,) = settle(loose_rows, embed_grad)
    loose = jnp.sum(quad_swap(loose_rows).reshape(share, 128, D), axis=0).T
    enc_units = rows_of(
        [
            tmatmul(enc_down_narrow, enc_down_wide),
            tmatmul(enc_up_narrow, enc_up_wide),
            tmatmul(enc_attn_narrow, enc_attn_wide),
            tmatmul(conv_narrow, conv_wide),
            loose,
        ],
        4,
    )
    dec_rows, (enc_units,) = settle(dec_rows, enc_units)
    enc_down_units, enc_up_units, enc_attn_units, conv_units, loose_units = enc_units
    dec_quads = quad_rows(dec_rows.reshape(cores, -1, 4 * unit))
    loose_own = jnp.transpose(loose_units, (1, 0, 2)).reshape(-1, share * 128)
    odd_end = 3 * MELS + TLEN
    vec_grad = loose_own[:, odd_end : odd_end + NVEC]
    last_unit = jnp.pad(loose_own[:, :odd_end], ((0, 0), (0, unit - odd_end)))
    per = D // unit
    blocks = pl.cdiv(matrices.shape[1], unit)
    first_lane = lax.broadcasted_iota(jnp.int32, (1, 2), 1) == 0
    once = [enc_down_units, enc_up_units, enc_attn_units, conv_units[: 3 * per], loose_own]
    embed_totals = (jnp.sum(embed_grad * embed_grad), count_bad(embed_grad))
    first = (replica == 0).astype(jnp.float32)
    sums = total_of(
        jnp.where(
            first_lane,
            jnp.sum(dec_rows * dec_rows) + first * (embed_totals[0] + sum(jnp.sum(part * part) for part in once)),
            count_bad(dec_rows) + first * (embed_totals[1] + sum(count_bad(part) for part in once)),
        ),
        1,
        True,
    )
    total_squares, total_bad = sums[0, 0], sums[0, 1]
    gradient_norm = jnp.sqrt(total_squares)
    factor = CLIP_AT / jnp.maximum(gradient_norm, CLIP_AT)
    steps = step_count[0].astype(jnp.float32)
    first_fix = 1.0 / (1.0 - jnp.power(jnp.float32(BETA_ONE), steps))
    second_fix = 1.0 / (1.0 - jnp.power(jnp.float32(BETA_TWO), steps))
    scalars = jnp.stack([factor, first_fix, second_fix])
    emb_moment, emb_square, emb_update, emb_sums = moment_pass(
        scalars, embedding, embed_moment, embed_square, embed_grad, vocab_rows // 7, D
    )
    emb_sums, (dec_quads,) = settle(emb_sums, dec_quads)
    down_units, up_units, attn_units, cross_units = [
        dec_quads[:, :, part * unit : (part + 1) * unit] for part in range(4)
    ]
    mat_grad = jnp.concatenate(
        [
            enc_attn_units[per:],
            enc_attn_units[:per],
            enc_up_units,
            enc_down_units,
            attn_units[per:],
            attn_units[:per],
            cross_units[:per],
            cross_units[2 * per :],
            cross_units[per : 2 * per],
            up_units,
            down_units,
            conv_units[: 3 * per],
            last_unit[None],
            jnp.zeros((-blocks % 4,) + last_unit.shape, jnp.float32),
        ],
        axis=0,
    )
    mat_moment, mat_square, mat_update, mat_sums = moment_pass(
        scalars, matrices, matrix_moment, matrix_square, mat_grad, matrices.shape[0], unit
    )
    vec_moment, vec_square, vec_update = moments(
        vectors, vector_moment, vector_square, vec_grad, factor, first_fix, second_fix
    )
    groups_all = len(names) + 2
    columns = matrices.shape[1]
    column = lax.broadcasted_iota(jnp.int32, (groups_all, columns), 1)
    group = lax.broadcasted_iota(jnp.int32, (groups_all, columns), 0)
    group_of = sum((column >= bounds[piece][1]).astype(jnp.int32) for piece in names)
    in_group = group_of == group
    by_column = jnp.transpose(mat_sums, (1, 0, 2)).reshape(2, -1)[:, :columns]
    lone = jnp.stack([jnp.sum(vectors * vectors), jnp.sum(vec_update * vec_update)])
    place = lax.broadcasted_iota(jnp.int32, (2, groups_all), 1)
    both = jnp.sum(jnp.where(in_group[None], by_column[:, None, :], 0.0), axis=2)
    both = jnp.where(place == groups_all - 2, jnp.sum(emb_sums, axis=(0, 2))[:, None], both)
    both = jnp.where(place == groups_all - 1, lone[:, None], both)
    norms = jnp.sqrt(total_of(both, 2))
    weight_norms, update_norms = norms[0], norms[1]
    ratio = weight_norms / update_norms
    ratio_columns = jnp.sum(jnp.where(in_group, ratio[:, None], 0.0), axis=0)
    new_matrices = matrices - RATE * ratio_columns[None, :] * mat_update
    new_embedding = embedding - RATE * ratio[len(names)] * emb_update
    new_vectors = vectors - RATE * ratio[len(names) + 1] * vec_update
    mean_loss = loss_sum / jnp.sum(text_lengths).astype(jnp.float32)
    group_norms = jnp.stack([weight_norms, update_norms], axis=1)
    return (
        mean_loss,
        total_bad.astype(jnp.int32),
        gradient_norm,
        group_norms,
        new_matrices,
        mat_moment,
        mat_square,
        new_embedding,
        emb_moment,
        emb_square,
        new_vectors,
        vec_moment,
        vec_square,
    )


def solution(mesh):
    placed = (
        P(("rep", "fsdp"), None, None),
        P(("rep", "fsdp"), None),
        P(),
        P(("rep", "fsdp")),
        P(),
        P(),
        P("fsdp", None),
        P("fsdp", None),
        P("fsdp", None),
        P("fsdp", None),
        P("fsdp", None),
        P("fsdp", None),
        P("fsdp", None),
        P("fsdp", None),
        P("fsdp", None),
    )
    return jax.shard_map(
        on_device,
        mesh=mesh,
        in_specs=placed,
        out_specs=(
            P(),
            P(),
            P(),
            P(),
            P("fsdp", None),
            P("fsdp", None),
            P("fsdp", None),
            P("fsdp", None),
            P("fsdp", None),
            P("fsdp", None),
            P("fsdp", None),
            P("fsdp", None),
            P("fsdp", None),
        ),
        check_vma=False,
    )
```

```python
import functools

import jax
import jax.numpy as jnp
from jax import lax
from jax.experimental import pallas as pl
from jax.experimental.pallas import tpu as pltpu
from jax.sharding import PartitionSpec as P

D = 768
H = 12
HD = 64
FF = 3072
MELS = 80
TLEN = 128
LANGTOK = 50259
NVEC = 35


LN_EPS = 1e-05
SMOOTH = 0.1
CLIP_AT = 1.0
BETA_ONE = 0.9
BETA_TWO = 0.999
ADAM_EPS = 1e-06
DECAY = 0.01
RATE = 0.5
NEG_BIG = -1e30
class EncSlots:
    norm_gain = 2
    norm_bias = 3
    query_bias = 4
    value_bias = 5
    out_bias = 6
    mlp_gain = 7
    mlp_bias = 8
    up_bias = 9
    down_bias = 13
    final_gain = 14
    final_bias = 15


class DecSlots:
    norm_gain = 16
    norm_bias = 17
    query_bias = 18
    value_bias = 19
    out_bias = 20
    cross_gain = 21
    cross_bias = 22
    xquery_bias = 23
    xvalue_bias = 24
    xout_bias = 25
    mlp_gain = 26
    mlp_bias = 27
    up_bias = 28
    down_bias = 32
    final_gain = 33
    final_bias = 34


CORES = 2
LINE = 4


def mesh_shape():
    members = lax.axis_size("fsdp")
    return (lax.axis_size("rep"), LINE, members // (LINE * CORES), CORES)


def places():
    reps, line, side, cores = mesh_shape()
    index = lax.axis_index("fsdp")
    return (
        lax.axis_index("rep"),
        index // (side * cores),
        (index // cores) % side,
        index % cores,
    )


def send(values, move):
    reps, line, side, cores = mesh_shape()
    members = line * side * cores
    pairs = []
    for rep in range(reps):
        for far in range(line):
            for near in range(side):
                for core in range(cores):
                    target = move(rep, far, near, core)
                    if target is None:
                        continue
                    rep_to, far_to, near_to, core_to = target
                    pairs.append(
                        (
                            rep * members + (far * side + near) * cores + core,
                            rep_to * members + (far_to * side + near_to) * cores + core_to,
                        )
                    )
    return lax.ppermute(values, ("rep", "fsdp"), pairs)


def send_core(values):
    return send(values, lambda rep, far, near, core: (rep, far, near, 1 - core))


def send_rep(values, shift):
    reps = lax.axis_size("rep")
    return send(values, lambda rep, far, near, core: ((rep + shift) % reps, far, near, core))


def pick(values, index, axis):
    return lax.dynamic_index_in_dim(values, index, axis, keepdims=False)


def block(values, index, width):
    return lax.dynamic_slice_in_dim(values, index * width, width, axis=1)


def share_count():
    return CORES * lax.axis_size("rep")


def quad_place():
    return lax.axis_index("rep") * CORES + lax.axis_index("fsdp") % CORES


def quad_swap(values):
    reps, members = lax.axis_size("rep"), lax.axis_size("fsdp")
    groups = [
        [rep * members + chip * CORES + core for rep in range(reps) for core in range(CORES)]
        for chip in range(members // CORES)
    ]
    return lax.all_to_all(values, ("rep", "fsdp"), 0, 0, axis_index_groups=groups, tiled=True)


def message_body(plan, *refs):
    *sources, packed = refs
    offset = 0
    for which, start, rows, columns in plan:
        packed[offset : offset + rows, :] = sources[which][:, start : start + columns]
        offset = offset + rows


def message_of(pieces, columns):
    sources = []
    plan = []
    for values, start in pieces:
        which = [position for position, held in enumerate(sources) if held is values]
        if not which:
            which = [len(sources)]
            sources.append(values)
        plan.append((which[0], start, values.shape[0], columns))
    total = sum(rows for _, _, rows, _ in plan)
    return pl.pallas_call(
        functools.partial(message_body, plan),
        out_shape=jax.ShapeDtypeStruct((total, columns), sources[0].dtype),
        compiler_params=pltpu.CompilerParams(vmem_limit_bytes=40 << 20),
    )(*sources)


def exchange(*makers):
    share, unit = share_count(), unit_width()
    batches = [makers] if unit == D else [(maker,) for maker in makers]
    arrays, views = [], []
    for batch in batches:
        pieces = [make(place) for place in range(share) for make in batch]
        columns = pieces[0][0].shape[1] if len(batch) == 1 and pieces[0][2] else unit
        message = message_of([piece[:2] for piece in pieces], columns)
        rows = [pieces[position][0].shape[0] for position in range(len(batch))]
        for position in range(len(batch)):
            views.append((len(arrays), sum(rows[:position]), rows[position], sum(rows)))
        arrays.append(quad_swap(message))
    return arrays, views


def settle(value, *others):
    flat, tree = jax.tree.flatten((value, others))
    return jax.tree.unflatten(tree, lax.optimization_barrier(flat))


def unit_width():
    return 4 * D // share_count()


def wide_for(*parts):
    unit = unit_width()

    def make(place):
        start = place * unit % sum(part.shape[1] for part in parts)
        for part in parts:
            if start < part.shape[1]:
                return (part, start, False)
            start = start - part.shape[1]

    return make


def narrow_for(choices):
    unit = unit_width()
    return lambda place: (choices[min(place * unit // D, len(choices) - 1)], 0, True)


def product_of(share, arrays, narrow, wide):
    total = None
    for place in range(share):
        rows = []
        for which, offset, count, step in (narrow, wide):
            start = place * step + offset
            rows.append(arrays[which][start : start + count, :])
        part = tmatmul(*rows)
        total = part if total is None else total + part
    return total


def products_body(share, pairs, stepped, *refs):
    *arrays, output = refs
    unit = output.shape[1] if stepped else output.shape[1] // len(pairs)
    for position, (narrow, wide) in enumerate(pairs):
        if stepped:

            @pl.when(pl.program_id(0) == position)
            def _():
                output[...] = product_of(share, arrays, narrow, wide)

        else:
            output[:, position * unit : (position + 1) * unit] = product_of(
                share, arrays, narrow, wide
            )


def products(pairs, arrays, stepped):
    share, unit = share_count(), unit_width()
    count = len(pairs)
    body = functools.partial(products_body, share, pairs, stepped)
    shape = jax.ShapeDtypeStruct((D, count * unit), jnp.float32)
    params = pltpu.CompilerParams(vmem_limit_bytes=56 << 20)
    if not stepped:
        return pl.pallas_call(
            body, out_shape=shape, cost_estimate=estimate(11), compiler_params=params
        )(*arrays)
    return pl.pallas_call(
        body,
        grid=(count,),
        out_shape=shape,
        in_specs=[fixed(held.shape) for held in arrays],
        out_specs=pl.BlockSpec((D, unit), lambda step: (0, step)),
        cost_estimate=estimate(10),
        compiler_params=params,
    )(*arrays)


def shifted(view, by):
    return (view[0] + by,) + view[1:]


def quad_rows(by_core):
    reps = lax.axis_size("rep")
    message = jnp.concatenate([by_core] * reps, axis=0)
    swapped = quad_swap(message.reshape(-1, by_core.shape[2]))
    return swapped.reshape(message.shape)


def scatter_body(cored, count, values, output, *scratch):
    reps, line, side, cores = mesh_shape()
    rep, far, near, core = places()
    members = line * side * cores
    if cored:
        core_in, core_sum = scratch[:2]
        scratch = scratch[2:]
    near_in, near_sum, far_in, leaving, landing = scratch
    wide = output.shape[-1] // count

    def at(far_to, near_to, core_to):
        return {"fsdp": (far_to * side + near_to) * cores + core_to}

    barrier = pltpu.get_barrier_semaphore()
    partners = [at(lax.rem(far + step, line), near, core) for step in range(1, line)]
    partners += [at(far, lax.rem(near + step, side), core) for step in range(1, side)]
    if cored:
        partners.append(at(far, near, 1 - core))
    for partner in partners:
        pl.semaphore_signal(barrier, inc=1, device_id=partner)
    pl.semaphore_wait(barrier, len(partners))

    started = []

    def start(source, target, device):
        slot = len(started)
        copy = pltpu.make_async_remote_copy(
            src_ref=source,
            dst_ref=target,
            send_sem=leaving.at[slot],
            recv_sem=landing.at[slot],
            device_id=device,
        )
        copy.start()
        started.append(copy)
        return copy

    spans = [pl.ds(part * wide, wide) for part in range(count)]
    core_moves = []
    if cored:
        for part in range(count):
            core_moves.append(
                start(
                    values.at[:, :, 1 - core, :, spans[part]],
                    core_in.at[part],
                    at(far, near, 1 - core),
                )
            )
    near_moves = []
    for part in range(count):
        if cored:
            core_moves[part].wait_recv()
            core_sum[part] = values[:, :, core, :, spans[part]] + core_in[part]
        moves = []
        for step in range(1, side):
            there = lax.rem(near + step, side)
            source = core_sum.at[part, :, there] if cored else values.at[:, there, :, spans[part]]
            moves.append(start(source, near_in.at[part, step - 1], at(far, there, core)))
        near_moves.append(moves)
    far_moves = []
    for part in range(count):
        total = core_sum[part, :, near] if cored else values[:, near, :, spans[part]]
        for step, move in enumerate(near_moves[part]):
            move.wait_recv()
            total = total + near_in[part, step]
        near_sum[part] = total
        moves = []
        for step in range(1, line):
            there = lax.rem(far + step, line)
            moves.append(
                start(near_sum.at[part, there], far_in.at[part, step - 1], at(there, near, core))
            )
        far_moves.append(moves)
    for part in range(count):
        total = near_sum[part, far]
        for step, move in enumerate(far_moves[part]):
            move.wait_recv()
            total = total + far_in[part, step]
        output[:, spans[part]] = total
    for move in started:
        move.wait_send()


def scatter_sum(values, count, cored, tag):
    reps, line, side, cores = mesh_shape()
    rows = values.shape[0] // (line * side * (cores if cored else 1))
    width = values.shape[1]
    wide = width // count
    kind = values.dtype
    shape = (line, side) + ((cores,) if cored else ()) + (rows, width)
    copies = count * ((1 if cored else 0) + (side - 1) + (line - 1))
    cube = (count, line, side, rows, wide)
    scratch = [pltpu.VMEM(cube, kind), pltpu.VMEM(cube, kind)] if cored else []
    scratch += [
        pltpu.VMEM((count, side - 1, line, rows, wide), kind),
        pltpu.VMEM((count, line, rows, wide), kind),
        pltpu.VMEM((count, line - 1, rows, wide), kind),
        pltpu.SemaphoreType.DMA((copies,)),
        pltpu.SemaphoreType.DMA((copies,)),
    ]
    return pl.pallas_call(
        functools.partial(scatter_body, cored, count),
        out_shape=jax.ShapeDtypeStruct((rows, width), kind),
        in_specs=[pl.BlockSpec(memory_space=pltpu.VMEM)],
        out_specs=pl.BlockSpec(memory_space=pltpu.VMEM),
        scratch_shapes=scratch,
        cost_estimate=estimate(45),
        compiler_params=pltpu.CompilerParams(
            collective_id=tag, has_side_effects=True, vmem_limit_bytes=60 << 20
        ),
    )(values.reshape(shape))


def rows_body(pieces, count, *refs):
    reps, line, side, cores = mesh_shape()
    rep, far, near, core = places()
    total = len(pieces)
    values, outputs = refs[:count], refs[count : 2 * count]
    rest = refs[2 * count :]
    near_in, near_sum = rest[:total], rest[total : 2 * total]
    far_in, far_sum = rest[2 * total : 3 * total], rest[3 * total : 4 * total]
    leaving, landing = rest[4 * total :]
    place = rep * cores + core

    def at(rep_to, far_to, near_to, core_to):
        return {"rep": rep_to, "fsdp": (far_to * side + near_to) * cores + core_to}

    moves = [(turn, flip) for turn in range(reps) for flip in range(cores) if turn or flip]
    quad = [
        at(lax.rem(rep + turn, reps), far, near, 1 - core if flip else core)
        for turn, flip in moves
    ]
    line_peers = [at(rep, lax.rem(far + step, line), near, core) for step in range(1, line)]
    side_peers = [at(rep, far, lax.rem(near + step, side), core) for step in range(1, side)]
    barrier = pltpu.get_barrier_semaphore()
    for partner in line_peers + side_peers + quad:
        pl.semaphore_signal(barrier, inc=1, device_id=partner)
    pl.semaphore_wait(barrier, len(line_peers + side_peers + quad))

    started = []

    def start(source, target, device):
        slot = len(started)
        copy = pltpu.make_async_remote_copy(
            src_ref=source,
            dst_ref=target,
            send_sem=leaving.at[slot],
            recv_sem=landing.at[slot],
            device_id=device,
        )
        copy.start()
        started.append(copy)
        return copy

    near_moves = []
    for piece, (part, span) in enumerate(pieces):
        near_moves.append(
            [
                start(
                    values[part].at[:, lax.rem(near + step, side), :, span],
                    near_in[piece].at[step - 1],
                    side_peers[step - 1],
                )
                for step in range(1, side)
            ]
        )
    far_moves = []
    last_moves = []

    def finish(piece):
        part, span = pieces[piece]
        summed = near_sum[piece][far]
        for step, move in enumerate(far_moves[piece]):
            move.wait_recv()
            summed = summed + far_in[piece][step]
        far_sum[piece][...] = summed.reshape(far_sum[piece].shape)
        outputs[part][place, :, span] = far_sum[piece][core]
        for (turn, flip), device in zip(moves, quad):
            last_moves.append(
                start(
                    far_sum[piece].at[1 - core if flip else core],
                    outputs[part].at[place, :, span],
                    device,
                )
            )

    lag = 2
    for piece, (part, span) in enumerate(pieces):
        summed = values[part][:, near, :, span]
        for step, move in enumerate(near_moves[piece]):
            move.wait_recv()
            summed = summed + near_in[piece][step]
        near_sum[piece][...] = summed
        far_moves.append(
            [
                start(
                    near_sum[piece].at[lax.rem(far + step, line)],
                    far_in[piece].at[step - 1],
                    line_peers[step - 1],
                )
                for step in range(1, line)
            ]
        )
        if piece >= lag:
            finish(piece - lag)
    for piece in range(max(total - lag, 0), total):
        finish(piece)
    for move in last_moves:
        move.wait_recv()
    for move in started:
        move.wait_send()


def rows_of(parts, tag):
    reps, line, side, cores = mesh_shape()
    count = len(parts)
    rows = parts[0].shape[0] // (line * side)
    own = rows // cores
    widths = [part.shape[1] for part in parts]
    pieces = []
    for part, width in enumerate(widths):
        offset = 0
        while offset < width:
            size = min(384, width - offset)
            pieces.append((part, pl.ds(offset, size)))
            offset = offset + size
    sizes = [span.size for _, span in pieces]
    copies = len(pieces) * (side - 1 + line - 1 + reps * cores - 1)
    near_in = [pltpu.VMEM((side - 1, line, rows, size), jnp.float32) for size in sizes]
    near_sum = [pltpu.VMEM((line, rows, size), jnp.float32) for size in sizes]
    far_in = [pltpu.VMEM((line - 1, rows, size), jnp.float32) for size in sizes]
    far_sum = [pltpu.VMEM((cores, own, size), jnp.float32) for size in sizes]
    return pl.pallas_call(
        functools.partial(rows_body, pieces, count),
        out_shape=[
            jax.ShapeDtypeStruct((reps * cores, own, width), jnp.float32) for width in widths
        ],
        in_specs=[pl.BlockSpec(memory_space=pltpu.VMEM)] * count,
        out_specs=[pl.BlockSpec(memory_space=pltpu.VMEM)] * count,
        scratch_shapes=near_in
        + near_sum
        + far_in
        + far_sum
        + [pltpu.SemaphoreType.DMA((copies,)), pltpu.SemaphoreType.DMA((copies,))],
        cost_estimate=estimate(130),
        compiler_params=pltpu.CompilerParams(
            collective_id=tag, has_side_effects=True, vmem_limit_bytes=60 << 20
        ),
    )(*[part.reshape(line, side, rows, part.shape[1]) for part in parts])


def pack_body(*refs):
    *sources, packed = refs
    offset = 0
    for source in sources:
        if len(source.shape) == 1:
            packed[offset : offset + 1, :] = source[...].reshape(1, source.shape[0])
            offset = offset + 1
        else:
            packed[offset : offset + source.shape[0], :] = source[...]
            offset = offset + source.shape[0]
    packed[offset:, :] = jnp.zeros((packed.shape[0] - offset, packed.shape[1]), jnp.float32)


def packed_rows(sources, rows):
    return pl.pallas_call(
        pack_body,
        out_shape=jax.ShapeDtypeStruct((rows, D), jnp.float32),
        compiler_params=pltpu.CompilerParams(vmem_limit_bytes=32 << 20),
    )(*sources)


def moment_part(scalars, held, moment, square, raw):
    scaled = raw * scalars[0]
    new_moment = BETA_ONE * moment + (1.0 - BETA_ONE) * scaled
    new_square = BETA_TWO * square + (1.0 - BETA_TWO) * scaled * scaled
    update = (
        new_moment * scalars[1] / (jnp.sqrt(new_square * scalars[2]) + ADAM_EPS) + DECAY * held
    )
    held_sum = jnp.sum(held * held, axis=0, keepdims=True)
    return (new_moment, new_square, update, held_sum, jnp.sum(update * update, axis=0, keepdims=True))


def embed_body(
    scalars, weight, moment, square, head, lookup, moment_out, square_out, update_out, sums
):
    moment_out[...], square_out[...], update_out[...], held_sum, update_sum = moment_part(
        scalars, weight[...], moment[...], square[...], head[...] + lookup[...]
    )
    sums[0, 0:1, :] = held_sum
    sums[0, 1:2, :] = update_sum


def moment_estimate(weight):
    return pl.CostEstimate(
        flops=20 * weight.size, bytes_accessed=28 * weight.size, transcendentals=0
    )


def embed_moments(scalars, weight, moment, square, head, lookup):
    rows, columns = weight.shape
    spec = by_step(rows // VOCAB_STEPS, columns)
    shape = jax.ShapeDtypeStruct(weight.shape, jnp.float32)
    return pl.pallas_call(
        embed_body,
        grid=(VOCAB_STEPS,),
        out_shape=[shape] * 3 + [jax.ShapeDtypeStruct((VOCAB_STEPS, 2, columns), jnp.float32)],
        in_specs=[pl.BlockSpec(memory_space=pltpu.SMEM)] + [spec] * 5,
        out_specs=[spec] * 3 + [pl.BlockSpec((1, 2, columns), lambda step: (step, 0, 0))],
        cost_estimate=moment_estimate(weight),
        compiler_params=pltpu.CompilerParams(vmem_limit_bytes=48 << 20),
    )(scalars, weight, moment, square, head, lookup)


def matrix_body(
    scalars, weight, moment, square, enc, dec, last, moment_out, square_out, update_out, sums
):
    share, unit = enc.shape[0], enc.shape[2]
    per = D // unit
    turned = list(range(per, share)) + list(range(per))
    plain = list(range(share))
    crossed = plain[:per] + plain[2 * per :] + plain[per : 2 * per]
    orders = [turned, plain, plain, turned, crossed, plain, plain, plain[: 3 * per] + [None]]
    for step, order in enumerate(orders):
        source = dec if 3 <= step < 7 else enc

        @pl.when(pl.program_id(0) == step)
        def _():
            for part, place in enumerate(order):
                span = slice(part * unit, (part + 1) * unit)
                raw = last[...] if place is None else source[place]
                results = moment_part(
                    scalars, weight[:, span], moment[:, span], square[:, span], raw
                )
                moment_out[:, span], square_out[:, span], update_out[:, span] = results[:3]
                sums[0, 0:1, span] = results[3]
                sums[0, 1:2, span] = results[4]


def matrix_moments(scalars, weight, moment, square, enc, dec, last):
    rows, columns = weight.shape
    share, unit = share_count(), unit_width()
    spec = pl.BlockSpec((rows, 4 * D), lambda step: (0, step))

    def enc_place(step):
        return (0, 0, jnp.where(step < 3, 2 - step, 3))

    def dec_place(step):
        return (0, 0, jnp.where(step < 4, 2, jnp.where(step == 4, 3, jnp.where(step == 5, 1, 0))))

    shape = jax.ShapeDtypeStruct(weight.shape, jnp.float32)
    return pl.pallas_call(
        matrix_body,
        grid=(8,),
        out_shape=[shape] * 3 + [jax.ShapeDtypeStruct((8, 2, 4 * D), jnp.float32)],
        in_specs=[
            pl.BlockSpec(memory_space=pltpu.SMEM),
            spec,
            spec,
            spec,
            pl.BlockSpec((share, rows, unit), enc_place),
            pl.BlockSpec((share, rows, unit), dec_place),
            fixed(last.shape),
        ],
        out_specs=[spec] * 3 + [pl.BlockSpec((1, 2, 4 * D), lambda step: (step, 0, 0))],
        cost_estimate=moment_estimate(weight),
        compiler_params=pltpu.CompilerParams(vmem_limit_bytes=48 << 20),
    )(scalars, weight, moment, square, enc, dec, last)


def gather_body(everyone, values, gathered, leaving, landing):
    members = lax.axis_size("fsdp")
    reps = lax.axis_size("rep") if everyone else 1
    rep, member = lax.axis_index("rep"), lax.axis_index("fsdp")
    peers = []
    for turn in range(reps):
        for shift in range(members):
            if turn or shift:
                device = {"fsdp": lax.rem(member + shift, members)}
                if everyone:
                    device["rep"] = lax.rem(rep + turn, reps)
                peers.append(device)
    here = rep * members + member if everyone else member
    barrier = pltpu.get_barrier_semaphore()
    for peer in peers:
        pl.semaphore_signal(barrier, inc=1, device_id=peer)
    pl.semaphore_wait(barrier, len(peers))
    copies = []
    for slot, peer in enumerate(peers):
        copies.append(
            pltpu.make_async_remote_copy(
                src_ref=values,
                dst_ref=gathered.at[here],
                send_sem=leaving.at[slot],
                recv_sem=landing.at[slot],
                device_id=peer,
            )
        )
        copies[-1].start()
    gathered[here] = values[...]
    for copy in copies:
        copy.wait()


def gather_small(values, tag, everyone=False):
    count = lax.axis_size("fsdp") * (lax.axis_size("rep") if everyone else 1)
    return pl.pallas_call(
        functools.partial(gather_body, everyone),
        out_shape=jax.ShapeDtypeStruct((count,) + values.shape, values.dtype),
        in_specs=[pl.BlockSpec(memory_space=pltpu.VMEM)],
        out_specs=pl.BlockSpec(memory_space=pltpu.VMEM),
        scratch_shapes=[
            pltpu.SemaphoreType.DMA((count - 1,)),
            pltpu.SemaphoreType.DMA((count - 1,)),
        ],
        cost_estimate=estimate(8),
        compiler_params=pltpu.CompilerParams(collective_id=tag, has_side_effects=True),
    )(values)


def total_of(values, tag, everyone=False):
    rows, columns = values.shape
    padded = jnp.pad(values, ((0, 8 - rows), (0, 128 - columns)))
    return jnp.sum(gather_small(padded, tag, everyone), axis=0)[:rows, :columns]


def rows_gather_body(values, gathered, leaving, landing):
    reps, line, side, cores = mesh_shape()
    rep, far, near, core = places()

    def at(far_to, near_to, core_to):
        return {"fsdp": (far_to * side + near_to) * cores + core_to}

    line_peers = [at(lax.rem(far + step, line), near, core) for step in range(1, line)]
    side_peers = [at(far, lax.rem(near + step, side), core) for step in range(1, side)]
    twin = at(far, near, 1 - core)
    barrier = pltpu.get_barrier_semaphore()
    for partner in line_peers + side_peers + [twin]:
        pl.semaphore_signal(barrier, inc=1, device_id=partner)
    pl.semaphore_wait(barrier, len(line_peers + side_peers) + 1)
    started = []

    def start(source, target, device):
        slot = len(started)
        copy = pltpu.make_async_remote_copy(
            src_ref=source,
            dst_ref=target,
            send_sem=leaving.at[slot],
            recv_sem=landing.at[slot],
            device_id=device,
        )
        copy.start()
        started.append(copy)
        return copy

    line_moves, side_moves, core_moves = [], [], []
    for step in range(1, line):
        line_moves.append(start(values, gathered.at[far, near, core], line_peers[step - 1]))

    def pass_on(step):
        origin = lax.rem(far - step + line, line)
        held = values if step == 0 else gathered.at[origin, near, core]
        for turn in range(1, side):
            side_moves.append(
                (step, turn, start(held, gathered.at[origin, near, core], side_peers[turn - 1]))
            )
        core_moves.append(start(held, gathered.at[origin, near, core], twin))

    pass_on(0)
    gathered[far, near, core] = values[...]
    for step in range(1, line):
        line_moves[step - 1].wait_recv()
        pass_on(step)
    for step, turn, move in list(side_moves):
        move.wait_recv()
        origin = lax.rem(far - step + line, line)
        beside = lax.rem(near - turn + side, side)
        held = gathered.at[origin, beside, core]
        core_moves.append(start(held, gathered.at[origin, beside, core], twin))
    for move in core_moves:
        move.wait_recv()
    for move in started:
        move.wait_send()


def gather_rows(values, tag):
    reps, line, side, cores = mesh_shape()
    copies = line - 1 + line * (side - 1) + line * side
    shape = (line, side, cores) + values.shape
    return pl.pallas_call(
        rows_gather_body,
        out_shape=jax.ShapeDtypeStruct(shape, values.dtype),
        in_specs=[pl.BlockSpec(memory_space=pltpu.VMEM)],
        out_specs=pl.BlockSpec(memory_space=pltpu.VMEM),
        scratch_shapes=[pltpu.SemaphoreType.DMA((copies,)), pltpu.SemaphoreType.DMA((copies,))],
        cost_estimate=estimate(26),
        compiler_params=pltpu.CompilerParams(
            collective_id=tag, has_side_effects=True, vmem_limit_bytes=32 << 20
        ),
    )(values).reshape(-1, values.shape[1])


VOCAB_STEPS = 7
TOKEN_SPAN = 512


def fixed(shape):
    return pl.BlockSpec(shape, lambda step: (0,) * len(shape), pipeline_mode=pl.Buffered(1))


def by_step(tall, wide):
    return pl.BlockSpec((tall, wide), lambda step: (step, 0))


def estimate(micros):
    return pl.CostEstimate(flops=0, bytes_accessed=micros * 3_600_000, transcendentals=0)


def token_spans(count):
    return [slice(start, start + TOKEN_SPAN) for start in range(0, count, TOKEN_SPAN)]


def stats_body(hidden, table, shut, keep, target, stats):
    step = pl.program_id(0)

    @pl.when(step == 0)
    def _():
        stats[0:1, :] = jnp.full((1, stats.shape[1]), NEG_BIG, jnp.float32)
        stats[1:, :] = jnp.zeros((stats.shape[0] - 1, stats.shape[1]), jnp.float32)

    tall = table.shape[0]
    part = table[...]
    row = lax.broadcasted_iota(jnp.int32, (tall, TOKEN_SPAN), 0) + step * tall
    for span in token_spans(stats.shape[1]):
        logits = matmul_t(part, hidden[span, :])
        masked = logits + shut[...]
        former = stats[0:1, span]
        top = jnp.maximum(former, jnp.max(masked, axis=0, keepdims=True))
        stats[1:2, span] = stats[1:2, span] * jnp.exp(former - top) + jnp.sum(
            jnp.exp(masked - top), axis=0, keepdims=True
        )
        stats[0:1, span] = top
        stats[2:3, span] += jnp.sum(
            jnp.where(row == target[:, span], logits, 0.0), axis=0, keepdims=True
        )
        stats[3:4, span] += jnp.sum(
            jnp.where(keep[...] > 0.0, logits, 0.0), axis=0, keepdims=True
        )


def vocab_stats(hidden, table, shut, keep, target):
    rows, vocab_rows = hidden.shape[0], table.shape[0]
    tall = vocab_rows // VOCAB_STEPS
    return pl.pallas_call(
        stats_body,
        grid=(VOCAB_STEPS,),
        out_shape=jax.ShapeDtypeStruct((4, rows), jnp.float32),
        in_specs=[
            fixed(hidden.shape),
            by_step(tall, D),
            by_step(tall, 1),
            by_step(tall, 1),
            fixed((1, rows)),
        ],
        out_specs=pl.BlockSpec((4, rows), lambda step: (0, 0)),
        cost_estimate=estimate(20),
        compiler_params=pltpu.CompilerParams(vmem_limit_bytes=60 << 20),
    )(hidden, table, shut, keep, target)


def slopes_into(slopes, hidden, table, shut, pull, target, log_norm):
    tall = table.shape[0]
    part = table[...]
    row = lax.broadcasted_iota(jnp.int32, (tall, TOKEN_SPAN), 0) + pl.program_id(0) * tall
    for span in token_spans(slopes.shape[1]):
        logits = matmul_t(part, hidden[span, :])
        soft = jnp.exp((logits - log_norm[:, span]) + shut[...])
        hits = jnp.where(row == target[:, span], 1.0 - SMOOTH, 0.0)
        slopes[:, span] = to_half(soft - hits - pull[...])


def own_body(
    hidden, table, shut, pull, target, log_norm, counted, table_grad, hidden_grad, slopes, total
):
    step = pl.program_id(0)
    slopes_into(slopes, hidden, table, shut, pull, target, log_norm)
    table_grad[...] = matmul(slopes[...], hidden[...])
    part = tmatmul(table[...], slopes[...])

    @pl.when(step == 0)
    def _():
        total[...] = part

    @pl.when(step > 0)
    def _():
        total[...] += part

    @pl.when(step == VOCAB_STEPS - 1)
    def _():
        hidden_grad[...] = jnp.where(counted[...] > 0.0, total[...], 0.0).T


def own_slopes(hidden, table, shut, pull, target, log_norm, counted):
    rows, vocab_rows = hidden.shape[0], table.shape[0]
    tall = vocab_rows // VOCAB_STEPS
    flat = fixed((1, rows))
    column = by_step(tall, 1)
    return pl.pallas_call(
        own_body,
        grid=(VOCAB_STEPS,),
        out_shape=[
            jax.ShapeDtypeStruct((vocab_rows, D), jnp.float32),
            jax.ShapeDtypeStruct((rows, D), jnp.float32),
        ],
        in_specs=[fixed(hidden.shape), by_step(tall, D), column, column, flat, flat, flat],
        out_specs=[by_step(tall, D), fixed((rows, D))],
        scratch_shapes=[pltpu.VMEM((tall, rows), jnp.bfloat16), pltpu.VMEM((D, rows), jnp.float32)],
        cost_estimate=estimate(46),
        compiler_params=pltpu.CompilerParams(vmem_limit_bytes=60 << 20),
    )(hidden, table, shut, pull, target, log_norm, counted)


def other_body(hidden, table, shut, pull, target, log_norm, former, table_grad, slopes):
    slopes_into(slopes, hidden, table, shut, pull, target, log_norm)
    table_grad[...] = former[...] + matmul(slopes[...], hidden[...])


def other_slopes(former, hidden, table, shut, pull, target, log_norm):
    rows, vocab_rows = hidden.shape[0], table.shape[0]
    tall = vocab_rows // VOCAB_STEPS
    flat = fixed((1, rows))
    column = by_step(tall, 1)
    return pl.pallas_call(
        other_body,
        grid=(VOCAB_STEPS,),
        out_shape=jax.ShapeDtypeStruct((vocab_rows, D), jnp.float32),
        in_specs=[
            fixed(hidden.shape),
            by_step(tall, D),
            column,
            column,
            flat,
            flat,
            by_step(tall, D),
        ],
        out_specs=by_step(tall, D),
        scratch_shapes=[pltpu.VMEM((tall, rows), jnp.bfloat16)],
        cost_estimate=estimate(27),
        compiler_params=pltpu.CompilerParams(vmem_limit_bytes=60 << 20),
    )(hidden, table, shut, pull, target, log_norm, former)


def reps_body(count, *refs):
    sources, gathered = refs[:count], refs[count : 2 * count]
    leaving, landing = refs[2 * count :]
    reps = lax.axis_size("rep")
    here = lax.axis_index("rep")
    peers = [{"rep": lax.rem(here + turn, reps)} for turn in range(1, reps)]
    barrier = pltpu.get_barrier_semaphore()
    for peer in peers:
        pl.semaphore_signal(barrier, inc=1, device_id=peer)
    pl.semaphore_wait(barrier, len(peers))
    copies = []
    for source, target in zip(sources, gathered):
        for peer in peers:
            copies.append(
                pltpu.make_async_remote_copy(
                    src_ref=source,
                    dst_ref=target.at[here],
                    send_sem=leaving.at[len(copies)],
                    recv_sem=landing.at[len(copies)],
                    device_id=peer,
                )
            )
            copies[-1].start()
        target[here] = source[...]
    for copy in copies:
        copy.wait()


def gather_reps(sources, tag):
    reps = lax.axis_size("rep")
    count = len(sources)
    copies = count * (reps - 1)
    return pl.pallas_call(
        functools.partial(reps_body, count),
        out_shape=[
            jax.ShapeDtypeStruct((reps,) + source.shape, source.dtype) for source in sources
        ],
        in_specs=[pl.BlockSpec(memory_space=pltpu.VMEM)] * count,
        out_specs=[pl.BlockSpec(memory_space=pltpu.VMEM)] * count,
        scratch_shapes=[pltpu.SemaphoreType.DMA((copies,)), pltpu.SemaphoreType.DMA((copies,))],
        cost_estimate=estimate(6),
        compiler_params=pltpu.CompilerParams(
            collective_id=tag, has_side_effects=True, vmem_limit_bytes=24 << 20
        ),
    )(*sources)


def layout(width, hidden, mels, text_len):
    names = (
        "eq",
        "eo",
        "eu",
        "ed",
        "dq",
        "do",
        "xq",
        "xk",
        "xo",
        "du",
        "dd",
        "c2",
        "c1",
        "dp",
    )
    widths = (
        3 * width,
        width,
        hidden,
        hidden,
        3 * width,
        width,
        width,
        2 * width,
        width,
        hidden,
        hidden,
        3 * width,
        3 * mels,
        text_len,
    )
    bounds = {}
    offset = 0
    for piece_name, extent in zip(names, widths):
        bounds[piece_name] = (offset, offset + extent)
        offset = offset + extent
    return (names, bounds)


def columns_of(weights, bounds, piece_name):
    span_start, span_stop = bounds[piece_name]
    return weights[:, span_start:span_stop]


def sinusoid(length, width):
    halfway = width // 2
    increment = jnp.log(10000.0) / (halfway - 1)
    rates = jnp.exp(-increment * jnp.arange(halfway, dtype=jnp.float32))
    angles = jnp.arange(length, dtype=jnp.float32)[:, None] * rates[None, :]
    return jnp.concatenate([jnp.sin(angles), jnp.cos(angles)], axis=1)


def layer_norm(inputs, gain, offset):
    average = jnp.mean(inputs, axis=-1, keepdims=True)
    centred = inputs - average
    spread = jnp.mean(centred * centred, axis=-1, keepdims=True)
    return centred * lax.rsqrt(spread + LN_EPS) * gain + offset


def norm_back(inputs, gain, offset, upstream):
    _, pull = jax.vjp(layer_norm, inputs, gain, offset)
    return pull(upstream)


def gelu_exact(values):
    return jax.nn.gelu(values, approximate=False)


def gelu_back(values, upstream):
    _, pull = jax.vjp(gelu_exact, values)
    return pull(upstream)[0]


def to_half(values):
    return values.astype(jnp.bfloat16)


def matmul(left, right):
    return jnp.dot(left, right, preferred_element_type=jnp.float32)


def matmul_t(left, right):
    return lax.dot_general(
        left, right, (((1,), (1,)), ((), ())), preferred_element_type=jnp.float32
    )


def tmatmul(left, right):
    return lax.dot_general(
        left, right, (((0,), (0,)), ((), ())), preferred_element_type=jnp.float32
    )


def head_pairs(width):
    lane = lax.broadcasted_iota(jnp.int32, (1, 2 * HD), 1)
    masks = [lane < HD, lane >= HD]
    return [(slice(start, start + 2 * HD), masks) for start in range(0, width, 2 * HD)]


def masked_half(values, mask):
    return jnp.where(mask, values, jnp.bfloat16(0.0))


def soft_rows(query_part, key_part, causal):
    scores = matmul_t(query_part, key_part) * HD ** (-0.5)
    if causal:
        rows = lax.broadcasted_iota(jnp.int32, scores.shape, 0)
        cols = lax.broadcasted_iota(jnp.int32, scores.shape, 1)
        scores = jnp.where(rows >= cols, scores, NEG_BIG)
    row_top = jnp.max(scores, axis=-1, keepdims=True)
    log_total = row_top + jnp.log(jnp.sum(jnp.exp(scores - row_top), axis=-1, keepdims=True))
    return jnp.exp(scores - log_total)


def attend_body(causal, queries, keys, values, attended):
    for span, masks in head_pairs(queries.shape[1]):
        query_pair, key_pair, value_pair = queries[:, span], keys[:, span], values[:, span]
        total = None
        for mask in masks:
            soft = soft_rows(masked_half(query_pair, mask), key_pair, causal)
            part = matmul(to_half(soft), masked_half(value_pair, mask))
            total = part if total is None else total + part
        attended[:, span] = to_half(total)


def attend(queries, keys_half, values_half, causal):
    return pl.pallas_call(
        functools.partial(attend_body, causal),
        out_shape=jax.ShapeDtypeStruct(queries.shape, jnp.bfloat16),
        cost_estimate=estimate(6),
        compiler_params=pltpu.CompilerParams(vmem_limit_bytes=32 << 20),
    )(queries, keys_half, values_half)


def attend_back_body(causal, queries, keys, values, upstream, grad_query, grad_key, grad_value, sums):
    for span, masks in head_pairs(queries.shape[1]):
        query_pair, key_pair, value_pair = queries[:, span], keys[:, span], values[:, span]
        up_pair = upstream[:, span]
        totals = None
        for mask in masks:
            query_part, up_part = masked_half(query_pair, mask), masked_half(up_pair, mask)
            soft = soft_rows(query_part, key_pair, causal)
            back_soft = matmul_t(up_part, value_pair)
            inner = jnp.sum(soft * back_soft, axis=-1, keepdims=True)
            back_scores = to_half(soft * (back_soft - inner) * HD ** (-0.5))
            parts = (
                matmul(back_scores, masked_half(key_pair, mask)),
                tmatmul(back_scores, query_part),
                tmatmul(to_half(soft), up_part),
            )
            totals = parts if totals is None else [x + y for x, y in zip(totals, parts)]
        grad_query[:, span] = to_half(totals[0])
        grad_key[:, span] = to_half(totals[1])
        grad_value[:, span] = to_half(totals[2])
        sums[0:1, span] = jnp.sum(totals[0], axis=0, keepdims=True)
        sums[1:2, span] = jnp.sum(totals[2], axis=0, keepdims=True)


def attend_back(queries, keys_half, values_half, causal, back_attended):
    half = [
        jax.ShapeDtypeStruct(part.shape, jnp.bfloat16)
        for part in (queries, keys_half, values_half)
    ]
    return pl.pallas_call(
        functools.partial(attend_back_body, causal),
        out_shape=half + [jax.ShapeDtypeStruct((2, queries.shape[1]), jnp.float32)],
        cost_estimate=estimate(12),
        compiler_params=pltpu.CompilerParams(vmem_limit_bytes=32 << 20),
    )(queries, keys_half, values_half, back_attended)


def self_block(stream, weights, small_params, slots, qkv_name, out_name, causal):
    normed = layer_norm(
        stream, small_params[:, slots.norm_gain], small_params[:, slots.norm_bias]
    )
    normed_half = to_half(normed)
    projected = matmul(normed_half, weights[qkv_name])
    queries = to_half(projected[:, :D] + small_params[:, slots.query_bias])
    keys_half = to_half(projected[:, D : 2 * D])
    values_half = to_half(projected[:, 2 * D :] + small_params[:, slots.value_bias])
    attended = attend(queries, keys_half, values_half, causal)
    output = (
        stream + matmul(attended, weights[out_name]) + small_params[:, slots.out_bias]
    )
    return (output, (stream, queries, keys_half, values_half), (normed_half, attended))


def self_block_back(
    saved, upstream, weights, small_params, slots, qkv_name, out_name, causal, vector_grads
):
    stream, queries, keys_half, values_half = saved
    grad_out = to_half(upstream)
    back_attended = to_half(matmul_t(grad_out, weights[out_name]))
    back_queries, back_keys, back_values, back_sums = attend_back(
        queries, keys_half, values_half, causal, back_attended
    )
    grad_proj = [back_queries, back_keys, back_values]
    back_normed = sum(
        matmul_t(part, weights[qkv_name][:, position * D : (position + 1) * D])
        for position, part in enumerate(grad_proj)
    )
    back_stream, back_gain, back_bias = norm_back(
        stream,
        small_params[:, slots.norm_gain],
        small_params[:, slots.norm_bias],
        back_normed,
    )
    vector_grads[slots.norm_gain] = back_gain
    vector_grads[slots.norm_bias] = back_bias
    vector_grads[slots.query_bias] = back_sums[0]
    vector_grads[slots.value_bias] = back_sums[1]
    vector_grads[slots.out_bias] = jnp.sum(upstream, axis=0)
    return (upstream + back_stream, grad_out, grad_proj)


def cross_block(stream, memory_half, weights, small_params):
    normed = layer_norm(
        stream, small_params[:, DecSlots.cross_gain], small_params[:, DecSlots.cross_bias]
    )
    normed_half = to_half(normed)
    queries = to_half(
        matmul(normed_half, weights["xq"]) + small_params[:, DecSlots.xquery_bias]
    )
    keyval = matmul(memory_half, weights["xk"])
    keys_half = to_half(keyval[:, :D])
    values_half = to_half(keyval[:, D:] + small_params[:, DecSlots.xvalue_bias])
    attended = attend(queries, keys_half, values_half, False)
    output = (
        stream + matmul(attended, weights["xo"]) + small_params[:, DecSlots.xout_bias]
    )
    return (output, (stream, queries, keys_half, values_half), (normed_half, attended))


def cross_block_back(saved, upstream, weights, small_params, vector_grads):
    stream, queries, keys_half, values_half = saved
    grad_out = to_half(upstream)
    back_attended = to_half(matmul_t(grad_out, weights["xo"]))
    grad_query, back_keys, back_values, back_sums = attend_back(
        queries, keys_half, values_half, False, back_attended
    )
    back_normed = matmul_t(grad_query, weights["xq"])
    grad_keyval = [back_keys, back_values]
    back_memory = matmul_t(back_keys, weights["xk"][:, :D]) + matmul_t(
        back_values, weights["xk"][:, D:]
    )
    back_stream, back_gain, back_bias = norm_back(
        stream,
        small_params[:, DecSlots.cross_gain],
        small_params[:, DecSlots.cross_bias],
        back_normed,
    )
    vector_grads[DecSlots.cross_gain] = back_gain
    vector_grads[DecSlots.cross_bias] = back_bias
    vector_grads[DecSlots.xquery_bias] = back_sums[0]
    vector_grads[DecSlots.xvalue_bias] = back_sums[1]
    vector_grads[DecSlots.xout_bias] = jnp.sum(upstream, axis=0)
    return (upstream + back_stream, back_memory, grad_out, grad_query, grad_keyval)


def mlp_block(stream, weights, small_params, slots, up_name, down_name):
    normed = layer_norm(
        stream, small_params[:, slots.mlp_gain], small_params[:, slots.mlp_bias]
    )
    normed_half = to_half(normed)
    up_bias = small_params[:, slots.up_bias : slots.up_bias + 4].T.reshape(-1)
    raised = matmul(normed_half, weights[up_name]) + up_bias
    active = to_half(gelu_exact(raised))
    output = (
        stream + matmul_t(active, weights[down_name]) + small_params[:, slots.down_bias]
    )
    return (output, (stream, raised), (normed_half, active))


def mlp_block_back(saved, upstream, weights, small_params, slots, up_name, down_name, vector_grads):
    stream, raised = saved
    grad_out = to_half(upstream)
    back_raised = gelu_back(raised, matmul(grad_out, weights[down_name]))
    bias_rows = jnp.sum(back_raised, axis=0).reshape(4, D)
    for quarter in range(4):
        vector_grads[slots.up_bias + quarter] = bias_rows[quarter]
    grad_raised = to_half(back_raised)
    back_normed = matmul_t(grad_raised, weights[up_name])
    back_stream, back_gain, back_bias = norm_back(
        stream, small_params[:, slots.mlp_gain], small_params[:, slots.mlp_bias], back_normed
    )
    vector_grads[slots.mlp_gain] = back_gain
    vector_grads[slots.mlp_bias] = back_bias
    vector_grads[slots.down_bias] = jnp.sum(upstream, axis=0)
    return (upstream + back_stream, grad_out, grad_raised)


def down_one(values):
    return jnp.pad(values, ((1, 0), (0, 0)))[:-1]


def up_one(values):
    return jnp.pad(values, ((0, 1), (0, 0)))[1:]


def stem_forward(mel_half, weights, small_params):
    bins, frames_in = mel_half.shape
    paired = mel_half.T.reshape(frames_in // 2, 2 * bins)
    mel_even, mel_odd = paired[:, :bins], paired[:, bins:]
    cols_even = jnp.concatenate([down_one(mel_odd), mel_even, mel_odd], axis=1)
    cols_odd = jnp.concatenate([mel_even, mel_odd, up_one(mel_even)], axis=1)
    pre_even = matmul_t(cols_even, weights["c1"]) + small_params[:, 0]
    pre_odd = matmul_t(cols_odd, weights["c1"]) + small_params[:, 0]
    act_even = to_half(gelu_exact(pre_even))
    act_odd = to_half(gelu_exact(pre_odd))
    taps = weights["c2"]
    conv_sum = (
        matmul(down_one(act_odd), taps[:, :D])
        + matmul(act_even, taps[:, D : 2 * D])
        + matmul(act_odd, taps[:, 2 * D :])
    )
    second_pre = conv_sum + small_params[:, 1]
    stream = gelu_exact(second_pre) + sinusoid(frames_in // 2, D)
    return (stream, (pre_even, pre_odd, second_pre), (cols_even, cols_odd, act_even, act_odd))


def stem_back(saved, upstream, weights, vector_grads):
    pre_even, pre_odd, second_pre = saved
    back_second = gelu_back(second_pre, upstream)
    vector_grads[1] = jnp.sum(back_second, axis=0)
    grad_second = to_half(back_second)
    taps = weights["c2"]
    back_even = gelu_back(pre_even, matmul_t(grad_second, taps[:, D : 2 * D]))
    back_odd = gelu_back(
        pre_odd,
        matmul_t(grad_second, taps[:, 2 * D :])
        + matmul_t(up_one(grad_second), taps[:, :D]),
    )
    vector_grads[0] = jnp.sum(back_even, axis=0) + jnp.sum(back_odd, axis=0)
    return (grad_second, to_half(back_even), to_half(back_odd))


def fill(values, rows):
    return jnp.pad(values, ((0, rows - values.shape[0]), (0, 0)))


def moments(weight, moment, square, gradient, factor, first_fix, second_fix):
    scaled = gradient * factor
    new_moment = BETA_ONE * moment + (1.0 - BETA_ONE) * scaled
    new_square = BETA_TWO * square + (1.0 - BETA_TWO) * scaled * scaled
    update = new_moment * first_fix / (jnp.sqrt(new_square * second_fix) + ADAM_EPS) + DECAY * weight
    return (new_moment, new_square, update)


def count_bad(values):
    return jnp.sum(jnp.where(jnp.isfinite(values), 0.0, 1.0))


def on_device(
    mel_frames,
    text_ids,
    text_lengths,
    language,
    vocab_mask,
    step_count,
    matrices,
    matrix_moment,
    matrix_square,
    embedding,
    embed_moment,
    embed_square,
    vectors,
    vector_moment,
    vector_square,
):
    names, bounds = layout(D, FF, MELS, TLEN)
    reps = lax.axis_size("rep")
    members = lax.axis_size("fsdp")
    replica = lax.axis_index("rep")
    member = lax.axis_index("fsdp")
    first_names = ("c1", "c2", "eq", "eo", "eu", "ed", "dp")
    last_names = ("dq", "do", "xq", "xk", "xo", "du", "dd")
    first_half = jnp.concatenate(
        [to_half(columns_of(matrices, bounds, piece)) for piece in first_names]
        + [to_half(vectors)],
        axis=1,
    )
    last_half = jnp.concatenate(
        [to_half(columns_of(matrices, bounds, piece)) for piece in last_names], axis=1
    )
    weights = {}
    for batch, batch_half in ((first_names, first_half), (last_names, last_half)):
        gathered = lax.all_gather(batch_half, "fsdp", axis=0, tiled=True)
        offset = 0
        for piece in batch:
            extent = bounds[piece][1] - bounds[piece][0]
            weights[piece] = gathered[:, offset : offset + extent]
            offset = offset + extent
        if batch is first_names:
            small_params = gathered[:, offset:].astype(jnp.float32)
    inputs_ids = jnp.concatenate([LANGTOK + language, text_ids[0, :-1]])[None, :]
    ids_all = lax.all_gather(
        jnp.concatenate([inputs_ids, text_ids], axis=1), ("rep", "fsdp"), axis=0, tiled=True
    ).reshape(reps, members, 2, TLEN)
    order = [(replica - shift) % reps for shift in range(reps)]
    ids_by_shift = [pick(ids_all, place, 0) for place in order]
    group_inputs = [ids[:, 0].reshape(-1) for ids in ids_by_shift]
    group_targets = [ids[:, 1].reshape(-1) for ids in ids_by_shift]
    counts_by_shift = [
        (
            lax.broadcasted_iota(jnp.int32, (members, TLEN), 1)
            < lax.dynamic_slice_in_dim(text_lengths, place * members, members)[:, None]
        ).reshape(-1)
        for place in order
    ]
    vocab_rows = embedding.shape[0]
    vocab_start = member * vocab_rows
    embed_half = to_half(embedding)
    vocab_iota = lax.broadcasted_iota(jnp.int32, (members * TLEN, vocab_rows), 1)
    input_hot = [to_half(ids[:, None] - vocab_start == vocab_iota) for ids in group_inputs]
    embedded = scatter_sum(
        matmul(input_hot[0], embed_half).astype(jnp.bfloat16), 3, True, 3
    ).astype(jnp.float32)
    enc_zero, stem_saved, stem_acts = stem_forward(mel_frames[0], weights, small_params)
    enc_one, enc_self, enc_self_acts = self_block(
        enc_zero, weights, small_params, EncSlots, "eq", "eo", False
    )
    enc_two, enc_mlp, enc_mlp_acts = mlp_block(
        enc_one, weights, small_params, EncSlots, "eu", "ed"
    )
    memory_half = to_half(
        layer_norm(
            enc_two,
            small_params[:, EncSlots.final_gain],
            small_params[:, EncSlots.final_bias],
        )
    )
    cols_even, cols_odd, act_even, act_odd = stem_acts
    enc_early, enc_early_views = exchange(
        narrow_for([enc_self_acts[1], enc_self_acts[0]]),
        narrow_for([enc_mlp_acts[0]]),
        narrow_for([down_one(act_odd), act_even, act_odd]),
        wide_for(enc_mlp_acts[1]),
    )
    embedded, (enc_early,) = settle(embedded, enc_early)
    dec_zero = embedded + weights["dp"].T.astype(jnp.float32)
    dec_one, dec_self, dec_self_acts = self_block(
        dec_zero, weights, small_params, DecSlots, "dq", "do", True
    )
    dec_two, dec_cross, dec_cross_acts = cross_block(dec_one, memory_half, weights, small_params)
    dec_three, dec_mlp, dec_mlp_acts = mlp_block(
        dec_two, weights, small_params, DecSlots, "du", "dd"
    )
    frames = memory_half.shape[0]
    dec_early, dec_early_views = exchange(
        narrow_for([dec_self_acts[1], dec_self_acts[0]]),
        narrow_for([dec_mlp_acts[0]]),
        wide_for(dec_mlp_acts[1]),
        narrow_for(
            [fill(dec_cross_acts[0], frames), fill(dec_cross_acts[1], frames), memory_half]
        ),
    )
    final_out = layer_norm(
        dec_three,
        small_params[:, DecSlots.final_gain],
        small_params[:, DecSlots.final_bias],
    )
    final_half = to_half(final_out)
    gathered_hidden = gather_rows(final_half, 5)
    vocab_keep = lax.dynamic_slice_in_dim(vocab_mask, vocab_start, vocab_rows) == 1
    keep_column = vocab_keep.astype(jnp.float32)[:, None]
    shut_column = jnp.where(vocab_keep, 0.0, -jnp.inf)[:, None]
    vocab_count = jnp.sum(vocab_mask).astype(jnp.float32)
    pull_column = SMOOTH * keep_column / vocab_count
    local_targets = [(ids - vocab_start)[None, :] for ids in group_targets]
    stats = gather_small(
        vocab_stats(
            gathered_hidden, embed_half, shut_column, keep_column, local_targets[0]
        ).reshape(-1, 128),
        0,
    ).reshape(members, 4, members * TLEN)
    row_top = jnp.max(stats[:, 0], axis=0)
    row_sums = jnp.sum(stats[:, 1] * jnp.exp(stats[:, 0] - row_top[None]), axis=0)
    target_logit = jnp.sum(stats[:, 2], axis=0)
    logit_total = jnp.sum(stats[:, 3], axis=0)
    log_norm = row_top + jnp.log(row_sums)
    log_norm, (dec_early,) = settle(log_norm, dec_early)
    entropy = log_norm - (1.0 - SMOOTH) * target_logit - SMOOTH * logit_total / vocab_count
    norm_and_loss = jnp.stack([log_norm, jnp.where(counts_by_shift[0], entropy, 0.0)])
    final_by_rep, norms_by_rep = gather_reps(
        [final_half, norm_and_loss.reshape(-1, 128)], 7
    )
    norms_by_shift = [
        pick(norms_by_rep, place, 0).reshape(norm_and_loss.shape) for place in order
    ]
    hidden_by_shift = [gathered_hidden] + [
        lax.all_gather(pick(final_by_rep, place, 0), "fsdp", axis=0, tiled=True)
        for place in order[1:]
    ]
    loss_sum = sum(jnp.sum(part[1]) for part in norms_by_shift)

    head_grad, hidden_part = own_slopes(
        jnp.where(counts_by_shift[0][:, None], gathered_hidden, jnp.bfloat16(0.0)),
        embed_half,
        shut_column,
        pull_column,
        local_targets[0],
        norms_by_shift[0][0:1],
        counts_by_shift[0].astype(jnp.float32)[None, :],
    )
    back_hidden = scatter_sum(hidden_part, 6, True, 6)
    vector_grads = {}
    back_three, final_gain, final_bias = norm_back(
        dec_three,
        small_params[:, DecSlots.final_gain],
        small_params[:, DecSlots.final_bias],
        back_hidden,
    )
    vector_grads[DecSlots.final_gain] = final_gain
    vector_grads[DecSlots.final_bias] = final_bias
    back_two, dec_down_grad, dec_up_grad = mlp_block_back(
        dec_mlp, back_three, weights, small_params, DecSlots, "du", "dd", vector_grads
    )
    back_two, (hidden_by_shift,) = settle(back_two, hidden_by_shift)
    back_one, back_memory, xout_grad, xquery_grad, xkeyval_grad = cross_block_back(
        dec_cross, back_two, weights, small_params, vector_grads
    )
    back_zero, dec_out_grad, dec_qkv_grad = self_block_back(
        dec_self, back_one, weights, small_params, DecSlots, "dq", "do", True, vector_grads
    )
    dec_late, dec_late_views = exchange(
        narrow_for([dec_down_grad]),
        wide_for(dec_up_grad),
        wide_for(dec_out_grad, *dec_qkv_grad),
        wide_for(fill(xquery_grad, frames), fill(xout_grad, frames), *xkeyval_grad),
    )
    unit = unit_width()
    share = 4 * D // unit
    cores = CORES
    groups = [list(range(place, members, cores)) for place in range(cores)]
    back_half = to_half(back_zero)
    (back_stack,) = gather_reps([back_half], 8)
    gathered_back = lax.all_gather(back_stack, "fsdp", axis=0)
    for shift in range(1, reps):
        head_grad = other_slopes(
            head_grad,
            jnp.where(counts_by_shift[shift][:, None], hidden_by_shift[shift], jnp.bfloat16(0.0)),
            embed_half,
            shut_column,
            pull_column,
            local_targets[shift],
            norms_by_shift[shift][0:1],
        )
    dec_late, (head_grad,) = settle(dec_late, head_grad)
    early = len(dec_early)
    attn_narrow, up_narrow, down_wide, cross_narrow = dec_early_views
    down_narrow, up_wide, attn_wide, cross_wide = [
        shifted(view, early) for view in dec_late_views
    ]
    dec_products = products(
        [
            (down_narrow, down_wide),
            (up_narrow, up_wide),
            (attn_narrow, attn_wide),
            (cross_narrow, cross_wide),
        ],
        dec_early + dec_late,
        True,
    )
    back_memory, (dec_products,) = settle(back_memory, dec_products)
    dec_rows = lax.psum_scatter(
        dec_products, "fsdp", scatter_dimension=0, axis_index_groups=groups, tiled=True
    )
    back_enc_two, enc_gain, enc_bias = norm_back(
        enc_two,
        small_params[:, EncSlots.final_gain],
        small_params[:, EncSlots.final_bias],
        back_memory,
    )
    vector_grads[EncSlots.final_gain] = enc_gain
    vector_grads[EncSlots.final_bias] = enc_bias
    back_enc_one, enc_down_grad, enc_up_grad = mlp_block_back(
        enc_mlp, back_enc_two, weights, small_params, EncSlots, "eu", "ed", vector_grads
    )
    enc_late, enc_late_views = exchange(narrow_for([enc_down_grad]), wide_for(enc_up_grad))
    back_enc_zero, enc_out_grad, enc_qkv_grad = self_block_back(
        enc_self, back_enc_one, weights, small_params, EncSlots, "eq", "eo", False, vector_grads
    )
    grad_second, grad_even, grad_odd = stem_back(stem_saved, back_enc_zero, weights, vector_grads)
    grad_second, (gathered_back, enc_late) = settle(grad_second, gathered_back, enc_late)
    enc_last, enc_last_views = exchange(
        wide_for(enc_out_grad, *enc_qkv_grad), wide_for(grad_second)
    )
    first_grad = tmatmul(cols_even, grad_even) + tmatmul(cols_odd, grad_odd)
    loose_rows = packed_rows(
        [first_grad, back_zero] + [vector_grads[column] for column in range(NVEC)], share * 128
    )
    hot_all = to_half(
        ids_all[:, :, 0].transpose(1, 0, 2).reshape(-1, 1)
        - vocab_start
        == lax.broadcasted_iota(jnp.int32, (reps * members * TLEN, vocab_rows), 1)
    )
    lookup = tmatmul(hot_all, gathered_back.reshape(-1, D))
    loose_rows, (lookup, enc_last) = settle(loose_rows, lookup, enc_last)
    embed_grad = head_grad + lookup
    loose = jnp.sum(quad_swap(loose_rows).reshape(share, 128, D), axis=0).T
    early, late = len(enc_early), len(enc_early) + len(enc_late)
    attn_narrow, up_narrow, conv_narrow, down_wide = enc_early_views
    down_narrow, up_wide = [shifted(view, early) for view in enc_late_views]
    attn_wide, conv_wide = [shifted(view, late) for view in enc_last_views]
    enc_units = rows_of(
        [
            products(
                [
                    (down_narrow, down_wide),
                    (up_narrow, up_wide),
                    (attn_narrow, attn_wide),
                    (conv_narrow, conv_wide),
                ],
                enc_early + enc_late + enc_last,
                False,
            ),
            loose,
        ],
        4,
    )
    dec_rows, (enc_units,) = settle(dec_rows, enc_units)
    enc_quads, loose_units = enc_units
    per = D // unit
    dec_quads = quad_rows(dec_rows.reshape(cores, -1, 4 * unit))
    loose_own = jnp.transpose(loose_units, (1, 0, 2)).reshape(-1, share * 128)
    odd_end = 3 * MELS + TLEN
    vec_grad = loose_own[:, odd_end : odd_end + NVEC]
    last_unit = jnp.pad(loose_own[:, :odd_end], ((0, 0), (0, unit - odd_end)))
    first_lane = lax.broadcasted_iota(jnp.int32, (1, 2), 1) == 0
    once = [enc_quads[:, :, : 3 * unit], enc_quads[: 3 * per, :, 3 * unit :], loose_own]
    embed_totals = (jnp.sum(embed_grad * embed_grad), count_bad(embed_grad))
    first = (replica == 0).astype(jnp.float32)
    squares = embed_totals[0] + sum(jnp.sum(part * part) for part in once)
    bad = embed_totals[1] + sum(count_bad(part) for part in once)
    sums = total_of(
        jnp.where(
            first_lane,
            jnp.sum(dec_rows * dec_rows) + first * squares,
            count_bad(dec_rows) + first * bad,
        ),
        1,
        True,
    )
    total_squares, total_bad = sums[0, 0], sums[0, 1]
    gradient_norm = jnp.sqrt(total_squares)
    factor = CLIP_AT / jnp.maximum(gradient_norm, CLIP_AT)
    steps = step_count[0].astype(jnp.float32)
    first_fix = 1.0 / (1.0 - jnp.power(jnp.float32(BETA_ONE), steps))
    second_fix = 1.0 / (1.0 - jnp.power(jnp.float32(BETA_TWO), steps))
    scalars = jnp.stack([factor, first_fix, second_fix])
    emb_moment, emb_square, emb_update, emb_sums = embed_moments(
        scalars, embedding, embed_moment, embed_square, head_grad, lookup
    )
    emb_sums, (dec_quads,) = settle(emb_sums, dec_quads)
    mat_moment, mat_square, mat_update, mat_sums = matrix_moments(
        scalars, matrices, matrix_moment, matrix_square, enc_quads, dec_quads, last_unit
    )
    vec_moment, vec_square, vec_update = moments(
        vectors, vector_moment, vector_square, vec_grad, factor, first_fix, second_fix
    )
    groups_all = len(names) + 2
    columns = matrices.shape[1]
    column = lax.broadcasted_iota(jnp.int32, (groups_all, columns), 1)
    group = lax.broadcasted_iota(jnp.int32, (groups_all, columns), 0)
    group_of = sum((column >= bounds[piece][1]).astype(jnp.int32) for piece in names)
    in_group = group_of == group
    by_column = jnp.transpose(mat_sums, (1, 0, 2)).reshape(2, -1)[:, :columns]
    lone = jnp.stack([jnp.sum(vectors * vectors), jnp.sum(vec_update * vec_update)])
    place = lax.broadcasted_iota(jnp.int32, (2, groups_all), 1)
    both = jnp.sum(jnp.where(in_group[None], by_column[:, None, :], 0.0), axis=2)
    both = jnp.where(place == groups_all - 2, jnp.sum(emb_sums, axis=(0, 2))[:, None], both)
    both = jnp.where(place == groups_all - 1, lone[:, None], both)
    norms = jnp.sqrt(total_of(both, 2))
    weight_norms, update_norms = norms[0], norms[1]
    ratio = weight_norms / update_norms
    ratio_columns = jnp.sum(jnp.where(in_group, ratio[:, None], 0.0), axis=0)
    new_matrices = matrices - RATE * ratio_columns[None, :] * mat_update
    new_embedding = embedding - RATE * ratio[len(names)] * emb_update
    new_vectors = vectors - RATE * ratio[len(names) + 1] * vec_update
    mean_loss = loss_sum / jnp.sum(text_lengths).astype(jnp.float32)
    group_norms = jnp.stack([weight_norms, update_norms], axis=1)
    return (
        mean_loss,
        total_bad.astype(jnp.int32),
        gradient_norm,
        group_norms,
        new_matrices,
        mat_moment,
        mat_square,
        new_embedding,
        emb_moment,
        emb_square,
        new_vectors,
        vec_moment,
        vec_square,
    )


def solution(mesh):
    placed = (
        P(("rep", "fsdp"), None, None),
        P(("rep", "fsdp"), None),
        P(),
        P(("rep", "fsdp")),
        P(),
        P(),
        P("fsdp", None),
        P("fsdp", None),
        P("fsdp", None),
        P("fsdp", None),
        P("fsdp", None),
        P("fsdp", None),
        P("fsdp", None),
        P("fsdp", None),
        P("fsdp", None),
    )
    return jax.shard_map(
        on_device,
        mesh=mesh,
        in_specs=placed,
        out_specs=(
            P(),
            P(),
            P(),
            P(),
            P("fsdp", None),
            P("fsdp", None),
            P("fsdp", None),
            P("fsdp", None),
            P("fsdp", None),
            P("fsdp", None),
            P("fsdp", None),
            P("fsdp", None),
            P("fsdp", None),
        ),
        check_vma=False,
    )
```

```python
import functools

import jax
import jax.numpy as jnp
from jax import lax
from jax.experimental import pallas as pl
from jax.experimental.pallas import tpu as pltpu
from jax.sharding import PartitionSpec as P

D = 768
H = 12
HD = 64
FF = 3072
MELS = 80
TLEN = 128
LANGTOK = 50259
NVEC = 35


LN_EPS = 1e-05
SMOOTH = 0.1
CLIP_AT = 1.0
BETA_ONE = 0.9
BETA_TWO = 0.999
ADAM_EPS = 1e-06
DECAY = 0.01
RATE = 0.5
NEG_BIG = -1e30
class EncSlots:
    norm_gain = 2
    norm_bias = 3
    query_bias = 4
    value_bias = 5
    out_bias = 6
    mlp_gain = 7
    mlp_bias = 8
    up_bias = 9
    down_bias = 13
    final_gain = 14
    final_bias = 15


class DecSlots:
    norm_gain = 16
    norm_bias = 17
    query_bias = 18
    value_bias = 19
    out_bias = 20
    cross_gain = 21
    cross_bias = 22
    xquery_bias = 23
    xvalue_bias = 24
    xout_bias = 25
    mlp_gain = 26
    mlp_bias = 27
    up_bias = 28
    down_bias = 32
    final_gain = 33
    final_bias = 34


CORES = 2
LINE = 4


def mesh_shape():
    members = lax.axis_size("fsdp")
    return (lax.axis_size("rep"), LINE, members // (LINE * CORES), CORES)


def places():
    reps, line, side, cores = mesh_shape()
    index = lax.axis_index("fsdp")
    return (
        lax.axis_index("rep"),
        index // (side * cores),
        (index // cores) % side,
        index % cores,
    )


def send(values, move):
    reps, line, side, cores = mesh_shape()
    members = line * side * cores
    pairs = []
    for rep in range(reps):
        for far in range(line):
            for near in range(side):
                for core in range(cores):
                    target = move(rep, far, near, core)
                    if target is None:
                        continue
                    rep_to, far_to, near_to, core_to = target
                    pairs.append(
                        (
                            rep * members + (far * side + near) * cores + core,
                            rep_to * members + (far_to * side + near_to) * cores + core_to,
                        )
                    )
    return lax.ppermute(values, ("rep", "fsdp"), pairs)


def send_core(values):
    return send(values, lambda rep, far, near, core: (rep, far, near, 1 - core))


def send_rep(values, shift):
    reps = lax.axis_size("rep")
    return send(values, lambda rep, far, near, core: ((rep + shift) % reps, far, near, core))


def pick(values, index, axis):
    return lax.dynamic_index_in_dim(values, index, axis, keepdims=False)


def block(values, index, width):
    return lax.dynamic_slice_in_dim(values, index * width, width, axis=1)


def share_count():
    return CORES * lax.axis_size("rep")


def quad_place():
    return lax.axis_index("rep") * CORES + lax.axis_index("fsdp") % CORES


def quad_swap(values):
    reps, members = lax.axis_size("rep"), lax.axis_size("fsdp")
    groups = [
        [rep * members + chip * CORES + core for rep in range(reps) for core in range(CORES)]
        for chip in range(members // CORES)
    ]
    return lax.all_to_all(values, ("rep", "fsdp"), 0, 0, axis_index_groups=groups, tiled=True)


def message_body(plan, *refs):
    *sources, packed = refs
    offset = 0
    for which, start, rows, columns in plan:
        packed[offset : offset + rows, :] = sources[which][:, start : start + columns]
        offset = offset + rows


def message_of(pieces, columns):
    sources = []
    plan = []
    for values, start in pieces:
        which = [position for position, held in enumerate(sources) if held is values]
        if not which:
            which = [len(sources)]
            sources.append(values)
        plan.append((which[0], start, values.shape[0], columns))
    total = sum(rows for _, _, rows, _ in plan)
    return pl.pallas_call(
        functools.partial(message_body, plan),
        out_shape=jax.ShapeDtypeStruct((total, columns), sources[0].dtype),
        compiler_params=pltpu.CompilerParams(vmem_limit_bytes=40 << 20),
    )(*sources)


def exchange(*makers):
    share, unit = share_count(), unit_width()
    batches = [makers] if unit == D else [(maker,) for maker in makers]
    arrays, views = [], []
    for batch in batches:
        pieces = [make(place) for place in range(share) for make in batch]
        columns = pieces[0][0].shape[1] if len(batch) == 1 and pieces[0][2] else unit
        message = message_of([piece[:2] for piece in pieces], columns)
        rows = [pieces[position][0].shape[0] for position in range(len(batch))]
        for position in range(len(batch)):
            views.append((len(arrays), sum(rows[:position]), rows[position], sum(rows)))
        arrays.append(quad_swap(message))
    return arrays, views


def settle(value, *others):
    flat, tree = jax.tree.flatten((value, others))
    return jax.tree.unflatten(tree, lax.optimization_barrier(flat))


def unit_width():
    return 4 * D // share_count()


def wide_for(*parts):
    unit = unit_width()

    def make(place):
        start = place * unit % sum(part.shape[1] for part in parts)
        for part in parts:
            if start < part.shape[1]:
                return (part, start, False)
            start = start - part.shape[1]

    return make


def narrow_for(choices):
    unit = unit_width()
    return lambda place: (choices[min(place * unit // D, len(choices) - 1)], 0, True)


def product_of(share, arrays, narrow, wide):
    total = None
    for place in range(share):
        rows = []
        for which, offset, count, step in (narrow, wide):
            start = place * step + offset
            rows.append(arrays[which][start : start + count, :])
        part = tmatmul(*rows)
        total = part if total is None else total + part
    return total


def products_body(share, pairs, stepped, *refs):
    *arrays, output = refs
    unit = output.shape[1] if stepped else output.shape[1] // len(pairs)
    for position, (narrow, wide) in enumerate(pairs):
        if stepped:

            @pl.when(pl.program_id(0) == position)
            def _():
                output[...] = product_of(share, arrays, narrow, wide)

        else:
            output[:, position * unit : (position + 1) * unit] = product_of(
                share, arrays, narrow, wide
            )


def products(pairs, arrays, stepped):
    share, unit = share_count(), unit_width()
    count = len(pairs)
    body = functools.partial(products_body, share, pairs, stepped)
    shape = jax.ShapeDtypeStruct((D, count * unit), jnp.float32)
    params = pltpu.CompilerParams(vmem_limit_bytes=56 << 20)
    if not stepped:
        return pl.pallas_call(
            body, out_shape=shape, cost_estimate=estimate(11), compiler_params=params
        )(*arrays)
    return pl.pallas_call(
        body,
        grid=(count,),
        out_shape=shape,
        in_specs=[fixed(held.shape) for held in arrays],
        out_specs=pl.BlockSpec((D, unit), lambda step: (0, step)),
        cost_estimate=estimate(10),
        compiler_params=params,
    )(*arrays)


def shifted(view, by):
    return (view[0] + by,) + view[1:]


def quad_rows(by_core):
    reps = lax.axis_size("rep")
    message = jnp.concatenate([by_core] * reps, axis=0)
    swapped = quad_swap(message.reshape(-1, by_core.shape[2]))
    return swapped.reshape(message.shape)


def scatter_body(cored, count, values, output, *scratch):
    reps, line, side, cores = mesh_shape()
    rep, far, near, core = places()
    members = line * side * cores
    if cored:
        core_in, core_sum = scratch[:2]
        scratch = scratch[2:]
    near_in, near_sum, far_in, leaving, landing = scratch
    wide = output.shape[-1] // count

    def at(far_to, near_to, core_to):
        return {"fsdp": (far_to * side + near_to) * cores + core_to}

    barrier = pltpu.get_barrier_semaphore()
    partners = [at(lax.rem(far + step, line), near, core) for step in range(1, line)]
    partners += [at(far, lax.rem(near + step, side), core) for step in range(1, side)]
    if cored:
        partners.append(at(far, near, 1 - core))
    for partner in partners:
        pl.semaphore_signal(barrier, inc=1, device_id=partner)
    pl.semaphore_wait(barrier, len(partners))

    started = []

    def start(source, target, device):
        slot = len(started)
        copy = pltpu.make_async_remote_copy(
            src_ref=source,
            dst_ref=target,
            send_sem=leaving.at[slot],
            recv_sem=landing.at[slot],
            device_id=device,
        )
        copy.start()
        started.append(copy)
        return copy

    spans = [pl.ds(part * wide, wide) for part in range(count)]
    core_moves = []
    if cored:
        for part in range(count):
            core_moves.append(
                start(
                    values.at[:, :, 1 - core, :, spans[part]],
                    core_in.at[part],
                    at(far, near, 1 - core),
                )
            )
    near_moves = []
    for part in range(count):
        if cored:
            core_moves[part].wait_recv()
            core_sum[part] = values[:, :, core, :, spans[part]] + core_in[part]
        moves = []
        for step in range(1, side):
            there = lax.rem(near + step, side)
            source = core_sum.at[part, :, there] if cored else values.at[:, there, :, spans[part]]
            moves.append(start(source, near_in.at[part, step - 1], at(far, there, core)))
        near_moves.append(moves)
    far_moves = []
    for part in range(count):
        total = core_sum[part, :, near] if cored else values[:, near, :, spans[part]]
        for step, move in enumerate(near_moves[part]):
            move.wait_recv()
            total = total + near_in[part, step]
        near_sum[part] = total
        moves = []
        for step in range(1, line):
            there = lax.rem(far + step, line)
            moves.append(
                start(near_sum.at[part, there], far_in.at[part, step - 1], at(there, near, core))
            )
        far_moves.append(moves)
    for part in range(count):
        total = near_sum[part, far]
        for step, move in enumerate(far_moves[part]):
            move.wait_recv()
            total = total + far_in[part, step]
        output[:, spans[part]] = total
    for move in started:
        move.wait_send()


def scatter_sum(values, count, cored, tag):
    reps, line, side, cores = mesh_shape()
    rows = values.shape[0] // (line * side * (cores if cored else 1))
    width = values.shape[1]
    wide = width // count
    kind = values.dtype
    shape = (line, side) + ((cores,) if cored else ()) + (rows, width)
    copies = count * ((1 if cored else 0) + (side - 1) + (line - 1))
    cube = (count, line, side, rows, wide)
    scratch = [pltpu.VMEM(cube, kind), pltpu.VMEM(cube, kind)] if cored else []
    scratch += [
        pltpu.VMEM((count, side - 1, line, rows, wide), kind),
        pltpu.VMEM((count, line, rows, wide), kind),
        pltpu.VMEM((count, line - 1, rows, wide), kind),
        pltpu.SemaphoreType.DMA((copies,)),
        pltpu.SemaphoreType.DMA((copies,)),
    ]
    return pl.pallas_call(
        functools.partial(scatter_body, cored, count),
        out_shape=jax.ShapeDtypeStruct((rows, width), kind),
        in_specs=[pl.BlockSpec(memory_space=pltpu.VMEM)],
        out_specs=pl.BlockSpec(memory_space=pltpu.VMEM),
        scratch_shapes=scratch,
        cost_estimate=estimate(45),
        compiler_params=pltpu.CompilerParams(
            collective_id=tag, has_side_effects=True, vmem_limit_bytes=60 << 20
        ),
    )(values.reshape(shape))


def rows_body(pieces, count, *refs):
    reps, line, side, cores = mesh_shape()
    rep, far, near, core = places()
    total = len(pieces)
    values, outputs = refs[:count], refs[count : 2 * count]
    rest = refs[2 * count :]
    near_in, near_sum = rest[:total], rest[total : 2 * total]
    far_in, far_sum = rest[2 * total : 3 * total], rest[3 * total : 4 * total]
    leaving, landing = rest[4 * total :]
    place = rep * cores + core

    def at(rep_to, far_to, near_to, core_to):
        return {"rep": rep_to, "fsdp": (far_to * side + near_to) * cores + core_to}

    moves = [(turn, flip) for turn in range(reps) for flip in range(cores) if turn or flip]
    quad = [
        at(lax.rem(rep + turn, reps), far, near, 1 - core if flip else core)
        for turn, flip in moves
    ]
    line_peers = [at(rep, lax.rem(far + step, line), near, core) for step in range(1, line)]
    side_peers = [at(rep, far, lax.rem(near + step, side), core) for step in range(1, side)]
    barrier = pltpu.get_barrier_semaphore()
    for partner in line_peers + side_peers + quad:
        pl.semaphore_signal(barrier, inc=1, device_id=partner)
    pl.semaphore_wait(barrier, len(line_peers + side_peers + quad))

    started = []

    def start(source, target, device):
        slot = len(started)
        copy = pltpu.make_async_remote_copy(
            src_ref=source,
            dst_ref=target,
            send_sem=leaving.at[slot],
            recv_sem=landing.at[slot],
            device_id=device,
        )
        copy.start()
        started.append(copy)
        return copy

    near_moves = []
    for piece, (part, span) in enumerate(pieces):
        near_moves.append(
            [
                start(
                    values[part].at[:, lax.rem(near + step, side), :, span],
                    near_in[piece].at[step - 1],
                    side_peers[step - 1],
                )
                for step in range(1, side)
            ]
        )
    far_moves = []
    last_moves = []

    def finish(piece):
        part, span = pieces[piece]
        summed = near_sum[piece][far]
        for step, move in enumerate(far_moves[piece]):
            move.wait_recv()
            summed = summed + far_in[piece][step]
        far_sum[piece][...] = summed.reshape(far_sum[piece].shape)
        outputs[part][place, :, span] = far_sum[piece][core]
        for (turn, flip), device in zip(moves, quad):
            last_moves.append(
                start(
                    far_sum[piece].at[1 - core if flip else core],
                    outputs[part].at[place, :, span],
                    device,
                )
            )

    lag = 2
    for piece, (part, span) in enumerate(pieces):
        summed = values[part][:, near, :, span]
        for step, move in enumerate(near_moves[piece]):
            move.wait_recv()
            summed = summed + near_in[piece][step]
        near_sum[piece][...] = summed
        far_moves.append(
            [
                start(
                    near_sum[piece].at[lax.rem(far + step, line)],
                    far_in[piece].at[step - 1],
                    line_peers[step - 1],
                )
                for step in range(1, line)
            ]
        )
        if piece >= lag:
            finish(piece - lag)
    for piece in range(max(total - lag, 0), total):
        finish(piece)
    for move in last_moves:
        move.wait_recv()
    for move in started:
        move.wait_send()


def rows_of(parts, tag):
    reps, line, side, cores = mesh_shape()
    count = len(parts)
    rows = parts[0].shape[0] // (line * side)
    own = rows // cores
    widths = [part.shape[1] for part in parts]
    pieces = []
    for part, width in enumerate(widths):
        offset = 0
        while offset < width:
            size = min(256, width - offset)
            pieces.append((part, pl.ds(offset, size)))
            offset = offset + size
    sizes = [span.size for _, span in pieces]
    copies = len(pieces) * (side - 1 + line - 1 + reps * cores - 1)
    near_in = [pltpu.VMEM((side - 1, line, rows, size), jnp.float32) for size in sizes]
    near_sum = [pltpu.VMEM((line, rows, size), jnp.float32) for size in sizes]
    far_in = [pltpu.VMEM((line - 1, rows, size), jnp.float32) for size in sizes]
    far_sum = [pltpu.VMEM((cores, own, size), jnp.float32) for size in sizes]
    return pl.pallas_call(
        functools.partial(rows_body, pieces, count),
        out_shape=[
            jax.ShapeDtypeStruct((reps * cores, own, width), jnp.float32) for width in widths
        ],
        in_specs=[pl.BlockSpec(memory_space=pltpu.VMEM)] * count,
        out_specs=[pl.BlockSpec(memory_space=pltpu.VMEM)] * count,
        scratch_shapes=near_in
        + near_sum
        + far_in
        + far_sum
        + [pltpu.SemaphoreType.DMA((copies,)), pltpu.SemaphoreType.DMA((copies,))],
        cost_estimate=estimate(130),
        compiler_params=pltpu.CompilerParams(
            collective_id=tag, has_side_effects=True, vmem_limit_bytes=60 << 20
        ),
    )(*[part.reshape(line, side, rows, part.shape[1]) for part in parts])


def pack_body(*refs):
    *sources, packed = refs
    offset = 0
    for source in sources:
        if len(source.shape) == 1:
            packed[offset : offset + 1, :] = source[...].reshape(1, source.shape[0])
            offset = offset + 1
        else:
            packed[offset : offset + source.shape[0], :] = source[...]
            offset = offset + source.shape[0]
    packed[offset:, :] = jnp.zeros((packed.shape[0] - offset, packed.shape[1]), jnp.float32)


def packed_rows(sources, rows):
    return pl.pallas_call(
        pack_body,
        out_shape=jax.ShapeDtypeStruct((rows, D), jnp.float32),
        compiler_params=pltpu.CompilerParams(vmem_limit_bytes=32 << 20),
    )(*sources)


def moment_part(scalars, held, moment, square, raw):
    scaled = raw * scalars[0]
    new_moment = BETA_ONE * moment + (1.0 - BETA_ONE) * scaled
    new_square = BETA_TWO * square + (1.0 - BETA_TWO) * scaled * scaled
    update = (
        new_moment * scalars[1] / (jnp.sqrt(new_square * scalars[2]) + ADAM_EPS) + DECAY * held
    )
    held_sum = jnp.sum(held * held, axis=0, keepdims=True)
    return (new_moment, new_square, update, held_sum, jnp.sum(update * update, axis=0, keepdims=True))


def embed_body(
    scalars, weight, moment, square, head, lookup, moment_out, square_out, update_out, sums
):
    moment_out[...], square_out[...], update_out[...], held_sum, update_sum = moment_part(
        scalars, weight[...], moment[...], square[...], head[...] + lookup[...]
    )
    sums[0, 0:1, :] = held_sum
    sums[0, 1:2, :] = update_sum


def moment_estimate(weight):
    return pl.CostEstimate(
        flops=20 * weight.size, bytes_accessed=28 * weight.size, transcendentals=0
    )


def embed_moments(scalars, weight, moment, square, head, lookup):
    rows, columns = weight.shape
    spec = by_step(rows // VOCAB_STEPS, columns)
    shape = jax.ShapeDtypeStruct(weight.shape, jnp.float32)
    return pl.pallas_call(
        embed_body,
        grid=(VOCAB_STEPS,),
        out_shape=[shape] * 3 + [jax.ShapeDtypeStruct((VOCAB_STEPS, 2, columns), jnp.float32)],
        in_specs=[pl.BlockSpec(memory_space=pltpu.SMEM)] + [spec] * 5,
        out_specs=[spec] * 3 + [pl.BlockSpec((1, 2, columns), lambda step: (step, 0, 0))],
        cost_estimate=moment_estimate(weight),
        compiler_params=pltpu.CompilerParams(vmem_limit_bytes=48 << 20),
    )(scalars, weight, moment, square, head, lookup)


def matrix_body(
    scalars, weight, moment, square, enc, dec, last, moment_out, square_out, update_out, sums
):
    share, unit = enc.shape[0], enc.shape[2]
    per = D // unit
    turned = list(range(per, share)) + list(range(per))
    plain = list(range(share))
    crossed = plain[:per] + plain[2 * per :] + plain[per : 2 * per]
    orders = [turned, plain, plain, turned, crossed, plain, plain, plain[: 3 * per] + [None]]
    for step, order in enumerate(orders):
        source = dec if 3 <= step < 7 else enc

        @pl.when(pl.program_id(0) == step)
        def _():
            for part, place in enumerate(order):
                span = slice(part * unit, (part + 1) * unit)
                raw = last[...] if place is None else source[place]
                results = moment_part(
                    scalars, weight[:, span], moment[:, span], square[:, span], raw
                )
                moment_out[:, span], square_out[:, span], update_out[:, span] = results[:3]
                sums[0, 0:1, span] = results[3]
                sums[0, 1:2, span] = results[4]


def matrix_moments(scalars, weight, moment, square, enc, dec, last):
    rows, columns = weight.shape
    share, unit = share_count(), unit_width()
    spec = pl.BlockSpec((rows, 4 * D), lambda step: (0, step))

    def enc_place(step):
        return (0, 0, jnp.where(step < 3, 2 - step, 3))

    def dec_place(step):
        return (0, 0, jnp.where(step < 4, 2, jnp.where(step == 4, 3, jnp.where(step == 5, 1, 0))))

    shape = jax.ShapeDtypeStruct(weight.shape, jnp.float32)
    return pl.pallas_call(
        matrix_body,
        grid=(8,),
        out_shape=[shape] * 3 + [jax.ShapeDtypeStruct((8, 2, 4 * D), jnp.float32)],
        in_specs=[
            pl.BlockSpec(memory_space=pltpu.SMEM),
            spec,
            spec,
            spec,
            pl.BlockSpec((share, rows, unit), enc_place),
            pl.BlockSpec((share, rows, unit), dec_place),
            fixed(last.shape),
        ],
        out_specs=[spec] * 3 + [pl.BlockSpec((1, 2, 4 * D), lambda step: (step, 0, 0))],
        cost_estimate=moment_estimate(weight),
        compiler_params=pltpu.CompilerParams(vmem_limit_bytes=48 << 20),
    )(scalars, weight, moment, square, enc, dec, last)


def gather_body(everyone, values, gathered, leaving, landing):
    members = lax.axis_size("fsdp")
    reps = lax.axis_size("rep") if everyone else 1
    rep, member = lax.axis_index("rep"), lax.axis_index("fsdp")
    peers = []
    for turn in range(reps):
        for shift in range(members):
            if turn or shift:
                device = {"fsdp": lax.rem(member + shift, members)}
                if everyone:
                    device["rep"] = lax.rem(rep + turn, reps)
                peers.append(device)
    here = rep * members + member if everyone else member
    barrier = pltpu.get_barrier_semaphore()
    for peer in peers:
        pl.semaphore_signal(barrier, inc=1, device_id=peer)
    pl.semaphore_wait(barrier, len(peers))
    copies = []
    for slot, peer in enumerate(peers):
        copies.append(
            pltpu.make_async_remote_copy(
                src_ref=values,
                dst_ref=gathered.at[here],
                send_sem=leaving.at[slot],
                recv_sem=landing.at[slot],
                device_id=peer,
            )
        )
        copies[-1].start()
    gathered[here] = values[...]
    for copy in copies:
        copy.wait()


def gather_small(values, tag, everyone=False):
    count = lax.axis_size("fsdp") * (lax.axis_size("rep") if everyone else 1)
    return pl.pallas_call(
        functools.partial(gather_body, everyone),
        out_shape=jax.ShapeDtypeStruct((count,) + values.shape, values.dtype),
        in_specs=[pl.BlockSpec(memory_space=pltpu.VMEM)],
        out_specs=pl.BlockSpec(memory_space=pltpu.VMEM),
        scratch_shapes=[
            pltpu.SemaphoreType.DMA((count - 1,)),
            pltpu.SemaphoreType.DMA((count - 1,)),
        ],
        cost_estimate=estimate(8),
        compiler_params=pltpu.CompilerParams(collective_id=tag, has_side_effects=True),
    )(values)


def total_of(values, tag, everyone=False):
    rows, columns = values.shape
    padded = jnp.pad(values, ((0, 8 - rows), (0, 128 - columns)))
    return jnp.sum(gather_small(padded, tag, everyone), axis=0)[:rows, :columns]


def rows_gather_body(values, gathered, leaving, landing):
    reps, line, side, cores = mesh_shape()
    rep, far, near, core = places()

    def at(far_to, near_to, core_to):
        return {"fsdp": (far_to * side + near_to) * cores + core_to}

    line_peers = [at(lax.rem(far + step, line), near, core) for step in range(1, line)]
    side_peers = [at(far, lax.rem(near + step, side), core) for step in range(1, side)]
    twin = at(far, near, 1 - core)
    barrier = pltpu.get_barrier_semaphore()
    for partner in line_peers + side_peers + [twin]:
        pl.semaphore_signal(barrier, inc=1, device_id=partner)
    pl.semaphore_wait(barrier, len(line_peers + side_peers) + 1)
    started = []

    def start(source, target, device):
        slot = len(started)
        copy = pltpu.make_async_remote_copy(
            src_ref=source,
            dst_ref=target,
            send_sem=leaving.at[slot],
            recv_sem=landing.at[slot],
            device_id=device,
        )
        copy.start()
        started.append(copy)
        return copy

    line_moves, side_moves, core_moves = [], [], []
    for step in range(1, line):
        line_moves.append(start(values, gathered.at[far, near, core], line_peers[step - 1]))

    def pass_on(step):
        origin = lax.rem(far - step + line, line)
        held = values if step == 0 else gathered.at[origin, near, core]
        for turn in range(1, side):
            side_moves.append(
                (step, turn, start(held, gathered.at[origin, near, core], side_peers[turn - 1]))
            )
        core_moves.append(start(held, gathered.at[origin, near, core], twin))

    pass_on(0)
    gathered[far, near, core] = values[...]
    for step in range(1, line):
        line_moves[step - 1].wait_recv()
        pass_on(step)
    for step, turn, move in list(side_moves):
        move.wait_recv()
        origin = lax.rem(far - step + line, line)
        beside = lax.rem(near - turn + side, side)
        held = gathered.at[origin, beside, core]
        core_moves.append(start(held, gathered.at[origin, beside, core], twin))
    for move in core_moves:
        move.wait_recv()
    for move in started:
        move.wait_send()


def gather_rows(values, tag):
    reps, line, side, cores = mesh_shape()
    copies = line - 1 + line * (side - 1) + line * side
    shape = (line, side, cores) + values.shape
    return pl.pallas_call(
        rows_gather_body,
        out_shape=jax.ShapeDtypeStruct(shape, values.dtype),
        in_specs=[pl.BlockSpec(memory_space=pltpu.VMEM)],
        out_specs=pl.BlockSpec(memory_space=pltpu.VMEM),
        scratch_shapes=[pltpu.SemaphoreType.DMA((copies,)), pltpu.SemaphoreType.DMA((copies,))],
        cost_estimate=estimate(26),
        compiler_params=pltpu.CompilerParams(
            collective_id=tag, has_side_effects=True, vmem_limit_bytes=32 << 20
        ),
    )(values).reshape(-1, values.shape[1])


VOCAB_STEPS = 7
TOKEN_SPAN = 512


def fixed(shape):
    return pl.BlockSpec(shape, lambda step: (0,) * len(shape), pipeline_mode=pl.Buffered(1))


def by_step(tall, wide):
    return pl.BlockSpec((tall, wide), lambda step: (step, 0))


def estimate(micros):
    return pl.CostEstimate(flops=0, bytes_accessed=micros * 3_600_000, transcendentals=0)


def token_spans(count):
    return [slice(start, start + TOKEN_SPAN) for start in range(0, count, TOKEN_SPAN)]


def stats_body(hidden, table, shut, keep, target, stats):
    step = pl.program_id(0)

    @pl.when(step == 0)
    def _():
        stats[0:1, :] = jnp.full((1, stats.shape[1]), NEG_BIG, jnp.float32)
        stats[1:, :] = jnp.zeros((stats.shape[0] - 1, stats.shape[1]), jnp.float32)

    tall = table.shape[0]
    part = table[...]
    row = lax.broadcasted_iota(jnp.int32, (tall, TOKEN_SPAN), 0) + step * tall
    for span in token_spans(stats.shape[1]):
        logits = matmul_t(part, hidden[span, :])
        masked = logits + shut[...]
        former = stats[0:1, span]
        top = jnp.maximum(former, jnp.max(masked, axis=0, keepdims=True))
        stats[1:2, span] = stats[1:2, span] * jnp.exp(former - top) + jnp.sum(
            jnp.exp(masked - top), axis=0, keepdims=True
        )
        stats[0:1, span] = top
        stats[2:3, span] += jnp.sum(
            jnp.where(row == target[:, span], logits, 0.0), axis=0, keepdims=True
        )
        stats[3:4, span] += jnp.sum(
            jnp.where(keep[...] > 0.0, logits, 0.0), axis=0, keepdims=True
        )


def vocab_stats(hidden, table, shut, keep, target):
    rows, vocab_rows = hidden.shape[0], table.shape[0]
    tall = vocab_rows // VOCAB_STEPS
    return pl.pallas_call(
        stats_body,
        grid=(VOCAB_STEPS,),
        out_shape=jax.ShapeDtypeStruct((4, rows), jnp.float32),
        in_specs=[
            fixed(hidden.shape),
            by_step(tall, D),
            by_step(tall, 1),
            by_step(tall, 1),
            fixed((1, rows)),
        ],
        out_specs=pl.BlockSpec((4, rows), lambda step: (0, 0)),
        cost_estimate=estimate(20),
        compiler_params=pltpu.CompilerParams(vmem_limit_bytes=60 << 20),
    )(hidden, table, shut, keep, target)


def slopes_into(slopes, hidden, table, shut, pull, target, log_norm):
    tall = table.shape[0]
    part = table[...]
    row = lax.broadcasted_iota(jnp.int32, (tall, TOKEN_SPAN), 0) + pl.program_id(0) * tall
    for span in token_spans(slopes.shape[1]):
        logits = matmul_t(part, hidden[span, :])
        soft = jnp.exp((logits - log_norm[:, span]) + shut[...])
        hits = jnp.where(row == target[:, span], 1.0 - SMOOTH, 0.0)
        slopes[:, span] = to_half(soft - hits - pull[...])


def own_body(
    hidden, table, shut, pull, target, log_norm, counted, table_grad, hidden_grad, slopes, total
):
    step = pl.program_id(0)
    slopes_into(slopes, hidden, table, shut, pull, target, log_norm)
    table_grad[...] = matmul(slopes[...], hidden[...])
    part = tmatmul(table[...], slopes[...])

    @pl.when(step == 0)
    def _():
        total[...] = part

    @pl.when(step > 0)
    def _():
        total[...] += part

    @pl.when(step == VOCAB_STEPS - 1)
    def _():
        hidden_grad[...] = jnp.where(counted[...] > 0.0, total[...], 0.0).T


def own_slopes(hidden, table, shut, pull, target, log_norm, counted):
    rows, vocab_rows = hidden.shape[0], table.shape[0]
    tall = vocab_rows // VOCAB_STEPS
    flat = fixed((1, rows))
    column = by_step(tall, 1)
    return pl.pallas_call(
        own_body,
        grid=(VOCAB_STEPS,),
        out_shape=[
            jax.ShapeDtypeStruct((vocab_rows, D), jnp.float32),
            jax.ShapeDtypeStruct((rows, D), jnp.float32),
        ],
        in_specs=[fixed(hidden.shape), by_step(tall, D), column, column, flat, flat, flat],
        out_specs=[by_step(tall, D), fixed((rows, D))],
        scratch_shapes=[pltpu.VMEM((tall, rows), jnp.bfloat16), pltpu.VMEM((D, rows), jnp.float32)],
        cost_estimate=estimate(46),
        compiler_params=pltpu.CompilerParams(vmem_limit_bytes=60 << 20),
    )(hidden, table, shut, pull, target, log_norm, counted)


def other_body(hidden, table, shut, pull, target, log_norm, former, table_grad, slopes):
    slopes_into(slopes, hidden, table, shut, pull, target, log_norm)
    table_grad[...] = former[...] + matmul(slopes[...], hidden[...])


def other_slopes(former, hidden, table, shut, pull, target, log_norm):
    rows, vocab_rows = hidden.shape[0], table.shape[0]
    tall = vocab_rows // VOCAB_STEPS
    flat = fixed((1, rows))
    column = by_step(tall, 1)
    return pl.pallas_call(
        other_body,
        grid=(VOCAB_STEPS,),
        out_shape=jax.ShapeDtypeStruct((vocab_rows, D), jnp.float32),
        in_specs=[
            fixed(hidden.shape),
            by_step(tall, D),
            column,
            column,
            flat,
            flat,
            by_step(tall, D),
        ],
        out_specs=by_step(tall, D),
        scratch_shapes=[pltpu.VMEM((tall, rows), jnp.bfloat16)],
        cost_estimate=estimate(27),
        compiler_params=pltpu.CompilerParams(vmem_limit_bytes=60 << 20),
    )(hidden, table, shut, pull, target, log_norm, former)


def reps_body(count, *refs):
    sources, gathered = refs[:count], refs[count : 2 * count]
    leaving, landing = refs[2 * count :]
    reps = lax.axis_size("rep")
    here = lax.axis_index("rep")
    peers = [{"rep": lax.rem(here + turn, reps)} for turn in range(1, reps)]
    barrier = pltpu.get_barrier_semaphore()
    for peer in peers:
        pl.semaphore_signal(barrier, inc=1, device_id=peer)
    pl.semaphore_wait(barrier, len(peers))
    copies = []
    for source, target in zip(sources, gathered):
        for peer in peers:
            copies.append(
                pltpu.make_async_remote_copy(
                    src_ref=source,
                    dst_ref=target.at[here],
                    send_sem=leaving.at[len(copies)],
                    recv_sem=landing.at[len(copies)],
                    device_id=peer,
                )
            )
            copies[-1].start()
        target[here] = source[...]
    for copy in copies:
        copy.wait()


def gather_reps(sources, tag):
    reps = lax.axis_size("rep")
    count = len(sources)
    copies = count * (reps - 1)
    return pl.pallas_call(
        functools.partial(reps_body, count),
        out_shape=[
            jax.ShapeDtypeStruct((reps,) + source.shape, source.dtype) for source in sources
        ],
        in_specs=[pl.BlockSpec(memory_space=pltpu.VMEM)] * count,
        out_specs=[pl.BlockSpec(memory_space=pltpu.VMEM)] * count,
        scratch_shapes=[pltpu.SemaphoreType.DMA((copies,)), pltpu.SemaphoreType.DMA((copies,))],
        cost_estimate=estimate(6),
        compiler_params=pltpu.CompilerParams(
            collective_id=tag, has_side_effects=True, vmem_limit_bytes=24 << 20
        ),
    )(*sources)


def join_body(values, joined, gathered, leaving, landing):
    gather_body(False, values, gathered, leaving, landing)
    members = lax.axis_size("fsdp")
    top = gathered[0, 0:1, :]
    for place in range(1, members):
        top = jnp.maximum(top, gathered[place, 0:1, :])
    total = jnp.zeros_like(top)
    target = jnp.zeros_like(top)
    whole = jnp.zeros_like(top)
    for place in range(members):
        total = total + gathered[place, 1:2, :] * jnp.exp(gathered[place, 0:1, :] - top)
        target = target + gathered[place, 2:3, :]
        whole = whole + gathered[place, 3:4, :]
    joined[0:1, :] = top + jnp.log(total)
    joined[1:2, :] = target
    joined[2:3, :] = whole


def join_stats(values, tag):
    count = lax.axis_size("fsdp")
    return pl.pallas_call(
        join_body,
        out_shape=jax.ShapeDtypeStruct((3, values.shape[1]), values.dtype),
        in_specs=[pl.BlockSpec(memory_space=pltpu.VMEM)],
        out_specs=pl.BlockSpec(memory_space=pltpu.VMEM),
        scratch_shapes=[
            pltpu.VMEM((count,) + values.shape, values.dtype),
            pltpu.SemaphoreType.DMA((count - 1,)),
            pltpu.SemaphoreType.DMA((count - 1,)),
        ],
        cost_estimate=estimate(8),
        compiler_params=pltpu.CompilerParams(collective_id=tag, has_side_effects=True),
    )(values)


def layout(width, hidden, mels, text_len):
    names = (
        "eq",
        "eo",
        "eu",
        "ed",
        "dq",
        "do",
        "xq",
        "xk",
        "xo",
        "du",
        "dd",
        "c2",
        "c1",
        "dp",
    )
    widths = (
        3 * width,
        width,
        hidden,
        hidden,
        3 * width,
        width,
        width,
        2 * width,
        width,
        hidden,
        hidden,
        3 * width,
        3 * mels,
        text_len,
    )
    bounds = {}
    offset = 0
    for piece_name, extent in zip(names, widths):
        bounds[piece_name] = (offset, offset + extent)
        offset = offset + extent
    return (names, bounds)


def columns_of(weights, bounds, piece_name):
    span_start, span_stop = bounds[piece_name]
    return weights[:, span_start:span_stop]


def sinusoid(length, width):
    halfway = width // 2
    increment = jnp.log(10000.0) / (halfway - 1)
    rates = jnp.exp(-increment * jnp.arange(halfway, dtype=jnp.float32))
    angles = jnp.arange(length, dtype=jnp.float32)[:, None] * rates[None, :]
    return jnp.concatenate([jnp.sin(angles), jnp.cos(angles)], axis=1)


def layer_norm(inputs, gain, offset):
    average = jnp.mean(inputs, axis=-1, keepdims=True)
    centred = inputs - average
    spread = jnp.mean(centred * centred, axis=-1, keepdims=True)
    return centred * lax.rsqrt(spread + LN_EPS) * gain + offset


def norm_back(inputs, gain, offset, upstream):
    _, pull = jax.vjp(layer_norm, inputs, gain, offset)
    return pull(upstream)


def gelu_exact(values):
    return jax.nn.gelu(values, approximate=False)


def gelu_back(values, upstream):
    _, pull = jax.vjp(gelu_exact, values)
    return pull(upstream)[0]


def to_half(values):
    return values.astype(jnp.bfloat16)


def matmul(left, right):
    return jnp.dot(left, right, preferred_element_type=jnp.float32)


def matmul_t(left, right):
    return lax.dot_general(
        left, right, (((1,), (1,)), ((), ())), preferred_element_type=jnp.float32
    )


def tmatmul(left, right):
    return lax.dot_general(
        left, right, (((0,), (0,)), ((), ())), preferred_element_type=jnp.float32
    )


def head_pairs(width):
    lane = lax.broadcasted_iota(jnp.int32, (1, 2 * HD), 1)
    masks = [lane < HD, lane >= HD]
    return [(slice(start, start + 2 * HD), masks) for start in range(0, width, 2 * HD)]


def masked_half(values, mask):
    return jnp.where(mask, values, jnp.bfloat16(0.0))


def soft_rows(query_part, key_part, causal):
    scores = matmul_t(query_part, key_part) * HD ** (-0.5)
    if causal:
        rows = lax.broadcasted_iota(jnp.int32, scores.shape, 0)
        cols = lax.broadcasted_iota(jnp.int32, scores.shape, 1)
        scores = jnp.where(rows >= cols, scores, NEG_BIG)
    row_top = jnp.max(scores, axis=-1, keepdims=True)
    log_total = row_top + jnp.log(jnp.sum(jnp.exp(scores - row_top), axis=-1, keepdims=True))
    return jnp.exp(scores - log_total)


def attend_body(causal, queries, keys, values, attended):
    for span, masks in head_pairs(queries.shape[1]):
        query_pair, key_pair, value_pair = queries[:, span], keys[:, span], values[:, span]
        total = None
        for mask in masks:
            soft = soft_rows(masked_half(query_pair, mask), key_pair, causal)
            part = matmul(to_half(soft), masked_half(value_pair, mask))
            total = part if total is None else total + part
        attended[:, span] = to_half(total)


def attend(queries, keys_half, values_half, causal):
    return pl.pallas_call(
        functools.partial(attend_body, causal),
        out_shape=jax.ShapeDtypeStruct(queries.shape, jnp.bfloat16),
        cost_estimate=estimate(6),
        compiler_params=pltpu.CompilerParams(vmem_limit_bytes=32 << 20),
    )(queries, keys_half, values_half)


def attend_back_body(causal, queries, keys, values, upstream, grad_query, grad_key, grad_value, sums):
    for span, masks in head_pairs(queries.shape[1]):
        query_pair, key_pair, value_pair = queries[:, span], keys[:, span], values[:, span]
        up_pair = upstream[:, span]
        totals = None
        for mask in masks:
            query_part, up_part = masked_half(query_pair, mask), masked_half(up_pair, mask)
            soft = soft_rows(query_part, key_pair, causal)
            back_soft = matmul_t(up_part, value_pair)
            inner = jnp.sum(soft * back_soft, axis=-1, keepdims=True)
            back_scores = to_half(soft * (back_soft - inner) * HD ** (-0.5))
            parts = (
                matmul(back_scores, masked_half(key_pair, mask)),
                tmatmul(back_scores, query_part),
                tmatmul(to_half(soft), up_part),
            )
            totals = parts if totals is None else [x + y for x, y in zip(totals, parts)]
        grad_query[:, span] = to_half(totals[0])
        grad_key[:, span] = to_half(totals[1])
        grad_value[:, span] = to_half(totals[2])
        sums[0:1, span] = jnp.sum(totals[0], axis=0, keepdims=True)
        sums[1:2, span] = jnp.sum(totals[2], axis=0, keepdims=True)


def attend_back(queries, keys_half, values_half, causal, back_attended):
    half = [
        jax.ShapeDtypeStruct(part.shape, jnp.bfloat16)
        for part in (queries, keys_half, values_half)
    ]
    return pl.pallas_call(
        functools.partial(attend_back_body, causal),
        out_shape=half + [jax.ShapeDtypeStruct((2, queries.shape[1]), jnp.float32)],
        cost_estimate=estimate(12),
        compiler_params=pltpu.CompilerParams(vmem_limit_bytes=32 << 20),
    )(queries, keys_half, values_half, back_attended)


def self_block(stream, weights, small_params, slots, qkv_name, out_name, causal):
    normed = layer_norm(
        stream, small_params[:, slots.norm_gain], small_params[:, slots.norm_bias]
    )
    normed_half = to_half(normed)
    projected = matmul(normed_half, weights[qkv_name])
    queries = to_half(projected[:, :D] + small_params[:, slots.query_bias])
    keys_half = to_half(projected[:, D : 2 * D])
    values_half = to_half(projected[:, 2 * D :] + small_params[:, slots.value_bias])
    attended = attend(queries, keys_half, values_half, causal)
    output = (
        stream + matmul(attended, weights[out_name]) + small_params[:, slots.out_bias]
    )
    return (output, (stream, queries, keys_half, values_half), (normed_half, attended))


def self_block_back(
    saved, upstream, weights, small_params, slots, qkv_name, out_name, causal, vector_grads
):
    stream, queries, keys_half, values_half = saved
    grad_out = to_half(upstream)
    back_attended = to_half(matmul_t(grad_out, weights[out_name]))
    back_queries, back_keys, back_values, back_sums = attend_back(
        queries, keys_half, values_half, causal, back_attended
    )
    grad_proj = [back_queries, back_keys, back_values]
    back_normed = sum(
        matmul_t(part, weights[qkv_name][:, position * D : (position + 1) * D])
        for position, part in enumerate(grad_proj)
    )
    back_stream, back_gain, back_bias = norm_back(
        stream,
        small_params[:, slots.norm_gain],
        small_params[:, slots.norm_bias],
        back_normed,
    )
    vector_grads[slots.norm_gain] = back_gain
    vector_grads[slots.norm_bias] = back_bias
    vector_grads[slots.query_bias] = back_sums[0]
    vector_grads[slots.value_bias] = back_sums[1]
    vector_grads[slots.out_bias] = jnp.sum(upstream, axis=0)
    return (upstream + back_stream, grad_out, grad_proj)


def cross_block(stream, memory_half, weights, small_params):
    normed = layer_norm(
        stream, small_params[:, DecSlots.cross_gain], small_params[:, DecSlots.cross_bias]
    )
    normed_half = to_half(normed)
    queries = to_half(
        matmul(normed_half, weights["xq"]) + small_params[:, DecSlots.xquery_bias]
    )
    keyval = matmul(memory_half, weights["xk"])
    keys_half = to_half(keyval[:, :D])
    values_half = to_half(keyval[:, D:] + small_params[:, DecSlots.xvalue_bias])
    attended = attend(queries, keys_half, values_half, False)
    output = (
        stream + matmul(attended, weights["xo"]) + small_params[:, DecSlots.xout_bias]
    )
    return (output, (stream, queries, keys_half, values_half), (normed_half, attended))


def cross_block_back(saved, upstream, weights, small_params, vector_grads):
    stream, queries, keys_half, values_half = saved
    grad_out = to_half(upstream)
    back_attended = to_half(matmul_t(grad_out, weights["xo"]))
    grad_query, back_keys, back_values, back_sums = attend_back(
        queries, keys_half, values_half, False, back_attended
    )
    back_normed = matmul_t(grad_query, weights["xq"])
    grad_keyval = [back_keys, back_values]
    back_memory = matmul_t(back_keys, weights["xk"][:, :D]) + matmul_t(
        back_values, weights["xk"][:, D:]
    )
    back_stream, back_gain, back_bias = norm_back(
        stream,
        small_params[:, DecSlots.cross_gain],
        small_params[:, DecSlots.cross_bias],
        back_normed,
    )
    vector_grads[DecSlots.cross_gain] = back_gain
    vector_grads[DecSlots.cross_bias] = back_bias
    vector_grads[DecSlots.xquery_bias] = back_sums[0]
    vector_grads[DecSlots.xvalue_bias] = back_sums[1]
    vector_grads[DecSlots.xout_bias] = jnp.sum(upstream, axis=0)
    return (upstream + back_stream, back_memory, grad_out, grad_query, grad_keyval)


def mlp_block(stream, weights, small_params, slots, up_name, down_name):
    normed = layer_norm(
        stream, small_params[:, slots.mlp_gain], small_params[:, slots.mlp_bias]
    )
    normed_half = to_half(normed)
    up_bias = small_params[:, slots.up_bias : slots.up_bias + 4].T.reshape(-1)
    raised = matmul(normed_half, weights[up_name]) + up_bias
    active = to_half(gelu_exact(raised))
    output = (
        stream + matmul_t(active, weights[down_name]) + small_params[:, slots.down_bias]
    )
    return (output, (stream, raised), (normed_half, active))


def mlp_block_back(saved, upstream, weights, small_params, slots, up_name, down_name, vector_grads):
    stream, raised = saved
    grad_out = to_half(upstream)
    back_raised = gelu_back(raised, matmul(grad_out, weights[down_name]))
    bias_rows = jnp.sum(back_raised, axis=0).reshape(4, D)
    for quarter in range(4):
        vector_grads[slots.up_bias + quarter] = bias_rows[quarter]
    grad_raised = to_half(back_raised)
    back_normed = matmul_t(grad_raised, weights[up_name])
    back_stream, back_gain, back_bias = norm_back(
        stream, small_params[:, slots.mlp_gain], small_params[:, slots.mlp_bias], back_normed
    )
    vector_grads[slots.mlp_gain] = back_gain
    vector_grads[slots.mlp_bias] = back_bias
    vector_grads[slots.down_bias] = jnp.sum(upstream, axis=0)
    return (upstream + back_stream, grad_out, grad_raised)


def down_one(values):
    return jnp.pad(values, ((1, 0), (0, 0)))[:-1]


def up_one(values):
    return jnp.pad(values, ((0, 1), (0, 0)))[1:]


def stem_forward(mel_half, weights, small_params):
    bins, frames_in = mel_half.shape
    paired = mel_half.T.reshape(frames_in // 2, 2 * bins)
    mel_even, mel_odd = paired[:, :bins], paired[:, bins:]
    cols_even = jnp.concatenate([down_one(mel_odd), mel_even, mel_odd], axis=1)
    cols_odd = jnp.concatenate([mel_even, mel_odd, up_one(mel_even)], axis=1)
    pre_even = matmul_t(cols_even, weights["c1"]) + small_params[:, 0]
    pre_odd = matmul_t(cols_odd, weights["c1"]) + small_params[:, 0]
    act_even = to_half(gelu_exact(pre_even))
    act_odd = to_half(gelu_exact(pre_odd))
    taps = weights["c2"]
    conv_sum = (
        matmul(down_one(act_odd), taps[:, :D])
        + matmul(act_even, taps[:, D : 2 * D])
        + matmul(act_odd, taps[:, 2 * D :])
    )
    second_pre = conv_sum + small_params[:, 1]
    stream = gelu_exact(second_pre) + sinusoid(frames_in // 2, D)
    return (stream, (pre_even, pre_odd, second_pre), (cols_even, cols_odd, act_even, act_odd))


def stem_back(saved, upstream, weights, vector_grads):
    pre_even, pre_odd, second_pre = saved
    back_second = gelu_back(second_pre, upstream)
    vector_grads[1] = jnp.sum(back_second, axis=0)
    grad_second = to_half(back_second)
    taps = weights["c2"]
    back_even = gelu_back(pre_even, matmul_t(grad_second, taps[:, D : 2 * D]))
    back_odd = gelu_back(
        pre_odd,
        matmul_t(grad_second, taps[:, 2 * D :])
        + matmul_t(up_one(grad_second), taps[:, :D]),
    )
    vector_grads[0] = jnp.sum(back_even, axis=0) + jnp.sum(back_odd, axis=0)
    return (grad_second, to_half(back_even), to_half(back_odd))


def fill(values, rows):
    return jnp.pad(values, ((0, rows - values.shape[0]), (0, 0)))


def moments(weight, moment, square, gradient, factor, first_fix, second_fix):
    scaled = gradient * factor
    new_moment = BETA_ONE * moment + (1.0 - BETA_ONE) * scaled
    new_square = BETA_TWO * square + (1.0 - BETA_TWO) * scaled * scaled
    update = new_moment * first_fix / (jnp.sqrt(new_square * second_fix) + ADAM_EPS) + DECAY * weight
    return (new_moment, new_square, update)


def count_bad(values):
    return jnp.sum(jnp.where(jnp.isfinite(values), 0.0, 1.0))


def on_device(
    mel_frames,
    text_ids,
    text_lengths,
    language,
    vocab_mask,
    step_count,
    matrices,
    matrix_moment,
    matrix_square,
    embedding,
    embed_moment,
    embed_square,
    vectors,
    vector_moment,
    vector_square,
):
    names, bounds = layout(D, FF, MELS, TLEN)
    reps = lax.axis_size("rep")
    members = lax.axis_size("fsdp")
    replica = lax.axis_index("rep")
    member = lax.axis_index("fsdp")
    first_names = ("c1", "c2", "eq", "eo", "eu", "ed", "dp")
    last_names = ("dq", "do", "xq", "xk", "xo", "du", "dd")
    first_half = jnp.concatenate(
        [to_half(columns_of(matrices, bounds, piece)) for piece in first_names]
        + [to_half(vectors)],
        axis=1,
    )
    last_half = jnp.concatenate(
        [to_half(columns_of(matrices, bounds, piece)) for piece in last_names], axis=1
    )
    weights = {}
    for batch, batch_half in ((first_names, first_half), (last_names, last_half)):
        gathered = lax.all_gather(batch_half, "fsdp", axis=0, tiled=True)
        offset = 0
        for piece in batch:
            extent = bounds[piece][1] - bounds[piece][0]
            weights[piece] = gathered[:, offset : offset + extent]
            offset = offset + extent
        if batch is first_names:
            small_params = gathered[:, offset:].astype(jnp.float32)
    inputs_ids = jnp.concatenate([LANGTOK + language, text_ids[0, :-1]])[None, :]
    ids_all = lax.all_gather(
        jnp.concatenate([inputs_ids, text_ids], axis=1), ("rep", "fsdp"), axis=0, tiled=True
    ).reshape(reps, members, 2, TLEN)
    order = [(replica - shift) % reps for shift in range(reps)]
    ids_by_shift = [pick(ids_all, place, 0) for place in order]
    group_inputs = [ids[:, 0].reshape(-1) for ids in ids_by_shift]
    group_targets = [ids[:, 1].reshape(-1) for ids in ids_by_shift]
    counts_by_shift = [
        (
            lax.broadcasted_iota(jnp.int32, (members, TLEN), 1)
            < lax.dynamic_slice_in_dim(text_lengths, place * members, members)[:, None]
        ).reshape(-1)
        for place in order
    ]
    vocab_rows = embedding.shape[0]
    vocab_start = member * vocab_rows
    embed_half = to_half(embedding)
    vocab_iota = lax.broadcasted_iota(jnp.int32, (members * TLEN, vocab_rows), 1)
    input_hot = [to_half(ids[:, None] - vocab_start == vocab_iota) for ids in group_inputs]
    embedded = scatter_sum(
        matmul(input_hot[0], embed_half).astype(jnp.bfloat16), 3, True, 3
    ).astype(jnp.float32)
    enc_zero, stem_saved, stem_acts = stem_forward(mel_frames[0], weights, small_params)
    vocab_keep = lax.dynamic_slice_in_dim(vocab_mask, vocab_start, vocab_rows) == 1
    keep_column = vocab_keep.astype(jnp.float32)[:, None]
    shut_column = jnp.where(vocab_keep, 0.0, -jnp.inf)[:, None]
    vocab_count = jnp.sum(vocab_mask).astype(jnp.float32)
    pull_column = SMOOTH * keep_column / vocab_count
    local_targets = [(ids - vocab_start)[None, :] for ids in group_targets]
    groups_all = len(names) + 2
    columns = matrices.shape[1]
    column = lax.broadcasted_iota(jnp.int32, (groups_all, columns), 1)
    group = lax.broadcasted_iota(jnp.int32, (groups_all, columns), 0)
    group_of = sum((column >= bounds[piece][1]).astype(jnp.int32) for piece in names)
    in_group = group_of == group
    vectors, vector_moment, vector_square = vectors.T, vector_moment.T, vector_square.T
    counted_row = counts_by_shift[0].astype(jnp.float32)[None, :]
    enc_zero, (
        shut_column,
        keep_column,
        pull_column,
        local_targets,
        counted_row,
        in_group,
        vectors,
        vector_moment,
        vector_square,
    ) = settle(
        enc_zero,
        shut_column,
        keep_column,
        pull_column,
        local_targets,
        counted_row,
        in_group,
        vectors,
        vector_moment,
        vector_square,
    )
    enc_one, enc_self, enc_self_acts = self_block(
        enc_zero, weights, small_params, EncSlots, "eq", "eo", False
    )
    enc_two, enc_mlp, enc_mlp_acts = mlp_block(
        enc_one, weights, small_params, EncSlots, "eu", "ed"
    )
    memory_half = to_half(
        layer_norm(
            enc_two,
            small_params[:, EncSlots.final_gain],
            small_params[:, EncSlots.final_bias],
        )
    )
    cols_even, cols_odd, act_even, act_odd = stem_acts
    enc_early, enc_early_views = exchange(
        narrow_for([enc_self_acts[1], enc_self_acts[0]]),
        narrow_for([enc_mlp_acts[0]]),
        narrow_for([down_one(act_odd), act_even, act_odd]),
        wide_for(enc_mlp_acts[1]),
    )
    embedded, (enc_early,) = settle(embedded, enc_early)
    dec_zero = embedded + weights["dp"].T.astype(jnp.float32)
    dec_one, dec_self, dec_self_acts = self_block(
        dec_zero, weights, small_params, DecSlots, "dq", "do", True
    )
    dec_two, dec_cross, dec_cross_acts = cross_block(dec_one, memory_half, weights, small_params)
    dec_three, dec_mlp, dec_mlp_acts = mlp_block(
        dec_two, weights, small_params, DecSlots, "du", "dd"
    )
    frames = memory_half.shape[0]
    dec_early, dec_early_views = exchange(
        narrow_for([dec_self_acts[1], dec_self_acts[0]]),
        narrow_for([dec_mlp_acts[0]]),
        wide_for(dec_mlp_acts[1]),
        narrow_for(
            [fill(dec_cross_acts[0], frames), fill(dec_cross_acts[1], frames), memory_half]
        ),
    )
    final_out = layer_norm(
        dec_three,
        small_params[:, DecSlots.final_gain],
        small_params[:, DecSlots.final_bias],
    )
    final_half = to_half(final_out)
    gathered_hidden = gather_rows(final_half, 5)
    stats = join_stats(
        vocab_stats(gathered_hidden, embed_half, shut_column, keep_column, local_targets[0]), 0
    )
    log_norm, target_logit, logit_total = stats[0], stats[1], stats[2]
    log_norm, (dec_early,) = settle(log_norm, dec_early)
    entropy = log_norm - (1.0 - SMOOTH) * target_logit - SMOOTH * logit_total / vocab_count
    norm_and_loss = jnp.stack([log_norm, jnp.where(counts_by_shift[0], entropy, 0.0)])
    final_by_rep, norms_by_rep = gather_reps(
        [final_half, norm_and_loss], 7
    )
    norms_by_shift = [
        pick(norms_by_rep, place, 0) for place in order
    ]
    hidden_by_shift = [gathered_hidden] + [
        lax.all_gather(pick(final_by_rep, place, 0), "fsdp", axis=0, tiled=True)
        for place in order[1:]
    ]
    loss_sum = sum(jnp.sum(part[1]) for part in norms_by_shift)

    head_grad, hidden_part = own_slopes(
        jnp.where(counts_by_shift[0][:, None], gathered_hidden, jnp.bfloat16(0.0)),
        embed_half,
        shut_column,
        pull_column,
        local_targets[0],
        norms_by_shift[0][0:1],
        counted_row,
    )
    back_hidden = scatter_sum(hidden_part, 6, True, 6)
    vector_grads = {}
    back_three, final_gain, final_bias = norm_back(
        dec_three,
        small_params[:, DecSlots.final_gain],
        small_params[:, DecSlots.final_bias],
        back_hidden,
    )
    vector_grads[DecSlots.final_gain] = final_gain
    vector_grads[DecSlots.final_bias] = final_bias
    back_two, dec_down_grad, dec_up_grad = mlp_block_back(
        dec_mlp, back_three, weights, small_params, DecSlots, "du", "dd", vector_grads
    )
    back_two, (hidden_by_shift,) = settle(back_two, hidden_by_shift)
    back_one, back_memory, xout_grad, xquery_grad, xkeyval_grad = cross_block_back(
        dec_cross, back_two, weights, small_params, vector_grads
    )
    back_zero, dec_out_grad, dec_qkv_grad = self_block_back(
        dec_self, back_one, weights, small_params, DecSlots, "dq", "do", True, vector_grads
    )
    dec_late, dec_late_views = exchange(
        narrow_for([dec_down_grad]),
        wide_for(dec_up_grad),
        wide_for(dec_out_grad, *dec_qkv_grad),
        wide_for(fill(xquery_grad, frames), fill(xout_grad, frames), *xkeyval_grad),
    )
    unit = unit_width()
    share = 4 * D // unit
    cores = CORES
    groups = [list(range(place, members, cores)) for place in range(cores)]
    back_half = to_half(back_zero)
    (back_stack,) = gather_reps([back_half], 8)
    gathered_back = lax.all_gather(back_stack, "fsdp", axis=0)
    for shift in range(1, reps):
        head_grad = other_slopes(
            head_grad,
            jnp.where(counts_by_shift[shift][:, None], hidden_by_shift[shift], jnp.bfloat16(0.0)),
            embed_half,
            shut_column,
            pull_column,
            local_targets[shift],
            norms_by_shift[shift][0:1],
        )
    dec_late, (head_grad,) = settle(dec_late, head_grad)
    early = len(dec_early)
    attn_narrow, up_narrow, down_wide, cross_narrow = dec_early_views
    down_narrow, up_wide, attn_wide, cross_wide = [
        shifted(view, early) for view in dec_late_views
    ]
    dec_products = products(
        [
            (down_narrow, down_wide),
            (up_narrow, up_wide),
            (attn_narrow, attn_wide),
            (cross_narrow, cross_wide),
        ],
        dec_early + dec_late,
        True,
    )
    back_memory, (dec_products,) = settle(back_memory, dec_products)
    dec_rows = lax.psum_scatter(
        dec_products, "fsdp", scatter_dimension=0, axis_index_groups=groups, tiled=True
    )
    back_enc_two, enc_gain, enc_bias = norm_back(
        enc_two,
        small_params[:, EncSlots.final_gain],
        small_params[:, EncSlots.final_bias],
        back_memory,
    )
    vector_grads[EncSlots.final_gain] = enc_gain
    vector_grads[EncSlots.final_bias] = enc_bias
    back_enc_one, enc_down_grad, enc_up_grad = mlp_block_back(
        enc_mlp, back_enc_two, weights, small_params, EncSlots, "eu", "ed", vector_grads
    )
    enc_late, enc_late_views = exchange(narrow_for([enc_down_grad]), wide_for(enc_up_grad))
    back_enc_zero, enc_out_grad, enc_qkv_grad = self_block_back(
        enc_self, back_enc_one, weights, small_params, EncSlots, "eq", "eo", False, vector_grads
    )
    grad_second, grad_even, grad_odd = stem_back(stem_saved, back_enc_zero, weights, vector_grads)
    grad_second, (gathered_back, enc_late) = settle(grad_second, gathered_back, enc_late)
    enc_last, enc_last_views = exchange(
        wide_for(enc_out_grad, *enc_qkv_grad), wide_for(grad_second)
    )
    first_grad = tmatmul(cols_even, grad_even) + tmatmul(cols_odd, grad_odd)
    loose_rows = packed_rows(
        [first_grad, back_zero] + [vector_grads[column] for column in range(NVEC)], share * 128
    )
    hot_all = to_half(
        ids_all[:, :, 0].transpose(1, 0, 2).reshape(-1, 1)
        - vocab_start
        == lax.broadcasted_iota(jnp.int32, (reps * members * TLEN, vocab_rows), 1)
    )
    lookup = tmatmul(hot_all, gathered_back.reshape(-1, D))
    loose_rows, (lookup, enc_last) = settle(loose_rows, lookup, enc_last)
    embed_grad = head_grad + lookup
    loose = jnp.sum(quad_swap(loose_rows).reshape(share, 128, D), axis=0).T
    embed_totals = (jnp.sum(embed_grad * embed_grad), count_bad(embed_grad))
    loose, (embed_totals,) = settle(loose, embed_totals)
    early, late = len(enc_early), len(enc_early) + len(enc_late)
    attn_narrow, up_narrow, conv_narrow, down_wide = enc_early_views
    down_narrow, up_wide = [shifted(view, early) for view in enc_late_views]
    attn_wide, conv_wide = [shifted(view, late) for view in enc_last_views]
    enc_units = rows_of(
        [
            products(
                [
                    (down_narrow, down_wide),
                    (up_narrow, up_wide),
                    (attn_narrow, attn_wide),
                    (conv_narrow, conv_wide),
                ],
                enc_early + enc_late + enc_last,
                False,
            ),
            loose,
        ],
        4,
    )
    dec_rows, (enc_units,) = settle(dec_rows, enc_units)
    enc_quads, loose_units = enc_units
    per = D // unit
    dec_quads = quad_rows(dec_rows.reshape(cores, -1, 4 * unit))
    loose_own = jnp.transpose(loose_units, (1, 0, 2)).reshape(-1, share * 128)
    odd_end = 3 * MELS + TLEN
    vec_grad = loose_own[:, odd_end : odd_end + NVEC]
    last_unit = jnp.pad(loose_own[:, :odd_end], ((0, 0), (0, unit - odd_end)))
    first_lane = lax.broadcasted_iota(jnp.int32, (1, 2), 1) == 0
    once = [enc_quads[:, :, : 3 * unit], enc_quads[: 3 * per, :, 3 * unit :], loose_own]
    first = (replica == 0).astype(jnp.float32)
    squares = embed_totals[0] + sum(jnp.sum(part * part) for part in once)
    bad = embed_totals[1] + sum(count_bad(part) for part in once)
    sums = total_of(
        jnp.where(
            first_lane,
            jnp.sum(dec_rows * dec_rows) + first * squares,
            count_bad(dec_rows) + first * bad,
        ),
        1,
        True,
    )
    total_squares, total_bad = sums[0, 0], sums[0, 1]
    gradient_norm = jnp.sqrt(total_squares)
    factor = CLIP_AT / jnp.maximum(gradient_norm, CLIP_AT)
    steps = step_count[0].astype(jnp.float32)
    first_fix = 1.0 / (1.0 - jnp.power(jnp.float32(BETA_ONE), steps))
    second_fix = 1.0 / (1.0 - jnp.power(jnp.float32(BETA_TWO), steps))
    scalars = jnp.stack([factor, first_fix, second_fix])
    emb_moment, emb_square, emb_update, emb_sums = embed_moments(
        scalars, embedding, embed_moment, embed_square, head_grad, lookup
    )
    emb_sums, (dec_quads,) = settle(emb_sums, dec_quads)
    mat_moment, mat_square, mat_update, mat_sums = matrix_moments(
        scalars, matrices, matrix_moment, matrix_square, enc_quads, dec_quads, last_unit
    )
    vec_moment, vec_square, vec_update = moments(
        vectors, vector_moment, vector_square, vec_grad.T, factor, first_fix, second_fix
    )
    by_column = jnp.transpose(mat_sums, (1, 0, 2)).reshape(2, -1)[:, :columns]
    lone = jnp.stack([jnp.sum(vectors * vectors), jnp.sum(vec_update * vec_update)])
    place = lax.broadcasted_iota(jnp.int32, (2, groups_all), 1)
    both = jnp.sum(jnp.where(in_group[None], by_column[:, None, :], 0.0), axis=2)
    both = jnp.where(place == groups_all - 2, jnp.sum(emb_sums, axis=(0, 2))[:, None], both)
    both = jnp.where(place == groups_all - 1, lone[:, None], both)
    norms = jnp.sqrt(total_of(both, 2))
    weight_norms, update_norms = norms[0], norms[1]
    ratio = weight_norms / update_norms
    ratio_columns = jnp.sum(jnp.where(in_group, ratio[:, None], 0.0), axis=0)
    new_matrices = matrices - RATE * ratio_columns[None, :] * mat_update
    new_embedding = embedding - RATE * ratio[len(names)] * emb_update
    new_vectors = vectors - RATE * ratio[len(names) + 1] * vec_update
    mean_loss = loss_sum / jnp.sum(text_lengths).astype(jnp.float32)
    group_norms = jnp.stack([weight_norms, update_norms], axis=1)
    return (
        mean_loss,
        total_bad.astype(jnp.int32),
        gradient_norm,
        group_norms,
        new_matrices,
        mat_moment,
        mat_square,
        new_embedding,
        emb_moment,
        emb_square,
        new_vectors.T,
        vec_moment.T,
        vec_square.T,
    )


def solution(mesh):
    placed = (
        P(("rep", "fsdp"), None, None),
        P(("rep", "fsdp"), None),
        P(),
        P(("rep", "fsdp")),
        P(),
        P(),
        P("fsdp", None),
        P("fsdp", None),
        P("fsdp", None),
        P("fsdp", None),
        P("fsdp", None),
        P("fsdp", None),
        P("fsdp", None),
        P("fsdp", None),
        P("fsdp", None),
    )
    return jax.shard_map(
        on_device,
        mesh=mesh,
        in_specs=placed,
        out_specs=(
            P(),
            P(),
            P(),
            P(),
            P("fsdp", None),
            P("fsdp", None),
            P("fsdp", None),
            P("fsdp", None),
            P("fsdp", None),
            P("fsdp", None),
            P("fsdp", None),
            P("fsdp", None),
            P("fsdp", None),
        ),
        check_vma=False,
    )
```

```python
import functools

import jax
import jax.numpy as jnp
from jax import lax
from jax.experimental import pallas as pl
from jax.experimental.pallas import tpu as pltpu
from jax.sharding import PartitionSpec as P

D = 768
H = 12
HD = 64
FF = 3072
MELS = 80
TLEN = 128
LANGTOK = 50259
NVEC = 35


LN_EPS = 1e-05
SMOOTH = 0.1
CLIP_AT = 1.0
BETA_ONE = 0.9
BETA_TWO = 0.999
ADAM_EPS = 1e-06
DECAY = 0.01
RATE = 0.5
NEG_BIG = -1e30
class EncSlots:
    norm_gain = 2
    norm_bias = 3
    query_bias = 4
    value_bias = 5
    out_bias = 6
    mlp_gain = 7
    mlp_bias = 8
    up_bias = 9
    down_bias = 13
    final_gain = 14
    final_bias = 15


class DecSlots:
    norm_gain = 16
    norm_bias = 17
    query_bias = 18
    value_bias = 19
    out_bias = 20
    cross_gain = 21
    cross_bias = 22
    xquery_bias = 23
    xvalue_bias = 24
    xout_bias = 25
    mlp_gain = 26
    mlp_bias = 27
    up_bias = 28
    down_bias = 32
    final_gain = 33
    final_bias = 34


CORES = 2
LINE = 4


def mesh_shape():
    members = lax.axis_size("fsdp")
    return (lax.axis_size("rep"), LINE, members // (LINE * CORES), CORES)


def places():
    reps, line, side, cores = mesh_shape()
    index = lax.axis_index("fsdp")
    return (
        lax.axis_index("rep"),
        index // (side * cores),
        (index // cores) % side,
        index % cores,
    )


def send(values, move):
    reps, line, side, cores = mesh_shape()
    members = line * side * cores
    pairs = []
    for rep in range(reps):
        for far in range(line):
            for near in range(side):
                for core in range(cores):
                    target = move(rep, far, near, core)
                    if target is None:
                        continue
                    rep_to, far_to, near_to, core_to = target
                    pairs.append(
                        (
                            rep * members + (far * side + near) * cores + core,
                            rep_to * members + (far_to * side + near_to) * cores + core_to,
                        )
                    )
    return lax.ppermute(values, ("rep", "fsdp"), pairs)


def send_core(values):
    return send(values, lambda rep, far, near, core: (rep, far, near, 1 - core))


def send_rep(values, shift):
    reps = lax.axis_size("rep")
    return send(values, lambda rep, far, near, core: ((rep + shift) % reps, far, near, core))


def pick(values, index, axis):
    return lax.dynamic_index_in_dim(values, index, axis, keepdims=False)


def block(values, index, width):
    return lax.dynamic_slice_in_dim(values, index * width, width, axis=1)


def share_count():
    return CORES * lax.axis_size("rep")


def quad_place():
    return lax.axis_index("rep") * CORES + lax.axis_index("fsdp") % CORES


def quad_swap(values):
    reps, members = lax.axis_size("rep"), lax.axis_size("fsdp")
    groups = [
        [rep * members + chip * CORES + core for rep in range(reps) for core in range(CORES)]
        for chip in range(members // CORES)
    ]
    return lax.all_to_all(values, ("rep", "fsdp"), 0, 0, axis_index_groups=groups, tiled=True)


def message_body(plan, *refs):
    *sources, packed = refs
    offset = 0
    for which, start, rows, columns in plan:
        packed[offset : offset + rows, :] = sources[which][:, start : start + columns]
        offset = offset + rows


def message_of(pieces, columns):
    sources = []
    plan = []
    for values, start in pieces:
        which = [position for position, held in enumerate(sources) if held is values]
        if not which:
            which = [len(sources)]
            sources.append(values)
        plan.append((which[0], start, values.shape[0], columns))
    total = sum(rows for _, _, rows, _ in plan)
    return pl.pallas_call(
        functools.partial(message_body, plan),
        out_shape=jax.ShapeDtypeStruct((total, columns), sources[0].dtype),
        compiler_params=pltpu.CompilerParams(vmem_limit_bytes=40 << 20),
    )(*sources)


def exchange(*makers):
    share, unit = share_count(), unit_width()
    batches = [makers] if unit == D else [(maker,) for maker in makers]
    arrays, views = [], []
    for batch in batches:
        pieces = [make(place) for place in range(share) for make in batch]
        columns = pieces[0][0].shape[1] if len(batch) == 1 and pieces[0][2] else unit
        message = message_of([piece[:2] for piece in pieces], columns)
        rows = [pieces[position][0].shape[0] for position in range(len(batch))]
        for position in range(len(batch)):
            views.append((len(arrays), sum(rows[:position]), rows[position], sum(rows)))
        arrays.append(quad_swap(message))
    return arrays, views


def settle(value, *others):
    flat, tree = jax.tree.flatten((value, others))
    return jax.tree.unflatten(tree, lax.optimization_barrier(flat))


def unit_width():
    return 4 * D // share_count()


def wide_for(*parts):
    unit = unit_width()

    def make(place):
        start = place * unit % sum(part.shape[1] for part in parts)
        for part in parts:
            if start < part.shape[1]:
                return (part, start, False)
            start = start - part.shape[1]

    return make


def narrow_for(choices):
    unit = unit_width()
    return lambda place: (choices[min(place * unit // D, len(choices) - 1)], 0, True)


def product_of(share, arrays, narrow, wide):
    total = None
    for place in range(share):
        rows = []
        for which, offset, count, step in (narrow, wide):
            start = place * step + offset
            rows.append(arrays[which][start : start + count, :])
        part = tmatmul(*rows)
        total = part if total is None else total + part
    return total


def products_body(share, pairs, stepped, *refs):
    *arrays, output = refs
    unit = output.shape[1] if stepped else output.shape[1] // len(pairs)
    for position, (narrow, wide) in enumerate(pairs):
        if stepped:

            @pl.when(pl.program_id(0) == position)
            def _():
                output[...] = product_of(share, arrays, narrow, wide)

        else:
            output[:, position * unit : (position + 1) * unit] = product_of(
                share, arrays, narrow, wide
            )


def products(pairs, arrays, stepped):
    share, unit = share_count(), unit_width()
    count = len(pairs)
    body = functools.partial(products_body, share, pairs, stepped)
    shape = jax.ShapeDtypeStruct((D, count * unit), jnp.float32)
    params = pltpu.CompilerParams(vmem_limit_bytes=56 << 20)
    if not stepped:
        return pl.pallas_call(
            body, out_shape=shape, cost_estimate=estimate(11), compiler_params=params
        )(*arrays)
    return pl.pallas_call(
        body,
        grid=(count,),
        out_shape=shape,
        in_specs=[fixed(held.shape) for held in arrays],
        out_specs=pl.BlockSpec((D, unit), lambda step: (0, step)),
        cost_estimate=estimate(10),
        compiler_params=params,
    )(*arrays)


def shifted(view, by):
    return (view[0] + by,) + view[1:]


def quad_rows(by_core):
    reps = lax.axis_size("rep")
    message = jnp.concatenate([by_core] * reps, axis=0)
    swapped = quad_swap(message.reshape(-1, by_core.shape[2]))
    return swapped.reshape(message.shape)


def scatter_body(cored, count, values, output, *scratch):
    reps, line, side, cores = mesh_shape()
    rep, far, near, core = places()
    members = line * side * cores
    if cored:
        core_in, core_sum = scratch[:2]
        scratch = scratch[2:]
    near_in, near_sum, far_in, leaving, landing = scratch
    wide = output.shape[-1] // count

    def at(far_to, near_to, core_to):
        return {"fsdp": (far_to * side + near_to) * cores + core_to}

    barrier = pltpu.get_barrier_semaphore()
    partners = [at(lax.rem(far + step, line), near, core) for step in range(1, line)]
    partners += [at(far, lax.rem(near + step, side), core) for step in range(1, side)]
    if cored:
        partners.append(at(far, near, 1 - core))
    for partner in partners:
        pl.semaphore_signal(barrier, inc=1, device_id=partner)
    pl.semaphore_wait(barrier, len(partners))

    started = []

    def start(source, target, device):
        slot = len(started)
        copy = pltpu.make_async_remote_copy(
            src_ref=source,
            dst_ref=target,
            send_sem=leaving.at[slot],
            recv_sem=landing.at[slot],
            device_id=device,
        )
        copy.start()
        started.append(copy)
        return copy

    spans = [pl.ds(part * wide, wide) for part in range(count)]
    core_moves = []
    if cored:
        for part in range(count):
            core_moves.append(
                start(
                    values.at[:, :, 1 - core, :, spans[part]],
                    core_in.at[part],
                    at(far, near, 1 - core),
                )
            )
    near_moves = []
    for part in range(count):
        if cored:
            core_moves[part].wait_recv()
            core_sum[part] = values[:, :, core, :, spans[part]] + core_in[part]
        moves = []
        for step in range(1, side):
            there = lax.rem(near + step, side)
            source = core_sum.at[part, :, there] if cored else values.at[:, there, :, spans[part]]
            moves.append(start(source, near_in.at[part, step - 1], at(far, there, core)))
        near_moves.append(moves)
    far_moves = []
    for part in range(count):
        total = core_sum[part, :, near] if cored else values[:, near, :, spans[part]]
        for step, move in enumerate(near_moves[part]):
            move.wait_recv()
            total = total + near_in[part, step]
        near_sum[part] = total
        moves = []
        for step in range(1, line):
            there = lax.rem(far + step, line)
            moves.append(
                start(near_sum.at[part, there], far_in.at[part, step - 1], at(there, near, core))
            )
        far_moves.append(moves)
    for part in range(count):
        total = near_sum[part, far]
        for step, move in enumerate(far_moves[part]):
            move.wait_recv()
            total = total + far_in[part, step]
        output[:, spans[part]] = total
    for move in started:
        move.wait_send()


def scatter_sum(values, count, cored, tag):
    reps, line, side, cores = mesh_shape()
    rows = values.shape[0] // (line * side * (cores if cored else 1))
    width = values.shape[1]
    wide = width // count
    kind = values.dtype
    shape = (line, side) + ((cores,) if cored else ()) + (rows, width)
    copies = count * ((1 if cored else 0) + (side - 1) + (line - 1))
    cube = (count, line, side, rows, wide)
    scratch = [pltpu.VMEM(cube, kind), pltpu.VMEM(cube, kind)] if cored else []
    scratch += [
        pltpu.VMEM((count, side - 1, line, rows, wide), kind),
        pltpu.VMEM((count, line, rows, wide), kind),
        pltpu.VMEM((count, line - 1, rows, wide), kind),
        pltpu.SemaphoreType.DMA((copies,)),
        pltpu.SemaphoreType.DMA((copies,)),
    ]
    return pl.pallas_call(
        functools.partial(scatter_body, cored, count),
        out_shape=jax.ShapeDtypeStruct((rows, width), kind),
        in_specs=[pl.BlockSpec(memory_space=pltpu.VMEM)],
        out_specs=pl.BlockSpec(memory_space=pltpu.VMEM),
        scratch_shapes=scratch,
        cost_estimate=estimate(45),
        compiler_params=pltpu.CompilerParams(
            collective_id=tag, has_side_effects=True, vmem_limit_bytes=60 << 20
        ),
    )(values.reshape(shape))


def rows_body(pieces, count, *refs):
    reps, line, side, cores = mesh_shape()
    rep, far, near, core = places()
    total = len(pieces)
    values, outputs = refs[:count], refs[count : 2 * count]
    rest = refs[2 * count :]
    near_in, near_sum = rest[:total], rest[total : 2 * total]
    far_in, far_sum = rest[2 * total : 3 * total], rest[3 * total : 4 * total]
    leaving, landing = rest[4 * total :]
    place = rep * cores + core

    def at(rep_to, far_to, near_to, core_to):
        return {"rep": rep_to, "fsdp": (far_to * side + near_to) * cores + core_to}

    moves = [(turn, flip) for turn in range(reps) for flip in range(cores) if turn or flip]
    quad = [
        at(lax.rem(rep + turn, reps), far, near, 1 - core if flip else core)
        for turn, flip in moves
    ]
    line_peers = [at(rep, lax.rem(far + step, line), near, core) for step in range(1, line)]
    side_peers = [at(rep, far, lax.rem(near + step, side), core) for step in range(1, side)]
    barrier = pltpu.get_barrier_semaphore()
    for partner in line_peers + side_peers + quad:
        pl.semaphore_signal(barrier, inc=1, device_id=partner)
    pl.semaphore_wait(barrier, len(line_peers + side_peers + quad))

    started = []

    def start(source, target, device):
        slot = len(started)
        copy = pltpu.make_async_remote_copy(
            src_ref=source,
            dst_ref=target,
            send_sem=leaving.at[slot],
            recv_sem=landing.at[slot],
            device_id=device,
        )
        copy.start()
        started.append(copy)
        return copy

    near_moves = []
    for piece, (part, span) in enumerate(pieces):
        near_moves.append(
            [
                start(
                    values[part].at[:, lax.rem(near + step, side), :, span],
                    near_in[piece].at[step - 1],
                    side_peers[step - 1],
                )
                for step in range(1, side)
            ]
        )
    far_moves = []
    last_moves = []

    def finish(piece):
        part, span = pieces[piece]
        summed = near_sum[piece][far]
        for step, move in enumerate(far_moves[piece]):
            move.wait_recv()
            summed = summed + far_in[piece][step]
        far_sum[piece][...] = summed.reshape(far_sum[piece].shape)
        outputs[part][place, :, span] = far_sum[piece][core]
        for (turn, flip), device in zip(moves, quad):
            last_moves.append(
                start(
                    far_sum[piece].at[1 - core if flip else core],
                    outputs[part].at[place, :, span],
                    device,
                )
            )

    lag = 4
    for piece, (part, span) in enumerate(pieces):
        summed = values[part][:, near, :, span]
        for step, move in enumerate(near_moves[piece]):
            move.wait_recv()
            summed = summed + near_in[piece][step]
        near_sum[piece][...] = summed
        far_moves.append(
            [
                start(
                    near_sum[piece].at[lax.rem(far + step, line)],
                    far_in[piece].at[step - 1],
                    line_peers[step - 1],
                )
                for step in range(1, line)
            ]
        )
        if piece >= lag:
            finish(piece - lag)
    for piece in range(max(total - lag, 0), total):
        finish(piece)
    for move in last_moves:
        move.wait_recv()
    for move in started:
        move.wait_send()


def rows_of(parts, tag):
    reps, line, side, cores = mesh_shape()
    count = len(parts)
    rows = parts[0].shape[0] // (line * side)
    own = rows // cores
    widths = [part.shape[1] for part in parts]
    pieces = []
    for part, width in enumerate(widths):
        offset = 0
        while offset < width:
            size = min(256, width - offset)
            pieces.append((part, pl.ds(offset, size)))
            offset = offset + size
    sizes = [span.size for _, span in pieces]
    copies = len(pieces) * (side - 1 + line - 1 + reps * cores - 1)
    near_in = [pltpu.VMEM((side - 1, line, rows, size), jnp.float32) for size in sizes]
    near_sum = [pltpu.VMEM((line, rows, size), jnp.float32) for size in sizes]
    far_in = [pltpu.VMEM((line - 1, rows, size), jnp.float32) for size in sizes]
    far_sum = [pltpu.VMEM((cores, own, size), jnp.float32) for size in sizes]
    return pl.pallas_call(
        functools.partial(rows_body, pieces, count),
        out_shape=[
            jax.ShapeDtypeStruct((reps * cores, own, width), jnp.float32) for width in widths
        ],
        in_specs=[pl.BlockSpec(memory_space=pltpu.VMEM)] * count,
        out_specs=[pl.BlockSpec(memory_space=pltpu.VMEM)] * count,
        scratch_shapes=near_in
        + near_sum
        + far_in
        + far_sum
        + [pltpu.SemaphoreType.DMA((copies,)), pltpu.SemaphoreType.DMA((copies,))],
        cost_estimate=estimate(130),
        compiler_params=pltpu.CompilerParams(
            collective_id=tag, has_side_effects=True, vmem_limit_bytes=60 << 20
        ),
    )(*[part.reshape(line, side, rows, part.shape[1]) for part in parts])


def pack_body(*refs):
    *sources, packed = refs
    offset = 0
    for source in sources:
        if len(source.shape) == 1:
            packed[offset : offset + 1, :] = source[...].reshape(1, source.shape[0])
            offset = offset + 1
        else:
            packed[offset : offset + source.shape[0], :] = source[...]
            offset = offset + source.shape[0]
    packed[offset:, :] = jnp.zeros((packed.shape[0] - offset, packed.shape[1]), jnp.float32)


def packed_rows(sources, rows):
    return pl.pallas_call(
        pack_body,
        out_shape=jax.ShapeDtypeStruct((rows, D), jnp.float32),
        compiler_params=pltpu.CompilerParams(vmem_limit_bytes=32 << 20),
    )(*sources)


def moment_part(scalars, held, moment, square, raw):
    scaled = raw * scalars[0]
    new_moment = BETA_ONE * moment + (1.0 - BETA_ONE) * scaled
    new_square = BETA_TWO * square + (1.0 - BETA_TWO) * scaled * scaled
    update = (
        new_moment * scalars[1] / (jnp.sqrt(new_square * scalars[2]) + ADAM_EPS) + DECAY * held
    )
    held_sum = jnp.sum(held * held, axis=0, keepdims=True)
    return (new_moment, new_square, update, held_sum, jnp.sum(update * update, axis=0, keepdims=True))


def embed_body(
    scalars, weight, moment, square, head, lookup, moment_out, square_out, update_out, sums
):
    moment_out[...], square_out[...], update_out[...], held_sum, update_sum = moment_part(
        scalars, weight[...], moment[...], square[...], head[...] + lookup[...]
    )
    sums[0, 0:1, :] = held_sum
    sums[0, 1:2, :] = update_sum


def moment_estimate(weight):
    return pl.CostEstimate(
        flops=20 * weight.size, bytes_accessed=28 * weight.size, transcendentals=0
    )


def embed_moments(scalars, weight, moment, square, head, lookup):
    rows, columns = weight.shape
    spec = by_step(rows // VOCAB_STEPS, columns)
    shape = jax.ShapeDtypeStruct(weight.shape, jnp.float32)
    return pl.pallas_call(
        embed_body,
        grid=(VOCAB_STEPS,),
        out_shape=[shape] * 3 + [jax.ShapeDtypeStruct((VOCAB_STEPS, 2, columns), jnp.float32)],
        in_specs=[pl.BlockSpec(memory_space=pltpu.SMEM)] + [spec] * 5,
        out_specs=[spec] * 3 + [pl.BlockSpec((1, 2, columns), lambda step: (step, 0, 0))],
        cost_estimate=moment_estimate(weight),
        compiler_params=pltpu.CompilerParams(vmem_limit_bytes=48 << 20),
    )(scalars, weight, moment, square, head, lookup)


def matrix_body(
    scalars, weight, moment, square, enc, dec, last, moment_out, square_out, update_out, sums
):
    share, unit = enc.shape[0], enc.shape[2]
    per = D // unit
    turned = list(range(per, share)) + list(range(per))
    plain = list(range(share))
    crossed = plain[:per] + plain[2 * per :] + plain[per : 2 * per]
    orders = [turned, plain, plain, turned, crossed, plain, plain, plain[: 3 * per] + [None]]
    for step, order in enumerate(orders):
        source = dec if 3 <= step < 7 else enc

        @pl.when(pl.program_id(0) == step)
        def _():
            for part, place in enumerate(order):
                span = slice(part * unit, (part + 1) * unit)
                raw = last[...] if place is None else source[place]
                results = moment_part(
                    scalars, weight[:, span], moment[:, span], square[:, span], raw
                )
                moment_out[:, span], square_out[:, span], update_out[:, span] = results[:3]
                sums[0, 0:1, span] = results[3]
                sums[0, 1:2, span] = results[4]


def matrix_moments(scalars, weight, moment, square, enc, dec, last):
    rows, columns = weight.shape
    share, unit = share_count(), unit_width()
    spec = pl.BlockSpec((rows, 4 * D), lambda step: (0, step))

    def enc_place(step):
        return (0, 0, jnp.where(step < 3, 2 - step, 3))

    def dec_place(step):
        return (0, 0, jnp.where(step < 4, 2, jnp.where(step == 4, 3, jnp.where(step == 5, 1, 0))))

    shape = jax.ShapeDtypeStruct(weight.shape, jnp.float32)
    return pl.pallas_call(
        matrix_body,
        grid=(8,),
        out_shape=[shape] * 3 + [jax.ShapeDtypeStruct((8, 2, 4 * D), jnp.float32)],
        in_specs=[
            pl.BlockSpec(memory_space=pltpu.SMEM),
            spec,
            spec,
            spec,
            pl.BlockSpec((share, rows, unit), enc_place),
            pl.BlockSpec((share, rows, unit), dec_place),
            fixed(last.shape),
        ],
        out_specs=[spec] * 3 + [pl.BlockSpec((1, 2, 4 * D), lambda step: (step, 0, 0))],
        cost_estimate=moment_estimate(weight),
        compiler_params=pltpu.CompilerParams(vmem_limit_bytes=48 << 20),
    )(scalars, weight, moment, square, enc, dec, last)


def gather_body(everyone, values, gathered, leaving, landing):
    members = lax.axis_size("fsdp")
    reps = lax.axis_size("rep") if everyone else 1
    rep, member = lax.axis_index("rep"), lax.axis_index("fsdp")
    peers = []
    for turn in range(reps):
        for shift in range(members):
            if turn or shift:
                device = {"fsdp": lax.rem(member + shift, members)}
                if everyone:
                    device["rep"] = lax.rem(rep + turn, reps)
                peers.append(device)
    here = rep * members + member if everyone else member
    barrier = pltpu.get_barrier_semaphore()
    for peer in peers:
        pl.semaphore_signal(barrier, inc=1, device_id=peer)
    pl.semaphore_wait(barrier, len(peers))
    copies = []
    for slot, peer in enumerate(peers):
        copies.append(
            pltpu.make_async_remote_copy(
                src_ref=values,
                dst_ref=gathered.at[here],
                send_sem=leaving.at[slot],
                recv_sem=landing.at[slot],
                device_id=peer,
            )
        )
        copies[-1].start()
    gathered[here] = values[...]
    for copy in copies:
        copy.wait()


def gather_small(values, tag, everyone=False):
    count = lax.axis_size("fsdp") * (lax.axis_size("rep") if everyone else 1)
    return pl.pallas_call(
        functools.partial(gather_body, everyone),
        out_shape=jax.ShapeDtypeStruct((count,) + values.shape, values.dtype),
        in_specs=[pl.BlockSpec(memory_space=pltpu.VMEM)],
        out_specs=pl.BlockSpec(memory_space=pltpu.VMEM),
        scratch_shapes=[
            pltpu.SemaphoreType.DMA((count - 1,)),
            pltpu.SemaphoreType.DMA((count - 1,)),
        ],
        cost_estimate=estimate(8),
        compiler_params=pltpu.CompilerParams(collective_id=tag, has_side_effects=True),
    )(values)


def total_of(values, tag, everyone=False):
    rows, columns = values.shape
    padded = jnp.pad(values, ((0, 8 - rows), (0, 128 - columns)))
    return jnp.sum(gather_small(padded, tag, everyone), axis=0)[:rows, :columns]


def rows_gather_body(values, gathered, leaving, landing):
    reps, line, side, cores = mesh_shape()
    rep, far, near, core = places()

    def at(far_to, near_to, core_to):
        return {"fsdp": (far_to * side + near_to) * cores + core_to}

    line_peers = [at(lax.rem(far + step, line), near, core) for step in range(1, line)]
    side_peers = [at(far, lax.rem(near + step, side), core) for step in range(1, side)]
    twin = at(far, near, 1 - core)
    barrier = pltpu.get_barrier_semaphore()
    for partner in line_peers + side_peers + [twin]:
        pl.semaphore_signal(barrier, inc=1, device_id=partner)
    pl.semaphore_wait(barrier, len(line_peers + side_peers) + 1)
    started = []

    def start(source, target, device):
        slot = len(started)
        copy = pltpu.make_async_remote_copy(
            src_ref=source,
            dst_ref=target,
            send_sem=leaving.at[slot],
            recv_sem=landing.at[slot],
            device_id=device,
        )
        copy.start()
        started.append(copy)
        return copy

    line_moves, side_moves, core_moves = [], [], []
    for step in range(1, line):
        line_moves.append(start(values, gathered.at[far, near, core], line_peers[step - 1]))

    def pass_on(step):
        origin = lax.rem(far - step + line, line)
        held = values if step == 0 else gathered.at[origin, near, core]
        for turn in range(1, side):
            side_moves.append(
                (step, turn, start(held, gathered.at[origin, near, core], side_peers[turn - 1]))
            )
        core_moves.append(start(held, gathered.at[origin, near, core], twin))

    pass_on(0)
    gathered[far, near, core] = values[...]
    for step in range(1, line):
        line_moves[step - 1].wait_recv()
        pass_on(step)
    for step, turn, move in list(side_moves):
        move.wait_recv()
        origin = lax.rem(far - step + line, line)
        beside = lax.rem(near - turn + side, side)
        held = gathered.at[origin, beside, core]
        core_moves.append(start(held, gathered.at[origin, beside, core], twin))
    for move in core_moves:
        move.wait_recv()
    for move in started:
        move.wait_send()


def gather_rows(values, tag):
    reps, line, side, cores = mesh_shape()
    copies = line - 1 + line * (side - 1) + line * side
    shape = (line, side, cores) + values.shape
    return pl.pallas_call(
        rows_gather_body,
        out_shape=jax.ShapeDtypeStruct(shape, values.dtype),
        in_specs=[pl.BlockSpec(memory_space=pltpu.VMEM)],
        out_specs=pl.BlockSpec(memory_space=pltpu.VMEM),
        scratch_shapes=[pltpu.SemaphoreType.DMA((copies,)), pltpu.SemaphoreType.DMA((copies,))],
        cost_estimate=estimate(26),
        compiler_params=pltpu.CompilerParams(
            collective_id=tag, has_side_effects=True, vmem_limit_bytes=32 << 20
        ),
    )(values).reshape(-1, values.shape[1])


VOCAB_STEPS = 7
TOKEN_SPAN = 512


def fixed(shape):
    return pl.BlockSpec(shape, lambda step: (0,) * len(shape), pipeline_mode=pl.Buffered(1))


def by_step(tall, wide):
    return pl.BlockSpec((tall, wide), lambda step: (step, 0))


def estimate(micros):
    return pl.CostEstimate(flops=0, bytes_accessed=micros * 3_600_000, transcendentals=0)


def token_spans(count):
    return [slice(start, start + TOKEN_SPAN) for start in range(0, count, TOKEN_SPAN)]


def stats_body(hidden, table, shut, keep, target, stats):
    step = pl.program_id(0)

    @pl.when(step == 0)
    def _():
        stats[0:1, :] = jnp.full((1, stats.shape[1]), NEG_BIG, jnp.float32)
        stats[1:, :] = jnp.zeros((stats.shape[0] - 1, stats.shape[1]), jnp.float32)

    tall = table.shape[0]
    part = table[...]
    row = lax.broadcasted_iota(jnp.int32, (tall, TOKEN_SPAN), 0) + step * tall
    for span in token_spans(stats.shape[1]):
        logits = matmul_t(part, hidden[span, :])
        masked = logits + shut[...]
        former = stats[0:1, span]
        top = jnp.maximum(former, jnp.max(masked, axis=0, keepdims=True))
        stats[1:2, span] = stats[1:2, span] * jnp.exp(former - top) + jnp.sum(
            jnp.exp(masked - top), axis=0, keepdims=True
        )
        stats[0:1, span] = top
        stats[2:3, span] += jnp.sum(
            jnp.where(row == target[:, span], logits, 0.0), axis=0, keepdims=True
        )
        stats[3:4, span] += jnp.sum(
            jnp.where(keep[...] > 0.0, logits, 0.0), axis=0, keepdims=True
        )


def vocab_stats(hidden, table, shut, keep, target):
    rows, vocab_rows = hidden.shape[0], table.shape[0]
    tall = vocab_rows // VOCAB_STEPS
    return pl.pallas_call(
        stats_body,
        grid=(VOCAB_STEPS,),
        out_shape=jax.ShapeDtypeStruct((4, rows), jnp.float32),
        in_specs=[
            fixed(hidden.shape),
            by_step(tall, D),
            by_step(tall, 1),
            by_step(tall, 1),
            fixed((1, rows)),
        ],
        out_specs=pl.BlockSpec((4, rows), lambda step: (0, 0)),
        cost_estimate=estimate(20),
        compiler_params=pltpu.CompilerParams(vmem_limit_bytes=60 << 20),
    )(hidden, table, shut, keep, target)


def slopes_into(slopes, hidden, table, shut, pull, target, log_norm):
    tall = table.shape[0]
    part = table[...]
    row = lax.broadcasted_iota(jnp.int32, (tall, TOKEN_SPAN), 0) + pl.program_id(0) * tall
    for span in token_spans(slopes.shape[1]):
        logits = matmul_t(part, hidden[span, :])
        soft = jnp.exp((logits - log_norm[:, span]) + shut[...])
        hits = jnp.where(row == target[:, span], 1.0 - SMOOTH, 0.0)
        slopes[:, span] = to_half(soft - hits - pull[...])


def own_body(
    hidden, table, shut, pull, target, log_norm, counted, table_grad, hidden_grad, slopes, total
):
    step = pl.program_id(0)
    slopes_into(slopes, hidden, table, shut, pull, target, log_norm)
    table_grad[...] = matmul(slopes[...], hidden[...])
    part = tmatmul(table[...], slopes[...])

    @pl.when(step == 0)
    def _():
        total[...] = part

    @pl.when(step > 0)
    def _():
        total[...] += part

    @pl.when(step == VOCAB_STEPS - 1)
    def _():
        hidden_grad[...] = jnp.where(counted[...] > 0.0, total[...], 0.0).T


def own_slopes(hidden, table, shut, pull, target, log_norm, counted):
    rows, vocab_rows = hidden.shape[0], table.shape[0]
    tall = vocab_rows // VOCAB_STEPS
    flat = fixed((1, rows))
    column = by_step(tall, 1)
    return pl.pallas_call(
        own_body,
        grid=(VOCAB_STEPS,),
        out_shape=[
            jax.ShapeDtypeStruct((vocab_rows, D), jnp.float32),
            jax.ShapeDtypeStruct((rows, D), jnp.float32),
        ],
        in_specs=[fixed(hidden.shape), by_step(tall, D), column, column, flat, flat, flat],
        out_specs=[by_step(tall, D), fixed((rows, D))],
        scratch_shapes=[pltpu.VMEM((tall, rows), jnp.bfloat16), pltpu.VMEM((D, rows), jnp.float32)],
        cost_estimate=estimate(46),
        compiler_params=pltpu.CompilerParams(vmem_limit_bytes=60 << 20),
    )(hidden, table, shut, pull, target, log_norm, counted)


def other_body(hidden, table, shut, pull, target, log_norm, former, table_grad, slopes):
    slopes_into(slopes, hidden, table, shut, pull, target, log_norm)
    table_grad[...] = former[...] + matmul(slopes[...], hidden[...])


def other_slopes(former, hidden, table, shut, pull, target, log_norm):
    rows, vocab_rows = hidden.shape[0], table.shape[0]
    tall = vocab_rows // VOCAB_STEPS
    flat = fixed((1, rows))
    column = by_step(tall, 1)
    return pl.pallas_call(
        other_body,
        grid=(VOCAB_STEPS,),
        out_shape=jax.ShapeDtypeStruct((vocab_rows, D), jnp.float32),
        in_specs=[
            fixed(hidden.shape),
            by_step(tall, D),
            column,
            column,
            flat,
            flat,
            by_step(tall, D),
        ],
        out_specs=by_step(tall, D),
        scratch_shapes=[pltpu.VMEM((tall, rows), jnp.bfloat16)],
        cost_estimate=estimate(27),
        compiler_params=pltpu.CompilerParams(vmem_limit_bytes=60 << 20),
    )(hidden, table, shut, pull, target, log_norm, former)


def reps_body(count, *refs):
    sources, gathered = refs[:count], refs[count : 2 * count]
    leaving, landing = refs[2 * count :]
    reps = lax.axis_size("rep")
    here = lax.axis_index("rep")
    peers = [{"rep": lax.rem(here + turn, reps)} for turn in range(1, reps)]
    barrier = pltpu.get_barrier_semaphore()
    for peer in peers:
        pl.semaphore_signal(barrier, inc=1, device_id=peer)
    pl.semaphore_wait(barrier, len(peers))
    copies = []
    for source, target in zip(sources, gathered):
        for peer in peers:
            copies.append(
                pltpu.make_async_remote_copy(
                    src_ref=source,
                    dst_ref=target.at[here],
                    send_sem=leaving.at[len(copies)],
                    recv_sem=landing.at[len(copies)],
                    device_id=peer,
                )
            )
            copies[-1].start()
        target[here] = source[...]
    for copy in copies:
        copy.wait()


def gather_reps(sources, tag):
    reps = lax.axis_size("rep")
    count = len(sources)
    copies = count * (reps - 1)
    return pl.pallas_call(
        functools.partial(reps_body, count),
        out_shape=[
            jax.ShapeDtypeStruct((reps,) + source.shape, source.dtype) for source in sources
        ],
        in_specs=[pl.BlockSpec(memory_space=pltpu.VMEM)] * count,
        out_specs=[pl.BlockSpec(memory_space=pltpu.VMEM)] * count,
        scratch_shapes=[pltpu.SemaphoreType.DMA((copies,)), pltpu.SemaphoreType.DMA((copies,))],
        cost_estimate=estimate(6),
        compiler_params=pltpu.CompilerParams(
            collective_id=tag, has_side_effects=True, vmem_limit_bytes=24 << 20
        ),
    )(*sources)


def join_body(values, joined, gathered, leaving, landing):
    gather_body(False, values, gathered, leaving, landing)
    members = lax.axis_size("fsdp")
    top = gathered[0, 0:1, :]
    for place in range(1, members):
        top = jnp.maximum(top, gathered[place, 0:1, :])
    total = jnp.zeros_like(top)
    target = jnp.zeros_like(top)
    whole = jnp.zeros_like(top)
    for place in range(members):
        total = total + gathered[place, 1:2, :] * jnp.exp(gathered[place, 0:1, :] - top)
        target = target + gathered[place, 2:3, :]
        whole = whole + gathered[place, 3:4, :]
    joined[0:1, :] = top + jnp.log(total)
    joined[1:2, :] = target
    joined[2:3, :] = whole


def join_stats(values, tag):
    count = lax.axis_size("fsdp")
    return pl.pallas_call(
        join_body,
        out_shape=jax.ShapeDtypeStruct((3, values.shape[1]), values.dtype),
        in_specs=[pl.BlockSpec(memory_space=pltpu.VMEM)],
        out_specs=pl.BlockSpec(memory_space=pltpu.VMEM),
        scratch_shapes=[
            pltpu.VMEM((count,) + values.shape, values.dtype),
            pltpu.SemaphoreType.DMA((count - 1,)),
            pltpu.SemaphoreType.DMA((count - 1,)),
        ],
        cost_estimate=estimate(8),
        compiler_params=pltpu.CompilerParams(collective_id=tag, has_side_effects=True),
    )(values)


def layout(width, hidden, mels, text_len):
    names = (
        "eq",
        "eo",
        "eu",
        "ed",
        "dq",
        "do",
        "xq",
        "xk",
        "xo",
        "du",
        "dd",
        "c2",
        "c1",
        "dp",
    )
    widths = (
        3 * width,
        width,
        hidden,
        hidden,
        3 * width,
        width,
        width,
        2 * width,
        width,
        hidden,
        hidden,
        3 * width,
        3 * mels,
        text_len,
    )
    bounds = {}
    offset = 0
    for piece_name, extent in zip(names, widths):
        bounds[piece_name] = (offset, offset + extent)
        offset = offset + extent
    return (names, bounds)


def columns_of(weights, bounds, piece_name):
    span_start, span_stop = bounds[piece_name]
    return weights[:, span_start:span_stop]


def sinusoid(length, width):
    halfway = width // 2
    increment = jnp.log(10000.0) / (halfway - 1)
    rates = jnp.exp(-increment * jnp.arange(halfway, dtype=jnp.float32))
    angles = jnp.arange(length, dtype=jnp.float32)[:, None] * rates[None, :]
    return jnp.concatenate([jnp.sin(angles), jnp.cos(angles)], axis=1)


def layer_norm(inputs, gain, offset):
    average = jnp.mean(inputs, axis=-1, keepdims=True)
    centred = inputs - average
    spread = jnp.mean(centred * centred, axis=-1, keepdims=True)
    return centred * lax.rsqrt(spread + LN_EPS) * gain + offset


def norm_back(inputs, gain, offset, upstream):
    _, pull = jax.vjp(layer_norm, inputs, gain, offset)
    return pull(upstream)


def gelu_exact(values):
    return jax.nn.gelu(values, approximate=False)


def gelu_back(values, upstream):
    _, pull = jax.vjp(gelu_exact, values)
    return pull(upstream)[0]


def to_half(values):
    return values.astype(jnp.bfloat16)


def matmul(left, right):
    return jnp.dot(left, right, preferred_element_type=jnp.float32)


def matmul_t(left, right):
    return lax.dot_general(
        left, right, (((1,), (1,)), ((), ())), preferred_element_type=jnp.float32
    )


def tmatmul(left, right):
    return lax.dot_general(
        left, right, (((0,), (0,)), ((), ())), preferred_element_type=jnp.float32
    )


def head_pairs(width):
    lane = lax.broadcasted_iota(jnp.int32, (1, 2 * HD), 1)
    masks = [lane < HD, lane >= HD]
    return [(slice(start, start + 2 * HD), masks) for start in range(0, width, 2 * HD)]


def masked_half(values, mask):
    return jnp.where(mask, values, jnp.bfloat16(0.0))


def soft_rows(query_part, key_part, causal):
    scores = matmul_t(query_part, key_part) * HD ** (-0.5)
    if causal:
        rows = lax.broadcasted_iota(jnp.int32, scores.shape, 0)
        cols = lax.broadcasted_iota(jnp.int32, scores.shape, 1)
        scores = jnp.where(rows >= cols, scores, NEG_BIG)
    row_top = jnp.max(scores, axis=-1, keepdims=True)
    log_total = row_top + jnp.log(jnp.sum(jnp.exp(scores - row_top), axis=-1, keepdims=True))
    return jnp.exp(scores - log_total)


def attend_body(causal, queries, keys, values, attended):
    for span, masks in head_pairs(queries.shape[1]):
        query_pair, key_pair, value_pair = queries[:, span], keys[:, span], values[:, span]
        total = None
        for mask in masks:
            soft = soft_rows(masked_half(query_pair, mask), key_pair, causal)
            part = matmul(to_half(soft), masked_half(value_pair, mask))
            total = part if total is None else total + part
        attended[:, span] = to_half(total)


def attend(queries, keys_half, values_half, causal):
    return pl.pallas_call(
        functools.partial(attend_body, causal),
        out_shape=jax.ShapeDtypeStruct(queries.shape, jnp.bfloat16),
        cost_estimate=estimate(6),
        compiler_params=pltpu.CompilerParams(vmem_limit_bytes=32 << 20),
    )(queries, keys_half, values_half)


def attend_back_body(causal, queries, keys, values, upstream, grad_query, grad_key, grad_value, sums):
    for span, masks in head_pairs(queries.shape[1]):
        query_pair, key_pair, value_pair = queries[:, span], keys[:, span], values[:, span]
        up_pair = upstream[:, span]
        totals = None
        for mask in masks:
            query_part, up_part = masked_half(query_pair, mask), masked_half(up_pair, mask)
            soft = soft_rows(query_part, key_pair, causal)
            back_soft = matmul_t(up_part, value_pair)
            inner = jnp.sum(soft * back_soft, axis=-1, keepdims=True)
            back_scores = to_half(soft * (back_soft - inner) * HD ** (-0.5))
            parts = (
                matmul(back_scores, masked_half(key_pair, mask)),
                tmatmul(back_scores, query_part),
                tmatmul(to_half(soft), up_part),
            )
            totals = parts if totals is None else [x + y for x, y in zip(totals, parts)]
        grad_query[:, span] = to_half(totals[0])
        grad_key[:, span] = to_half(totals[1])
        grad_value[:, span] = to_half(totals[2])
        sums[0:1, span] = jnp.sum(totals[0], axis=0, keepdims=True)
        sums[1:2, span] = jnp.sum(totals[2], axis=0, keepdims=True)


def attend_back(queries, keys_half, values_half, causal, back_attended):
    half = [
        jax.ShapeDtypeStruct(part.shape, jnp.bfloat16)
        for part in (queries, keys_half, values_half)
    ]
    return pl.pallas_call(
        functools.partial(attend_back_body, causal),
        out_shape=half + [jax.ShapeDtypeStruct((2, queries.shape[1]), jnp.float32)],
        cost_estimate=estimate(12),
        compiler_params=pltpu.CompilerParams(vmem_limit_bytes=32 << 20),
    )(queries, keys_half, values_half, back_attended)


def self_block(stream, weights, small_params, slots, qkv_name, out_name, causal):
    normed = layer_norm(
        stream, small_params[:, slots.norm_gain], small_params[:, slots.norm_bias]
    )
    normed_half = to_half(normed)
    projected = matmul(normed_half, weights[qkv_name])
    queries = to_half(projected[:, :D] + small_params[:, slots.query_bias])
    keys_half = to_half(projected[:, D : 2 * D])
    values_half = to_half(projected[:, 2 * D :] + small_params[:, slots.value_bias])
    attended = attend(queries, keys_half, values_half, causal)
    output = (
        stream + matmul(attended, weights[out_name]) + small_params[:, slots.out_bias]
    )
    return (output, (stream, queries, keys_half, values_half), (normed_half, attended))


def self_block_back(
    saved, upstream, weights, small_params, slots, qkv_name, out_name, causal, vector_grads
):
    stream, queries, keys_half, values_half = saved
    grad_out = to_half(upstream)
    back_attended = to_half(matmul_t(grad_out, weights[out_name]))
    back_queries, back_keys, back_values, back_sums = attend_back(
        queries, keys_half, values_half, causal, back_attended
    )
    grad_proj = [back_queries, back_keys, back_values]
    back_normed = sum(
        matmul_t(part, weights[qkv_name][:, position * D : (position + 1) * D])
        for position, part in enumerate(grad_proj)
    )
    back_stream, back_gain, back_bias = norm_back(
        stream,
        small_params[:, slots.norm_gain],
        small_params[:, slots.norm_bias],
        back_normed,
    )
    vector_grads[slots.norm_gain] = back_gain
    vector_grads[slots.norm_bias] = back_bias
    vector_grads[slots.query_bias] = back_sums[0]
    vector_grads[slots.value_bias] = back_sums[1]
    vector_grads[slots.out_bias] = jnp.sum(upstream, axis=0)
    return (upstream + back_stream, grad_out, grad_proj)


def cross_block(stream, memory_half, weights, small_params):
    normed = layer_norm(
        stream, small_params[:, DecSlots.cross_gain], small_params[:, DecSlots.cross_bias]
    )
    normed_half = to_half(normed)
    queries = to_half(
        matmul(normed_half, weights["xq"]) + small_params[:, DecSlots.xquery_bias]
    )
    keyval = matmul(memory_half, weights["xk"])
    keys_half = to_half(keyval[:, :D])
    values_half = to_half(keyval[:, D:] + small_params[:, DecSlots.xvalue_bias])
    attended = attend(queries, keys_half, values_half, False)
    output = (
        stream + matmul(attended, weights["xo"]) + small_params[:, DecSlots.xout_bias]
    )
    return (output, (stream, queries, keys_half, values_half), (normed_half, attended))


def cross_block_back(saved, upstream, weights, small_params, vector_grads):
    stream, queries, keys_half, values_half = saved
    grad_out = to_half(upstream)
    back_attended = to_half(matmul_t(grad_out, weights["xo"]))
    grad_query, back_keys, back_values, back_sums = attend_back(
        queries, keys_half, values_half, False, back_attended
    )
    back_normed = matmul_t(grad_query, weights["xq"])
    grad_keyval = [back_keys, back_values]
    back_memory = matmul_t(back_keys, weights["xk"][:, :D]) + matmul_t(
        back_values, weights["xk"][:, D:]
    )
    back_stream, back_gain, back_bias = norm_back(
        stream,
        small_params[:, DecSlots.cross_gain],
        small_params[:, DecSlots.cross_bias],
        back_normed,
    )
    vector_grads[DecSlots.cross_gain] = back_gain
    vector_grads[DecSlots.cross_bias] = back_bias
    vector_grads[DecSlots.xquery_bias] = back_sums[0]
    vector_grads[DecSlots.xvalue_bias] = back_sums[1]
    vector_grads[DecSlots.xout_bias] = jnp.sum(upstream, axis=0)
    return (upstream + back_stream, back_memory, grad_out, grad_query, grad_keyval)


def mlp_block(stream, weights, small_params, slots, up_name, down_name):
    normed = layer_norm(
        stream, small_params[:, slots.mlp_gain], small_params[:, slots.mlp_bias]
    )
    normed_half = to_half(normed)
    up_bias = small_params[:, slots.up_bias : slots.up_bias + 4].T.reshape(-1)
    raised = matmul(normed_half, weights[up_name]) + up_bias
    active = to_half(gelu_exact(raised))
    output = (
        stream + matmul_t(active, weights[down_name]) + small_params[:, slots.down_bias]
    )
    return (output, (stream, raised), (normed_half, active))


def mlp_block_back(saved, upstream, weights, small_params, slots, up_name, down_name, vector_grads):
    stream, raised = saved
    grad_out = to_half(upstream)
    back_raised = gelu_back(raised, matmul(grad_out, weights[down_name]))
    bias_rows = jnp.sum(back_raised, axis=0).reshape(4, D)
    for quarter in range(4):
        vector_grads[slots.up_bias + quarter] = bias_rows[quarter]
    grad_raised = to_half(back_raised)
    back_normed = matmul_t(grad_raised, weights[up_name])
    back_stream, back_gain, back_bias = norm_back(
        stream, small_params[:, slots.mlp_gain], small_params[:, slots.mlp_bias], back_normed
    )
    vector_grads[slots.mlp_gain] = back_gain
    vector_grads[slots.mlp_bias] = back_bias
    vector_grads[slots.down_bias] = jnp.sum(upstream, axis=0)
    return (upstream + back_stream, grad_out, grad_raised)


def down_one(values):
    return jnp.pad(values, ((1, 0), (0, 0)))[:-1]


def up_one(values):
    return jnp.pad(values, ((0, 1), (0, 0)))[1:]


def stem_forward(mel_half, weights, small_params):
    bins, frames_in = mel_half.shape
    paired = mel_half.T.reshape(frames_in // 2, 2 * bins)
    mel_even, mel_odd = paired[:, :bins], paired[:, bins:]
    cols_even = jnp.concatenate([down_one(mel_odd), mel_even, mel_odd], axis=1)
    cols_odd = jnp.concatenate([mel_even, mel_odd, up_one(mel_even)], axis=1)
    pre_even = matmul_t(cols_even, weights["c1"]) + small_params[:, 0]
    pre_odd = matmul_t(cols_odd, weights["c1"]) + small_params[:, 0]
    act_even = to_half(gelu_exact(pre_even))
    act_odd = to_half(gelu_exact(pre_odd))
    taps = weights["c2"]
    conv_sum = (
        matmul(down_one(act_odd), taps[:, :D])
        + matmul(act_even, taps[:, D : 2 * D])
        + matmul(act_odd, taps[:, 2 * D :])
    )
    second_pre = conv_sum + small_params[:, 1]
    stream = gelu_exact(second_pre) + sinusoid(frames_in // 2, D)
    return (stream, (pre_even, pre_odd, second_pre), (cols_even, cols_odd, act_even, act_odd))


def stem_back(saved, upstream, weights, vector_grads):
    pre_even, pre_odd, second_pre = saved
    back_second = gelu_back(second_pre, upstream)
    vector_grads[1] = jnp.sum(back_second, axis=0)
    grad_second = to_half(back_second)
    taps = weights["c2"]
    back_even = gelu_back(pre_even, matmul_t(grad_second, taps[:, D : 2 * D]))
    back_odd = gelu_back(
        pre_odd,
        matmul_t(grad_second, taps[:, 2 * D :])
        + matmul_t(up_one(grad_second), taps[:, :D]),
    )
    vector_grads[0] = jnp.sum(back_even, axis=0) + jnp.sum(back_odd, axis=0)
    return (grad_second, to_half(back_even), to_half(back_odd))


def fill(values, rows):
    return jnp.pad(values, ((0, rows - values.shape[0]), (0, 0)))


def moments(weight, moment, square, gradient, factor, first_fix, second_fix):
    scaled = gradient * factor
    new_moment = BETA_ONE * moment + (1.0 - BETA_ONE) * scaled
    new_square = BETA_TWO * square + (1.0 - BETA_TWO) * scaled * scaled
    update = new_moment * first_fix / (jnp.sqrt(new_square * second_fix) + ADAM_EPS) + DECAY * weight
    return (new_moment, new_square, update)


def count_bad(values):
    return jnp.sum(jnp.where(jnp.isfinite(values), 0.0, 1.0))


def on_device(
    mel_frames,
    text_ids,
    text_lengths,
    language,
    vocab_mask,
    step_count,
    matrices,
    matrix_moment,
    matrix_square,
    embedding,
    embed_moment,
    embed_square,
    vectors,
    vector_moment,
    vector_square,
):
    names, bounds = layout(D, FF, MELS, TLEN)
    reps = lax.axis_size("rep")
    members = lax.axis_size("fsdp")
    replica = lax.axis_index("rep")
    member = lax.axis_index("fsdp")
    first_names = ("c1", "c2", "eq", "eo", "eu", "ed", "dp")
    last_names = ("dq", "do", "xq", "xk", "xo", "du", "dd")
    first_half = jnp.concatenate(
        [to_half(columns_of(matrices, bounds, piece)) for piece in first_names]
        + [to_half(vectors)],
        axis=1,
    )
    last_half = jnp.concatenate(
        [to_half(columns_of(matrices, bounds, piece)) for piece in last_names], axis=1
    )
    weights = {}
    for batch, batch_half in ((first_names, first_half), (last_names, last_half)):
        gathered = lax.all_gather(batch_half, "fsdp", axis=0, tiled=True)
        offset = 0
        for piece in batch:
            extent = bounds[piece][1] - bounds[piece][0]
            weights[piece] = gathered[:, offset : offset + extent]
            offset = offset + extent
        if batch is first_names:
            small_params = gathered[:, offset:].astype(jnp.float32)
    inputs_ids = jnp.concatenate([LANGTOK + language, text_ids[0, :-1]])[None, :]
    ids_all = lax.all_gather(
        jnp.concatenate([inputs_ids, text_ids], axis=1), ("rep", "fsdp"), axis=0, tiled=True
    ).reshape(reps, members, 2, TLEN)
    order = [(replica - shift) % reps for shift in range(reps)]
    ids_by_shift = [pick(ids_all, place, 0) for place in order]
    group_inputs = [ids[:, 0].reshape(-1) for ids in ids_by_shift]
    group_targets = [ids[:, 1].reshape(-1) for ids in ids_by_shift]
    counts_by_shift = [
        (
            lax.broadcasted_iota(jnp.int32, (members, TLEN), 1)
            < lax.dynamic_slice_in_dim(text_lengths, place * members, members)[:, None]
        ).reshape(-1)
        for place in order
    ]
    vocab_rows = embedding.shape[0]
    vocab_start = member * vocab_rows
    embed_half = to_half(embedding)
    vocab_iota = lax.broadcasted_iota(jnp.int32, (members * TLEN, vocab_rows), 1)
    input_hot = [to_half(ids[:, None] - vocab_start == vocab_iota) for ids in group_inputs]
    embedded = scatter_sum(
        matmul(input_hot[0], embed_half).astype(jnp.bfloat16), 3, True, 3
    ).astype(jnp.float32)
    enc_zero, stem_saved, stem_acts = stem_forward(mel_frames[0], weights, small_params)
    vocab_keep = lax.dynamic_slice_in_dim(vocab_mask, vocab_start, vocab_rows) == 1
    keep_column = vocab_keep.astype(jnp.float32)[:, None]
    shut_column = jnp.where(vocab_keep, 0.0, -jnp.inf)[:, None]
    vocab_count = jnp.sum(vocab_mask).astype(jnp.float32)
    pull_column = SMOOTH * keep_column / vocab_count
    local_targets = [(ids - vocab_start)[None, :] for ids in group_targets]
    groups_all = len(names) + 2
    columns = matrices.shape[1]
    column = lax.broadcasted_iota(jnp.int32, (groups_all, columns), 1)
    group = lax.broadcasted_iota(jnp.int32, (groups_all, columns), 0)
    group_of = sum((column >= bounds[piece][1]).astype(jnp.int32) for piece in names)
    in_group = group_of == group
    vectors, vector_moment, vector_square = vectors.T, vector_moment.T, vector_square.T
    counted_row = counts_by_shift[0].astype(jnp.float32)[None, :]
    enc_zero, (
        shut_column,
        keep_column,
        pull_column,
        local_targets,
        counted_row,
        in_group,
        vectors,
        vector_moment,
        vector_square,
    ) = settle(
        enc_zero,
        shut_column,
        keep_column,
        pull_column,
        local_targets,
        counted_row,
        in_group,
        vectors,
        vector_moment,
        vector_square,
    )
    enc_one, enc_self, enc_self_acts = self_block(
        enc_zero, weights, small_params, EncSlots, "eq", "eo", False
    )
    enc_two, enc_mlp, enc_mlp_acts = mlp_block(
        enc_one, weights, small_params, EncSlots, "eu", "ed"
    )
    memory_half = to_half(
        layer_norm(
            enc_two,
            small_params[:, EncSlots.final_gain],
            small_params[:, EncSlots.final_bias],
        )
    )
    cols_even, cols_odd, act_even, act_odd = stem_acts
    enc_early, enc_early_views = exchange(
        narrow_for([enc_self_acts[1], enc_self_acts[0]]),
        narrow_for([enc_mlp_acts[0]]),
        narrow_for([down_one(act_odd), act_even, act_odd]),
        wide_for(enc_mlp_acts[1]),
    )
    embedded, (enc_early,) = settle(embedded, enc_early)
    dec_zero = embedded + weights["dp"].T.astype(jnp.float32)
    dec_one, dec_self, dec_self_acts = self_block(
        dec_zero, weights, small_params, DecSlots, "dq", "do", True
    )
    dec_two, dec_cross, dec_cross_acts = cross_block(dec_one, memory_half, weights, small_params)
    dec_three, dec_mlp, dec_mlp_acts = mlp_block(
        dec_two, weights, small_params, DecSlots, "du", "dd"
    )
    frames = memory_half.shape[0]
    dec_early, dec_early_views = exchange(
        narrow_for([dec_self_acts[1], dec_self_acts[0]]),
        narrow_for([dec_mlp_acts[0]]),
        wide_for(dec_mlp_acts[1]),
        narrow_for(
            [fill(dec_cross_acts[0], frames), fill(dec_cross_acts[1], frames), memory_half]
        ),
    )
    final_out = layer_norm(
        dec_three,
        small_params[:, DecSlots.final_gain],
        small_params[:, DecSlots.final_bias],
    )
    final_half = to_half(final_out)
    gathered_hidden = gather_rows(final_half, 5)
    stats = join_stats(
        vocab_stats(gathered_hidden, embed_half, shut_column, keep_column, local_targets[0]), 0
    )
    log_norm, target_logit, logit_total = stats[0], stats[1], stats[2]
    log_norm, (dec_early,) = settle(log_norm, dec_early)
    entropy = log_norm - (1.0 - SMOOTH) * target_logit - SMOOTH * logit_total / vocab_count
    norm_and_loss = jnp.stack([log_norm, jnp.where(counts_by_shift[0], entropy, 0.0)])
    final_by_rep, norms_by_rep = gather_reps(
        [final_half, norm_and_loss], 7
    )
    norms_by_shift = [
        pick(norms_by_rep, place, 0) for place in order
    ]
    hidden_by_shift = [gathered_hidden] + [
        lax.all_gather(pick(final_by_rep, place, 0), "fsdp", axis=0, tiled=True)
        for place in order[1:]
    ]
    loss_sum = sum(jnp.sum(part[1]) for part in norms_by_shift)

    head_grad, hidden_part = own_slopes(
        jnp.where(counts_by_shift[0][:, None], gathered_hidden, jnp.bfloat16(0.0)),
        embed_half,
        shut_column,
        pull_column,
        local_targets[0],
        norms_by_shift[0][0:1],
        counted_row,
    )
    back_hidden = scatter_sum(hidden_part, 6, True, 6)
    vector_grads = {}
    back_three, final_gain, final_bias = norm_back(
        dec_three,
        small_params[:, DecSlots.final_gain],
        small_params[:, DecSlots.final_bias],
        back_hidden,
    )
    vector_grads[DecSlots.final_gain] = final_gain
    vector_grads[DecSlots.final_bias] = final_bias
    back_two, dec_down_grad, dec_up_grad = mlp_block_back(
        dec_mlp, back_three, weights, small_params, DecSlots, "du", "dd", vector_grads
    )
    back_two, (hidden_by_shift,) = settle(back_two, hidden_by_shift)
    back_one, back_memory, xout_grad, xquery_grad, xkeyval_grad = cross_block_back(
        dec_cross, back_two, weights, small_params, vector_grads
    )
    back_zero, dec_out_grad, dec_qkv_grad = self_block_back(
        dec_self, back_one, weights, small_params, DecSlots, "dq", "do", True, vector_grads
    )
    dec_late, dec_late_views = exchange(
        narrow_for([dec_down_grad]),
        wide_for(dec_up_grad),
        wide_for(dec_out_grad, *dec_qkv_grad),
        wide_for(fill(xquery_grad, frames), fill(xout_grad, frames), *xkeyval_grad),
    )
    unit = unit_width()
    share = 4 * D // unit
    cores = CORES
    groups = [list(range(place, members, cores)) for place in range(cores)]
    back_half = to_half(back_zero)
    (back_stack,) = gather_reps([back_half], 8)
    gathered_back = lax.all_gather(back_stack, "fsdp", axis=0)
    for shift in range(1, reps):
        head_grad = other_slopes(
            head_grad,
            jnp.where(counts_by_shift[shift][:, None], hidden_by_shift[shift], jnp.bfloat16(0.0)),
            embed_half,
            shut_column,
            pull_column,
            local_targets[shift],
            norms_by_shift[shift][0:1],
        )
    dec_late, (head_grad,) = settle(dec_late, head_grad)
    early = len(dec_early)
    attn_narrow, up_narrow, down_wide, cross_narrow = dec_early_views
    down_narrow, up_wide, attn_wide, cross_wide = [
        shifted(view, early) for view in dec_late_views
    ]
    dec_products = products(
        [
            (down_narrow, down_wide),
            (up_narrow, up_wide),
            (attn_narrow, attn_wide),
            (cross_narrow, cross_wide),
        ],
        dec_early + dec_late,
        True,
    )
    back_memory, (dec_products,) = settle(back_memory, dec_products)
    dec_rows = lax.psum_scatter(
        dec_products, "fsdp", scatter_dimension=0, axis_index_groups=groups, tiled=True
    )
    back_enc_two, enc_gain, enc_bias = norm_back(
        enc_two,
        small_params[:, EncSlots.final_gain],
        small_params[:, EncSlots.final_bias],
        back_memory,
    )
    vector_grads[EncSlots.final_gain] = enc_gain
    vector_grads[EncSlots.final_bias] = enc_bias
    back_enc_one, enc_down_grad, enc_up_grad = mlp_block_back(
        enc_mlp, back_enc_two, weights, small_params, EncSlots, "eu", "ed", vector_grads
    )
    enc_late, enc_late_views = exchange(narrow_for([enc_down_grad]), wide_for(enc_up_grad))
    back_enc_zero, enc_out_grad, enc_qkv_grad = self_block_back(
        enc_self, back_enc_one, weights, small_params, EncSlots, "eq", "eo", False, vector_grads
    )
    grad_second, grad_even, grad_odd = stem_back(stem_saved, back_enc_zero, weights, vector_grads)
    grad_second, (gathered_back, enc_late) = settle(grad_second, gathered_back, enc_late)
    enc_last, enc_last_views = exchange(
        wide_for(enc_out_grad, *enc_qkv_grad), wide_for(grad_second)
    )
    first_grad = tmatmul(cols_even, grad_even) + tmatmul(cols_odd, grad_odd)
    loose_rows = packed_rows(
        [first_grad, back_zero] + [vector_grads[column] for column in range(NVEC)], share * 128
    )
    hot_all = to_half(
        ids_all[:, :, 0].transpose(1, 0, 2).reshape(-1, 1)
        - vocab_start
        == lax.broadcasted_iota(jnp.int32, (reps * members * TLEN, vocab_rows), 1)
    )
    lookup = tmatmul(hot_all, gathered_back.reshape(-1, D))
    loose_rows, (lookup, enc_last) = settle(loose_rows, lookup, enc_last)
    embed_grad = head_grad + lookup
    loose = jnp.sum(quad_swap(loose_rows).reshape(share, 128, D), axis=0).T
    embed_totals = (jnp.sum(embed_grad * embed_grad), count_bad(embed_grad))
    loose, (embed_totals,) = settle(loose, embed_totals)
    early, late = len(enc_early), len(enc_early) + len(enc_late)
    attn_narrow, up_narrow, conv_narrow, down_wide = enc_early_views
    down_narrow, up_wide = [shifted(view, early) for view in enc_late_views]
    attn_wide, conv_wide = [shifted(view, late) for view in enc_last_views]
    enc_units = rows_of(
        [
            products(
                [
                    (down_narrow, down_wide),
                    (up_narrow, up_wide),
                    (attn_narrow, attn_wide),
                    (conv_narrow, conv_wide),
                ],
                enc_early + enc_late + enc_last,
                False,
            ),
            loose,
        ],
        4,
    )
    dec_rows, (enc_units,) = settle(dec_rows, enc_units)
    enc_quads, loose_units = enc_units
    per = D // unit
    dec_quads = quad_rows(dec_rows.reshape(cores, -1, 4 * unit))
    loose_own = jnp.transpose(loose_units, (1, 0, 2)).reshape(-1, share * 128)
    odd_end = 3 * MELS + TLEN
    vec_grad = loose_own[:, odd_end : odd_end + NVEC]
    last_unit = jnp.pad(loose_own[:, :odd_end], ((0, 0), (0, unit - odd_end)))
    first_lane = lax.broadcasted_iota(jnp.int32, (1, 2), 1) == 0
    once = [enc_quads[:, :, : 3 * unit], enc_quads[: 3 * per, :, 3 * unit :], loose_own]
    first = (replica == 0).astype(jnp.float32)
    squares = embed_totals[0] + sum(jnp.sum(part * part) for part in once)
    bad = embed_totals[1] + sum(count_bad(part) for part in once)
    sums = total_of(
        jnp.where(
            first_lane,
            jnp.sum(dec_rows * dec_rows) + first * squares,
            count_bad(dec_rows) + first * bad,
        ),
        1,
        True,
    )
    total_squares, total_bad = sums[0, 0], sums[0, 1]
    gradient_norm = jnp.sqrt(total_squares)
    factor = CLIP_AT / jnp.maximum(gradient_norm, CLIP_AT)
    steps = step_count[0].astype(jnp.float32)
    first_fix = 1.0 / (1.0 - jnp.power(jnp.float32(BETA_ONE), steps))
    second_fix = 1.0 / (1.0 - jnp.power(jnp.float32(BETA_TWO), steps))
    scalars = jnp.stack([factor, first_fix, second_fix])
    emb_moment, emb_square, emb_update, emb_sums = embed_moments(
        scalars, embedding, embed_moment, embed_square, head_grad, lookup
    )
    emb_sums, (dec_quads,) = settle(emb_sums, dec_quads)
    mat_moment, mat_square, mat_update, mat_sums = matrix_moments(
        scalars, matrices, matrix_moment, matrix_square, enc_quads, dec_quads, last_unit
    )
    vec_moment, vec_square, vec_update = moments(
        vectors, vector_moment, vector_square, vec_grad.T, factor, first_fix, second_fix
    )
    by_column = jnp.transpose(mat_sums, (1, 0, 2)).reshape(2, -1)[:, :columns]
    lone = jnp.stack([jnp.sum(vectors * vectors), jnp.sum(vec_update * vec_update)])
    place = lax.broadcasted_iota(jnp.int32, (2, groups_all), 1)
    both = jnp.sum(jnp.where(in_group[None], by_column[:, None, :], 0.0), axis=2)
    both = jnp.where(place == groups_all - 2, jnp.sum(emb_sums, axis=(0, 2))[:, None], both)
    both = jnp.where(place == groups_all - 1, lone[:, None], both)
    norms = jnp.sqrt(total_of(both, 2))
    weight_norms, update_norms = norms[0], norms[1]
    ratio = weight_norms / update_norms
    ratio_columns = jnp.sum(jnp.where(in_group, ratio[:, None], 0.0), axis=0)
    new_matrices = matrices - RATE * ratio_columns[None, :] * mat_update
    new_embedding = embedding - RATE * ratio[len(names)] * emb_update
    new_vectors = vectors - RATE * ratio[len(names) + 1] * vec_update
    mean_loss = loss_sum / jnp.sum(text_lengths).astype(jnp.float32)
    group_norms = jnp.stack([weight_norms, update_norms], axis=1)
    return (
        mean_loss,
        total_bad.astype(jnp.int32),
        gradient_norm,
        group_norms,
        new_matrices,
        mat_moment,
        mat_square,
        new_embedding,
        emb_moment,
        emb_square,
        new_vectors.T,
        vec_moment.T,
        vec_square.T,
    )


def solution(mesh):
    placed = (
        P(("rep", "fsdp"), None, None),
        P(("rep", "fsdp"), None),
        P(),
        P(("rep", "fsdp")),
        P(),
        P(),
        P("fsdp", None),
        P("fsdp", None),
        P("fsdp", None),
        P("fsdp", None),
        P("fsdp", None),
        P("fsdp", None),
        P("fsdp", None),
        P("fsdp", None),
        P("fsdp", None),
    )
    return jax.shard_map(
        on_device,
        mesh=mesh,
        in_specs=placed,
        out_specs=(
            P(),
            P(),
            P(),
            P(),
            P("fsdp", None),
            P("fsdp", None),
            P("fsdp", None),
            P("fsdp", None),
            P("fsdp", None),
            P("fsdp", None),
            P("fsdp", None),
            P("fsdp", None),
            P("fsdp", None),
        ),
        check_vma=False,
    )
```
